128 devices in a mesh: gy: 16 (over z_hi, x, core), gz: 8 (over z_lo, y).
Axes of the slice: x: 4, y: 4, z: 4 (z_hi: 2, z_lo: 2; z = z_hi * 2 + z_lo), core: 2. Of those that a mesh axis runs over, the one named last changes fastest.
Arguments:
- reference_image: bfloat16 [64, 1024, 4096], P(None, 'gy', 'gz'), may hold values from -6 to 6
- deformed: bfloat16 [64, 1024, 4096], P(None, 'gy', 'gz'), may hold values from -12 to 12
- displacement: bfloat16 [3, 64, 1024, 4096], P(None, None, 'gy', 'gz'), may hold values from -1 to 1
- plane_factors: float32 [2, 32, 8, 128], P(None, None, None, 'gy'), may hold values from -2.5 to 2.5
- depth_factors: float32 [2, 32, 4096], P(None, None, 'gz'), may hold values from -6 to 6
Outputs:
- residual: bfloat16 [64, 1024, 4096], P(None, 'gy', 'gz')
- step_plane: float32 [2, 32, 8, 128], P(None, None, None, 'gy')
- step_depth: float32 [2, 32, 4096], P(None, None, 'gz')
The draws below stay inside these ranges and needn't reach their ends.
All inputs are finite; a program needn't handle non-finite values.
Results may differ from the reference program's by a relative error of at most 0.0004.
Values may be sent and summed in bfloat16 or wider, within the bound.
A program may use at most 256 MiB of HBM per device.

```python
import jax
import jax.numpy as jnp
from jax import lax

SLAB = 64
STRIP_Y = 64
RANK = 32
KNOT = 8
NODES_X = 8
FULL_Y = 1024
FULL_Z = 4096
NODES_Y = 128
N_GY = 16


def draw_deformed(key, part):
    along_y = (jnp.arange(FULL_Y, dtype=jnp.float32) / FULL_Y)[None, :, None]
    along_z = (jnp.arange(FULL_Z, dtype=jnp.float32) / FULL_Z)[None, None, :]
    scale = 0.4 + 1.2 * along_y + 1.2 * along_z
    noise = jax.random.truncated_normal(key, -4.0, 4.0, (SLAB, FULL_Y, FULL_Z), jnp.float32)
    values = scale * noise
    return values.astype(jnp.bfloat16)


def block_levels(stream_key, shape, pieces, least, largest):
    gain, own = 1.0, jax.random.fold_in(stream_key, 6)
    for position, parts in pieces:
        steps = jnp.exp(jax.random.uniform(jax.random.fold_in(own, position), (parts,), jnp.float32, least / len(pieces), largest / len(pieces)))
        gain = gain * jnp.repeat(steps, shape[position] // parts).reshape([-1 if axis == position else 1 for axis in range(len(shape))])
    return gain


def bell_draw(key, shape, width, most, cuts=(), held_as=jnp.bfloat16):
    values = jax.random.normal(key, shape, jnp.float32) * width
    if len(cuts) > 0:
        values = block_levels(key, shape, cuts, -0.22, 0.18) * values
    return jnp.clip(values, min=-most, max=most).astype(held_as)


def setup_inputs(seed: int = 0) -> dict:
    splits = jax.random.split(jax.random.key(seed), 6)
    return {
        "reference_image": bell_draw(splits[0], (SLAB, FULL_Y, FULL_Z), 1.0, 6.0, ((1, 16), (2, 8))),
        "deformed": draw_deformed(jax.random.fold_in(splits[5], 71), 0),
        "displacement": jnp.clip(jax.random.uniform(splits[2], (3, SLAB, FULL_Y, FULL_Z), jnp.float32, -1.0, 1.0) * block_levels(splits[2], (3, SLAB, FULL_Y, FULL_Z), ((2, 16), (3, 8)), -0.4, 0.0), -1.0, 1.0).astype(jnp.bfloat16),
        "plane_factors": bell_draw(splits[3], (2, RANK, NODES_X, NODES_Y), 0.18, 2.5, ((3, 16),), jnp.float32),
        "depth_factors": bell_draw(splits[4], (2, RANK, FULL_Z), 1.0, 6.0, ((2, 8),), jnp.float32),
    }


epsilon = 1e-6
damping = 0.01
highest = lax.Precision.HIGHEST


def tent_weights(shift):
    moved = shift.astype(jnp.float32)
    return [jnp.maximum(0.0, 1.0 - jnp.abs(moved - offset)) for offset in (-1.0, 0.0, 1.0)]


def warp_image(padded, displacement):
    depth_x, width_y, width_z = displacement.shape[1:]
    weight_x = tent_weights(displacement[0])
    weight_y = tent_weights(displacement[1])
    weight_z = tent_weights(displacement[2])
    summed = jnp.zeros((depth_x, width_y, width_z), jnp.float32)
    for along_x in range(3):
        for along_y in range(3):
            partial_z = jnp.zeros((depth_x, width_y, width_z), jnp.float32)
            for along_z in range(3):
                window = padded[along_x:along_x + depth_x, along_y:along_y + width_y, along_z:along_z + width_z]
                partial_z = partial_z + weight_z[along_z] * window.astype(jnp.float32)
            summed = summed + weight_x[along_x] * weight_y[along_y] * partial_z
    return summed


def expand_nodes(nodes):
    return jnp.repeat(jnp.repeat(nodes, KNOT, axis=2), KNOT, axis=3)


def reduce_nodes(field):
    leading = field.shape[:-2]
    depth_x, width_y = field.shape[-2:]
    shaped = field.reshape(leading + (depth_x // KNOT, KNOT, width_y // KNOT, KNOT))
    return jnp.sum(shaped, axis=(-3, -1))


def contract_rank(left, right):
    return lax.dot_general(left, right, (((0,), (0,)), ((), ())), precision=highest)


def contract_cells(left, right):
    return jnp.dot(left, right, precision=highest)


def contract_depth(left, right):
    return lax.dot_general(left, right, (((1,), (1,)), ((), ())), precision=highest)


def strip_terms(image, padded, displacement, plane_voxels, depth_factors):
    depth_x, width_y, width_z = image.shape
    cells = depth_x * width_y
    warped = warp_image(padded, displacement).reshape(cells, width_z)
    values = image.astype(jnp.float32).reshape(cells, width_z)
    flat_plane = plane_voxels.reshape(2, plane_voxels.shape[1], cells)
    contrast = contract_rank(flat_plane[0], depth_factors[0])
    brightness = contract_rank(flat_plane[1], depth_factors[1])
    misfit = warped - contrast * values - brightness
    product = misfit * values
    squares = values * values
    grad_depth = -jnp.stack([contract_cells(flat_plane[0], product), contract_cells(flat_plane[1], misfit)])
    level_sum = jnp.sum(flat_plane[1] * flat_plane[1], axis=1)
    diag_depth = jnp.stack([contract_cells(flat_plane[0] * flat_plane[0], squares),
                            jnp.broadcast_to(level_sum[:, None], (level_sum.shape[0], width_z))])
    grad_voxels = -jnp.stack([contract_depth(depth_factors[0], product), contract_depth(depth_factors[1], misfit)])
    diag_voxels = contract_depth(depth_factors[0] * depth_factors[0], squares)
    grad_plane = reduce_nodes(grad_voxels.reshape(2, -1, depth_x, width_y))
    first_diag = reduce_nodes(diag_voxels.reshape(-1, depth_x, width_y))
    depth_level = KNOT * KNOT * jnp.sum(depth_factors[1] * depth_factors[1], axis=1)
    diag_plane = jnp.stack([first_diag, jnp.broadcast_to(depth_level[:, None, None], first_diag.shape)])
    squared_sum = jnp.sum(misfit * misfit)
    residual = misfit.reshape(depth_x, width_y, width_z).astype(jnp.bfloat16)
    return residual, squared_sum, grad_plane, diag_plane, grad_depth, diag_depth


def reference(reference_image, deformed, displacement, plane_factors, depth_factors):
    padded = jnp.pad(deformed, 1)
    plane_voxels = expand_nodes(plane_factors)

    def one_strip(strip):
        start = (strip * STRIP_Y).astype(jnp.int32)
        image_part = lax.dynamic_slice_in_dim(reference_image, start, STRIP_Y, 1)
        padded_part = lax.dynamic_slice_in_dim(padded, start, STRIP_Y + 2, 1)
        shift_part = lax.dynamic_slice_in_dim(displacement, start, STRIP_Y, 2)
        plane_part = lax.dynamic_slice_in_dim(plane_voxels, start, STRIP_Y, 3)
        return strip_terms(image_part, padded_part, shift_part, plane_part, depth_factors)

    strips = jnp.arange(N_GY, dtype=jnp.int32)
    residual, squared_sums, grad_plane, diag_plane, grad_depth, diag_depth = lax.map(one_strip, strips)
    residual = jnp.transpose(residual, (1, 0, 2, 3)).reshape(SLAB, FULL_Y, FULL_Z)
    energy = jnp.sum(squared_sums)
    grad_plane = jnp.transpose(grad_plane, (1, 2, 3, 0, 4)).reshape(2, RANK, NODES_X, NODES_Y)
    diag_plane = jnp.transpose(diag_plane, (1, 2, 3, 0, 4)).reshape(2, RANK, NODES_X, NODES_Y)
    grad_depth = jnp.sum(grad_depth, axis=0)
    diag_depth = jnp.sum(diag_depth, axis=0)
    lam_plane = damping * RANK * energy / (NODES_X * NODES_Y)
    lam_depth = damping * energy / FULL_Z
    step_plane = -grad_plane / (diag_plane + lam_plane + epsilon)
    step_depth = -grad_depth / (diag_depth + lam_depth + epsilon)
    return residual, step_plane, step_depth
```

```python
import jax
import jax.numpy as jnp
from jax import lax
from jax.experimental import pallas as pl
from jax.experimental.pallas import tpu as pltpu
from jax.sharding import PartitionSpec as P

RANK = 32
KNOT = 8

epsilon = 1e-06
damping = 0.01
highest = lax.Precision.HIGHEST

ROWS = 16
LANES = 256


def neighbours(part, axis, forward):
    count = lax.axis_size(axis)
    if forward:
        pairs = [(i, i + 1) for i in range(count - 1)]
    else:
        pairs = [(i + 1, i) for i in range(count - 1)]
    return lax.ppermute(part, axis, pairs)


def padded_deformed(deformed):
    depth_x, width_y, width_z = deformed.shape
    low_y = neighbours(deformed[:, width_y - 1 :, :], "gy", True)
    high_y = neighbours(deformed[:, :1, :], "gy", False)
    gap_y = jnp.zeros((depth_x, 6, width_z), deformed.dtype)
    rimmed = jnp.concatenate([deformed, high_y, gap_y, low_y], axis=1)
    low_z = neighbours(rimmed[:, :, width_z - 1 :], "gz", True)
    high_z = neighbours(rimmed[:, :, :1], "gz", False)
    gap_z = jnp.zeros((depth_x, rimmed.shape[1], 126), deformed.dtype)
    return jnp.concatenate([rimmed, high_z, gap_z, low_z], axis=2)


def lerp(base, other, weight):
    return base + weight * (other - base)


def strip_kernel(dpad_ref, disp_ref, image_ref, contrast_ref, bright_ref,
                 res_ref, prod_ref, mis_ref, sq_ref, energy_ref, shifts_ref):
    block = pl.program_id(0)
    depth_x = dpad_ref.shape[0]
    pad_y, pad_z = dpad_ref.shape[1], dpad_ref.shape[2]
    width_y, width_z = image_ref.shape[1], image_ref.shape[2]

    def source_plane(p, carry):
        plane_x = block * KNOT - 1 + p
        valid = jnp.logical_and(plane_x >= 0, plane_x < depth_x)
        safe = jnp.clip(plane_x, 0, depth_x - 1)
        plane = dpad_ref[safe].astype(jnp.float32)
        plane = jnp.where(valid, plane, 0.0)
        by_y = (pltpu.roll(plane, 1, 0), plane, pltpu.roll(plane, pad_y - 1, 0))
        for b in range(3):
            rows = by_y[b][:width_y]
            by_z = (pltpu.roll(rows, 1, 1), rows, pltpu.roll(rows, pad_z - 1, 1))
            for c in range(3):
                shifts_ref[p, 3 * b + c] = by_z[c][:, :width_z]
        return carry

    lax.fori_loop(0, KNOT + 2, source_plane, 0)

    chunks_y = width_y // ROWS
    chunks_z = width_z // LANES

    def chunk(k, energy):
        r0 = pl.multiple_of((k // chunks_z) * ROWS, ROWS)
        c0 = pl.multiple_of((k % chunks_z) * LANES, LANES)
        rs = pl.ds(r0, ROWS)
        cs = pl.ds(c0, LANES)
        contrast = contrast_ref[0, rs, cs]
        bright = bright_ref[0, rs, cs]

        def plane(xl, acc):
            prod_acc, mis_acc, sq_acc, e_acc = acc

            def src(a, b, c):
                return shifts_ref[xl + 1 + a, 3 * (b + 1) + (c + 1), rs, cs]

            sx = disp_ref[0, xl, rs, cs].astype(jnp.float32)
            sy = disp_ref[1, xl, rs, cs].astype(jnp.float32)
            sz = disp_ref[2, xl, rs, cs].astype(jnp.float32)
            gx, gy, gz = sx > 0, sy > 0, sz > 0
            ax, ay, az = jnp.abs(sx), jnp.abs(sy), jnp.abs(sz)
            xs = {}
            for b in (-1, 0, 1):
                for c in (-1, 0, 1):
                    xs[b, c] = jnp.where(gx, src(1, b, c), src(-1, b, c))
            y0 = {c: jnp.where(gy, src(0, 1, c), src(0, -1, c)) for c in (-1, 0, 1)}
            y1 = {c: jnp.where(gy, xs[1, c], xs[-1, c]) for c in (-1, 0, 1)}
            centre = src(0, 0, 0)
            z00 = jnp.where(gz, src(0, 0, 1), src(0, 0, -1))
            z01 = jnp.where(gz, y0[1], y0[-1])
            z10 = jnp.where(gz, xs[0, 1], xs[0, -1])
            z11 = jnp.where(gz, y1[1], y1[-1])
            l00 = lerp(centre, z00, az)
            l01 = lerp(y0[0], z01, az)
            l10 = lerp(xs[0, 0], z10, az)
            l11 = lerp(y1[0], z11, az)
            m0 = lerp(l00, l01, ay)
            m1 = lerp(l10, l11, ay)
            warped = lerp(m0, m1, ax)
            values = image_ref[xl, rs, cs].astype(jnp.float32)
            misfit = warped - contrast * values - bright
            res_ref[xl, rs, cs] = misfit.astype(res_ref.dtype)
            return (prod_acc + misfit * values, mis_acc + misfit,
                    sq_acc + values * values, e_acc + misfit * misfit)

        zero = jnp.zeros((ROWS, LANES), jnp.float32)
        prod_acc, mis_acc, sq_acc, e_acc = lax.fori_loop(
            0, KNOT, plane, (zero, zero, zero, energy))
        prod_ref[0, rs, cs] = prod_acc
        mis_ref[0, rs, cs] = mis_acc
        sq_ref[0, rs, cs] = sq_acc
        return e_acc

    energy = lax.fori_loop(0, chunks_y * chunks_z, chunk,
                           jnp.zeros((ROWS, LANES), jnp.float32))
    energy_ref[0] = energy


def strip_sums(dpad, displacement, image, contrast_y, bright_y):
    depth_x, width_y, width_z = image.shape
    nodes = depth_x // KNOT
    f32 = jnp.float32
    block_sum = jax.ShapeDtypeStruct((nodes, width_y, width_z), f32)
    node_spec = pl.BlockSpec((1, width_y, width_z), lambda i: (i, 0, 0))
    return pl.pallas_call(
        strip_kernel,
        grid=(nodes,),
        in_specs=[
            pl.BlockSpec(memory_space=pltpu.VMEM),
            pl.BlockSpec((3, KNOT, width_y, width_z), lambda i: (0, i, 0, 0)),
            pl.BlockSpec((KNOT, width_y, width_z), lambda i: (i, 0, 0)),
            node_spec,
            node_spec,
        ],
        out_specs=[
            pl.BlockSpec((KNOT, width_y, width_z), lambda i: (i, 0, 0)),
            node_spec,
            node_spec,
            node_spec,
            pl.BlockSpec((1, ROWS, LANES), lambda i: (i, 0, 0)),
        ],
        out_shape=[
            jax.ShapeDtypeStruct(image.shape, jnp.bfloat16),
            block_sum,
            block_sum,
            block_sum,
            jax.ShapeDtypeStruct((nodes, ROWS, LANES), f32),
        ],
        scratch_shapes=[pltpu.VMEM((KNOT + 2, 9, width_y, width_z), f32)],
        compiler_params=pltpu.CompilerParams(
            dimension_semantics=("arbitrary",), vmem_limit_bytes=60 * 1024 * 1024),
    )(dpad, displacement, image, contrast_y, bright_y)


def node_sums(field):
    nodes, width_y, width_z = field.shape
    return field.reshape(nodes, width_y // KNOT, KNOT, width_z).sum(axis=2)


def local(reference_image, deformed, displacement, plane_factors, depth_factors):
    dpad = padded_deformed(deformed)
    fields = jnp.einsum("krij,krz->kijz", plane_factors, depth_factors, precision=highest)
    fields = jnp.repeat(fields, KNOT, axis=2)
    residual, prod, mis, sq, energy_parts = strip_sums(
        dpad, displacement, reference_image, fields[0], fields[1])
    prod, mis, sq = node_sums(prod), node_sums(mis), node_sums(sq)
    local_energy = jnp.sum(energy_parts)

    first, second = plane_factors[0], plane_factors[1]
    grad_depth = -jnp.stack([
        jnp.einsum("rij,ijz->rz", first, prod, precision=highest),
        jnp.einsum("rij,ijz->rz", second, mis, precision=highest)])
    first_depth = jnp.einsum("rij,ijz->rz", first * first, sq, precision=highest)
    level_sum = KNOT * KNOT * jnp.sum(second * second, axis=(1, 2))
    grad_plane = -jnp.stack([
        jnp.einsum("rz,ijz->rij", depth_factors[0], prod, precision=highest),
        jnp.einsum("rz,ijz->rij", depth_factors[1], mis, precision=highest)])
    first_diag = jnp.einsum("rz,ijz->rij", depth_factors[0] * depth_factors[0], sq, precision=highest)
    depth_level = KNOT * KNOT * jnp.sum(depth_factors[1] * depth_factors[1], axis=1)

    grad_plane, first_diag, depth_level, row_energy = lax.psum(
        (grad_plane, first_diag, depth_level, local_energy), "gz")
    grad_depth, first_depth, level_sum, energy = lax.psum(
        (grad_depth, first_depth, level_sum, row_energy), "gy")

    nodes_x = plane_factors.shape[2]
    nodes_y = plane_factors.shape[3] * lax.axis_size("gy")
    full_z = depth_factors.shape[2] * lax.axis_size("gz")
    diag_plane = jnp.stack(
        [first_diag, jnp.broadcast_to(depth_level[:, None, None], first_diag.shape)])
    lam_plane = damping * RANK * energy / (nodes_x * nodes_y)
    lam_depth = damping * energy / full_z
    step_plane = -grad_plane / (diag_plane + lam_plane + epsilon)
    diag_depth = jnp.stack([first_depth, jnp.broadcast_to(level_sum[:, None], first_depth.shape)])
    step_depth = -grad_depth / (diag_depth + lam_depth + epsilon)
    return (residual, step_plane, step_depth)


def solution(mesh):
    placed = (
        P(None, "gy", "gz"),
        P(None, "gy", "gz"),
        P(None, None, "gy", "gz"),
        P(None, None, None, "gy"),
        P(None, None, "gz"),
    )
    return jax.shard_map(
        local,
        mesh=mesh,
        in_specs=placed,
        out_specs=(P(None, "gy", "gz"), P(None, None, None, "gy"), P(None, None, "gz")),
        check_vma=False,
    )
```

```python
import functools

import jax
import jax.numpy as jnp
from jax import lax
from jax.experimental import pallas as pl
from jax.experimental.pallas import tpu as pltpu
from jax.sharding import PartitionSpec as P

RANK = 32
KNOT = 8

epsilon = 1e-06
damping = 0.01
highest = lax.Precision.HIGHEST

ROWS = 16
LANES = 256


def neighbours(part, axis, forward):
    count = lax.axis_size(axis)
    if forward:
        pairs = [(i, i + 1) for i in range(count - 1)]
    else:
        pairs = [(i + 1, i) for i in range(count - 1)]
    return lax.ppermute(part, axis, pairs)


def padded_deformed(deformed):
    depth_x, width_y, width_z = deformed.shape
    low_y = neighbours(deformed[:, width_y - 1 :, :], "gy", True)
    high_y = neighbours(deformed[:, :1, :], "gy", False)
    gap_y = jnp.zeros((depth_x, 6, width_z), deformed.dtype)
    rimmed = jnp.concatenate([deformed, high_y, gap_y, low_y], axis=1)
    low_z = neighbours(rimmed[:, :, width_z - 1 :], "gz", True)
    high_z = neighbours(rimmed[:, :, :1], "gz", False)
    gap_z = jnp.zeros((depth_x, rimmed.shape[1], 126), deformed.dtype)
    return jnp.concatenate([rimmed, high_z, gap_z, low_z], axis=2)


def lerp(base, other, weight):
    return base + weight * (other - base)


def strip_kernel(dpad_ref, disp_ref, image_ref, contrast_ref, bright_ref,
                 res_ref, prod_ref, mis_ref, sq_ref, energy_ref, shifts_ref):
    block = pl.program_id(0)
    depth_x = dpad_ref.shape[0]
    pad_y, pad_z = dpad_ref.shape[1], dpad_ref.shape[2]
    width_y, width_z = image_ref.shape[1], image_ref.shape[2]

    def source_plane(p, carry):
        plane_x = block * KNOT - 1 + p
        valid = jnp.logical_and(plane_x >= 0, plane_x < depth_x)
        safe = jnp.clip(plane_x, 0, depth_x - 1)
        plane = dpad_ref[safe].astype(jnp.float32)
        plane = jnp.where(valid, plane, 0.0)
        by_y = (pltpu.roll(plane, 1, 0), plane, pltpu.roll(plane, pad_y - 1, 0))
        for b in range(3):
            rows = by_y[b][:width_y]
            by_z = (pltpu.roll(rows, 1, 1), rows, pltpu.roll(rows, pad_z - 1, 1))
            for c in range(3):
                shifts_ref[p, 3 * b + c] = by_z[c][:, :width_z]
        return carry

    lax.fori_loop(0, KNOT + 2, source_plane, 0)

    chunks_y = width_y // ROWS
    chunks_z = width_z // LANES

    def chunk(k, energy):
        r0 = pl.multiple_of((k // chunks_z) * ROWS, ROWS)
        c0 = pl.multiple_of((k % chunks_z) * LANES, LANES)
        rs = pl.ds(r0, ROWS)
        cs = pl.ds(c0, LANES)
        contrast = contrast_ref[0, rs, cs]
        bright = bright_ref[0, rs, cs]

        def plane(xl, acc):
            prod_acc, mis_acc, sq_acc, e_acc = acc

            def src(a, b, c):
                return shifts_ref[xl + 1 + a, 3 * (b + 1) + (c + 1), rs, cs]

            sx = disp_ref[0, xl, rs, cs].astype(jnp.float32)
            sy = disp_ref[1, xl, rs, cs].astype(jnp.float32)
            sz = disp_ref[2, xl, rs, cs].astype(jnp.float32)
            gx, gy, gz = sx > 0, sy > 0, sz > 0
            ax, ay, az = jnp.abs(sx), jnp.abs(sy), jnp.abs(sz)
            xs = {}
            for b in (-1, 0, 1):
                for c in (-1, 0, 1):
                    xs[b, c] = jnp.where(gx, src(1, b, c), src(-1, b, c))
            y0 = {c: jnp.where(gy, src(0, 1, c), src(0, -1, c)) for c in (-1, 0, 1)}
            y1 = {c: jnp.where(gy, xs[1, c], xs[-1, c]) for c in (-1, 0, 1)}
            centre = src(0, 0, 0)
            z00 = jnp.where(gz, src(0, 0, 1), src(0, 0, -1))
            z01 = jnp.where(gz, y0[1], y0[-1])
            z10 = jnp.where(gz, xs[0, 1], xs[0, -1])
            z11 = jnp.where(gz, y1[1], y1[-1])
            l00 = lerp(centre, z00, az)
            l01 = lerp(y0[0], z01, az)
            l10 = lerp(xs[0, 0], z10, az)
            l11 = lerp(y1[0], z11, az)
            m0 = lerp(l00, l01, ay)
            m1 = lerp(l10, l11, ay)
            warped = lerp(m0, m1, ax)
            values = image_ref[xl, rs, cs].astype(jnp.float32)
            misfit = warped - contrast * values - bright
            res_ref[xl, rs, cs] = misfit.astype(res_ref.dtype)
            return (prod_acc + misfit * values, mis_acc + misfit,
                    sq_acc + values * values, e_acc + misfit * misfit)

        zero = jnp.zeros((ROWS, LANES), jnp.float32)
        prod_acc, mis_acc, sq_acc, e_acc = lax.fori_loop(
            0, KNOT, plane, (zero, zero, zero, energy))
        prod_ref[0, rs, cs] = prod_acc
        mis_ref[0, rs, cs] = mis_acc
        sq_ref[0, rs, cs] = sq_acc
        return e_acc

    energy = lax.fori_loop(0, chunks_y * chunks_z, chunk,
                           jnp.zeros((ROWS, LANES), jnp.float32))
    energy_ref[0] = energy


def strip_sums(dpad, displacement, image, contrast_y, bright_y):
    depth_x, width_y, width_z = image.shape
    nodes = depth_x // KNOT
    f32 = jnp.float32
    block_sum = jax.ShapeDtypeStruct((nodes, width_y, width_z), f32)
    node_spec = pl.BlockSpec((1, width_y, width_z), lambda i: (i, 0, 0))
    return pl.pallas_call(
        strip_kernel,
        grid=(nodes,),
        in_specs=[
            pl.BlockSpec(memory_space=pltpu.VMEM),
            pl.BlockSpec((3, KNOT, width_y, width_z), lambda i: (0, i, 0, 0)),
            pl.BlockSpec((KNOT, width_y, width_z), lambda i: (i, 0, 0)),
            node_spec,
            node_spec,
        ],
        out_specs=[
            pl.BlockSpec((KNOT, width_y, width_z), lambda i: (i, 0, 0)),
            node_spec,
            node_spec,
            node_spec,
            pl.BlockSpec((1, ROWS, LANES), lambda i: (i, 0, 0)),
        ],
        out_shape=[
            jax.ShapeDtypeStruct(image.shape, jnp.bfloat16),
            block_sum,
            block_sum,
            block_sum,
            jax.ShapeDtypeStruct((nodes, ROWS, LANES), f32),
        ],
        scratch_shapes=[pltpu.VMEM((KNOT + 2, 9, width_y, width_z), f32)],
        compiler_params=pltpu.CompilerParams(
            dimension_semantics=("arbitrary",), vmem_limit_bytes=60 * 1024 * 1024),
    )(dpad, displacement, image, contrast_y, bright_y)


def node_sums(field):
    nodes, width_y, width_z = field.shape
    return field.reshape(nodes, width_y // KNOT, KNOT, width_z).sum(axis=2)


def gather_sum_kernel(axis, n, part_ref, out_ref, landed, summed, gathered,
                      send_one, recv_one, send_two, recv_two):
    me = lax.axis_index(axis)
    barrier = pltpu.get_barrier_semaphore()
    for d in range(1, n):
        pl.semaphore_signal(barrier, inc=1, device_id={axis: lax.rem(me + d, n)},
                            device_id_type=pl.DeviceIdType.MESH)
    pl.semaphore_wait(barrier, n - 1)

    def scatter(d):
        target = lax.rem(me + d, n)
        return pltpu.make_async_remote_copy(
            src_ref=part_ref.at[target], dst_ref=landed.at[me],
            send_sem=send_one.at[target], recv_sem=recv_one.at[me],
            device_id={axis: target}, device_id_type=pl.DeviceIdType.MESH)

    def arrival(d, buffer, sem, source_ref):
        source = lax.rem(me + n - d, n)
        return pltpu.make_async_remote_copy(
            src_ref=source_ref, dst_ref=buffer.at[source],
            send_sem=sem.at[source], recv_sem=sem.at[source],
            device_id={axis: source}, device_id_type=pl.DeviceIdType.MESH)

    outgoing = [scatter(d) for d in range(1, n)]
    for copy in outgoing:
        copy.start()
    total = part_ref[me]
    for d in range(1, n):
        arrival(d, landed, recv_one, part_ref.at[0]).wait_recv()
        total = total + landed[lax.rem(me + n - d, n)]
    summed[...] = total
    for copy in outgoing:
        copy.wait_send()

    def gather(d):
        target = lax.rem(me + d, n)
        return pltpu.make_async_remote_copy(
            src_ref=summed, dst_ref=gathered.at[me],
            send_sem=send_two.at[target], recv_sem=recv_two.at[me],
            device_id={axis: target}, device_id_type=pl.DeviceIdType.MESH)

    outgoing = [gather(d) for d in range(1, n)]
    for copy in outgoing:
        copy.start()
    out_ref[me] = total
    for d in range(1, n):
        arrival(d, gathered, recv_two, summed).wait_recv()
        source = lax.rem(me + n - d, n)
        out_ref[source] = gathered[source]
    for copy in outgoing:
        copy.wait_send()


def gather_sum(parts, axis, tag):
    n = lax.axis_size(axis)
    chunk = parts.shape[1:]
    return pl.pallas_call(
        functools.partial(gather_sum_kernel, axis, n),
        out_shape=jax.ShapeDtypeStruct(parts.shape, parts.dtype),
        in_specs=[pl.BlockSpec(memory_space=pltpu.VMEM)],
        out_specs=pl.BlockSpec(memory_space=pltpu.VMEM),
        scratch_shapes=[
            pltpu.VMEM(parts.shape, parts.dtype),
            pltpu.VMEM(chunk, parts.dtype),
            pltpu.VMEM(parts.shape, parts.dtype),
            pltpu.SemaphoreType.DMA((n,)),
            pltpu.SemaphoreType.DMA((n,)),
            pltpu.SemaphoreType.DMA((n,)),
            pltpu.SemaphoreType.DMA((n,)),
        ],
        compiler_params=pltpu.CompilerParams(collective_id=tag, has_side_effects=True),
    )(parts)


def all_sum(main, extras, axis, tag):
    n = lax.axis_size(axis)
    rows = -(-main.shape[0] // (n * 128))
    main = jnp.pad(main, (0, n * rows * 128 - main.shape[0])).reshape(n, rows, 128)
    tail = jnp.pad(extras, (0, 128 - extras.shape[0]))
    tail = jnp.broadcast_to(tail, (n, 1, 128))
    spare = -(-(rows + 1) // 8) * 8 - rows - 1
    parts = jnp.concatenate([main, tail, jnp.zeros((n, spare, 128), main.dtype)], axis=1)
    summed = gather_sum(parts, axis, tag)
    return summed[:, :rows].reshape(-1), summed[0, rows]


def local(reference_image, deformed, displacement, plane_factors, depth_factors):
    dpad = padded_deformed(deformed)
    fields = jnp.einsum("krij,krz->kijz", plane_factors, depth_factors, precision=highest)
    fields = jnp.repeat(fields, KNOT, axis=2)
    residual, prod, mis, sq, energy_parts = strip_sums(
        dpad, displacement, reference_image, fields[0], fields[1])
    prod, mis, sq = node_sums(prod), node_sums(mis), node_sums(sq)
    local_energy = jnp.sum(energy_parts)

    first, second = plane_factors[0], plane_factors[1]
    grad_depth = -jnp.stack([
        jnp.einsum("rij,ijz->rz", first, prod, precision=highest),
        jnp.einsum("rij,ijz->rz", second, mis, precision=highest)])
    first_depth = jnp.einsum("rij,ijz->rz", first * first, sq, precision=highest)
    level_sum = KNOT * KNOT * jnp.sum(second * second, axis=(1, 2))
    grad_plane = -jnp.stack([
        jnp.einsum("rz,ijz->rij", depth_factors[0], prod, precision=highest),
        jnp.einsum("rz,ijz->rij", depth_factors[1], mis, precision=highest)])
    first_diag = jnp.einsum("rz,ijz->rij", depth_factors[0] * depth_factors[0], sq, precision=highest)
    depth_level = KNOT * KNOT * jnp.sum(depth_factors[1] * depth_factors[1], axis=1)

    plane_terms = jnp.concatenate([grad_plane.reshape(-1), first_diag.reshape(-1)])
    plane_terms, plane_extra = all_sum(
        plane_terms, jnp.concatenate([depth_level, local_energy[None]]), "gz", 1)
    grad_plane = plane_terms[: grad_plane.size].reshape(grad_plane.shape)
    first_diag = plane_terms[grad_plane.size : grad_plane.size + first_diag.size].reshape(first_diag.shape)
    depth_level, row_energy = plane_extra[:RANK], plane_extra[RANK]
    depth_terms = jnp.concatenate([grad_depth.reshape(-1), first_depth.reshape(-1)])
    depth_terms, depth_extra = all_sum(
        depth_terms, jnp.concatenate([level_sum, row_energy[None]]), "gy", 2)
    grad_depth = depth_terms[: grad_depth.size].reshape(grad_depth.shape)
    first_depth = depth_terms[grad_depth.size : grad_depth.size + first_depth.size].reshape(first_depth.shape)
    level_sum, energy = depth_extra[:RANK], depth_extra[RANK]

    nodes_x = plane_factors.shape[2]
    nodes_y = plane_factors.shape[3] * lax.axis_size("gy")
    full_z = depth_factors.shape[2] * lax.axis_size("gz")
    diag_plane = jnp.stack(
        [first_diag, jnp.broadcast_to(depth_level[:, None, None], first_diag.shape)])
    lam_plane = damping * RANK * energy / (nodes_x * nodes_y)
    lam_depth = damping * energy / full_z
    step_plane = -grad_plane / (diag_plane + lam_plane + epsilon)
    diag_depth = jnp.stack([first_depth, jnp.broadcast_to(level_sum[:, None], first_depth.shape)])
    step_depth = -grad_depth / (diag_depth + lam_depth + epsilon)
    return (residual, step_plane, step_depth)


def solution(mesh):
    placed = (
        P(None, "gy", "gz"),
        P(None, "gy", "gz"),
        P(None, None, "gy", "gz"),
        P(None, None, None, "gy"),
        P(None, None, "gz"),
    )
    return jax.shard_map(
        local,
        mesh=mesh,
        in_specs=placed,
        out_specs=(P(None, "gy", "gz"), P(None, None, None, "gy"), P(None, None, "gz")),
        check_vma=False,
    )
```

```python
import functools

import jax
import jax.numpy as jnp
from jax import lax
from jax.experimental import pallas as pl
from jax.experimental.pallas import tpu as pltpu
from jax.sharding import PartitionSpec as P

RANK = 32
KNOT = 8

epsilon = 1e-06
damping = 0.01
highest = lax.Precision.HIGHEST

ROWS = 16
LANES = 256


def neighbours(part, axis, forward):
    count = lax.axis_size(axis)
    if forward:
        pairs = [(i, i + 1) for i in range(count - 1)]
    else:
        pairs = [(i + 1, i) for i in range(count - 1)]
    return lax.ppermute(part, axis, pairs)


def halo_blocks(deformed):
    depth_x, width_y, width_z = deformed.shape
    low_y = neighbours(deformed[:, width_y - 1 :, :], "gy", True)
    high_y = neighbours(deformed[:, :1, :], "gy", False)
    gap_y = jnp.zeros((depth_x, 6, width_z), deformed.dtype)
    rows = jnp.concatenate([high_y, gap_y, low_y], axis=1)
    first = jnp.concatenate([deformed[:, :, :1], rows[:, :, :1]], axis=1)
    last = jnp.concatenate([deformed[:, :, width_z - 1 :], rows[:, :, width_z - 1 :]], axis=1)
    low_z = neighbours(last, "gz", True)
    high_z = neighbours(first, "gz", False)
    gap_z = jnp.zeros((depth_x, first.shape[1], 126), deformed.dtype)
    columns = jnp.concatenate([high_z, gap_z, low_z], axis=2)
    return rows.astype(jnp.float32), columns.astype(jnp.float32)


def lerp(base, other, weight):
    return base + weight * (other - base)


def strip_kernel(prev_ref, main_ref, next_ref, rows_ref, cols_ref, disp_ref, image_ref,
                 contrast_ref, bright_ref,
                 res_ref, prod_ref, mis_ref, sq_ref, energy_ref, pad_ref, shifts_ref):
    block = pl.program_id(0)
    depth_x = rows_ref.shape[0]
    width_y, width_z = image_ref.shape[1], image_ref.shape[2]
    pad_y, pad_z = pad_ref.shape

    def source_plane(p, plane):
        plane_x = block * KNOT - 1 + p
        valid = jnp.logical_and(plane_x >= 0, plane_x < depth_x)
        safe = jnp.clip(plane_x, 0, depth_x - 1)
        pad_ref[:width_y, :width_z] = plane.astype(jnp.float32)
        pad_ref[width_y:, :width_z] = rows_ref[safe]
        pad_ref[:, width_z:] = cols_ref[safe]
        whole = jnp.where(valid, pad_ref[...], 0.0)
        by_y = (pltpu.roll(whole, 1, 0), whole, pltpu.roll(whole, pad_y - 1, 0))
        for b in range(3):
            part = by_y[b][:width_y]
            by_z = (pltpu.roll(part, 1, 1), part, pltpu.roll(part, pad_z - 1, 1))
            for c in range(3):
                shifts_ref[p, 3 * b + c] = by_z[c][:, :width_z]

    source_plane(0, prev_ref[0])

    def inner_plane(p, carry):
        source_plane(p, main_ref[p - 1])
        return carry

    lax.fori_loop(1, KNOT + 1, inner_plane, 0)
    source_plane(KNOT + 1, next_ref[0])

    chunks_y = width_y // ROWS
    chunks_z = width_z // LANES

    def chunk(k, energy):
        r0 = pl.multiple_of((k // chunks_z) * ROWS, ROWS)
        c0 = pl.multiple_of((k % chunks_z) * LANES, LANES)
        rs = pl.ds(r0, ROWS)
        cs = pl.ds(c0, LANES)
        contrast = contrast_ref[0, rs, cs]
        bright = bright_ref[0, rs, cs]

        def plane(xl, acc):
            prod_acc, mis_acc, sq_acc, e_acc = acc

            def src(a, b, c):
                return shifts_ref[xl + 1 + a, 3 * (b + 1) + (c + 1), rs, cs]

            sx = disp_ref[0, xl, rs, cs].astype(jnp.float32)
            sy = disp_ref[1, xl, rs, cs].astype(jnp.float32)
            sz = disp_ref[2, xl, rs, cs].astype(jnp.float32)
            gx, gy, gz = sx > 0, sy > 0, sz > 0
            ax, ay, az = jnp.abs(sx), jnp.abs(sy), jnp.abs(sz)
            xs = {}
            for b in (-1, 0, 1):
                for c in (-1, 0, 1):
                    xs[b, c] = jnp.where(gx, src(1, b, c), src(-1, b, c))
            y0 = {c: jnp.where(gy, src(0, 1, c), src(0, -1, c)) for c in (-1, 0, 1)}
            y1 = {c: jnp.where(gy, xs[1, c], xs[-1, c]) for c in (-1, 0, 1)}
            centre = src(0, 0, 0)
            z00 = jnp.where(gz, src(0, 0, 1), src(0, 0, -1))
            z01 = jnp.where(gz, y0[1], y0[-1])
            z10 = jnp.where(gz, xs[0, 1], xs[0, -1])
            z11 = jnp.where(gz, y1[1], y1[-1])
            l00 = lerp(centre, z00, az)
            l01 = lerp(y0[0], z01, az)
            l10 = lerp(xs[0, 0], z10, az)
            l11 = lerp(y1[0], z11, az)
            m0 = lerp(l00, l01, ay)
            m1 = lerp(l10, l11, ay)
            warped = lerp(m0, m1, ax)
            values = image_ref[xl, rs, cs].astype(jnp.float32)
            misfit = warped - contrast * values - bright
            res_ref[xl, rs, cs] = misfit.astype(res_ref.dtype)
            return (prod_acc + misfit * values, mis_acc + misfit,
                    sq_acc + values * values, e_acc + misfit * misfit)

        zero = jnp.zeros((ROWS, LANES), jnp.float32)
        prod_acc, mis_acc, sq_acc, e_acc = lax.fori_loop(
            0, KNOT, plane, (zero, zero, zero, energy))
        prod_ref[0, rs, cs] = prod_acc
        mis_ref[0, rs, cs] = mis_acc
        sq_ref[0, rs, cs] = sq_acc
        return e_acc

    energy = lax.fori_loop(0, chunks_y * chunks_z, chunk,
                           jnp.zeros((ROWS, LANES), jnp.float32))
    energy_ref[0] = energy


def strip_sums(deformed, rows, cols, displacement, image, contrast_y, bright_y):
    depth_x, width_y, width_z = image.shape
    nodes = depth_x // KNOT
    f32 = jnp.float32
    block_sum = jax.ShapeDtypeStruct((nodes, width_y, width_z), f32)
    node_spec = pl.BlockSpec((1, width_y, width_z), lambda i: (i, 0, 0))
    plane_spec = pl.BlockSpec((KNOT, width_y, width_z), lambda i: (i, 0, 0))
    return pl.pallas_call(
        strip_kernel,
        grid=(nodes,),
        in_specs=[
            pl.BlockSpec((1, width_y, width_z), lambda i: (jnp.maximum(i * KNOT - 1, 0), 0, 0)),
            plane_spec,
            pl.BlockSpec((1, width_y, width_z),
                         lambda i: (jnp.minimum(i * KNOT + KNOT, depth_x - 1), 0, 0)),
            pl.BlockSpec(memory_space=pltpu.VMEM),
            pl.BlockSpec(memory_space=pltpu.VMEM),
            pl.BlockSpec((3, KNOT, width_y, width_z), lambda i: (0, i, 0, 0)),
            plane_spec,
            node_spec,
            node_spec,
        ],
        out_specs=[
            plane_spec,
            node_spec,
            node_spec,
            node_spec,
            pl.BlockSpec((1, ROWS, LANES), lambda i: (i, 0, 0)),
        ],
        out_shape=[
            jax.ShapeDtypeStruct(image.shape, jnp.bfloat16),
            block_sum,
            block_sum,
            block_sum,
            jax.ShapeDtypeStruct((nodes, ROWS, LANES), f32),
        ],
        scratch_shapes=[
            pltpu.VMEM((width_y + rows.shape[1], width_z + cols.shape[2]), f32),
            pltpu.VMEM((KNOT + 2, 9, width_y, width_z), f32),
        ],
        compiler_params=pltpu.CompilerParams(
            dimension_semantics=("arbitrary",), vmem_limit_bytes=60 * 1024 * 1024),
    )(deformed, deformed, deformed, rows, cols, displacement, image, contrast_y, bright_y)


def node_sums(field):
    nodes, width_y, width_z = field.shape
    return field.reshape(nodes, width_y // KNOT, KNOT, width_z).sum(axis=2)


def gather_sum_kernel(axis, n, part_ref, out_ref, landed, summed, gathered,
                      send_one, recv_one, send_two, recv_two):
    me = lax.axis_index(axis)
    barrier = pltpu.get_barrier_semaphore()
    for d in range(1, n):
        pl.semaphore_signal(barrier, inc=1, device_id={axis: lax.rem(me + d, n)},
                            device_id_type=pl.DeviceIdType.MESH)
    pl.semaphore_wait(barrier, n - 1)

    def scatter(d):
        target = lax.rem(me + d, n)
        return pltpu.make_async_remote_copy(
            src_ref=part_ref.at[target], dst_ref=landed.at[me],
            send_sem=send_one.at[target], recv_sem=recv_one.at[me],
            device_id={axis: target}, device_id_type=pl.DeviceIdType.MESH)

    def arrival(d, buffer, sem, source_ref):
        source = lax.rem(me + n - d, n)
        return pltpu.make_async_remote_copy(
            src_ref=source_ref, dst_ref=buffer.at[source],
            send_sem=sem.at[source], recv_sem=sem.at[source],
            device_id={axis: source}, device_id_type=pl.DeviceIdType.MESH)

    outgoing = [scatter(d) for d in range(1, n)]
    for copy in outgoing:
        copy.start()
    total = part_ref[me]
    for d in range(1, n):
        arrival(d, landed, recv_one, part_ref.at[0]).wait_recv()
        total = total + landed[lax.rem(me + n - d, n)]
    summed[...] = total
    for copy in outgoing:
        copy.wait_send()

    def gather(d):
        target = lax.rem(me + d, n)
        return pltpu.make_async_remote_copy(
            src_ref=summed, dst_ref=gathered.at[me],
            send_sem=send_two.at[target], recv_sem=recv_two.at[me],
            device_id={axis: target}, device_id_type=pl.DeviceIdType.MESH)

    outgoing = [gather(d) for d in range(1, n)]
    for copy in outgoing:
        copy.start()
    out_ref[me] = total
    for d in range(1, n):
        arrival(d, gathered, recv_two, summed).wait_recv()
        source = lax.rem(me + n - d, n)
        out_ref[source] = gathered[source]
    for copy in outgoing:
        copy.wait_send()


def gather_sum(parts, axis, tag):
    n = lax.axis_size(axis)
    chunk = parts.shape[1:]
    return pl.pallas_call(
        functools.partial(gather_sum_kernel, axis, n),
        out_shape=jax.ShapeDtypeStruct(parts.shape, parts.dtype),
        in_specs=[pl.BlockSpec(memory_space=pltpu.VMEM)],
        out_specs=pl.BlockSpec(memory_space=pltpu.VMEM),
        scratch_shapes=[
            pltpu.VMEM(parts.shape, parts.dtype),
            pltpu.VMEM(chunk, parts.dtype),
            pltpu.VMEM(parts.shape, parts.dtype),
            pltpu.SemaphoreType.DMA((n,)),
            pltpu.SemaphoreType.DMA((n,)),
            pltpu.SemaphoreType.DMA((n,)),
            pltpu.SemaphoreType.DMA((n,)),
        ],
        compiler_params=pltpu.CompilerParams(collective_id=tag, has_side_effects=True),
    )(parts)


def all_sum(main, extras, axis, tag):
    n = lax.axis_size(axis)
    rows = -(-main.shape[0] // (n * 128))
    main = jnp.pad(main, (0, n * rows * 128 - main.shape[0])).reshape(n, rows, 128)
    tail = jnp.pad(extras, (0, 128 - extras.shape[0]))
    tail = jnp.broadcast_to(tail, (n, 1, 128))
    spare = -(-(rows + 1) // 8) * 8 - rows - 1
    parts = jnp.concatenate([main, tail, jnp.zeros((n, spare, 128), main.dtype)], axis=1)
    summed = gather_sum(parts, axis, tag)
    return summed[:, :rows].reshape(-1), summed[0, rows]


def local(reference_image, deformed, displacement, plane_factors, depth_factors):
    rows, cols = halo_blocks(deformed)
    fields = jnp.einsum("krij,krz->kijz", plane_factors, depth_factors, precision=highest)
    fields = jnp.repeat(fields, KNOT, axis=2)
    residual, prod, mis, sq, energy_parts = strip_sums(
        deformed, rows, cols, displacement, reference_image, fields[0], fields[1])
    prod, mis, sq = node_sums(prod), node_sums(mis), node_sums(sq)
    local_energy = jnp.sum(energy_parts)

    first, second = plane_factors[0], plane_factors[1]
    grad_depth = -jnp.stack([
        jnp.einsum("rij,ijz->rz", first, prod, precision=highest),
        jnp.einsum("rij,ijz->rz", second, mis, precision=highest)])
    first_depth = jnp.einsum("rij,ijz->rz", first * first, sq, precision=highest)
    level_sum = KNOT * KNOT * jnp.sum(second * second, axis=(1, 2))
    grad_plane = -jnp.stack([
        jnp.einsum("rz,ijz->rij", depth_factors[0], prod, precision=highest),
        jnp.einsum("rz,ijz->rij", depth_factors[1], mis, precision=highest)])
    first_diag = jnp.einsum("rz,ijz->rij", depth_factors[0] * depth_factors[0], sq, precision=highest)
    depth_level = KNOT * KNOT * jnp.sum(depth_factors[1] * depth_factors[1], axis=1)

    plane_terms = jnp.concatenate([grad_plane.reshape(-1), first_diag.reshape(-1)])
    plane_terms, plane_extra = all_sum(
        plane_terms, jnp.concatenate([depth_level, local_energy[None]]), "gz", 1)
    grad_plane = plane_terms[: grad_plane.size].reshape(grad_plane.shape)
    first_diag = plane_terms[grad_plane.size : grad_plane.size + first_diag.size].reshape(first_diag.shape)
    depth_level, row_energy = plane_extra[:RANK], plane_extra[RANK]
    depth_terms = jnp.concatenate([grad_depth.reshape(-1), first_depth.reshape(-1)])
    depth_terms, depth_extra = all_sum(
        depth_terms, jnp.concatenate([level_sum, row_energy[None]]), "gy", 2)
    grad_depth = depth_terms[: grad_depth.size].reshape(grad_depth.shape)
    first_depth = depth_terms[grad_depth.size : grad_depth.size + first_depth.size].reshape(first_depth.shape)
    level_sum, energy = depth_extra[:RANK], depth_extra[RANK]

    nodes_x = plane_factors.shape[2]
    nodes_y = plane_factors.shape[3] * lax.axis_size("gy")
    full_z = depth_factors.shape[2] * lax.axis_size("gz")
    diag_plane = jnp.stack(
        [first_diag, jnp.broadcast_to(depth_level[:, None, None], first_diag.shape)])
    lam_plane = damping * RANK * energy / (nodes_x * nodes_y)
    lam_depth = damping * energy / full_z
    step_plane = -grad_plane / (diag_plane + lam_plane + epsilon)
    diag_depth = jnp.stack([first_depth, jnp.broadcast_to(level_sum[:, None], first_depth.shape)])
    step_depth = -grad_depth / (diag_depth + lam_depth + epsilon)
    return (residual, step_plane, step_depth)


def solution(mesh):
    placed = (
        P(None, "gy", "gz"),
        P(None, "gy", "gz"),
        P(None, None, "gy", "gz"),
        P(None, None, None, "gy"),
        P(None, None, "gz"),
    )
    return jax.shard_map(
        local,
        mesh=mesh,
        in_specs=placed,
        out_specs=(P(None, "gy", "gz"), P(None, None, None, "gy"), P(None, None, "gz")),
        check_vma=False,
    )
```

```python
import functools

import jax
import jax.numpy as jnp
from jax import lax
from jax.experimental import pallas as pl
from jax.experimental.pallas import tpu as pltpu
from jax.sharding import PartitionSpec as P

RANK = 32
KNOT = 8

epsilon = 1e-06
damping = 0.01
highest = lax.Precision.HIGHEST

ROWS = 16
LANES = 256


def neighbours(part, axis, forward):
    count = lax.axis_size(axis)
    if forward:
        pairs = [(i, i + 1) for i in range(count - 1)]
    else:
        pairs = [(i + 1, i) for i in range(count - 1)]
    return lax.ppermute(part, axis, pairs)


def halo_blocks(deformed):
    depth_x, width_y, width_z = deformed.shape
    low_y = neighbours(deformed[:, width_y - 1 :, :], "gy", True)
    high_y = neighbours(deformed[:, :1, :], "gy", False)
    gap_y = jnp.zeros((depth_x, 6, width_z), deformed.dtype)
    rows = jnp.concatenate([high_y, gap_y, low_y], axis=1)
    first = jnp.concatenate([deformed[:, :, :1], rows[:, :, :1]], axis=1)
    last = jnp.concatenate([deformed[:, :, width_z - 1 :], rows[:, :, width_z - 1 :]], axis=1)
    low_z = neighbours(last, "gz", True)
    high_z = neighbours(first, "gz", False)
    gap_z = jnp.zeros((depth_x, first.shape[1], 126), deformed.dtype)
    columns = jnp.concatenate([high_z, gap_z, low_z], axis=2)
    return rows.astype(jnp.float32), columns.astype(jnp.float32)


def lerp(base, other, weight):
    return base + weight * (other - base)


def strip_kernel(prev_ref, main_ref, next_ref, rows_ref, cols_ref, disp_ref, image_ref,
                 contrast_ref, bright_ref,
                 res_ref, prod_ref, mis_ref, sq_ref, energy_ref, pad_ref, shifts_ref):
    block = pl.program_id(0)
    depth_x = rows_ref.shape[0]
    width_y, width_z = image_ref.shape[1], image_ref.shape[2]
    pad_y, pad_z = pad_ref.shape

    def source_plane(p, plane):
        plane_x = block * KNOT - 1 + p
        valid = jnp.logical_and(plane_x >= 0, plane_x < depth_x)
        safe = jnp.clip(plane_x, 0, depth_x - 1)
        pad_ref[:width_y, :width_z] = plane.astype(jnp.float32)
        pad_ref[width_y:, :width_z] = rows_ref[safe]
        pad_ref[:, width_z:] = cols_ref[safe]
        whole = jnp.where(valid, pad_ref[...], 0.0)
        by_y = (pltpu.roll(whole, 1, 0), whole, pltpu.roll(whole, pad_y - 1, 0))
        for b in range(3):
            part = by_y[b][:width_y]
            by_z = (pltpu.roll(part, 1, 1), part, pltpu.roll(part, pad_z - 1, 1))
            for c in range(3):
                shifts_ref[p, 3 * b + c] = by_z[c][:, :width_z]

    source_plane(0, prev_ref[0])

    def inner_plane(p, carry):
        source_plane(p, main_ref[p - 1])
        return carry

    lax.fori_loop(1, KNOT + 1, inner_plane, 0)
    source_plane(KNOT + 1, next_ref[0])

    chunks_y = width_y // ROWS
    chunks_z = width_z // LANES

    def chunk(k, energy):
        r0 = pl.multiple_of((k // chunks_z) * ROWS, ROWS)
        c0 = pl.multiple_of((k % chunks_z) * LANES, LANES)
        rs = pl.ds(r0, ROWS)
        cs = pl.ds(c0, LANES)
        contrast = contrast_ref[0, rs, cs]
        bright = bright_ref[0, rs, cs]

        def plane(xl, acc):
            prod_acc, mis_acc, sq_acc, e_acc = acc

            def src(a, b, c):
                return shifts_ref[xl + 1 + a, 3 * (b + 1) + (c + 1), rs, cs]

            sx = disp_ref[0, xl, rs, cs].astype(jnp.float32)
            sy = disp_ref[1, xl, rs, cs].astype(jnp.float32)
            sz = disp_ref[2, xl, rs, cs].astype(jnp.float32)
            gx, gy, gz = sx > 0, sy > 0, sz > 0
            ax, ay, az = jnp.abs(sx), jnp.abs(sy), jnp.abs(sz)
            xs = {}
            for b in (-1, 0, 1):
                for c in (-1, 0, 1):
                    xs[b, c] = jnp.where(gx, src(1, b, c), src(-1, b, c))
            y0 = {c: jnp.where(gy, src(0, 1, c), src(0, -1, c)) for c in (-1, 0, 1)}
            y1 = {c: jnp.where(gy, xs[1, c], xs[-1, c]) for c in (-1, 0, 1)}
            centre = src(0, 0, 0)
            z00 = jnp.where(gz, src(0, 0, 1), src(0, 0, -1))
            z01 = jnp.where(gz, y0[1], y0[-1])
            z10 = jnp.where(gz, xs[0, 1], xs[0, -1])
            z11 = jnp.where(gz, y1[1], y1[-1])
            l00 = lerp(centre, z00, az)
            l01 = lerp(y0[0], z01, az)
            l10 = lerp(xs[0, 0], z10, az)
            l11 = lerp(y1[0], z11, az)
            m0 = lerp(l00, l01, ay)
            m1 = lerp(l10, l11, ay)
            warped = lerp(m0, m1, ax)
            values = image_ref[xl, rs, cs].astype(jnp.float32)
            misfit = warped - contrast * values - bright
            res_ref[xl, rs, cs] = misfit.astype(res_ref.dtype)
            return (prod_acc + misfit * values, mis_acc + misfit,
                    sq_acc + values * values, e_acc + misfit * misfit)

        zero = jnp.zeros((ROWS, LANES), jnp.float32)
        prod_acc, mis_acc, sq_acc, e_acc = lax.fori_loop(
            0, KNOT, plane, (zero, zero, zero, energy))
        prod_ref[0, rs, cs] = prod_acc
        mis_ref[0, rs, cs] = mis_acc
        sq_ref[0, rs, cs] = sq_acc
        return e_acc

    energy = lax.fori_loop(0, chunks_y * chunks_z, chunk,
                           jnp.zeros((ROWS, LANES), jnp.float32))
    energy_ref[0] = energy


def strip_sums(deformed, rows, cols, displacement, image, contrast_y, bright_y):
    depth_x, width_y, width_z = image.shape
    nodes = depth_x // KNOT
    f32 = jnp.float32
    block_sum = jax.ShapeDtypeStruct((nodes, width_y, width_z), f32)
    node_spec = pl.BlockSpec((1, width_y, width_z), lambda i: (i, 0, 0))
    plane_spec = pl.BlockSpec((KNOT, width_y, width_z), lambda i: (i, 0, 0))
    return pl.pallas_call(
        strip_kernel,
        grid=(nodes,),
        in_specs=[
            pl.BlockSpec((1, width_y, width_z), lambda i: (jnp.maximum(i * KNOT - 1, 0), 0, 0)),
            plane_spec,
            pl.BlockSpec((1, width_y, width_z),
                         lambda i: (jnp.minimum(i * KNOT + KNOT, depth_x - 1), 0, 0)),
            pl.BlockSpec(memory_space=pltpu.VMEM),
            pl.BlockSpec(memory_space=pltpu.VMEM),
            pl.BlockSpec((3, KNOT, width_y, width_z), lambda i: (0, i, 0, 0)),
            plane_spec,
            node_spec,
            node_spec,
        ],
        out_specs=[
            plane_spec,
            node_spec,
            node_spec,
            node_spec,
            pl.BlockSpec((1, ROWS, LANES), lambda i: (i, 0, 0)),
        ],
        out_shape=[
            jax.ShapeDtypeStruct(image.shape, jnp.bfloat16),
            block_sum,
            block_sum,
            block_sum,
            jax.ShapeDtypeStruct((nodes, ROWS, LANES), f32),
        ],
        scratch_shapes=[
            pltpu.VMEM((width_y + rows.shape[1], width_z + cols.shape[2]), f32),
            pltpu.VMEM((KNOT + 2, 9, width_y, width_z), f32),
        ],
        compiler_params=pltpu.CompilerParams(
            dimension_semantics=("arbitrary",), vmem_limit_bytes=60 * 1024 * 1024),
    )(deformed, deformed, deformed, rows, cols, displacement, image, contrast_y, bright_y)


def node_sums(field):
    nodes, width_y, width_z = field.shape
    return field.reshape(nodes, width_y // KNOT, KNOT, width_z).sum(axis=2)


def exchange(axis, n, me, d, src, buffer, send_sem, recv_sem):
    target = lax.rem(me + d, n)
    return pltpu.make_async_remote_copy(
        src_ref=src(target), dst_ref=buffer.at[me],
        send_sem=send_sem.at[target], recv_sem=recv_sem.at[me],
        device_id={axis: target}, device_id_type=pl.DeviceIdType.MESH)


def arrival(axis, n, me, d, src_ref, buffer, sem):
    source = lax.rem(me + n - d, n)
    return pltpu.make_async_remote_copy(
        src_ref=src_ref, dst_ref=buffer.at[source],
        send_sem=sem.at[source], recv_sem=sem.at[source],
        device_id={axis: source}, device_id_type=pl.DeviceIdType.MESH)


def both_sums_kernel(nz, ny, plane_row, depth_row, plane_ref, depth_ref, plane_out, depth_out,
                     plane_landed, depth_landed, plane_summed, depth_summed,
                     plane_gathered, depth_gathered, sems):
    mz, my = lax.axis_index("gz"), lax.axis_index("gy")
    barrier = pltpu.get_barrier_semaphore()
    for d in range(1, nz):
        pl.semaphore_signal(barrier, inc=1, device_id={"gz": lax.rem(mz + d, nz)},
                            device_id_type=pl.DeviceIdType.MESH)
    for d in range(1, ny):
        pl.semaphore_signal(barrier, inc=1, device_id={"gy": lax.rem(my + d, ny)},
                            device_id_type=pl.DeviceIdType.MESH)
    pl.semaphore_wait(barrier, nz - 1 + ny - 1)
    zs1, zr1, zs2, zr2, ys1, yr1, ys2, yr2 = sems

    z_out = [exchange("gz", nz, mz, d, lambda t: plane_ref.at[t], plane_landed, zs1, zr1)
             for d in range(1, nz)]
    y_out = [exchange("gy", ny, my, d, lambda t: depth_ref.at[t], depth_landed, ys1, yr1)
             for d in range(1, ny)]
    for copy in z_out + y_out:
        copy.start()
    depth_total = depth_ref[my]
    for d in range(1, ny):
        arrival("gy", ny, my, d, depth_ref.at[0], depth_landed, yr1).wait_recv()
        depth_total = depth_total + depth_landed[lax.rem(my + ny - d, ny)]
    depth_summed[...] = depth_total
    plane_total = plane_ref[mz]
    for d in range(1, nz):
        arrival("gz", nz, mz, d, plane_ref.at[0], plane_landed, zr1).wait_recv()
        plane_total = plane_total + plane_landed[lax.rem(mz + nz - d, nz)]
    rows = lax.broadcasted_iota(jnp.int32, plane_total.shape, 0)
    lanes = lax.broadcasted_iota(jnp.int32, plane_total.shape, 1)
    slot = jnp.logical_and(rows == plane_row, lanes == RANK)
    depth_slot = jnp.logical_and(
        lax.broadcasted_iota(jnp.int32, depth_total.shape, 0) == depth_row,
        lax.broadcasted_iota(jnp.int32, depth_total.shape, 1) == RANK)
    column_energy = jnp.sum(jnp.where(depth_slot, depth_total, 0.0))
    plane_total = jnp.where(slot, column_energy, plane_total)
    plane_summed[...] = plane_total
    for copy in z_out + y_out:
        copy.wait_send()

    z_out = [exchange("gz", nz, mz, d, lambda t: plane_summed, plane_gathered, zs2, zr2)
             for d in range(1, nz)]
    y_out = [exchange("gy", ny, my, d, lambda t: depth_summed, depth_gathered, ys2, yr2)
             for d in range(1, ny)]
    for copy in z_out + y_out:
        copy.start()
    plane_out[mz] = plane_total
    depth_out[my] = depth_total
    for d in range(1, nz):
        arrival("gz", nz, mz, d, plane_summed, plane_gathered, zr2).wait_recv()
        source = lax.rem(mz + nz - d, nz)
        plane_out[source] = plane_gathered[source]
    for d in range(1, ny):
        arrival("gy", ny, my, d, depth_summed, depth_gathered, yr2).wait_recv()
        source = lax.rem(my + ny - d, ny)
        depth_out[source] = depth_gathered[source]
    for copy in z_out + y_out:
        copy.wait_send()


def chunked(main, extras, n):
    rows = -(-main.shape[0] // (n * 128))
    main = jnp.pad(main, (0, n * rows * 128 - main.shape[0])).reshape(n, rows, 128)
    tail = jnp.pad(extras, (0, 128 - extras.shape[0]))
    tail = jnp.broadcast_to(tail, (n, 1, 128))
    spare = -(-(rows + 1) // 8) * 8 - rows - 1
    return jnp.concatenate([main, tail, jnp.zeros((n, spare, 128), main.dtype)], axis=1), rows


def both_sums(plane_parts, depth_parts, plane_row, depth_row):
    nz, ny = plane_parts.shape[0], depth_parts.shape[0]
    f32 = jnp.float32
    dma = pltpu.SemaphoreType.DMA
    return pl.pallas_call(
        functools.partial(both_sums_kernel, nz, ny, plane_row, depth_row),
        out_shape=[jax.ShapeDtypeStruct(plane_parts.shape, f32),
                   jax.ShapeDtypeStruct(depth_parts.shape, f32)],
        in_specs=[pl.BlockSpec(memory_space=pltpu.VMEM)] * 2,
        out_specs=[pl.BlockSpec(memory_space=pltpu.VMEM)] * 2,
        scratch_shapes=[
            pltpu.VMEM(plane_parts.shape, f32),
            pltpu.VMEM(depth_parts.shape, f32),
            pltpu.VMEM(plane_parts.shape[1:], f32),
            pltpu.VMEM(depth_parts.shape[1:], f32),
            pltpu.VMEM(plane_parts.shape, f32),
            pltpu.VMEM(depth_parts.shape, f32),
            [dma((nz,)), dma((nz,)), dma((nz,)), dma((nz,)),
             dma((ny,)), dma((ny,)), dma((ny,)), dma((ny,))],
        ],
        compiler_params=pltpu.CompilerParams(collective_id=1, has_side_effects=True),
    )(plane_parts, depth_parts)


def local(reference_image, deformed, displacement, plane_factors, depth_factors):
    rows, cols = halo_blocks(deformed)
    fields = jnp.einsum("krij,krz->kijz", plane_factors, depth_factors, precision=highest)
    fields = jnp.repeat(fields, KNOT, axis=2)
    residual, prod, mis, sq, energy_parts = strip_sums(
        deformed, rows, cols, displacement, reference_image, fields[0], fields[1])
    prod, mis, sq = node_sums(prod), node_sums(mis), node_sums(sq)
    local_energy = jnp.sum(energy_parts)

    first, second = plane_factors[0], plane_factors[1]
    grad_depth = -jnp.stack([
        jnp.einsum("rij,ijz->rz", first, prod, precision=highest),
        jnp.einsum("rij,ijz->rz", second, mis, precision=highest)])
    first_depth = jnp.einsum("rij,ijz->rz", first * first, sq, precision=highest)
    level_sum = KNOT * KNOT * jnp.sum(second * second, axis=(1, 2))
    grad_plane = -jnp.stack([
        jnp.einsum("rz,ijz->rij", depth_factors[0], prod, precision=highest),
        jnp.einsum("rz,ijz->rij", depth_factors[1], mis, precision=highest)])
    first_diag = jnp.einsum("rz,ijz->rij", depth_factors[0] * depth_factors[0], sq, precision=highest)
    depth_level = KNOT * KNOT * jnp.sum(depth_factors[1] * depth_factors[1], axis=1)

    nz, ny = lax.axis_size("gz"), lax.axis_size("gy")
    plane_terms = jnp.concatenate([grad_plane.reshape(-1), first_diag.reshape(-1)])
    depth_terms = jnp.concatenate([grad_depth.reshape(-1), first_depth.reshape(-1)])
    blank = jnp.zeros((), jnp.float32)
    plane_parts, plane_rows = chunked(plane_terms, jnp.concatenate([depth_level, blank[None]]), nz)
    depth_parts, depth_rows = chunked(depth_terms, jnp.concatenate([level_sum, local_energy[None]]), ny)
    plane_summed, depth_summed = both_sums(plane_parts, depth_parts, plane_rows, depth_rows)
    plane_terms = plane_summed[:, :plane_rows].reshape(-1)
    depth_terms = depth_summed[:, :depth_rows].reshape(-1)
    grad_plane = plane_terms[: grad_plane.size].reshape(grad_plane.shape)
    first_diag = plane_terms[grad_plane.size : grad_plane.size + first_diag.size].reshape(first_diag.shape)
    grad_depth = depth_terms[: grad_depth.size].reshape(grad_depth.shape)
    first_depth = depth_terms[grad_depth.size : grad_depth.size + first_depth.size].reshape(first_depth.shape)
    depth_level = plane_summed[0, plane_rows, :RANK]
    level_sum = depth_summed[0, depth_rows, :RANK]
    energy = jnp.sum(plane_summed[:, plane_rows, RANK])

    nodes_x = plane_factors.shape[2]
    nodes_y = plane_factors.shape[3] * lax.axis_size("gy")
    full_z = depth_factors.shape[2] * lax.axis_size("gz")
    diag_plane = jnp.stack(
        [first_diag, jnp.broadcast_to(depth_level[:, None, None], first_diag.shape)])
    lam_plane = damping * RANK * energy / (nodes_x * nodes_y)
    lam_depth = damping * energy / full_z
    step_plane = -grad_plane / (diag_plane + lam_plane + epsilon)
    diag_depth = jnp.stack([first_depth, jnp.broadcast_to(level_sum[:, None], first_depth.shape)])
    step_depth = -grad_depth / (diag_depth + lam_depth + epsilon)
    return (residual, step_plane, step_depth)


def solution(mesh):
    placed = (
        P(None, "gy", "gz"),
        P(None, "gy", "gz"),
        P(None, None, "gy", "gz"),
        P(None, None, None, "gy"),
        P(None, None, "gz"),
    )
    return jax.shard_map(
        local,
        mesh=mesh,
        in_specs=placed,
        out_specs=(P(None, "gy", "gz"), P(None, None, None, "gy"), P(None, None, "gz")),
        check_vma=False,
    )
```

```python
import functools

import jax
import jax.numpy as jnp
from jax import lax
from jax.experimental import pallas as pl
from jax.experimental.pallas import tpu as pltpu
from jax.sharding import PartitionSpec as P

RANK = 32
KNOT = 8

epsilon = 1e-06
damping = 0.01
highest = lax.Precision.HIGHEST

ROWS = 16
LANES = 256


def neighbours(part, axis, forward):
    count = lax.axis_size(axis)
    if forward:
        pairs = [(i, i + 1) for i in range(count - 1)]
    else:
        pairs = [(i + 1, i) for i in range(count - 1)]
    return lax.ppermute(part, axis, pairs)


def corner(part, step_y, step_z):
    ny, nz = lax.axis_size("gy"), lax.axis_size("gz")
    pairs = []
    for gy in range(ny):
        for gz in range(nz):
            ty, tz = gy + step_y, gz + step_z
            if 0 <= ty < ny and 0 <= tz < nz:
                pairs.append((gy * nz + gz, ty * nz + tz))
    return lax.ppermute(part, ("gy", "gz"), pairs)


def halo_blocks(deformed):
    depth_x, width_y, width_z = deformed.shape
    f32 = jnp.float32
    low_y = neighbours(deformed[:, width_y - 1, :], "gy", True)
    high_y = neighbours(deformed[:, 0, :], "gy", False)
    low_z = neighbours(deformed[:, :, width_z - 1], "gz", True)
    high_z = neighbours(deformed[:, :, 0], "gz", False)
    high_high = corner(deformed[:, 0, 0], -1, -1)
    high_low = corner(deformed[:, 0, width_z - 1], -1, 1)
    low_high = corner(deformed[:, width_y - 1, 0], 1, -1)
    low_low = corner(deformed[:, width_y - 1, width_z - 1], 1, 1)
    gap_y = jnp.zeros((depth_x, 6, width_z), f32)
    rows = jnp.concatenate([high_y[:, None].astype(f32), gap_y, low_y[:, None].astype(f32)], axis=1)
    gap = jnp.zeros((depth_x, 6), deformed.dtype)
    side_high = jnp.concatenate([high_z, high_high[:, None], gap, low_high[:, None]], axis=1)
    side_low = jnp.concatenate([low_z, high_low[:, None], gap, low_low[:, None]], axis=1)
    lanes = lax.broadcasted_iota(jnp.int32, (1, 1, 128), 2)
    cols = jnp.where(lanes == 0, side_high[:, :, None].astype(f32),
                     jnp.where(lanes == 127, side_low[:, :, None].astype(f32), 0.0))
    return rows, cols


def lerp(base, other, weight):
    return base + weight * (other - base)


def strip_kernel(prev_ref, main_ref, next_ref, rows_ref, cols_ref, disp_ref, image_ref,
                 contrast_ref, bright_ref,
                 res_ref, prod_ref, mis_ref, sq_ref, energy_ref, pad_ref, shifts_ref):
    block = pl.program_id(0)
    depth_x = rows_ref.shape[0]
    width_y, width_z = image_ref.shape[1], image_ref.shape[2]
    pad_y, pad_z = pad_ref.shape

    def source_plane(p, plane):
        plane_x = block * KNOT - 1 + p
        valid = jnp.logical_and(plane_x >= 0, plane_x < depth_x)
        safe = jnp.clip(plane_x, 0, depth_x - 1)
        pad_ref[:width_y, :width_z] = plane.astype(jnp.float32)
        pad_ref[width_y:, :width_z] = rows_ref[safe]
        pad_ref[:, width_z:] = cols_ref[safe]
        whole = jnp.where(valid, pad_ref[...], 0.0)
        by_y = (pltpu.roll(whole, 1, 0), whole, pltpu.roll(whole, pad_y - 1, 0))
        for b in range(3):
            part = by_y[b][:width_y]
            by_z = (pltpu.roll(part, 1, 1), part, pltpu.roll(part, pad_z - 1, 1))
            for c in range(3):
                shifts_ref[p, 3 * b + c] = by_z[c][:, :width_z]

    source_plane(0, prev_ref[0])

    def inner_plane(p, carry):
        source_plane(p, main_ref[p - 1])
        return carry

    lax.fori_loop(1, KNOT + 1, inner_plane, 0)
    source_plane(KNOT + 1, next_ref[0])

    chunks_y = width_y // ROWS
    chunks_z = width_z // LANES

    def chunk(k, energy):
        r0 = pl.multiple_of((k // chunks_z) * ROWS, ROWS)
        c0 = pl.multiple_of((k % chunks_z) * LANES, LANES)
        rs = pl.ds(r0, ROWS)
        cs = pl.ds(c0, LANES)
        contrast = contrast_ref[0, rs, cs]
        bright = bright_ref[0, rs, cs]

        def plane(xl, acc):
            prod_acc, mis_acc, sq_acc, e_acc = acc

            def src(a, b, c):
                return shifts_ref[xl + 1 + a, 3 * (b + 1) + (c + 1), rs, cs]

            sx = disp_ref[0, xl, rs, cs].astype(jnp.float32)
            sy = disp_ref[1, xl, rs, cs].astype(jnp.float32)
            sz = disp_ref[2, xl, rs, cs].astype(jnp.float32)
            gx, gy, gz = sx > 0, sy > 0, sz > 0
            ax, ay, az = jnp.abs(sx), jnp.abs(sy), jnp.abs(sz)
            xs = {}
            for b in (-1, 0, 1):
                for c in (-1, 0, 1):
                    xs[b, c] = jnp.where(gx, src(1, b, c), src(-1, b, c))
            y0 = {c: jnp.where(gy, src(0, 1, c), src(0, -1, c)) for c in (-1, 0, 1)}
            y1 = {c: jnp.where(gy, xs[1, c], xs[-1, c]) for c in (-1, 0, 1)}
            centre = src(0, 0, 0)
            z00 = jnp.where(gz, src(0, 0, 1), src(0, 0, -1))
            z01 = jnp.where(gz, y0[1], y0[-1])
            z10 = jnp.where(gz, xs[0, 1], xs[0, -1])
            z11 = jnp.where(gz, y1[1], y1[-1])
            l00 = lerp(centre, z00, az)
            l01 = lerp(y0[0], z01, az)
            l10 = lerp(xs[0, 0], z10, az)
            l11 = lerp(y1[0], z11, az)
            m0 = lerp(l00, l01, ay)
            m1 = lerp(l10, l11, ay)
            warped = lerp(m0, m1, ax)
            values = image_ref[xl, rs, cs].astype(jnp.float32)
            misfit = warped - contrast * values - bright
            res_ref[xl, rs, cs] = misfit.astype(res_ref.dtype)
            return (prod_acc + misfit * values, mis_acc + misfit,
                    sq_acc + values * values, e_acc + misfit * misfit)

        zero = jnp.zeros((ROWS, LANES), jnp.float32)
        prod_acc, mis_acc, sq_acc, e_acc = lax.fori_loop(
            0, KNOT, plane, (zero, zero, zero, energy))
        prod_ref[0, rs, cs] = prod_acc
        mis_ref[0, rs, cs] = mis_acc
        sq_ref[0, rs, cs] = sq_acc
        return e_acc

    energy = lax.fori_loop(0, chunks_y * chunks_z, chunk,
                           jnp.zeros((ROWS, LANES), jnp.float32))
    energy_ref[0] = energy


def strip_sums(deformed, rows, cols, displacement, image, contrast_y, bright_y):
    depth_x, width_y, width_z = image.shape
    nodes = depth_x // KNOT
    f32 = jnp.float32
    block_sum = jax.ShapeDtypeStruct((nodes, width_y, width_z), f32)
    node_spec = pl.BlockSpec((1, width_y, width_z), lambda i: (i, 0, 0))
    plane_spec = pl.BlockSpec((KNOT, width_y, width_z), lambda i: (i, 0, 0))
    return pl.pallas_call(
        strip_kernel,
        grid=(nodes,),
        in_specs=[
            pl.BlockSpec((1, width_y, width_z), lambda i: (jnp.maximum(i * KNOT - 1, 0), 0, 0)),
            plane_spec,
            pl.BlockSpec((1, width_y, width_z),
                         lambda i: (jnp.minimum(i * KNOT + KNOT, depth_x - 1), 0, 0)),
            pl.BlockSpec(memory_space=pltpu.VMEM),
            pl.BlockSpec(memory_space=pltpu.VMEM),
            pl.BlockSpec((3, KNOT, width_y, width_z), lambda i: (0, i, 0, 0)),
            plane_spec,
            node_spec,
            node_spec,
        ],
        out_specs=[
            plane_spec,
            node_spec,
            node_spec,
            node_spec,
            pl.BlockSpec((1, ROWS, LANES), lambda i: (i, 0, 0)),
        ],
        out_shape=[
            jax.ShapeDtypeStruct(image.shape, jnp.bfloat16),
            block_sum,
            block_sum,
            block_sum,
            jax.ShapeDtypeStruct((nodes, ROWS, LANES), f32),
        ],
        scratch_shapes=[
            pltpu.VMEM((width_y + rows.shape[1], width_z + cols.shape[2]), f32),
            pltpu.VMEM((KNOT + 2, 9, width_y, width_z), f32),
        ],
        compiler_params=pltpu.CompilerParams(
            dimension_semantics=("arbitrary",), vmem_limit_bytes=60 * 1024 * 1024),
    )(deformed, deformed, deformed, rows, cols, displacement, image, contrast_y, bright_y)


def node_sums(field):
    nodes, width_y, width_z = field.shape
    return field.reshape(nodes, width_y // KNOT, KNOT, width_z).sum(axis=2)


def exchange(axis, n, me, d, src, buffer, send_sem, recv_sem):
    target = lax.rem(me + d, n)
    return pltpu.make_async_remote_copy(
        src_ref=src(target), dst_ref=buffer.at[me],
        send_sem=send_sem.at[target], recv_sem=recv_sem.at[me],
        device_id={axis: target}, device_id_type=pl.DeviceIdType.MESH)


def arrival(axis, n, me, d, src_ref, buffer, sem):
    source = lax.rem(me + n - d, n)
    return pltpu.make_async_remote_copy(
        src_ref=src_ref, dst_ref=buffer.at[source],
        send_sem=sem.at[source], recv_sem=sem.at[source],
        device_id={axis: source}, device_id_type=pl.DeviceIdType.MESH)


def both_sums_kernel(nz, ny, plane_row, depth_row, plane_ref, depth_ref, plane_out, depth_out,
                     plane_landed, depth_landed, plane_summed, depth_summed,
                     plane_gathered, depth_gathered, sems):
    mz, my = lax.axis_index("gz"), lax.axis_index("gy")
    barrier = pltpu.get_barrier_semaphore()
    for d in range(1, nz):
        pl.semaphore_signal(barrier, inc=1, device_id={"gz": lax.rem(mz + d, nz)},
                            device_id_type=pl.DeviceIdType.MESH)
    for d in range(1, ny):
        pl.semaphore_signal(barrier, inc=1, device_id={"gy": lax.rem(my + d, ny)},
                            device_id_type=pl.DeviceIdType.MESH)
    pl.semaphore_wait(barrier, nz - 1 + ny - 1)
    zs1, zr1, zs2, zr2, ys1, yr1, ys2, yr2 = sems

    z_out = [exchange("gz", nz, mz, d, lambda t: plane_ref.at[t], plane_landed, zs1, zr1)
             for d in range(1, nz)]
    y_out = [exchange("gy", ny, my, d, lambda t: depth_ref.at[t], depth_landed, ys1, yr1)
             for d in range(1, ny)]
    for copy in z_out + y_out:
        copy.start()
    depth_total = depth_ref[my]
    for d in range(1, ny):
        arrival("gy", ny, my, d, depth_ref.at[0], depth_landed, yr1).wait_recv()
        depth_total = depth_total + depth_landed[lax.rem(my + ny - d, ny)]
    depth_summed[...] = depth_total
    plane_total = plane_ref[mz]
    for d in range(1, nz):
        arrival("gz", nz, mz, d, plane_ref.at[0], plane_landed, zr1).wait_recv()
        plane_total = plane_total + plane_landed[lax.rem(mz + nz - d, nz)]
    rows = lax.broadcasted_iota(jnp.int32, plane_total.shape, 0)
    lanes = lax.broadcasted_iota(jnp.int32, plane_total.shape, 1)
    slot = jnp.logical_and(rows == plane_row, lanes == RANK)
    depth_slot = jnp.logical_and(
        lax.broadcasted_iota(jnp.int32, depth_total.shape, 0) == depth_row,
        lax.broadcasted_iota(jnp.int32, depth_total.shape, 1) == RANK)
    column_energy = jnp.sum(jnp.where(depth_slot, depth_total, 0.0))
    plane_total = jnp.where(slot, column_energy, plane_total)
    plane_summed[...] = plane_total
    for copy in z_out + y_out:
        copy.wait_send()

    z_out = [exchange("gz", nz, mz, d, lambda t: plane_summed, plane_gathered, zs2, zr2)
             for d in range(1, nz)]
    y_out = [exchange("gy", ny, my, d, lambda t: depth_summed, depth_gathered, ys2, yr2)
             for d in range(1, ny)]
    for copy in z_out + y_out:
        copy.start()
    plane_out[mz] = plane_total
    depth_out[my] = depth_total
    for d in range(1, nz):
        arrival("gz", nz, mz, d, plane_summed, plane_gathered, zr2).wait_recv()
        source = lax.rem(mz + nz - d, nz)
        plane_out[source] = plane_gathered[source]
    for d in range(1, ny):
        arrival("gy", ny, my, d, depth_summed, depth_gathered, yr2).wait_recv()
        source = lax.rem(my + ny - d, ny)
        depth_out[source] = depth_gathered[source]
    for copy in z_out + y_out:
        copy.wait_send()


def chunked(main, extras, n):
    rows = -(-main.shape[0] // (n * 128))
    main = jnp.pad(main, (0, n * rows * 128 - main.shape[0])).reshape(n, rows, 128)
    tail = jnp.pad(extras, (0, 128 - extras.shape[0]))
    tail = jnp.broadcast_to(tail, (n, 1, 128))
    spare = -(-(rows + 1) // 8) * 8 - rows - 1
    return jnp.concatenate([main, tail, jnp.zeros((n, spare, 128), main.dtype)], axis=1), rows


def both_sums(plane_parts, depth_parts, plane_row, depth_row):
    nz, ny = plane_parts.shape[0], depth_parts.shape[0]
    f32 = jnp.float32
    dma = pltpu.SemaphoreType.DMA
    return pl.pallas_call(
        functools.partial(both_sums_kernel, nz, ny, plane_row, depth_row),
        out_shape=[jax.ShapeDtypeStruct(plane_parts.shape, f32),
                   jax.ShapeDtypeStruct(depth_parts.shape, f32)],
        in_specs=[pl.BlockSpec(memory_space=pltpu.VMEM)] * 2,
        out_specs=[pl.BlockSpec(memory_space=pltpu.VMEM)] * 2,
        scratch_shapes=[
            pltpu.VMEM(plane_parts.shape, f32),
            pltpu.VMEM(depth_parts.shape, f32),
            pltpu.VMEM(plane_parts.shape[1:], f32),
            pltpu.VMEM(depth_parts.shape[1:], f32),
            pltpu.VMEM(plane_parts.shape, f32),
            pltpu.VMEM(depth_parts.shape, f32),
            [dma((nz,)), dma((nz,)), dma((nz,)), dma((nz,)),
             dma((ny,)), dma((ny,)), dma((ny,)), dma((ny,))],
        ],
        compiler_params=pltpu.CompilerParams(collective_id=1, has_side_effects=True),
    )(plane_parts, depth_parts)


def local(reference_image, deformed, displacement, plane_factors, depth_factors):
    rows, cols = halo_blocks(deformed)
    fields = jnp.einsum("krij,krz->kijz", plane_factors, depth_factors, precision=highest)
    fields = jnp.repeat(fields, KNOT, axis=2)
    residual, prod, mis, sq, energy_parts = strip_sums(
        deformed, rows, cols, displacement, reference_image, fields[0], fields[1])
    prod, mis, sq = node_sums(prod), node_sums(mis), node_sums(sq)
    local_energy = jnp.sum(energy_parts)

    first, second = plane_factors[0], plane_factors[1]
    grad_depth = -jnp.stack([
        jnp.einsum("rij,ijz->rz", first, prod, precision=highest),
        jnp.einsum("rij,ijz->rz", second, mis, precision=highest)])
    first_depth = jnp.einsum("rij,ijz->rz", first * first, sq, precision=highest)
    level_sum = KNOT * KNOT * jnp.sum(second * second, axis=(1, 2))
    grad_plane = -jnp.stack([
        jnp.einsum("rz,ijz->rij", depth_factors[0], prod, precision=highest),
        jnp.einsum("rz,ijz->rij", depth_factors[1], mis, precision=highest)])
    first_diag = jnp.einsum("rz,ijz->rij", depth_factors[0] * depth_factors[0], sq, precision=highest)
    depth_level = KNOT * KNOT * jnp.sum(depth_factors[1] * depth_factors[1], axis=1)

    nz, ny = lax.axis_size("gz"), lax.axis_size("gy")
    plane_terms = jnp.concatenate([grad_plane.reshape(-1), first_diag.reshape(-1)])
    depth_terms = jnp.concatenate([grad_depth.reshape(-1), first_depth.reshape(-1)])
    blank = jnp.zeros((), jnp.float32)
    plane_parts, plane_rows = chunked(plane_terms, jnp.concatenate([depth_level, blank[None]]), nz)
    depth_parts, depth_rows = chunked(depth_terms, jnp.concatenate([level_sum, local_energy[None]]), ny)
    plane_summed, depth_summed = both_sums(plane_parts, depth_parts, plane_rows, depth_rows)
    plane_terms = plane_summed[:, :plane_rows].reshape(-1)
    depth_terms = depth_summed[:, :depth_rows].reshape(-1)
    grad_plane = plane_terms[: grad_plane.size].reshape(grad_plane.shape)
    first_diag = plane_terms[grad_plane.size : grad_plane.size + first_diag.size].reshape(first_diag.shape)
    grad_depth = depth_terms[: grad_depth.size].reshape(grad_depth.shape)
    first_depth = depth_terms[grad_depth.size : grad_depth.size + first_depth.size].reshape(first_depth.shape)
    depth_level = plane_summed[0, plane_rows, :RANK]
    level_sum = depth_summed[0, depth_rows, :RANK]
    energy = jnp.sum(plane_summed[:, plane_rows, RANK])

    nodes_x = plane_factors.shape[2]
    nodes_y = plane_factors.shape[3] * lax.axis_size("gy")
    full_z = depth_factors.shape[2] * lax.axis_size("gz")
    diag_plane = jnp.stack(
        [first_diag, jnp.broadcast_to(depth_level[:, None, None], first_diag.shape)])
    lam_plane = damping * RANK * energy / (nodes_x * nodes_y)
    lam_depth = damping * energy / full_z
    step_plane = -grad_plane / (diag_plane + lam_plane + epsilon)
    diag_depth = jnp.stack([first_depth, jnp.broadcast_to(level_sum[:, None], first_depth.shape)])
    step_depth = -grad_depth / (diag_depth + lam_depth + epsilon)
    return (residual, step_plane, step_depth)


def solution(mesh):
    placed = (
        P(None, "gy", "gz"),
        P(None, "gy", "gz"),
        P(None, None, "gy", "gz"),
        P(None, None, None, "gy"),
        P(None, None, "gz"),
    )
    return jax.shard_map(
        local,
        mesh=mesh,
        in_specs=placed,
        out_specs=(P(None, "gy", "gz"), P(None, None, None, "gy"), P(None, None, "gz")),
        check_vma=False,
    )
```

```python
import functools

import jax
import jax.numpy as jnp
from jax import lax
from jax.experimental import pallas as pl
from jax.experimental.pallas import tpu as pltpu
from jax.sharding import PartitionSpec as P

RANK = 32
KNOT = 8

epsilon = 1e-06
damping = 0.01
highest = lax.Precision.HIGHEST

ROWS = 16
LANES = 256


def neighbours(part, axis, forward):
    count = lax.axis_size(axis)
    if forward:
        pairs = [(i, i + 1) for i in range(count - 1)]
    else:
        pairs = [(i + 1, i) for i in range(count - 1)]
    return lax.ppermute(part, axis, pairs)


def halo_kernel(ny, nz, rows_ref, cols_ref, rows_out, cols_out, rows_got, cols_got,
                send_sems, recv_sems):
    my, mz = lax.axis_index("gy"), lax.axis_index("gz")
    up, down = lax.rem(my + 1, ny), lax.rem(my + ny - 1, ny)
    right, left = lax.rem(mz + 1, nz), lax.rem(mz + nz - 1, nz)
    plan = [
        (rows_ref.at[0], rows_got.at[0], (down, mz)),
        (rows_ref.at[1], rows_got.at[1], (up, mz)),
        (cols_ref.at[0], cols_got.at[0], (my, left)),
        (cols_ref.at[1], cols_got.at[1], (my, right)),
        (cols_ref.at[0], cols_got.at[2], (down, left)),
        (cols_ref.at[0], cols_got.at[3], (up, left)),
        (cols_ref.at[1], cols_got.at[4], (down, right)),
        (cols_ref.at[1], cols_got.at[5], (up, right)),
    ]
    barrier = pltpu.get_barrier_semaphore()
    for _, _, device in plan:
        pl.semaphore_signal(barrier, inc=1, device_id=device,
                            device_id_type=pl.DeviceIdType.MESH)
    pl.semaphore_wait(barrier, len(plan))
    copies = []
    for k, (source, slot, device) in enumerate(plan):
        copy = pltpu.make_async_remote_copy(
            src_ref=source, dst_ref=slot, send_sem=send_sems.at[k], recv_sem=recv_sems.at[k],
            device_id=device, device_id_type=pl.DeviceIdType.MESH)
        copy.start()
        copies.append(copy)
    for copy in copies:
        copy.wait()
    rows_out[...] = rows_got[...]
    cols_out[...] = cols_got[...]


def swap_halos(rows_send, cols_send):
    ny, nz = lax.axis_size("gy"), lax.axis_size("gz")
    dma = pltpu.SemaphoreType.DMA
    rows_shape = rows_send.shape
    cols_shape = (6,) + cols_send.shape[1:]
    return pl.pallas_call(
        functools.partial(halo_kernel, ny, nz),
        out_shape=[jax.ShapeDtypeStruct(rows_shape, rows_send.dtype),
                   jax.ShapeDtypeStruct(cols_shape, cols_send.dtype)],
        in_specs=[pl.BlockSpec(memory_space=pltpu.VMEM)] * 2,
        out_specs=[pl.BlockSpec(memory_space=pltpu.VMEM)] * 2,
        scratch_shapes=[
            pltpu.VMEM(rows_shape, rows_send.dtype),
            pltpu.VMEM(cols_shape, cols_send.dtype),
            dma((8,)),
            dma((8,)),
        ],
        compiler_params=pltpu.CompilerParams(collective_id=2, has_side_effects=True),
    )(rows_send, cols_send)


def halo_blocks(deformed):
    depth_x, width_y, width_z = deformed.shape
    f32 = jnp.float32
    ny, nz = lax.axis_size("gy"), lax.axis_size("gz")
    my, mz = lax.axis_index("gy"), lax.axis_index("gz")
    rows_send = jnp.stack([deformed[:, 0, :], deformed[:, width_y - 1, :]])
    cols_send = jnp.stack([deformed[:, :, 0], deformed[:, :, width_z - 1]])
    rows_got, cols_got = swap_halos(rows_send, cols_send)
    has_up = (my < ny - 1).astype(f32)
    has_down = (my > 0).astype(f32)
    has_right = (mz < nz - 1).astype(f32)
    has_left = (mz > 0).astype(f32)
    rows_got = rows_got.astype(f32)
    cols_got = cols_got.astype(f32)
    high_y = rows_got[0] * has_up
    low_y = rows_got[1] * has_down
    high_z = cols_got[0] * has_right
    low_z = cols_got[1] * has_left
    high_high = cols_got[2][:, 0] * (has_up * has_right)
    low_high = cols_got[3][:, width_y - 1] * (has_down * has_right)
    high_low = cols_got[4][:, 0] * (has_up * has_left)
    low_low = cols_got[5][:, width_y - 1] * (has_down * has_left)
    gap_y = jnp.zeros((depth_x, 6, width_z), f32)
    rows = jnp.concatenate([high_y[:, None], gap_y, low_y[:, None]], axis=1)
    gap = jnp.zeros((depth_x, 6), f32)
    side_high = jnp.concatenate([high_z, high_high[:, None], gap, low_high[:, None]], axis=1)
    side_low = jnp.concatenate([low_z, high_low[:, None], gap, low_low[:, None]], axis=1)
    lanes = lax.broadcasted_iota(jnp.int32, (1, 1, 128), 2)
    cols = jnp.where(lanes == 0, side_high[:, :, None],
                     jnp.where(lanes == 127, side_low[:, :, None], 0.0))
    return rows, cols


def lerp(base, other, weight):
    return base + weight * (other - base)


def strip_kernel(prev_ref, main_ref, next_ref, rows_ref, cols_ref, disp_ref, image_ref,
                 contrast_ref, bright_ref,
                 res_ref, prod_ref, mis_ref, sq_ref, energy_ref, pad_ref, shifts_ref):
    block = pl.program_id(0)
    depth_x = rows_ref.shape[0]
    width_y, width_z = image_ref.shape[1], image_ref.shape[2]
    pad_y, pad_z = pad_ref.shape

    def source_plane(p, plane):
        plane_x = block * KNOT - 1 + p
        valid = jnp.logical_and(plane_x >= 0, plane_x < depth_x)
        safe = jnp.clip(plane_x, 0, depth_x - 1)
        pad_ref[:width_y, :width_z] = plane.astype(jnp.float32)
        pad_ref[width_y:, :width_z] = rows_ref[safe]
        pad_ref[:, width_z:] = cols_ref[safe]
        whole = jnp.where(valid, pad_ref[...], 0.0)
        by_y = (pltpu.roll(whole, 1, 0), whole, pltpu.roll(whole, pad_y - 1, 0))
        for b in range(3):
            part = by_y[b][:width_y]
            by_z = (pltpu.roll(part, 1, 1), part, pltpu.roll(part, pad_z - 1, 1))
            for c in range(3):
                shifts_ref[p, 3 * b + c] = by_z[c][:, :width_z]

    source_plane(0, prev_ref[0])

    def inner_plane(p, carry):
        source_plane(p, main_ref[p - 1])
        return carry

    lax.fori_loop(1, KNOT + 1, inner_plane, 0)
    source_plane(KNOT + 1, next_ref[0])

    chunks_y = width_y // ROWS
    chunks_z = width_z // LANES

    def chunk(k, energy):
        r0 = pl.multiple_of((k // chunks_z) * ROWS, ROWS)
        c0 = pl.multiple_of((k % chunks_z) * LANES, LANES)
        rs = pl.ds(r0, ROWS)
        cs = pl.ds(c0, LANES)
        contrast = contrast_ref[0, rs, cs]
        bright = bright_ref[0, rs, cs]

        def plane(xl, acc):
            prod_acc, mis_acc, sq_acc, e_acc = acc

            def src(a, b, c):
                return shifts_ref[xl + 1 + a, 3 * (b + 1) + (c + 1), rs, cs]

            sx = disp_ref[0, xl, rs, cs].astype(jnp.float32)
            sy = disp_ref[1, xl, rs, cs].astype(jnp.float32)
            sz = disp_ref[2, xl, rs, cs].astype(jnp.float32)
            gx, gy, gz = sx > 0, sy > 0, sz > 0
            ax, ay, az = jnp.abs(sx), jnp.abs(sy), jnp.abs(sz)
            xs = {}
            for b in (-1, 0, 1):
                for c in (-1, 0, 1):
                    xs[b, c] = jnp.where(gx, src(1, b, c), src(-1, b, c))
            y0 = {c: jnp.where(gy, src(0, 1, c), src(0, -1, c)) for c in (-1, 0, 1)}
            y1 = {c: jnp.where(gy, xs[1, c], xs[-1, c]) for c in (-1, 0, 1)}
            centre = src(0, 0, 0)
            z00 = jnp.where(gz, src(0, 0, 1), src(0, 0, -1))
            z01 = jnp.where(gz, y0[1], y0[-1])
            z10 = jnp.where(gz, xs[0, 1], xs[0, -1])
            z11 = jnp.where(gz, y1[1], y1[-1])
            l00 = lerp(centre, z00, az)
            l01 = lerp(y0[0], z01, az)
            l10 = lerp(xs[0, 0], z10, az)
            l11 = lerp(y1[0], z11, az)
            m0 = lerp(l00, l01, ay)
            m1 = lerp(l10, l11, ay)
            warped = lerp(m0, m1, ax)
            values = image_ref[xl, rs, cs].astype(jnp.float32)
            misfit = warped - contrast * values - bright
            res_ref[xl, rs, cs] = misfit.astype(res_ref.dtype)
            return (prod_acc + misfit * values, mis_acc + misfit,
                    sq_acc + values * values, e_acc + misfit * misfit)

        zero = jnp.zeros((ROWS, LANES), jnp.float32)
        prod_acc, mis_acc, sq_acc, e_acc = lax.fori_loop(
            0, KNOT, plane, (zero, zero, zero, energy))
        prod_ref[0, rs, cs] = prod_acc
        mis_ref[0, rs, cs] = mis_acc
        sq_ref[0, rs, cs] = sq_acc
        return e_acc

    energy = lax.fori_loop(0, chunks_y * chunks_z, chunk,
                           jnp.zeros((ROWS, LANES), jnp.float32))
    energy_ref[0] = energy


def strip_sums(deformed, rows, cols, displacement, image, contrast_y, bright_y):
    depth_x, width_y, width_z = image.shape
    nodes = depth_x // KNOT
    f32 = jnp.float32
    block_sum = jax.ShapeDtypeStruct((nodes, width_y, width_z), f32)
    node_spec = pl.BlockSpec((1, width_y, width_z), lambda i: (i, 0, 0))
    plane_spec = pl.BlockSpec((KNOT, width_y, width_z), lambda i: (i, 0, 0))
    return pl.pallas_call(
        strip_kernel,
        grid=(nodes,),
        in_specs=[
            pl.BlockSpec((1, width_y, width_z), lambda i: (jnp.maximum(i * KNOT - 1, 0), 0, 0)),
            plane_spec,
            pl.BlockSpec((1, width_y, width_z),
                         lambda i: (jnp.minimum(i * KNOT + KNOT, depth_x - 1), 0, 0)),
            pl.BlockSpec(memory_space=pltpu.VMEM),
            pl.BlockSpec(memory_space=pltpu.VMEM),
            pl.BlockSpec((3, KNOT, width_y, width_z), lambda i: (0, i, 0, 0)),
            plane_spec,
            node_spec,
            node_spec,
        ],
        out_specs=[
            plane_spec,
            node_spec,
            node_spec,
            node_spec,
            pl.BlockSpec((1, ROWS, LANES), lambda i: (i, 0, 0)),
        ],
        out_shape=[
            jax.ShapeDtypeStruct(image.shape, jnp.bfloat16),
            block_sum,
            block_sum,
            block_sum,
            jax.ShapeDtypeStruct((nodes, ROWS, LANES), f32),
        ],
        scratch_shapes=[
            pltpu.VMEM((width_y + rows.shape[1], width_z + cols.shape[2]), f32),
            pltpu.VMEM((KNOT + 2, 9, width_y, width_z), f32),
        ],
        compiler_params=pltpu.CompilerParams(
            dimension_semantics=("arbitrary",), vmem_limit_bytes=60 * 1024 * 1024),
    )(deformed, deformed, deformed, rows, cols, displacement, image, contrast_y, bright_y)


def node_sums(field):
    nodes, width_y, width_z = field.shape
    return field.reshape(nodes, width_y // KNOT, KNOT, width_z).sum(axis=2)


def exchange(axis, n, me, d, src, buffer, send_sem, recv_sem):
    target = lax.rem(me + d, n)
    return pltpu.make_async_remote_copy(
        src_ref=src(target), dst_ref=buffer.at[me],
        send_sem=send_sem.at[target], recv_sem=recv_sem.at[me],
        device_id={axis: target}, device_id_type=pl.DeviceIdType.MESH)


def arrival(axis, n, me, d, src_ref, buffer, sem):
    source = lax.rem(me + n - d, n)
    return pltpu.make_async_remote_copy(
        src_ref=src_ref, dst_ref=buffer.at[source],
        send_sem=sem.at[source], recv_sem=sem.at[source],
        device_id={axis: source}, device_id_type=pl.DeviceIdType.MESH)


def both_sums_kernel(nz, ny, plane_row, depth_row, plane_ref, depth_ref, plane_out, depth_out,
                     plane_landed, depth_landed, plane_summed, depth_summed,
                     plane_gathered, depth_gathered, sems):
    mz, my = lax.axis_index("gz"), lax.axis_index("gy")
    barrier = pltpu.get_barrier_semaphore()
    for d in range(1, nz):
        pl.semaphore_signal(barrier, inc=1, device_id={"gz": lax.rem(mz + d, nz)},
                            device_id_type=pl.DeviceIdType.MESH)
    for d in range(1, ny):
        pl.semaphore_signal(barrier, inc=1, device_id={"gy": lax.rem(my + d, ny)},
                            device_id_type=pl.DeviceIdType.MESH)
    pl.semaphore_wait(barrier, nz - 1 + ny - 1)
    zs1, zr1, zs2, zr2, ys1, yr1, ys2, yr2 = sems

    z_out = [exchange("gz", nz, mz, d, lambda t: plane_ref.at[t], plane_landed, zs1, zr1)
             for d in range(1, nz)]
    y_out = [exchange("gy", ny, my, d, lambda t: depth_ref.at[t], depth_landed, ys1, yr1)
             for d in range(1, ny)]
    for copy in z_out + y_out:
        copy.start()
    depth_total = depth_ref[my]
    for d in range(1, ny):
        arrival("gy", ny, my, d, depth_ref.at[0], depth_landed, yr1).wait_recv()
        depth_total = depth_total + depth_landed[lax.rem(my + ny - d, ny)]
    depth_summed[...] = depth_total
    plane_total = plane_ref[mz]
    for d in range(1, nz):
        arrival("gz", nz, mz, d, plane_ref.at[0], plane_landed, zr1).wait_recv()
        plane_total = plane_total + plane_landed[lax.rem(mz + nz - d, nz)]
    rows = lax.broadcasted_iota(jnp.int32, plane_total.shape, 0)
    lanes = lax.broadcasted_iota(jnp.int32, plane_total.shape, 1)
    slot = jnp.logical_and(rows == plane_row, lanes == RANK)
    depth_slot = jnp.logical_and(
        lax.broadcasted_iota(jnp.int32, depth_total.shape, 0) == depth_row,
        lax.broadcasted_iota(jnp.int32, depth_total.shape, 1) == RANK)
    column_energy = jnp.sum(jnp.where(depth_slot, depth_total, 0.0))
    plane_total = jnp.where(slot, column_energy, plane_total)
    plane_summed[...] = plane_total
    for copy in z_out + y_out:
        copy.wait_send()

    z_out = [exchange("gz", nz, mz, d, lambda t: plane_summed, plane_gathered, zs2, zr2)
             for d in range(1, nz)]
    y_out = [exchange("gy", ny, my, d, lambda t: depth_summed, depth_gathered, ys2, yr2)
             for d in range(1, ny)]
    for copy in z_out + y_out:
        copy.start()
    plane_out[mz] = plane_total
    depth_out[my] = depth_total
    for d in range(1, nz):
        arrival("gz", nz, mz, d, plane_summed, plane_gathered, zr2).wait_recv()
        source = lax.rem(mz + nz - d, nz)
        plane_out[source] = plane_gathered[source]
    for d in range(1, ny):
        arrival("gy", ny, my, d, depth_summed, depth_gathered, yr2).wait_recv()
        source = lax.rem(my + ny - d, ny)
        depth_out[source] = depth_gathered[source]
    for copy in z_out + y_out:
        copy.wait_send()


def chunked(main, extras, n):
    rows = -(-main.shape[0] // (n * 128))
    main = jnp.pad(main, (0, n * rows * 128 - main.shape[0])).reshape(n, rows, 128)
    tail = jnp.pad(extras, (0, 128 - extras.shape[0]))
    tail = jnp.broadcast_to(tail, (n, 1, 128))
    spare = -(-(rows + 1) // 8) * 8 - rows - 1
    return jnp.concatenate([main, tail, jnp.zeros((n, spare, 128), main.dtype)], axis=1), rows


def both_sums(plane_parts, depth_parts, plane_row, depth_row):
    nz, ny = plane_parts.shape[0], depth_parts.shape[0]
    f32 = jnp.float32
    dma = pltpu.SemaphoreType.DMA
    return pl.pallas_call(
        functools.partial(both_sums_kernel, nz, ny, plane_row, depth_row),
        out_shape=[jax.ShapeDtypeStruct(plane_parts.shape, f32),
                   jax.ShapeDtypeStruct(depth_parts.shape, f32)],
        in_specs=[pl.BlockSpec(memory_space=pltpu.VMEM)] * 2,
        out_specs=[pl.BlockSpec(memory_space=pltpu.VMEM)] * 2,
        scratch_shapes=[
            pltpu.VMEM(plane_parts.shape, f32),
            pltpu.VMEM(depth_parts.shape, f32),
            pltpu.VMEM(plane_parts.shape[1:], f32),
            pltpu.VMEM(depth_parts.shape[1:], f32),
            pltpu.VMEM(plane_parts.shape, f32),
            pltpu.VMEM(depth_parts.shape, f32),
            [dma((nz,)), dma((nz,)), dma((nz,)), dma((nz,)),
             dma((ny,)), dma((ny,)), dma((ny,)), dma((ny,))],
        ],
        compiler_params=pltpu.CompilerParams(collective_id=1, has_side_effects=True),
    )(plane_parts, depth_parts)


def local(reference_image, deformed, displacement, plane_factors, depth_factors):
    rows, cols = halo_blocks(deformed)
    fields = jnp.einsum("krij,krz->kijz", plane_factors, depth_factors, precision=highest)
    fields = jnp.repeat(fields, KNOT, axis=2)
    residual, prod, mis, sq, energy_parts = strip_sums(
        deformed, rows, cols, displacement, reference_image, fields[0], fields[1])
    prod, mis, sq = node_sums(prod), node_sums(mis), node_sums(sq)
    local_energy = jnp.sum(energy_parts)

    first, second = plane_factors[0], plane_factors[1]
    grad_depth = -jnp.stack([
        jnp.einsum("rij,ijz->rz", first, prod, precision=highest),
        jnp.einsum("rij,ijz->rz", second, mis, precision=highest)])
    first_depth = jnp.einsum("rij,ijz->rz", first * first, sq, precision=highest)
    level_sum = KNOT * KNOT * jnp.sum(second * second, axis=(1, 2))
    grad_plane = -jnp.stack([
        jnp.einsum("rz,ijz->rij", depth_factors[0], prod, precision=highest),
        jnp.einsum("rz,ijz->rij", depth_factors[1], mis, precision=highest)])
    first_diag = jnp.einsum("rz,ijz->rij", depth_factors[0] * depth_factors[0], sq, precision=highest)
    depth_level = KNOT * KNOT * jnp.sum(depth_factors[1] * depth_factors[1], axis=1)

    nz, ny = lax.axis_size("gz"), lax.axis_size("gy")
    plane_terms = jnp.concatenate([grad_plane.reshape(-1), first_diag.reshape(-1)])
    depth_terms = jnp.concatenate([grad_depth.reshape(-1), first_depth.reshape(-1)])
    blank = jnp.zeros((), jnp.float32)
    plane_parts, plane_rows = chunked(plane_terms, jnp.concatenate([depth_level, blank[None]]), nz)
    depth_parts, depth_rows = chunked(depth_terms, jnp.concatenate([level_sum, local_energy[None]]), ny)
    plane_summed, depth_summed = both_sums(plane_parts, depth_parts, plane_rows, depth_rows)
    plane_terms = plane_summed[:, :plane_rows].reshape(-1)
    depth_terms = depth_summed[:, :depth_rows].reshape(-1)
    grad_plane = plane_terms[: grad_plane.size].reshape(grad_plane.shape)
    first_diag = plane_terms[grad_plane.size : grad_plane.size + first_diag.size].reshape(first_diag.shape)
    grad_depth = depth_terms[: grad_depth.size].reshape(grad_depth.shape)
    first_depth = depth_terms[grad_depth.size : grad_depth.size + first_depth.size].reshape(first_depth.shape)
    depth_level = plane_summed[0, plane_rows, :RANK]
    level_sum = depth_summed[0, depth_rows, :RANK]
    energy = jnp.sum(plane_summed[:, plane_rows, RANK])

    nodes_x = plane_factors.shape[2]
    nodes_y = plane_factors.shape[3] * lax.axis_size("gy")
    full_z = depth_factors.shape[2] * lax.axis_size("gz")
    diag_plane = jnp.stack(
        [first_diag, jnp.broadcast_to(depth_level[:, None, None], first_diag.shape)])
    lam_plane = damping * RANK * energy / (nodes_x * nodes_y)
    lam_depth = damping * energy / full_z
    step_plane = -grad_plane / (diag_plane + lam_plane + epsilon)
    diag_depth = jnp.stack([first_depth, jnp.broadcast_to(level_sum[:, None], first_depth.shape)])
    step_depth = -grad_depth / (diag_depth + lam_depth + epsilon)
    return (residual, step_plane, step_depth)


def solution(mesh):
    placed = (
        P(None, "gy", "gz"),
        P(None, "gy", "gz"),
        P(None, None, "gy", "gz"),
        P(None, None, None, "gy"),
        P(None, None, "gz"),
    )
    return jax.shard_map(
        local,
        mesh=mesh,
        in_specs=placed,
        out_specs=(P(None, "gy", "gz"), P(None, None, None, "gy"), P(None, None, "gz")),
        check_vma=False,
    )
```

```python
import functools

import jax
import jax.numpy as jnp
from jax import lax
from jax.experimental import pallas as pl
from jax.experimental.pallas import tpu as pltpu
from jax.sharding import PartitionSpec as P

RANK = 32
KNOT = 8

epsilon = 1e-06
damping = 0.01
highest = lax.Precision.HIGHEST

ROWS = 16
LANES = 256


def neighbours(part, axis, forward):
    count = lax.axis_size(axis)
    if forward:
        pairs = [(i, i + 1) for i in range(count - 1)]
    else:
        pairs = [(i + 1, i) for i in range(count - 1)]
    return lax.ppermute(part, axis, pairs)


def halo_kernel(ny, nz, rows_ref, cols_ref, rows_out, cols_out, rows_got, cols_got,
                send_sems, recv_sems):
    my, mz = lax.axis_index("gy"), lax.axis_index("gz")
    up, down = lax.rem(my + 1, ny), lax.rem(my + ny - 1, ny)
    right, left = lax.rem(mz + 1, nz), lax.rem(mz + nz - 1, nz)
    plan = [
        (rows_ref.at[0], rows_got.at[0], (down, mz)),
        (rows_ref.at[1], rows_got.at[1], (up, mz)),
        (cols_ref.at[0], cols_got.at[0], (my, left)),
        (cols_ref.at[1], cols_got.at[1], (my, right)),
        (cols_ref.at[0], cols_got.at[2], (down, left)),
        (cols_ref.at[0], cols_got.at[3], (up, left)),
        (cols_ref.at[1], cols_got.at[4], (down, right)),
        (cols_ref.at[1], cols_got.at[5], (up, right)),
    ]
    barrier = pltpu.get_barrier_semaphore()
    for _, _, device in plan:
        pl.semaphore_signal(barrier, inc=1, device_id=device,
                            device_id_type=pl.DeviceIdType.MESH)
    pl.semaphore_wait(barrier, len(plan))
    copies = []
    for k, (source, slot, device) in enumerate(plan):
        copy = pltpu.make_async_remote_copy(
            src_ref=source, dst_ref=slot, send_sem=send_sems.at[k], recv_sem=recv_sems.at[k],
            device_id=device, device_id_type=pl.DeviceIdType.MESH)
        copy.start()
        copies.append(copy)
    for copy in copies:
        copy.wait()
    rows_out[...] = rows_got[...]
    cols_out[...] = cols_got[...]


def swap_halos(rows_send, cols_send):
    ny, nz = lax.axis_size("gy"), lax.axis_size("gz")
    dma = pltpu.SemaphoreType.DMA
    rows_shape = rows_send.shape
    cols_shape = (6,) + cols_send.shape[1:]
    return pl.pallas_call(
        functools.partial(halo_kernel, ny, nz),
        out_shape=[jax.ShapeDtypeStruct(rows_shape, rows_send.dtype),
                   jax.ShapeDtypeStruct(cols_shape, cols_send.dtype)],
        in_specs=[pl.BlockSpec(memory_space=pltpu.VMEM)] * 2,
        out_specs=[pl.BlockSpec(memory_space=pltpu.VMEM)] * 2,
        scratch_shapes=[
            pltpu.VMEM(rows_shape, rows_send.dtype),
            pltpu.VMEM(cols_shape, cols_send.dtype),
            dma((8,)),
            dma((8,)),
        ],
        compiler_params=pltpu.CompilerParams(collective_id=2, has_side_effects=True),
    )(rows_send, cols_send)


def halo_blocks(deformed):
    depth_x, width_y, width_z = deformed.shape
    f32 = jnp.float32
    ny, nz = lax.axis_size("gy"), lax.axis_size("gz")
    my, mz = lax.axis_index("gy"), lax.axis_index("gz")
    rows_send = jnp.stack([deformed[:, 0, :], deformed[:, width_y - 1, :]])
    cols_send = jnp.stack([deformed[:, :, 0], deformed[:, :, width_z - 1]])
    rows_got, cols_got = swap_halos(rows_send, cols_send)
    has_up = (my < ny - 1).astype(f32)
    has_down = (my > 0).astype(f32)
    has_right = (mz < nz - 1).astype(f32)
    has_left = (mz > 0).astype(f32)
    rows_got = rows_got.astype(f32)
    cols_got = cols_got.astype(f32)
    high_y = rows_got[0] * has_up
    low_y = rows_got[1] * has_down
    high_z = cols_got[0] * has_right
    low_z = cols_got[1] * has_left
    high_high = cols_got[2][:, 0] * (has_up * has_right)
    low_high = cols_got[3][:, width_y - 1] * (has_down * has_right)
    high_low = cols_got[4][:, 0] * (has_up * has_left)
    low_low = cols_got[5][:, width_y - 1] * (has_down * has_left)
    rows = jnp.stack([high_y, low_y])
    gap = jnp.zeros((depth_x, 6), f32)
    side_high = jnp.concatenate([high_z, high_high[:, None], gap, low_high[:, None]], axis=1)
    side_low = jnp.concatenate([low_z, high_low[:, None], gap, low_low[:, None]], axis=1)
    sides = jnp.stack([side_high.T, side_low.T])
    sides = jnp.pad(sides, ((0, 0), (0, 0), (0, 128 - depth_x)))
    return rows, sides


def lerp(base, other, weight):
    return base + weight * (other - base)


def strip_kernel(prev_ref, main_ref, next_ref, rows_ref, sides_ref, disp_ref, image_ref,
                 fields_ref,
                 res_ref, prod_ref, mis_ref, sq_ref, energy_ref, pad_ref, shifts_ref):
    block = pl.program_id(0)
    depth_x = rows_ref.shape[1]
    width_y, width_z = image_ref.shape[1], image_ref.shape[2]
    pad_y, pad_z = pad_ref.shape
    pad_ref[width_y:, :width_z] = jnp.zeros((pad_y - width_y, width_z), jnp.float32)
    lane = lax.broadcasted_iota(jnp.int32, (pad_y, pad_z - width_z), 1)

    def source_plane(p, plane):
        plane_x = block * KNOT - 1 + p
        valid = jnp.logical_and(plane_x >= 0, plane_x < depth_x)
        safe = jnp.clip(plane_x, 0, depth_x - 1)
        pad_ref[:width_y, :width_z] = plane.astype(jnp.float32)
        pad_ref[pl.ds(width_y, 1), :width_z] = rows_ref[0, pl.ds(safe, 1), :]
        pad_ref[pl.ds(pad_y - 1, 1), :width_z] = rows_ref[1, pl.ds(safe, 1), :]
        high = jnp.sum(jnp.where(lane == safe, sides_ref[0], 0.0), axis=1, keepdims=True)
        low = jnp.sum(jnp.where(lane == safe, sides_ref[1], 0.0), axis=1, keepdims=True)
        pad_ref[:, width_z:] = jnp.where(lane == 0, high, jnp.where(lane == pad_z - width_z - 1, low, 0.0))
        whole = jnp.where(valid, pad_ref[...], 0.0)
        by_y = (pltpu.roll(whole, 1, 0), whole, pltpu.roll(whole, pad_y - 1, 0))
        for b in range(3):
            part = by_y[b][:width_y]
            by_z = (pltpu.roll(part, 1, 1), part, pltpu.roll(part, pad_z - 1, 1))
            for c in range(3):
                shifts_ref[p, 3 * b + c] = by_z[c][:, :width_z]

    source_plane(0, prev_ref[0])

    def inner_plane(p, carry):
        source_plane(p, main_ref[p - 1])
        return carry

    lax.fori_loop(1, KNOT + 1, inner_plane, 0)
    source_plane(KNOT + 1, next_ref[0])

    chunks_y = width_y // ROWS
    chunks_z = width_z // LANES

    def chunk(k, energy):
        r0 = pl.multiple_of((k // chunks_z) * ROWS, ROWS)
        c0 = pl.multiple_of((k % chunks_z) * LANES, LANES)
        rs = pl.ds(r0, ROWS)
        cs = pl.ds(c0, LANES)
        j0 = r0 // KNOT
        upper = lax.broadcasted_iota(jnp.int32, (ROWS, LANES), 0) < KNOT
        node = lax.broadcasted_iota(jnp.int32, (KNOT, LANES), 0)

        def node_row(k, j):
            return jnp.sum(jnp.where(node == j, fields_ref[k, 0, :, cs], 0.0), axis=0, keepdims=True)

        contrast = jnp.where(upper, node_row(0, j0), node_row(0, j0 + 1))
        bright = jnp.where(upper, node_row(1, j0), node_row(1, j0 + 1))

        def plane(xl, acc):
            prod_acc, mis_acc, sq_acc, e_acc = acc

            def src(a, b, c):
                return shifts_ref[xl + 1 + a, 3 * (b + 1) + (c + 1), rs, cs]

            sx = disp_ref[0, xl, rs, cs].astype(jnp.float32)
            sy = disp_ref[1, xl, rs, cs].astype(jnp.float32)
            sz = disp_ref[2, xl, rs, cs].astype(jnp.float32)
            gx, gy, gz = sx > 0, sy > 0, sz > 0
            ax, ay, az = jnp.abs(sx), jnp.abs(sy), jnp.abs(sz)
            xs = {}
            for b in (-1, 0, 1):
                for c in (-1, 0, 1):
                    xs[b, c] = jnp.where(gx, src(1, b, c), src(-1, b, c))
            y0 = {c: jnp.where(gy, src(0, 1, c), src(0, -1, c)) for c in (-1, 0, 1)}
            y1 = {c: jnp.where(gy, xs[1, c], xs[-1, c]) for c in (-1, 0, 1)}
            centre = src(0, 0, 0)
            z00 = jnp.where(gz, src(0, 0, 1), src(0, 0, -1))
            z01 = jnp.where(gz, y0[1], y0[-1])
            z10 = jnp.where(gz, xs[0, 1], xs[0, -1])
            z11 = jnp.where(gz, y1[1], y1[-1])
            l00 = lerp(centre, z00, az)
            l01 = lerp(y0[0], z01, az)
            l10 = lerp(xs[0, 0], z10, az)
            l11 = lerp(y1[0], z11, az)
            m0 = lerp(l00, l01, ay)
            m1 = lerp(l10, l11, ay)
            warped = lerp(m0, m1, ax)
            values = image_ref[xl, rs, cs].astype(jnp.float32)
            misfit = warped - contrast * values - bright
            res_ref[xl, rs, cs] = misfit.astype(res_ref.dtype)
            return (prod_acc + misfit * values, mis_acc + misfit,
                    sq_acc + values * values, e_acc + misfit * misfit)

        zero = jnp.zeros((ROWS, LANES), jnp.float32)
        prod_acc, mis_acc, sq_acc, e_acc = lax.fori_loop(
            0, KNOT, plane, (zero, zero, zero, energy))
        prod_ref[0, rs, cs] = prod_acc
        mis_ref[0, rs, cs] = mis_acc
        sq_ref[0, rs, cs] = sq_acc
        return e_acc

    energy = lax.fori_loop(0, chunks_y * chunks_z, chunk,
                           jnp.zeros((ROWS, LANES), jnp.float32))
    energy_ref[0] = energy


def strip_sums(deformed, rows, sides, displacement, image, fields):
    depth_x, width_y, width_z = image.shape
    nodes = depth_x // KNOT
    f32 = jnp.float32
    block_sum = jax.ShapeDtypeStruct((nodes, width_y, width_z), f32)
    node_spec = pl.BlockSpec((1, width_y, width_z), lambda i: (i, 0, 0))
    plane_spec = pl.BlockSpec((KNOT, width_y, width_z), lambda i: (i, 0, 0))
    return pl.pallas_call(
        strip_kernel,
        grid=(nodes,),
        in_specs=[
            pl.BlockSpec((1, width_y, width_z), lambda i: (jnp.maximum(i * KNOT - 1, 0), 0, 0)),
            plane_spec,
            pl.BlockSpec((1, width_y, width_z),
                         lambda i: (jnp.minimum(i * KNOT + KNOT, depth_x - 1), 0, 0)),
            pl.BlockSpec(memory_space=pltpu.VMEM),
            pl.BlockSpec(memory_space=pltpu.VMEM),
            pl.BlockSpec((3, KNOT, width_y, width_z), lambda i: (0, i, 0, 0)),
            plane_spec,
            pl.BlockSpec((2, 1) + fields.shape[2:], lambda i: (0, i, 0, 0)),
        ],
        out_specs=[
            plane_spec,
            node_spec,
            node_spec,
            node_spec,
            pl.BlockSpec((1, ROWS, LANES), lambda i: (i, 0, 0)),
        ],
        out_shape=[
            jax.ShapeDtypeStruct(image.shape, jnp.bfloat16),
            block_sum,
            block_sum,
            block_sum,
            jax.ShapeDtypeStruct((nodes, ROWS, LANES), f32),
        ],
        scratch_shapes=[
            pltpu.VMEM((sides.shape[1], width_z + 128), f32),
            pltpu.VMEM((KNOT + 2, 9, width_y, width_z), f32),
        ],
        compiler_params=pltpu.CompilerParams(
            dimension_semantics=("arbitrary",), vmem_limit_bytes=60 * 1024 * 1024),
    )(deformed, deformed, deformed, rows, sides, displacement, image, fields)


def node_sums(field):
    nodes, width_y, width_z = field.shape
    return field.reshape(nodes, width_y // KNOT, KNOT, width_z).sum(axis=2)


def exchange(axis, n, me, d, src, buffer, send_sem, recv_sem):
    target = lax.rem(me + d, n)
    return pltpu.make_async_remote_copy(
        src_ref=src(target), dst_ref=buffer.at[me],
        send_sem=send_sem.at[target], recv_sem=recv_sem.at[me],
        device_id={axis: target}, device_id_type=pl.DeviceIdType.MESH)


def arrival(axis, n, me, d, src_ref, buffer, sem):
    source = lax.rem(me + n - d, n)
    return pltpu.make_async_remote_copy(
        src_ref=src_ref, dst_ref=buffer.at[source],
        send_sem=sem.at[source], recv_sem=sem.at[source],
        device_id={axis: source}, device_id_type=pl.DeviceIdType.MESH)


def both_sums_kernel(nz, ny, plane_row, depth_row, plane_ref, depth_ref, plane_out, depth_out,
                     plane_landed, depth_landed, plane_summed, depth_summed,
                     plane_gathered, depth_gathered, sems):
    mz, my = lax.axis_index("gz"), lax.axis_index("gy")
    barrier = pltpu.get_barrier_semaphore()
    for d in range(1, nz):
        pl.semaphore_signal(barrier, inc=1, device_id={"gz": lax.rem(mz + d, nz)},
                            device_id_type=pl.DeviceIdType.MESH)
    for d in range(1, ny):
        pl.semaphore_signal(barrier, inc=1, device_id={"gy": lax.rem(my + d, ny)},
                            device_id_type=pl.DeviceIdType.MESH)
    pl.semaphore_wait(barrier, nz - 1 + ny - 1)
    zs1, zr1, zs2, zr2, ys1, yr1, ys2, yr2 = sems

    z_out = [exchange("gz", nz, mz, d, lambda t: plane_ref.at[t], plane_landed, zs1, zr1)
             for d in range(1, nz)]
    y_out = [exchange("gy", ny, my, d, lambda t: depth_ref.at[t], depth_landed, ys1, yr1)
             for d in range(1, ny)]
    for copy in z_out + y_out:
        copy.start()
    depth_total = depth_ref[my]
    for d in range(1, ny):
        arrival("gy", ny, my, d, depth_ref.at[0], depth_landed, yr1).wait_recv()
        depth_total = depth_total + depth_landed[lax.rem(my + ny - d, ny)]
    depth_summed[...] = depth_total
    plane_total = plane_ref[mz]
    for d in range(1, nz):
        arrival("gz", nz, mz, d, plane_ref.at[0], plane_landed, zr1).wait_recv()
        plane_total = plane_total + plane_landed[lax.rem(mz + nz - d, nz)]
    rows = lax.broadcasted_iota(jnp.int32, plane_total.shape, 0)
    lanes = lax.broadcasted_iota(jnp.int32, plane_total.shape, 1)
    slot = jnp.logical_and(rows == plane_row, lanes == RANK)
    depth_slot = jnp.logical_and(
        lax.broadcasted_iota(jnp.int32, depth_total.shape, 0) == depth_row,
        lax.broadcasted_iota(jnp.int32, depth_total.shape, 1) == RANK)
    column_energy = jnp.sum(jnp.where(depth_slot, depth_total, 0.0))
    plane_total = jnp.where(slot, column_energy, plane_total)
    plane_summed[...] = plane_total
    for copy in z_out + y_out:
        copy.wait_send()

    z_out = [exchange("gz", nz, mz, d, lambda t: plane_summed, plane_gathered, zs2, zr2)
             for d in range(1, nz)]
    y_out = [exchange("gy", ny, my, d, lambda t: depth_summed, depth_gathered, ys2, yr2)
             for d in range(1, ny)]
    for copy in z_out + y_out:
        copy.start()
    plane_out[mz] = plane_total
    depth_out[my] = depth_total
    for d in range(1, nz):
        arrival("gz", nz, mz, d, plane_summed, plane_gathered, zr2).wait_recv()
        source = lax.rem(mz + nz - d, nz)
        plane_out[source] = plane_gathered[source]
    for d in range(1, ny):
        arrival("gy", ny, my, d, depth_summed, depth_gathered, yr2).wait_recv()
        source = lax.rem(my + ny - d, ny)
        depth_out[source] = depth_gathered[source]
    for copy in z_out + y_out:
        copy.wait_send()


def chunked(main, extras, n):
    rows = -(-main.shape[0] // (n * 128))
    main = jnp.pad(main, (0, n * rows * 128 - main.shape[0])).reshape(n, rows, 128)
    tail = jnp.pad(extras, (0, 128 - extras.shape[0]))
    tail = jnp.broadcast_to(tail, (n, 1, 128))
    spare = -(-(rows + 1) // 8) * 8 - rows - 1
    return jnp.concatenate([main, tail, jnp.zeros((n, spare, 128), main.dtype)], axis=1), rows


def both_sums(plane_parts, depth_parts, plane_row, depth_row):
    nz, ny = plane_parts.shape[0], depth_parts.shape[0]
    f32 = jnp.float32
    dma = pltpu.SemaphoreType.DMA
    return pl.pallas_call(
        functools.partial(both_sums_kernel, nz, ny, plane_row, depth_row),
        out_shape=[jax.ShapeDtypeStruct(plane_parts.shape, f32),
                   jax.ShapeDtypeStruct(depth_parts.shape, f32)],
        in_specs=[pl.BlockSpec(memory_space=pltpu.VMEM)] * 2,
        out_specs=[pl.BlockSpec(memory_space=pltpu.VMEM)] * 2,
        scratch_shapes=[
            pltpu.VMEM(plane_parts.shape, f32),
            pltpu.VMEM(depth_parts.shape, f32),
            pltpu.VMEM(plane_parts.shape[1:], f32),
            pltpu.VMEM(depth_parts.shape[1:], f32),
            pltpu.VMEM(plane_parts.shape, f32),
            pltpu.VMEM(depth_parts.shape, f32),
            [dma((nz,)), dma((nz,)), dma((nz,)), dma((nz,)),
             dma((ny,)), dma((ny,)), dma((ny,)), dma((ny,))],
        ],
        compiler_params=pltpu.CompilerParams(collective_id=1, has_side_effects=True),
    )(plane_parts, depth_parts)


def local(reference_image, deformed, displacement, plane_factors, depth_factors):
    rows, sides = halo_blocks(deformed)
    fields = jnp.einsum("krij,krz->kijz", plane_factors, depth_factors, precision=highest)
    residual, prod, mis, sq, energy_parts = strip_sums(
        deformed, rows, sides, displacement, reference_image, fields)
    prod, mis, sq = node_sums(prod), node_sums(mis), node_sums(sq)
    local_energy = jnp.sum(energy_parts)

    first, second = plane_factors[0], plane_factors[1]
    grad_depth = -jnp.stack([
        jnp.einsum("rij,ijz->rz", first, prod, precision=highest),
        jnp.einsum("rij,ijz->rz", second, mis, precision=highest)])
    first_depth = jnp.einsum("rij,ijz->rz", first * first, sq, precision=highest)
    level_sum = KNOT * KNOT * jnp.sum(second * second, axis=(1, 2))
    grad_plane = -jnp.stack([
        jnp.einsum("rz,ijz->rij", depth_factors[0], prod, precision=highest),
        jnp.einsum("rz,ijz->rij", depth_factors[1], mis, precision=highest)])
    first_diag = jnp.einsum("rz,ijz->rij", depth_factors[0] * depth_factors[0], sq, precision=highest)
    depth_level = KNOT * KNOT * jnp.sum(depth_factors[1] * depth_factors[1], axis=1)

    nz, ny = lax.axis_size("gz"), lax.axis_size("gy")
    plane_terms = jnp.concatenate([grad_plane.reshape(-1), first_diag.reshape(-1)])
    depth_terms = jnp.concatenate([grad_depth.reshape(-1), first_depth.reshape(-1)])
    blank = jnp.zeros((), jnp.float32)
    plane_parts, plane_rows = chunked(plane_terms, jnp.concatenate([depth_level, blank[None]]), nz)
    depth_parts, depth_rows = chunked(depth_terms, jnp.concatenate([level_sum, local_energy[None]]), ny)
    plane_summed, depth_summed = both_sums(plane_parts, depth_parts, plane_rows, depth_rows)
    plane_terms = plane_summed[:, :plane_rows].reshape(-1)
    depth_terms = depth_summed[:, :depth_rows].reshape(-1)
    grad_plane = plane_terms[: grad_plane.size].reshape(grad_plane.shape)
    first_diag = plane_terms[grad_plane.size : grad_plane.size + first_diag.size].reshape(first_diag.shape)
    grad_depth = depth_terms[: grad_depth.size].reshape(grad_depth.shape)
    first_depth = depth_terms[grad_depth.size : grad_depth.size + first_depth.size].reshape(first_depth.shape)
    depth_level = plane_summed[0, plane_rows, :RANK]
    level_sum = depth_summed[0, depth_rows, :RANK]
    energy = jnp.sum(plane_summed[:, plane_rows, RANK])

    nodes_x = plane_factors.shape[2]
    nodes_y = plane_factors.shape[3] * lax.axis_size("gy")
    full_z = depth_factors.shape[2] * lax.axis_size("gz")
    diag_plane = jnp.stack(
        [first_diag, jnp.broadcast_to(depth_level[:, None, None], first_diag.shape)])
    lam_plane = damping * RANK * energy / (nodes_x * nodes_y)
    lam_depth = damping * energy / full_z
    step_plane = -grad_plane / (diag_plane + lam_plane + epsilon)
    diag_depth = jnp.stack([first_depth, jnp.broadcast_to(level_sum[:, None], first_depth.shape)])
    step_depth = -grad_depth / (diag_depth + lam_depth + epsilon)
    return (residual, step_plane, step_depth)


def solution(mesh):
    placed = (
        P(None, "gy", "gz"),
        P(None, "gy", "gz"),
        P(None, None, "gy", "gz"),
        P(None, None, None, "gy"),
        P(None, None, "gz"),
    )
    return jax.shard_map(
        local,
        mesh=mesh,
        in_specs=placed,
        out_specs=(P(None, "gy", "gz"), P(None, None, None, "gy"), P(None, None, "gz")),
        check_vma=False,
    )
```

```python
import functools

import jax
import jax.numpy as jnp
from jax import lax
from jax.experimental import pallas as pl
from jax.experimental.pallas import tpu as pltpu
from jax.sharding import PartitionSpec as P

RANK = 32
KNOT = 8

epsilon = 1e-06
damping = 0.01
highest = lax.Precision.HIGHEST

ROWS = 16
LANES = 256


def neighbours(part, axis, forward):
    count = lax.axis_size(axis)
    if forward:
        pairs = [(i, i + 1) for i in range(count - 1)]
    else:
        pairs = [(i + 1, i) for i in range(count - 1)]
    return lax.ppermute(part, axis, pairs)


def halo_kernel(ny, nz, rows_ref, cols_ref, rows_out, cols_out, rows_got, cols_got,
                send_sems, recv_sems):
    my, mz = lax.axis_index("gy"), lax.axis_index("gz")
    up, down = lax.rem(my + 1, ny), lax.rem(my + ny - 1, ny)
    right, left = lax.rem(mz + 1, nz), lax.rem(mz + nz - 1, nz)
    plan = [
        (rows_ref.at[0], rows_got.at[0], (down, mz)),
        (rows_ref.at[1], rows_got.at[1], (up, mz)),
        (cols_ref.at[0], cols_got.at[0], (my, left)),
        (cols_ref.at[1], cols_got.at[1], (my, right)),
        (cols_ref.at[0], cols_got.at[2], (down, left)),
        (cols_ref.at[0], cols_got.at[3], (up, left)),
        (cols_ref.at[1], cols_got.at[4], (down, right)),
        (cols_ref.at[1], cols_got.at[5], (up, right)),
    ]
    barrier = pltpu.get_barrier_semaphore()
    for _, _, device in plan:
        pl.semaphore_signal(barrier, inc=1, device_id=device,
                            device_id_type=pl.DeviceIdType.MESH)
    pl.semaphore_wait(barrier, len(plan))
    copies = []
    for k, (source, slot, device) in enumerate(plan):
        copy = pltpu.make_async_remote_copy(
            src_ref=source, dst_ref=slot, send_sem=send_sems.at[k], recv_sem=recv_sems.at[k],
            device_id=device, device_id_type=pl.DeviceIdType.MESH)
        copy.start()
        copies.append(copy)
    for copy in copies:
        copy.wait()
    rows_out[...] = rows_got[...]
    cols_out[...] = cols_got[...]


def swap_halos(rows_send, cols_send):
    ny, nz = lax.axis_size("gy"), lax.axis_size("gz")
    dma = pltpu.SemaphoreType.DMA
    rows_shape = rows_send.shape
    cols_shape = (6,) + cols_send.shape[1:]
    return pl.pallas_call(
        functools.partial(halo_kernel, ny, nz),
        out_shape=[jax.ShapeDtypeStruct(rows_shape, rows_send.dtype),
                   jax.ShapeDtypeStruct(cols_shape, cols_send.dtype)],
        in_specs=[pl.BlockSpec(memory_space=pltpu.VMEM)] * 2,
        out_specs=[pl.BlockSpec(memory_space=pltpu.VMEM)] * 2,
        scratch_shapes=[
            pltpu.VMEM(rows_shape, rows_send.dtype),
            pltpu.VMEM(cols_shape, cols_send.dtype),
            dma((8,)),
            dma((8,)),
        ],
        compiler_params=pltpu.CompilerParams(collective_id=2, has_side_effects=True),
    )(rows_send, cols_send)


def halo_blocks(deformed):
    depth_x, width_y, width_z = deformed.shape
    f32 = jnp.float32
    ny, nz = lax.axis_size("gy"), lax.axis_size("gz")
    my, mz = lax.axis_index("gy"), lax.axis_index("gz")
    rows_send = jnp.stack([deformed[:, 0, :], deformed[:, width_y - 1, :]])
    cols_send = jnp.stack([deformed[:, :, 0], deformed[:, :, width_z - 1]])
    rows_got, cols_got = swap_halos(rows_send, cols_send)
    has_up = (my < ny - 1).astype(f32)
    has_down = (my > 0).astype(f32)
    has_right = (mz < nz - 1).astype(f32)
    has_left = (mz > 0).astype(f32)
    rows_got = rows_got.astype(f32)
    cols_got = cols_got.astype(f32)
    high_y = rows_got[0] * has_up
    low_y = rows_got[1] * has_down
    high_z = cols_got[0] * has_right
    low_z = cols_got[1] * has_left
    high_high = cols_got[2][:, 0] * (has_up * has_right)
    low_high = cols_got[3][:, width_y - 1] * (has_down * has_right)
    high_low = cols_got[4][:, 0] * (has_up * has_left)
    low_low = cols_got[5][:, width_y - 1] * (has_down * has_left)
    rows = jnp.stack([high_y, low_y])
    gap = jnp.zeros((depth_x, 6), f32)
    side_high = jnp.concatenate([high_z, high_high[:, None], gap, low_high[:, None]], axis=1)
    side_low = jnp.concatenate([low_z, high_low[:, None], gap, low_low[:, None]], axis=1)
    sides = jnp.stack([side_high.T, side_low.T])
    sides = jnp.pad(sides, ((0, 0), (0, 0), (0, 128 - depth_x)))
    return rows, sides


def lerp(base, other, weight):
    return base + weight * (other - base)


def strip_kernel(prev_ref, main_ref, next_ref, rows_ref, sides_ref, disp_ref, image_ref,
                 fields_ref,
                 res_ref, prod_ref, mis_ref, sq_ref, energy_ref, pad_ref, edge_ref, shifts_ref):
    block = pl.program_id(0)
    depth_x = rows_ref.shape[1]
    width_y, width_z = image_ref.shape[1], image_ref.shape[2]
    pad_y, pad_z = pad_ref.shape[1], pad_ref.shape[2]
    side = pad_z - width_z
    blocks = pad_z // 128
    half = width_y // 2
    f32 = jnp.float32
    pad_ref[:, width_y:, :width_z] = jnp.zeros((pad_ref.shape[0], pad_y - width_y, width_z), f32)
    lane = lax.broadcasted_iota(jnp.int32, (pad_y, side), 1)
    lane_block = lax.broadcasted_iota(jnp.int32, (half, 128), 1)

    def source_plane(p, plane):
        plane_x = block * KNOT - 1 + p
        valid = jnp.logical_and(plane_x >= 0, plane_x < depth_x)
        safe = jnp.clip(plane_x, 0, depth_x - 1)
        held = pad_ref.at[p]
        held[:width_y, :width_z] = jnp.where(valid, plane.astype(f32), 0.0)
        held[pl.ds(width_y, 1), :width_z] = jnp.where(valid, rows_ref[0, pl.ds(safe, 1), :], 0.0)
        held[pl.ds(pad_y - 1, 1), :width_z] = jnp.where(valid, rows_ref[1, pl.ds(safe, 1), :], 0.0)
        high = jnp.sum(jnp.where(lane == safe, sides_ref[0], 0.0), axis=1, keepdims=True)
        low = jnp.sum(jnp.where(lane == safe, sides_ref[1], 0.0), axis=1, keepdims=True)
        column = jnp.where(lane == 0, high, jnp.where(lane == side - 1, low, 0.0))
        held[:, width_z:] = jnp.where(valid, column, 0.0)
        for k in range(blocks):
            lanes = slice(128 * k, 128 * k + 128)
            col = held[:, lanes]
            for b, shift in ((0, 1), (2, pad_y - 1)):
                moved = pltpu.roll(col, shift, 0)[:width_y]
                if k < blocks - 1:
                    shifts_ref[p, 3 * b + 1, :, lanes] = moved
                else:
                    edge_ref[b // 2] = moved
        for b in range(3):
            def piece(k, h):
                rows = slice(half * h, half * h + half)
                if b == 1:
                    return held[rows, 128 * k : 128 * k + 128]
                if k == blocks - 1:
                    return edge_ref[b // 2, rows, :]
                return shifts_ref[p, 3 * b + 1, rows, 128 * k : 128 * k + 128]

            for k in range(blocks - 1):
                for h in range(2):
                    rows = slice(half * h, half * h + half)
                    lanes = slice(128 * k, 128 * k + 128)
                    centre = piece(k, h)
                    before = piece(k - 1 if k > 0 else blocks - 1, h)
                    after = piece(k + 1, h)
                    shifts_ref[p, 3 * b, rows, lanes] = jnp.where(
                        lane_block == 0, pltpu.roll(before, 1, 1), pltpu.roll(centre, 1, 1))
                    shifts_ref[p, 3 * b + 2, rows, lanes] = jnp.where(
                        lane_block == 127, pltpu.roll(after, 127, 1), pltpu.roll(centre, 127, 1))

    source_plane(0, prev_ref[0])

    def inner_plane(p, carry):
        source_plane(p, main_ref[p - 1])
        return carry

    lax.fori_loop(1, KNOT + 1, inner_plane, 0)
    source_plane(KNOT + 1, next_ref[0])

    chunks_y = width_y // ROWS
    chunks_z = width_z // LANES

    def chunk(k, energy):
        r0 = pl.multiple_of((k // chunks_z) * ROWS, ROWS)
        c0 = pl.multiple_of((k % chunks_z) * LANES, LANES)
        rs = pl.ds(r0, ROWS)
        cs = pl.ds(c0, LANES)
        j0 = r0 // KNOT
        upper = lax.broadcasted_iota(jnp.int32, (ROWS, LANES), 0) < KNOT
        node = lax.broadcasted_iota(jnp.int32, (KNOT, LANES), 0)

        def node_row(k, j):
            return jnp.sum(jnp.where(node == j, fields_ref[k, 0, :, cs], 0.0), axis=0, keepdims=True)

        contrast = jnp.where(upper, node_row(0, j0), node_row(0, j0 + 1))
        bright = jnp.where(upper, node_row(1, j0), node_row(1, j0 + 1))

        def plane(xl, acc):
            prod_acc, mis_acc, sq_acc, e_acc = acc

            def src(a, b, c):
                if b == 0 and c == 0:
                    return pad_ref[xl + 1 + a, rs, cs]
                return shifts_ref[xl + 1 + a, 3 * (b + 1) + (c + 1), rs, cs]

            sx = disp_ref[0, xl, rs, cs].astype(jnp.float32)
            sy = disp_ref[1, xl, rs, cs].astype(jnp.float32)
            sz = disp_ref[2, xl, rs, cs].astype(jnp.float32)
            gx, gy, gz = sx > 0, sy > 0, sz > 0
            ax, ay, az = jnp.abs(sx), jnp.abs(sy), jnp.abs(sz)
            xs = {}
            for b in (-1, 0, 1):
                for c in (-1, 0, 1):
                    xs[b, c] = jnp.where(gx, src(1, b, c), src(-1, b, c))
            y0 = {c: jnp.where(gy, src(0, 1, c), src(0, -1, c)) for c in (-1, 0, 1)}
            y1 = {c: jnp.where(gy, xs[1, c], xs[-1, c]) for c in (-1, 0, 1)}
            centre = src(0, 0, 0)
            z00 = jnp.where(gz, src(0, 0, 1), src(0, 0, -1))
            z01 = jnp.where(gz, y0[1], y0[-1])
            z10 = jnp.where(gz, xs[0, 1], xs[0, -1])
            z11 = jnp.where(gz, y1[1], y1[-1])
            l00 = lerp(centre, z00, az)
            l01 = lerp(y0[0], z01, az)
            l10 = lerp(xs[0, 0], z10, az)
            l11 = lerp(y1[0], z11, az)
            m0 = lerp(l00, l01, ay)
            m1 = lerp(l10, l11, ay)
            warped = lerp(m0, m1, ax)
            values = image_ref[xl, rs, cs].astype(jnp.float32)
            misfit = warped - contrast * values - bright
            res_ref[xl, rs, cs] = misfit.astype(res_ref.dtype)
            return (prod_acc + misfit * values, mis_acc + misfit,
                    sq_acc + values * values, e_acc + misfit * misfit)

        zero = jnp.zeros((ROWS, LANES), jnp.float32)
        prod_acc, mis_acc, sq_acc, e_acc = lax.fori_loop(
            0, KNOT, plane, (zero, zero, zero, energy))
        prod_ref[0, rs, cs] = prod_acc
        mis_ref[0, rs, cs] = mis_acc
        sq_ref[0, rs, cs] = sq_acc
        return e_acc

    energy = lax.fori_loop(0, chunks_y * chunks_z, chunk,
                           jnp.zeros((ROWS, LANES), jnp.float32))
    energy_ref[0] = energy


def strip_sums(deformed, rows, sides, displacement, image, fields):
    depth_x, width_y, width_z = image.shape
    nodes = depth_x // KNOT
    f32 = jnp.float32
    block_sum = jax.ShapeDtypeStruct((nodes, width_y, width_z), f32)
    node_spec = pl.BlockSpec((1, width_y, width_z), lambda i: (i, 0, 0))
    plane_spec = pl.BlockSpec((KNOT, width_y, width_z), lambda i: (i, 0, 0))
    return pl.pallas_call(
        strip_kernel,
        grid=(nodes,),
        in_specs=[
            pl.BlockSpec((1, width_y, width_z), lambda i: (jnp.maximum(i * KNOT - 1, 0), 0, 0)),
            plane_spec,
            pl.BlockSpec((1, width_y, width_z),
                         lambda i: (jnp.minimum(i * KNOT + KNOT, depth_x - 1), 0, 0)),
            pl.BlockSpec(memory_space=pltpu.VMEM),
            pl.BlockSpec(memory_space=pltpu.VMEM),
            pl.BlockSpec((3, KNOT, width_y, width_z), lambda i: (0, i, 0, 0)),
            plane_spec,
            pl.BlockSpec((2, 1) + fields.shape[2:], lambda i: (0, i, 0, 0)),
        ],
        out_specs=[
            plane_spec,
            node_spec,
            node_spec,
            node_spec,
            pl.BlockSpec((1, ROWS, LANES), lambda i: (i, 0, 0)),
        ],
        out_shape=[
            jax.ShapeDtypeStruct(image.shape, jnp.bfloat16),
            block_sum,
            block_sum,
            block_sum,
            jax.ShapeDtypeStruct((nodes, ROWS, LANES), f32),
        ],
        scratch_shapes=[
            pltpu.VMEM((KNOT + 2, sides.shape[1], width_z + 128), f32),
            pltpu.VMEM((2, width_y, 128), f32),
            pltpu.VMEM((KNOT + 2, 9, width_y, width_z), f32),
        ],
        compiler_params=pltpu.CompilerParams(
            dimension_semantics=("arbitrary",), vmem_limit_bytes=60 * 1024 * 1024),
    )(deformed, deformed, deformed, rows, sides, displacement, image, fields)


def node_sums(field):
    nodes, width_y, width_z = field.shape
    return field.reshape(nodes, width_y // KNOT, KNOT, width_z).sum(axis=2)


def exchange(axis, n, me, d, src, buffer, send_sem, recv_sem):
    target = lax.rem(me + d, n)
    return pltpu.make_async_remote_copy(
        src_ref=src(target), dst_ref=buffer.at[me],
        send_sem=send_sem.at[target], recv_sem=recv_sem.at[me],
        device_id={axis: target}, device_id_type=pl.DeviceIdType.MESH)


def arrival(axis, n, me, d, src_ref, buffer, sem):
    source = lax.rem(me + n - d, n)
    return pltpu.make_async_remote_copy(
        src_ref=src_ref, dst_ref=buffer.at[source],
        send_sem=sem.at[source], recv_sem=sem.at[source],
        device_id={axis: source}, device_id_type=pl.DeviceIdType.MESH)


def both_sums_kernel(nz, ny, plane_row, depth_row, plane_ref, depth_ref, plane_out, depth_out,
                     plane_landed, depth_landed, plane_summed, depth_summed,
                     plane_gathered, depth_gathered, sems):
    mz, my = lax.axis_index("gz"), lax.axis_index("gy")
    barrier = pltpu.get_barrier_semaphore()
    for d in range(1, nz):
        pl.semaphore_signal(barrier, inc=1, device_id={"gz": lax.rem(mz + d, nz)},
                            device_id_type=pl.DeviceIdType.MESH)
    for d in range(1, ny):
        pl.semaphore_signal(barrier, inc=1, device_id={"gy": lax.rem(my + d, ny)},
                            device_id_type=pl.DeviceIdType.MESH)
    pl.semaphore_wait(barrier, nz - 1 + ny - 1)
    zs1, zr1, zs2, zr2, ys1, yr1, ys2, yr2 = sems

    z_out = [exchange("gz", nz, mz, d, lambda t: plane_ref.at[t], plane_landed, zs1, zr1)
             for d in range(1, nz)]
    y_out = [exchange("gy", ny, my, d, lambda t: depth_ref.at[t], depth_landed, ys1, yr1)
             for d in range(1, ny)]
    for copy in z_out + y_out:
        copy.start()
    depth_total = depth_ref[my]
    for d in range(1, ny):
        arrival("gy", ny, my, d, depth_ref.at[0], depth_landed, yr1).wait_recv()
        depth_total = depth_total + depth_landed[lax.rem(my + ny - d, ny)]
    depth_summed[...] = depth_total
    plane_total = plane_ref[mz]
    for d in range(1, nz):
        arrival("gz", nz, mz, d, plane_ref.at[0], plane_landed, zr1).wait_recv()
        plane_total = plane_total + plane_landed[lax.rem(mz + nz - d, nz)]
    rows = lax.broadcasted_iota(jnp.int32, plane_total.shape, 0)
    lanes = lax.broadcasted_iota(jnp.int32, plane_total.shape, 1)
    slot = jnp.logical_and(rows == plane_row, lanes == RANK)
    depth_slot = jnp.logical_and(
        lax.broadcasted_iota(jnp.int32, depth_total.shape, 0) == depth_row,
        lax.broadcasted_iota(jnp.int32, depth_total.shape, 1) == RANK)
    column_energy = jnp.sum(jnp.where(depth_slot, depth_total, 0.0))
    plane_total = jnp.where(slot, column_energy, plane_total)
    plane_summed[...] = plane_total
    for copy in z_out + y_out:
        copy.wait_send()

    z_out = [exchange("gz", nz, mz, d, lambda t: plane_summed, plane_gathered, zs2, zr2)
             for d in range(1, nz)]
    y_out = [exchange("gy", ny, my, d, lambda t: depth_summed, depth_gathered, ys2, yr2)
             for d in range(1, ny)]
    for copy in z_out + y_out:
        copy.start()
    plane_out[mz] = plane_total
    depth_out[my] = depth_total
    for d in range(1, nz):
        arrival("gz", nz, mz, d, plane_summed, plane_gathered, zr2).wait_recv()
        source = lax.rem(mz + nz - d, nz)
        plane_out[source] = plane_gathered[source]
    for d in range(1, ny):
        arrival("gy", ny, my, d, depth_summed, depth_gathered, yr2).wait_recv()
        source = lax.rem(my + ny - d, ny)
        depth_out[source] = depth_gathered[source]
    for copy in z_out + y_out:
        copy.wait_send()


def chunked(main, extras, n):
    rows = -(-main.shape[0] // (n * 128))
    main = jnp.pad(main, (0, n * rows * 128 - main.shape[0])).reshape(n, rows, 128)
    tail = jnp.pad(extras, (0, 128 - extras.shape[0]))
    tail = jnp.broadcast_to(tail, (n, 1, 128))
    spare = -(-(rows + 1) // 8) * 8 - rows - 1
    return jnp.concatenate([main, tail, jnp.zeros((n, spare, 128), main.dtype)], axis=1), rows


def both_sums(plane_parts, depth_parts, plane_row, depth_row):
    nz, ny = plane_parts.shape[0], depth_parts.shape[0]
    f32 = jnp.float32
    dma = pltpu.SemaphoreType.DMA
    return pl.pallas_call(
        functools.partial(both_sums_kernel, nz, ny, plane_row, depth_row),
        out_shape=[jax.ShapeDtypeStruct(plane_parts.shape, f32),
                   jax.ShapeDtypeStruct(depth_parts.shape, f32)],
        in_specs=[pl.BlockSpec(memory_space=pltpu.VMEM)] * 2,
        out_specs=[pl.BlockSpec(memory_space=pltpu.VMEM)] * 2,
        scratch_shapes=[
            pltpu.VMEM(plane_parts.shape, f32),
            pltpu.VMEM(depth_parts.shape, f32),
            pltpu.VMEM(plane_parts.shape[1:], f32),
            pltpu.VMEM(depth_parts.shape[1:], f32),
            pltpu.VMEM(plane_parts.shape, f32),
            pltpu.VMEM(depth_parts.shape, f32),
            [dma((nz,)), dma((nz,)), dma((nz,)), dma((nz,)),
             dma((ny,)), dma((ny,)), dma((ny,)), dma((ny,))],
        ],
        compiler_params=pltpu.CompilerParams(collective_id=1, has_side_effects=True),
    )(plane_parts, depth_parts)


def local(reference_image, deformed, displacement, plane_factors, depth_factors):
    rows, sides = halo_blocks(deformed)
    fields = jnp.einsum("krij,krz->kijz", plane_factors, depth_factors, precision=highest)
    residual, prod, mis, sq, energy_parts = strip_sums(
        deformed, rows, sides, displacement, reference_image, fields)
    prod, mis, sq = node_sums(prod), node_sums(mis), node_sums(sq)
    local_energy = jnp.sum(energy_parts)

    first, second = plane_factors[0], plane_factors[1]
    grad_depth = -jnp.stack([
        jnp.einsum("rij,ijz->rz", first, prod, precision=highest),
        jnp.einsum("rij,ijz->rz", second, mis, precision=highest)])
    first_depth = jnp.einsum("rij,ijz->rz", first * first, sq, precision=highest)
    level_sum = KNOT * KNOT * jnp.sum(second * second, axis=(1, 2))
    grad_plane = -jnp.stack([
        jnp.einsum("rz,ijz->rij", depth_factors[0], prod, precision=highest),
        jnp.einsum("rz,ijz->rij", depth_factors[1], mis, precision=highest)])
    first_diag = jnp.einsum("rz,ijz->rij", depth_factors[0] * depth_factors[0], sq, precision=highest)
    depth_level = KNOT * KNOT * jnp.sum(depth_factors[1] * depth_factors[1], axis=1)

    nz, ny = lax.axis_size("gz"), lax.axis_size("gy")
    plane_terms = jnp.concatenate([grad_plane.reshape(-1), first_diag.reshape(-1)])
    depth_terms = jnp.concatenate([grad_depth.reshape(-1), first_depth.reshape(-1)])
    blank = jnp.zeros((), jnp.float32)
    plane_parts, plane_rows = chunked(plane_terms, jnp.concatenate([depth_level, blank[None]]), nz)
    depth_parts, depth_rows = chunked(depth_terms, jnp.concatenate([level_sum, local_energy[None]]), ny)
    plane_summed, depth_summed = both_sums(plane_parts, depth_parts, plane_rows, depth_rows)
    plane_terms = plane_summed[:, :plane_rows].reshape(-1)
    depth_terms = depth_summed[:, :depth_rows].reshape(-1)
    grad_plane = plane_terms[: grad_plane.size].reshape(grad_plane.shape)
    first_diag = plane_terms[grad_plane.size : grad_plane.size + first_diag.size].reshape(first_diag.shape)
    grad_depth = depth_terms[: grad_depth.size].reshape(grad_depth.shape)
    first_depth = depth_terms[grad_depth.size : grad_depth.size + first_depth.size].reshape(first_depth.shape)
    depth_level = plane_summed[0, plane_rows, :RANK]
    level_sum = depth_summed[0, depth_rows, :RANK]
    energy = jnp.sum(plane_summed[:, plane_rows, RANK])

    nodes_x = plane_factors.shape[2]
    nodes_y = plane_factors.shape[3] * lax.axis_size("gy")
    full_z = depth_factors.shape[2] * lax.axis_size("gz")
    diag_plane = jnp.stack(
        [first_diag, jnp.broadcast_to(depth_level[:, None, None], first_diag.shape)])
    lam_plane = damping * RANK * energy / (nodes_x * nodes_y)
    lam_depth = damping * energy / full_z
    step_plane = -grad_plane / (diag_plane + lam_plane + epsilon)
    diag_depth = jnp.stack([first_depth, jnp.broadcast_to(level_sum[:, None], first_depth.shape)])
    step_depth = -grad_depth / (diag_depth + lam_depth + epsilon)
    return (residual, step_plane, step_depth)


def solution(mesh):
    placed = (
        P(None, "gy", "gz"),
        P(None, "gy", "gz"),
        P(None, None, "gy", "gz"),
        P(None, None, None, "gy"),
        P(None, None, "gz"),
    )
    return jax.shard_map(
        local,
        mesh=mesh,
        in_specs=placed,
        out_specs=(P(None, "gy", "gz"), P(None, None, None, "gy"), P(None, None, "gz")),
        check_vma=False,
    )
```

```python
import functools

import jax
import jax.numpy as jnp
from jax import lax
from jax.experimental import pallas as pl
from jax.experimental.pallas import tpu as pltpu
from jax.sharding import PartitionSpec as P

RANK = 32
KNOT = 8

epsilon = 1e-06
damping = 0.01
highest = lax.Precision.HIGHEST

ROWS = 16
LANES = 256


def neighbours(part, axis, forward):
    count = lax.axis_size(axis)
    if forward:
        pairs = [(i, i + 1) for i in range(count - 1)]
    else:
        pairs = [(i + 1, i) for i in range(count - 1)]
    return lax.ppermute(part, axis, pairs)


def halo_kernel(ny, nz, rows_ref, cols_ref, rows_out, cols_out, rows_got, cols_got,
                send_sems, recv_sems):
    my, mz = lax.axis_index("gy"), lax.axis_index("gz")
    up, down = lax.rem(my + 1, ny), lax.rem(my + ny - 1, ny)
    right, left = lax.rem(mz + 1, nz), lax.rem(mz + nz - 1, nz)
    plan = [
        (rows_ref.at[0], rows_got.at[0], (down, mz)),
        (rows_ref.at[1], rows_got.at[1], (up, mz)),
        (cols_ref.at[0], cols_got.at[0], (my, left)),
        (cols_ref.at[1], cols_got.at[1], (my, right)),
        (cols_ref.at[0], cols_got.at[2], (down, left)),
        (cols_ref.at[0], cols_got.at[3], (up, left)),
        (cols_ref.at[1], cols_got.at[4], (down, right)),
        (cols_ref.at[1], cols_got.at[5], (up, right)),
    ]
    barrier = pltpu.get_barrier_semaphore()
    for _, _, device in plan:
        pl.semaphore_signal(barrier, inc=1, device_id=device,
                            device_id_type=pl.DeviceIdType.MESH)
    pl.semaphore_wait(barrier, len(plan))
    copies = []
    for k, (source, slot, device) in enumerate(plan):
        copy = pltpu.make_async_remote_copy(
            src_ref=source, dst_ref=slot, send_sem=send_sems.at[k], recv_sem=recv_sems.at[k],
            device_id=device, device_id_type=pl.DeviceIdType.MESH)
        copy.start()
        copies.append(copy)
    for copy in copies:
        copy.wait()
    rows_out[...] = rows_got[...]
    cols_out[...] = cols_got[...]


def swap_halos(rows_send, cols_send):
    ny, nz = lax.axis_size("gy"), lax.axis_size("gz")
    dma = pltpu.SemaphoreType.DMA
    rows_shape = rows_send.shape
    cols_shape = (6,) + cols_send.shape[1:]
    return pl.pallas_call(
        functools.partial(halo_kernel, ny, nz),
        out_shape=[jax.ShapeDtypeStruct(rows_shape, rows_send.dtype),
                   jax.ShapeDtypeStruct(cols_shape, cols_send.dtype)],
        in_specs=[pl.BlockSpec(memory_space=pltpu.VMEM)] * 2,
        out_specs=[pl.BlockSpec(memory_space=pltpu.VMEM)] * 2,
        scratch_shapes=[
            pltpu.VMEM(rows_shape, rows_send.dtype),
            pltpu.VMEM(cols_shape, cols_send.dtype),
            dma((8,)),
            dma((8,)),
        ],
        compiler_params=pltpu.CompilerParams(collective_id=2, has_side_effects=True),
    )(rows_send, cols_send)


def halo_blocks(deformed):
    depth_x, width_y, width_z = deformed.shape
    f32 = jnp.float32
    ny, nz = lax.axis_size("gy"), lax.axis_size("gz")
    my, mz = lax.axis_index("gy"), lax.axis_index("gz")
    rows_send = jnp.stack([deformed[:, 0, :], deformed[:, width_y - 1, :]])
    cols_send = jnp.stack([deformed[:, :, 0], deformed[:, :, width_z - 1]])
    rows_got, cols_got = swap_halos(rows_send, cols_send)
    has_up = (my < ny - 1).astype(f32)
    has_down = (my > 0).astype(f32)
    has_right = (mz < nz - 1).astype(f32)
    has_left = (mz > 0).astype(f32)
    rows_got = rows_got.astype(f32)
    cols_got = cols_got.astype(f32)
    high_y = rows_got[0] * has_up
    low_y = rows_got[1] * has_down
    high_z = cols_got[0] * has_right
    low_z = cols_got[1] * has_left
    high_high = cols_got[2][:, 0] * (has_up * has_right)
    low_high = cols_got[3][:, width_y - 1] * (has_down * has_right)
    high_low = cols_got[4][:, 0] * (has_up * has_left)
    low_low = cols_got[5][:, width_y - 1] * (has_down * has_left)
    rows = jnp.stack([high_y, low_y])
    gap = jnp.zeros((depth_x, 6), f32)
    side_high = jnp.concatenate([high_z, high_high[:, None], gap, low_high[:, None]], axis=1)
    side_low = jnp.concatenate([low_z, high_low[:, None], gap, low_low[:, None]], axis=1)
    sides = jnp.stack([side_high.T, side_low.T])
    sides = jnp.pad(sides, ((0, 0), (0, 0), (0, 128 - depth_x)))
    return rows, sides


def lerp(base, other, weight):
    return base + weight * (other - base)


def strip_kernel(prev_ref, main_ref, next_ref, rows_ref, sides_ref, disp_ref, image_ref,
                 fields_ref,
                 res_ref, prod_ref, mis_ref, sq_ref, energy_ref, pad_ref, shifts_ref):
    block = pl.program_id(0)
    depth_x = rows_ref.shape[1]
    width_y, width_z = image_ref.shape[1], image_ref.shape[2]
    pad_y, pad_z = pad_ref.shape
    pad_ref[width_y:, :width_z] = jnp.zeros((pad_y - width_y, width_z), jnp.float32)
    lane = lax.broadcasted_iota(jnp.int32, (pad_y, pad_z - width_z), 1)

    def source_plane(p, plane):
        plane_x = block * KNOT - 1 + p
        valid = jnp.logical_and(plane_x >= 0, plane_x < depth_x)
        safe = jnp.clip(plane_x, 0, depth_x - 1)
        pad_ref[:width_y, :width_z] = plane.astype(jnp.float32)
        pad_ref[pl.ds(width_y, 1), :width_z] = rows_ref[0, pl.ds(safe, 1), :]
        pad_ref[pl.ds(pad_y - 1, 1), :width_z] = rows_ref[1, pl.ds(safe, 1), :]
        high = jnp.sum(jnp.where(lane == safe, sides_ref[0], 0.0), axis=1, keepdims=True)
        low = jnp.sum(jnp.where(lane == safe, sides_ref[1], 0.0), axis=1, keepdims=True)
        pad_ref[:, width_z:] = jnp.where(lane == 0, high, jnp.where(lane == pad_z - width_z - 1, low, 0.0))
        whole = jnp.where(valid, pad_ref[...], 0.0)
        by_y = (pltpu.roll(whole, 1, 0), whole, pltpu.roll(whole, pad_y - 1, 0))
        for b in range(3):
            part = by_y[b][:width_y]
            by_z = (pltpu.roll(part, 1, 1), part, pltpu.roll(part, pad_z - 1, 1))
            for c in range(3):
                shifts_ref[p, 3 * b + c] = by_z[c][:, :width_z]

    source_plane(0, prev_ref[0])

    def inner_plane(p, carry):
        source_plane(p, main_ref[p - 1])
        return carry

    lax.fori_loop(1, KNOT + 1, inner_plane, 0)
    source_plane(KNOT + 1, next_ref[0])

    chunks_y = width_y // ROWS
    chunks_z = width_z // LANES

    def chunk(k, energy):
        r0 = pl.multiple_of((k // chunks_z) * ROWS, ROWS)
        c0 = pl.multiple_of((k % chunks_z) * LANES, LANES)
        rs = pl.ds(r0, ROWS)
        cs = pl.ds(c0, LANES)
        j0 = r0 // KNOT
        upper = lax.broadcasted_iota(jnp.int32, (ROWS, LANES), 0) < KNOT
        node = lax.broadcasted_iota(jnp.int32, (KNOT, LANES), 0)

        def node_row(k, j):
            return jnp.sum(jnp.where(node == j, fields_ref[k, 0, :, cs], 0.0), axis=0, keepdims=True)

        contrast = jnp.where(upper, node_row(0, j0), node_row(0, j0 + 1))
        bright = jnp.where(upper, node_row(1, j0), node_row(1, j0 + 1))

        def plane(xl, acc):
            prod_acc, mis_acc, sq_acc, e_acc = acc

            def src(a, b, c):
                return shifts_ref[xl + 1 + a, 3 * (b + 1) + (c + 1), rs, cs]

            sx = disp_ref[0, xl, rs, cs].astype(jnp.float32)
            sy = disp_ref[1, xl, rs, cs].astype(jnp.float32)
            sz = disp_ref[2, xl, rs, cs].astype(jnp.float32)
            gx, gy, gz = sx > 0, sy > 0, sz > 0
            ax, ay, az = jnp.abs(sx), jnp.abs(sy), jnp.abs(sz)
            xs = {}
            for b in (-1, 0, 1):
                for c in (-1, 0, 1):
                    xs[b, c] = jnp.where(gx, src(1, b, c), src(-1, b, c))
            y0 = {c: jnp.where(gy, src(0, 1, c), src(0, -1, c)) for c in (-1, 0, 1)}
            y1 = {c: jnp.where(gy, xs[1, c], xs[-1, c]) for c in (-1, 0, 1)}
            centre = src(0, 0, 0)
            z00 = jnp.where(gz, src(0, 0, 1), src(0, 0, -1))
            z01 = jnp.where(gz, y0[1], y0[-1])
            z10 = jnp.where(gz, xs[0, 1], xs[0, -1])
            z11 = jnp.where(gz, y1[1], y1[-1])
            l00 = lerp(centre, z00, az)
            l01 = lerp(y0[0], z01, az)
            l10 = lerp(xs[0, 0], z10, az)
            l11 = lerp(y1[0], z11, az)
            m0 = lerp(l00, l01, ay)
            m1 = lerp(l10, l11, ay)
            warped = lerp(m0, m1, ax)
            values = image_ref[xl, rs, cs].astype(jnp.float32)
            misfit = warped - contrast * values - bright
            res_ref[xl, rs, cs] = misfit.astype(res_ref.dtype)
            return (prod_acc + misfit * values, mis_acc + misfit,
                    sq_acc + values * values, e_acc + misfit * misfit)

        zero = jnp.zeros((ROWS, LANES), jnp.float32)
        prod_acc, mis_acc, sq_acc, e_acc = lax.fori_loop(
            0, KNOT, plane, (zero, zero, zero, energy))
        ky = k // chunks_z
        for out_ref, acc in ((prod_ref, prod_acc), (mis_ref, mis_acc), (sq_ref, sq_acc)):
            for n in range(ROWS // KNOT):
                out_ref[0, ky, pl.ds(n, 1), cs] = jnp.sum(
                    acc[n * KNOT : (n + 1) * KNOT], axis=0, keepdims=True)
        return e_acc

    energy = lax.fori_loop(0, chunks_y * chunks_z, chunk,
                           jnp.zeros((ROWS, LANES), jnp.float32))
    energy_ref[0] = energy


def strip_sums(deformed, rows, sides, displacement, image, fields):
    depth_x, width_y, width_z = image.shape
    nodes = depth_x // KNOT
    f32 = jnp.float32
    pairs = ROWS // KNOT
    block_sum = jax.ShapeDtypeStruct((nodes, width_y // ROWS, pairs, width_z), f32)
    node_spec = pl.BlockSpec((1, width_y // ROWS, pairs, width_z), lambda i: (i, 0, 0, 0))
    plane_spec = pl.BlockSpec((KNOT, width_y, width_z), lambda i: (i, 0, 0))
    return pl.pallas_call(
        strip_kernel,
        grid=(nodes,),
        in_specs=[
            pl.BlockSpec((1, width_y, width_z), lambda i: (jnp.maximum(i * KNOT - 1, 0), 0, 0)),
            plane_spec,
            pl.BlockSpec((1, width_y, width_z),
                         lambda i: (jnp.minimum(i * KNOT + KNOT, depth_x - 1), 0, 0)),
            pl.BlockSpec(memory_space=pltpu.VMEM),
            pl.BlockSpec(memory_space=pltpu.VMEM),
            pl.BlockSpec((3, KNOT, width_y, width_z), lambda i: (0, i, 0, 0)),
            plane_spec,
            pl.BlockSpec((2, 1) + fields.shape[2:], lambda i: (0, i, 0, 0)),
        ],
        out_specs=[
            plane_spec,
            node_spec,
            node_spec,
            node_spec,
            pl.BlockSpec((1, ROWS, LANES), lambda i: (i, 0, 0)),
        ],
        out_shape=[
            jax.ShapeDtypeStruct(image.shape, jnp.bfloat16),
            block_sum,
            block_sum,
            block_sum,
            jax.ShapeDtypeStruct((nodes, ROWS, LANES), f32),
        ],
        scratch_shapes=[
            pltpu.VMEM((sides.shape[1], width_z + 128), f32),
            pltpu.VMEM((KNOT + 2, 9, width_y, width_z), f32),
        ],
        compiler_params=pltpu.CompilerParams(
            dimension_semantics=("arbitrary",), vmem_limit_bytes=60 * 1024 * 1024),
    )(deformed, deformed, deformed, rows, sides, displacement, image, fields)


def node_sums(field):
    nodes, chunks, pairs, width_z = field.shape
    return field.reshape(nodes, chunks * pairs, width_z)


def exchange(axis, n, me, d, src, buffer, send_sem, recv_sem):
    target = lax.rem(me + d, n)
    return pltpu.make_async_remote_copy(
        src_ref=src(target), dst_ref=buffer.at[me],
        send_sem=send_sem.at[target], recv_sem=recv_sem.at[me],
        device_id={axis: target}, device_id_type=pl.DeviceIdType.MESH)


def arrival(axis, n, me, d, src_ref, buffer, sem):
    source = lax.rem(me + n - d, n)
    return pltpu.make_async_remote_copy(
        src_ref=src_ref, dst_ref=buffer.at[source],
        send_sem=sem.at[source], recv_sem=sem.at[source],
        device_id={axis: source}, device_id_type=pl.DeviceIdType.MESH)


def both_sums_kernel(nz, ny, plane_row, depth_row, plane_ref, depth_ref, plane_out, depth_out,
                     plane_landed, depth_landed, plane_summed, depth_summed,
                     plane_gathered, depth_gathered, sems):
    mz, my = lax.axis_index("gz"), lax.axis_index("gy")
    barrier = pltpu.get_barrier_semaphore()
    for d in range(1, nz):
        pl.semaphore_signal(barrier, inc=1, device_id={"gz": lax.rem(mz + d, nz)},
                            device_id_type=pl.DeviceIdType.MESH)
    for d in range(1, ny):
        pl.semaphore_signal(barrier, inc=1, device_id={"gy": lax.rem(my + d, ny)},
                            device_id_type=pl.DeviceIdType.MESH)
    pl.semaphore_wait(barrier, nz - 1 + ny - 1)
    zs1, zr1, zs2, zr2, ys1, yr1, ys2, yr2 = sems

    z_out = [exchange("gz", nz, mz, d, lambda t: plane_ref.at[t], plane_landed, zs1, zr1)
             for d in range(1, nz)]
    y_out = [exchange("gy", ny, my, d, lambda t: depth_ref.at[t], depth_landed, ys1, yr1)
             for d in range(1, ny)]
    for copy in z_out + y_out:
        copy.start()
    depth_total = depth_ref[my]
    for d in range(1, ny):
        arrival("gy", ny, my, d, depth_ref.at[0], depth_landed, yr1).wait_recv()
        depth_total = depth_total + depth_landed[lax.rem(my + ny - d, ny)]
    depth_summed[...] = depth_total
    plane_total = plane_ref[mz]
    for d in range(1, nz):
        arrival("gz", nz, mz, d, plane_ref.at[0], plane_landed, zr1).wait_recv()
        plane_total = plane_total + plane_landed[lax.rem(mz + nz - d, nz)]
    rows = lax.broadcasted_iota(jnp.int32, plane_total.shape, 0)
    lanes = lax.broadcasted_iota(jnp.int32, plane_total.shape, 1)
    slot = jnp.logical_and(rows == plane_row, lanes == RANK)
    depth_slot = jnp.logical_and(
        lax.broadcasted_iota(jnp.int32, depth_total.shape, 0) == depth_row,
        lax.broadcasted_iota(jnp.int32, depth_total.shape, 1) == RANK)
    column_energy = jnp.sum(jnp.where(depth_slot, depth_total, 0.0))
    plane_total = jnp.where(slot, column_energy, plane_total)
    plane_summed[...] = plane_total
    for copy in z_out + y_out:
        copy.wait_send()

    z_out = [exchange("gz", nz, mz, d, lambda t: plane_summed, plane_gathered, zs2, zr2)
             for d in range(1, nz)]
    y_out = [exchange("gy", ny, my, d, lambda t: depth_summed, depth_gathered, ys2, yr2)
             for d in range(1, ny)]
    for copy in z_out + y_out:
        copy.start()
    plane_out[mz] = plane_total
    depth_out[my] = depth_total
    for d in range(1, nz):
        arrival("gz", nz, mz, d, plane_summed, plane_gathered, zr2).wait_recv()
        source = lax.rem(mz + nz - d, nz)
        plane_out[source] = plane_gathered[source]
    for d in range(1, ny):
        arrival("gy", ny, my, d, depth_summed, depth_gathered, yr2).wait_recv()
        source = lax.rem(my + ny - d, ny)
        depth_out[source] = depth_gathered[source]
    for copy in z_out + y_out:
        copy.wait_send()


def chunked(main, extras, n):
    rows = -(-main.shape[0] // (n * 128))
    main = jnp.pad(main, (0, n * rows * 128 - main.shape[0])).reshape(n, rows, 128)
    tail = jnp.pad(extras, (0, 128 - extras.shape[0]))
    tail = jnp.broadcast_to(tail, (n, 1, 128))
    spare = -(-(rows + 1) // 8) * 8 - rows - 1
    return jnp.concatenate([main, tail, jnp.zeros((n, spare, 128), main.dtype)], axis=1), rows


def both_sums(plane_parts, depth_parts, plane_row, depth_row):
    nz, ny = plane_parts.shape[0], depth_parts.shape[0]
    f32 = jnp.float32
    dma = pltpu.SemaphoreType.DMA
    return pl.pallas_call(
        functools.partial(both_sums_kernel, nz, ny, plane_row, depth_row),
        out_shape=[jax.ShapeDtypeStruct(plane_parts.shape, f32),
                   jax.ShapeDtypeStruct(depth_parts.shape, f32)],
        in_specs=[pl.BlockSpec(memory_space=pltpu.VMEM)] * 2,
        out_specs=[pl.BlockSpec(memory_space=pltpu.VMEM)] * 2,
        scratch_shapes=[
            pltpu.VMEM(plane_parts.shape, f32),
            pltpu.VMEM(depth_parts.shape, f32),
            pltpu.VMEM(plane_parts.shape[1:], f32),
            pltpu.VMEM(depth_parts.shape[1:], f32),
            pltpu.VMEM(plane_parts.shape, f32),
            pltpu.VMEM(depth_parts.shape, f32),
            [dma((nz,)), dma((nz,)), dma((nz,)), dma((nz,)),
             dma((ny,)), dma((ny,)), dma((ny,)), dma((ny,))],
        ],
        compiler_params=pltpu.CompilerParams(collective_id=1, has_side_effects=True),
    )(plane_parts, depth_parts)


def local(reference_image, deformed, displacement, plane_factors, depth_factors):
    rows, sides = halo_blocks(deformed)
    fields = jnp.einsum("krij,krz->kijz", plane_factors, depth_factors, precision=highest)
    residual, prod, mis, sq, energy_parts = strip_sums(
        deformed, rows, sides, displacement, reference_image, fields)
    prod, mis, sq = node_sums(prod), node_sums(mis), node_sums(sq)
    local_energy = jnp.sum(energy_parts)

    first, second = plane_factors[0], plane_factors[1]
    grad_depth = -jnp.stack([
        jnp.einsum("rij,ijz->rz", first, prod, precision=highest),
        jnp.einsum("rij,ijz->rz", second, mis, precision=highest)])
    first_depth = jnp.einsum("rij,ijz->rz", first * first, sq, precision=highest)
    level_sum = KNOT * KNOT * jnp.sum(second * second, axis=(1, 2))
    grad_plane = -jnp.stack([
        jnp.einsum("rz,ijz->rij", depth_factors[0], prod, precision=highest),
        jnp.einsum("rz,ijz->rij", depth_factors[1], mis, precision=highest)])
    first_diag = jnp.einsum("rz,ijz->rij", depth_factors[0] * depth_factors[0], sq, precision=highest)
    depth_level = KNOT * KNOT * jnp.sum(depth_factors[1] * depth_factors[1], axis=1)

    nz, ny = lax.axis_size("gz"), lax.axis_size("gy")
    plane_terms = jnp.concatenate([grad_plane.reshape(-1), first_diag.reshape(-1)])
    depth_terms = jnp.concatenate([grad_depth.reshape(-1), first_depth.reshape(-1)])
    blank = jnp.zeros((), jnp.float32)
    plane_parts, plane_rows = chunked(plane_terms, jnp.concatenate([depth_level, blank[None]]), nz)
    depth_parts, depth_rows = chunked(depth_terms, jnp.concatenate([level_sum, local_energy[None]]), ny)
    plane_summed, depth_summed = both_sums(plane_parts, depth_parts, plane_rows, depth_rows)
    plane_terms = plane_summed[:, :plane_rows].reshape(-1)
    depth_terms = depth_summed[:, :depth_rows].reshape(-1)
    grad_plane = plane_terms[: grad_plane.size].reshape(grad_plane.shape)
    first_diag = plane_terms[grad_plane.size : grad_plane.size + first_diag.size].reshape(first_diag.shape)
    grad_depth = depth_terms[: grad_depth.size].reshape(grad_depth.shape)
    first_depth = depth_terms[grad_depth.size : grad_depth.size + first_depth.size].reshape(first_depth.shape)
    depth_level = plane_summed[0, plane_rows, :RANK]
    level_sum = depth_summed[0, depth_rows, :RANK]
    energy = jnp.sum(plane_summed[:, plane_rows, RANK])

    nodes_x = plane_factors.shape[2]
    nodes_y = plane_factors.shape[3] * lax.axis_size("gy")
    full_z = depth_factors.shape[2] * lax.axis_size("gz")
    diag_plane = jnp.stack(
        [first_diag, jnp.broadcast_to(depth_level[:, None, None], first_diag.shape)])
    lam_plane = damping * RANK * energy / (nodes_x * nodes_y)
    lam_depth = damping * energy / full_z
    step_plane = -grad_plane / (diag_plane + lam_plane + epsilon)
    diag_depth = jnp.stack([first_depth, jnp.broadcast_to(level_sum[:, None], first_depth.shape)])
    step_depth = -grad_depth / (diag_depth + lam_depth + epsilon)
    return (residual, step_plane, step_depth)


def solution(mesh):
    placed = (
        P(None, "gy", "gz"),
        P(None, "gy", "gz"),
        P(None, None, "gy", "gz"),
        P(None, None, None, "gy"),
        P(None, None, "gz"),
    )
    return jax.shard_map(
        local,
        mesh=mesh,
        in_specs=placed,
        out_specs=(P(None, "gy", "gz"), P(None, None, None, "gy"), P(None, None, "gz")),
        check_vma=False,
    )
```

```python
import functools

import jax
import jax.numpy as jnp
from jax import lax
from jax.experimental import pallas as pl
from jax.experimental.pallas import tpu as pltpu
from jax.sharding import PartitionSpec as P

RANK = 32
KNOT = 8

epsilon = 1e-06
damping = 0.01
highest = lax.Precision.HIGHEST

ROWS = 16
LANES = 256


def neighbours(part, axis, forward):
    count = lax.axis_size(axis)
    if forward:
        pairs = [(i, i + 1) for i in range(count - 1)]
    else:
        pairs = [(i + 1, i) for i in range(count - 1)]
    return lax.ppermute(part, axis, pairs)


def halo_kernel(ny, nz, rows_ref, cols_ref, rows_out, cols_out, rows_got, cols_got,
                send_sems, recv_sems):
    my, mz = lax.axis_index("gy"), lax.axis_index("gz")
    up, down = lax.rem(my + 1, ny), lax.rem(my + ny - 1, ny)
    right, left = lax.rem(mz + 1, nz), lax.rem(mz + nz - 1, nz)
    plan = [
        (rows_ref.at[0], rows_got.at[0], (down, mz)),
        (rows_ref.at[1], rows_got.at[1], (up, mz)),
        (cols_ref.at[0], cols_got.at[0], (my, left)),
        (cols_ref.at[1], cols_got.at[1], (my, right)),
        (cols_ref.at[0], cols_got.at[2], (down, left)),
        (cols_ref.at[0], cols_got.at[3], (up, left)),
        (cols_ref.at[1], cols_got.at[4], (down, right)),
        (cols_ref.at[1], cols_got.at[5], (up, right)),
    ]
    barrier = pltpu.get_barrier_semaphore()
    for _, _, device in plan:
        pl.semaphore_signal(barrier, inc=1, device_id=device,
                            device_id_type=pl.DeviceIdType.MESH)
    pl.semaphore_wait(barrier, len(plan))
    copies = []
    for k, (source, slot, device) in enumerate(plan):
        copy = pltpu.make_async_remote_copy(
            src_ref=source, dst_ref=slot, send_sem=send_sems.at[k], recv_sem=recv_sems.at[k],
            device_id=device, device_id_type=pl.DeviceIdType.MESH)
        copy.start()
        copies.append(copy)
    for copy in copies:
        copy.wait()
    rows_out[...] = rows_got[...]
    cols_out[...] = cols_got[...]


def swap_halos(rows_send, cols_send):
    ny, nz = lax.axis_size("gy"), lax.axis_size("gz")
    dma = pltpu.SemaphoreType.DMA
    rows_shape = rows_send.shape
    cols_shape = (6,) + cols_send.shape[1:]
    return pl.pallas_call(
        functools.partial(halo_kernel, ny, nz),
        out_shape=[jax.ShapeDtypeStruct(rows_shape, rows_send.dtype),
                   jax.ShapeDtypeStruct(cols_shape, cols_send.dtype)],
        in_specs=[pl.BlockSpec(memory_space=pltpu.VMEM)] * 2,
        out_specs=[pl.BlockSpec(memory_space=pltpu.VMEM)] * 2,
        scratch_shapes=[
            pltpu.VMEM(rows_shape, rows_send.dtype),
            pltpu.VMEM(cols_shape, cols_send.dtype),
            dma((8,)),
            dma((8,)),
        ],
        compiler_params=pltpu.CompilerParams(collective_id=2, has_side_effects=True),
    )(rows_send, cols_send)


def halo_blocks(deformed):
    depth_x, width_y, width_z = deformed.shape
    f32 = jnp.float32
    ny, nz = lax.axis_size("gy"), lax.axis_size("gz")
    my, mz = lax.axis_index("gy"), lax.axis_index("gz")
    rows_send = jnp.stack([deformed[:, 0, :], deformed[:, width_y - 1, :]])
    cols_send = jnp.stack([deformed[:, :, 0], deformed[:, :, width_z - 1]])
    rows_got, cols_got = swap_halos(rows_send, cols_send)
    has_up = (my < ny - 1).astype(f32)
    has_down = (my > 0).astype(f32)
    has_right = (mz < nz - 1).astype(f32)
    has_left = (mz > 0).astype(f32)
    rows_got = rows_got.astype(f32)
    cols_got = cols_got.astype(f32)
    high_y = rows_got[0] * has_up
    low_y = rows_got[1] * has_down
    high_z = cols_got[0] * has_right
    low_z = cols_got[1] * has_left
    high_high = cols_got[2][:, 0] * (has_up * has_right)
    low_high = cols_got[3][:, width_y - 1] * (has_down * has_right)
    high_low = cols_got[4][:, 0] * (has_up * has_left)
    low_low = cols_got[5][:, width_y - 1] * (has_down * has_left)
    gap_y = jnp.zeros((depth_x, 6, width_z), f32)
    rows = jnp.concatenate([high_y[:, None], gap_y, low_y[:, None]], axis=1)
    gap = jnp.zeros((depth_x, 6), f32)
    side_high = jnp.concatenate([high_z, high_high[:, None], gap, low_high[:, None]], axis=1)
    side_low = jnp.concatenate([low_z, high_low[:, None], gap, low_low[:, None]], axis=1)
    lanes = lax.broadcasted_iota(jnp.int32, (1, 1, 128), 2)
    cols = jnp.where(lanes == 0, side_high[:, :, None],
                     jnp.where(lanes == 127, side_low[:, :, None], 0.0))
    return rows, cols


def lerp(base, other, weight):
    return base + weight * (other - base)


def strip_kernel(prev_ref, main_ref, next_ref, rows_ref, cols_ref, disp_ref, image_ref,
                 contrast_ref, bright_ref,
                 res_ref, prod_ref, mis_ref, sq_ref, energy_ref, pad_ref, shifts_ref):
    block = pl.program_id(0)
    depth_x = rows_ref.shape[0]
    width_y, width_z = image_ref.shape[1], image_ref.shape[2]
    pad_y, pad_z = pad_ref.shape

    def source_plane(p, plane):
        plane_x = block * KNOT - 1 + p
        valid = jnp.logical_and(plane_x >= 0, plane_x < depth_x)
        safe = jnp.clip(plane_x, 0, depth_x - 1)
        pad_ref[:width_y, :width_z] = plane.astype(jnp.float32)
        pad_ref[width_y:, :width_z] = rows_ref[safe]
        pad_ref[:, width_z:] = cols_ref[safe]
        whole = jnp.where(valid, pad_ref[...], 0.0)
        by_y = (pltpu.roll(whole, 1, 0), whole, pltpu.roll(whole, pad_y - 1, 0))
        for b in range(3):
            part = by_y[b][:width_y]
            by_z = (pltpu.roll(part, 1, 1), part, pltpu.roll(part, pad_z - 1, 1))
            for c in range(3):
                shifts_ref[p, 3 * b + c] = by_z[c][:, :width_z]

    source_plane(0, prev_ref[0])

    def inner_plane(p, carry):
        source_plane(p, main_ref[p - 1])
        return carry

    lax.fori_loop(1, KNOT + 1, inner_plane, 0)
    source_plane(KNOT + 1, next_ref[0])

    chunks_y = width_y // ROWS
    chunks_z = width_z // LANES

    def chunk(k, energy):
        r0 = pl.multiple_of((k // chunks_z) * ROWS, ROWS)
        c0 = pl.multiple_of((k % chunks_z) * LANES, LANES)
        rs = pl.ds(r0, ROWS)
        cs = pl.ds(c0, LANES)
        contrast = contrast_ref[0, rs, cs]
        bright = bright_ref[0, rs, cs]

        def plane(xl, acc):
            prod_acc, mis_acc, sq_acc, e_acc = acc

            def src(a, b, c):
                return shifts_ref[xl + 1 + a, 3 * (b + 1) + (c + 1), rs, cs]

            sx = disp_ref[0, xl, rs, cs].astype(jnp.float32)
            sy = disp_ref[1, xl, rs, cs].astype(jnp.float32)
            sz = disp_ref[2, xl, rs, cs].astype(jnp.float32)
            gx, gy, gz = sx > 0, sy > 0, sz > 0
            ax, ay, az = jnp.abs(sx), jnp.abs(sy), jnp.abs(sz)
            xs = {}
            for b in (-1, 0, 1):
                for c in (-1, 0, 1):
                    xs[b, c] = jnp.where(gx, src(1, b, c), src(-1, b, c))
            y0 = {c: jnp.where(gy, src(0, 1, c), src(0, -1, c)) for c in (-1, 0, 1)}
            y1 = {c: jnp.where(gy, xs[1, c], xs[-1, c]) for c in (-1, 0, 1)}
            centre = src(0, 0, 0)
            z00 = jnp.where(gz, src(0, 0, 1), src(0, 0, -1))
            z01 = jnp.where(gz, y0[1], y0[-1])
            z10 = jnp.where(gz, xs[0, 1], xs[0, -1])
            z11 = jnp.where(gz, y1[1], y1[-1])
            l00 = lerp(centre, z00, az)
            l01 = lerp(y0[0], z01, az)
            l10 = lerp(xs[0, 0], z10, az)
            l11 = lerp(y1[0], z11, az)
            m0 = lerp(l00, l01, ay)
            m1 = lerp(l10, l11, ay)
            warped = lerp(m0, m1, ax)
            values = image_ref[xl, rs, cs].astype(jnp.float32)
            misfit = warped - contrast * values - bright
            res_ref[xl, rs, cs] = misfit.astype(res_ref.dtype)
            return (prod_acc + misfit * values, mis_acc + misfit,
                    sq_acc + values * values, e_acc + misfit * misfit)

        zero = jnp.zeros((ROWS, LANES), jnp.float32)
        prod_acc, mis_acc, sq_acc, e_acc = lax.fori_loop(
            0, KNOT, plane, (zero, zero, zero, energy), unroll=2)
        prod_ref[0, rs, cs] = prod_acc
        mis_ref[0, rs, cs] = mis_acc
        sq_ref[0, rs, cs] = sq_acc
        return e_acc

    energy = lax.fori_loop(0, chunks_y * chunks_z, chunk,
                           jnp.zeros((ROWS, LANES), jnp.float32))
    energy_ref[0] = energy


def strip_sums(deformed, rows, cols, displacement, image, contrast_y, bright_y):
    depth_x, width_y, width_z = image.shape
    nodes = depth_x // KNOT
    f32 = jnp.float32
    block_sum = jax.ShapeDtypeStruct((nodes, width_y, width_z), f32)
    node_spec = pl.BlockSpec((1, width_y, width_z), lambda i: (i, 0, 0))
    plane_spec = pl.BlockSpec((KNOT, width_y, width_z), lambda i: (i, 0, 0))
    return pl.pallas_call(
        strip_kernel,
        grid=(nodes,),
        in_specs=[
            pl.BlockSpec((1, width_y, width_z), lambda i: (jnp.maximum(i * KNOT - 1, 0), 0, 0)),
            plane_spec,
            pl.BlockSpec((1, width_y, width_z),
                         lambda i: (jnp.minimum(i * KNOT + KNOT, depth_x - 1), 0, 0)),
            pl.BlockSpec(memory_space=pltpu.VMEM),
            pl.BlockSpec(memory_space=pltpu.VMEM),
            pl.BlockSpec((3, KNOT, width_y, width_z), lambda i: (0, i, 0, 0)),
            plane_spec,
            node_spec,
            node_spec,
        ],
        out_specs=[
            plane_spec,
            node_spec,
            node_spec,
            node_spec,
            pl.BlockSpec((1, ROWS, LANES), lambda i: (i, 0, 0)),
        ],
        out_shape=[
            jax.ShapeDtypeStruct(image.shape, jnp.bfloat16),
            block_sum,
            block_sum,
            block_sum,
            jax.ShapeDtypeStruct((nodes, ROWS, LANES), f32),
        ],
        scratch_shapes=[
            pltpu.VMEM((width_y + rows.shape[1], width_z + cols.shape[2]), f32),
            pltpu.VMEM((KNOT + 2, 9, width_y, width_z), f32),
        ],
        compiler_params=pltpu.CompilerParams(
            dimension_semantics=("arbitrary",), vmem_limit_bytes=60 * 1024 * 1024),
    )(deformed, deformed, deformed, rows, cols, displacement, image, contrast_y, bright_y)


def node_sums(field):
    nodes, width_y, width_z = field.shape
    return field.reshape(nodes, width_y // KNOT, KNOT, width_z).sum(axis=2)


def exchange(axis, n, me, d, src, buffer, send_sem, recv_sem):
    target = lax.rem(me + d, n)
    return pltpu.make_async_remote_copy(
        src_ref=src(target), dst_ref=buffer.at[me],
        send_sem=send_sem.at[target], recv_sem=recv_sem.at[me],
        device_id={axis: target}, device_id_type=pl.DeviceIdType.MESH)


def arrival(axis, n, me, d, src_ref, buffer, sem):
    source = lax.rem(me + n - d, n)
    return pltpu.make_async_remote_copy(
        src_ref=src_ref, dst_ref=buffer.at[source],
        send_sem=sem.at[source], recv_sem=sem.at[source],
        device_id={axis: source}, device_id_type=pl.DeviceIdType.MESH)


def both_sums_kernel(nz, ny, plane_row, depth_row, plane_ref, depth_ref, plane_out, depth_out,
                     plane_landed, depth_landed, plane_summed, depth_summed,
                     plane_gathered, depth_gathered, sems):
    mz, my = lax.axis_index("gz"), lax.axis_index("gy")
    barrier = pltpu.get_barrier_semaphore()
    for d in range(1, nz):
        pl.semaphore_signal(barrier, inc=1, device_id={"gz": lax.rem(mz + d, nz)},
                            device_id_type=pl.DeviceIdType.MESH)
    for d in range(1, ny):
        pl.semaphore_signal(barrier, inc=1, device_id={"gy": lax.rem(my + d, ny)},
                            device_id_type=pl.DeviceIdType.MESH)
    pl.semaphore_wait(barrier, nz - 1 + ny - 1)
    zs1, zr1, zs2, zr2, ys1, yr1, ys2, yr2 = sems

    z_out = [exchange("gz", nz, mz, d, lambda t: plane_ref.at[t], plane_landed, zs1, zr1)
             for d in range(1, nz)]
    y_out = [exchange("gy", ny, my, d, lambda t: depth_ref.at[t], depth_landed, ys1, yr1)
             for d in range(1, ny)]
    for copy in z_out + y_out:
        copy.start()
    depth_total = depth_ref[my]
    for d in range(1, ny):
        arrival("gy", ny, my, d, depth_ref.at[0], depth_landed, yr1).wait_recv()
        depth_total = depth_total + depth_landed[lax.rem(my + ny - d, ny)]
    depth_summed[...] = depth_total
    plane_total = plane_ref[mz]
    for d in range(1, nz):
        arrival("gz", nz, mz, d, plane_ref.at[0], plane_landed, zr1).wait_recv()
        plane_total = plane_total + plane_landed[lax.rem(mz + nz - d, nz)]
    rows = lax.broadcasted_iota(jnp.int32, plane_total.shape, 0)
    lanes = lax.broadcasted_iota(jnp.int32, plane_total.shape, 1)
    slot = jnp.logical_and(rows == plane_row, lanes == RANK)
    depth_slot = jnp.logical_and(
        lax.broadcasted_iota(jnp.int32, depth_total.shape, 0) == depth_row,
        lax.broadcasted_iota(jnp.int32, depth_total.shape, 1) == RANK)
    column_energy = jnp.sum(jnp.where(depth_slot, depth_total, 0.0))
    plane_total = jnp.where(slot, column_energy, plane_total)
    plane_summed[...] = plane_total
    for copy in z_out + y_out:
        copy.wait_send()

    z_out = [exchange("gz", nz, mz, d, lambda t: plane_summed, plane_gathered, zs2, zr2)
             for d in range(1, nz)]
    y_out = [exchange("gy", ny, my, d, lambda t: depth_summed, depth_gathered, ys2, yr2)
             for d in range(1, ny)]
    for copy in z_out + y_out:
        copy.start()
    plane_out[mz] = plane_total
    depth_out[my] = depth_total
    for d in range(1, nz):
        arrival("gz", nz, mz, d, plane_summed, plane_gathered, zr2).wait_recv()
        source = lax.rem(mz + nz - d, nz)
        plane_out[source] = plane_gathered[source]
    for d in range(1, ny):
        arrival("gy", ny, my, d, depth_summed, depth_gathered, yr2).wait_recv()
        source = lax.rem(my + ny - d, ny)
        depth_out[source] = depth_gathered[source]
    for copy in z_out + y_out:
        copy.wait_send()


def chunked(main, extras, n):
    rows = -(-main.shape[0] // (n * 128))
    main = jnp.pad(main, (0, n * rows * 128 - main.shape[0])).reshape(n, rows, 128)
    tail = jnp.pad(extras, (0, 128 - extras.shape[0]))
    tail = jnp.broadcast_to(tail, (n, 1, 128))
    spare = -(-(rows + 1) // 8) * 8 - rows - 1
    return jnp.concatenate([main, tail, jnp.zeros((n, spare, 128), main.dtype)], axis=1), rows


def both_sums(plane_parts, depth_parts, plane_row, depth_row):
    nz, ny = plane_parts.shape[0], depth_parts.shape[0]
    f32 = jnp.float32
    dma = pltpu.SemaphoreType.DMA
    return pl.pallas_call(
        functools.partial(both_sums_kernel, nz, ny, plane_row, depth_row),
        out_shape=[jax.ShapeDtypeStruct(plane_parts.shape, f32),
                   jax.ShapeDtypeStruct(depth_parts.shape, f32)],
        in_specs=[pl.BlockSpec(memory_space=pltpu.VMEM)] * 2,
        out_specs=[pl.BlockSpec(memory_space=pltpu.VMEM)] * 2,
        scratch_shapes=[
            pltpu.VMEM(plane_parts.shape, f32),
            pltpu.VMEM(depth_parts.shape, f32),
            pltpu.VMEM(plane_parts.shape[1:], f32),
            pltpu.VMEM(depth_parts.shape[1:], f32),
            pltpu.VMEM(plane_parts.shape, f32),
            pltpu.VMEM(depth_parts.shape, f32),
            [dma((nz,)), dma((nz,)), dma((nz,)), dma((nz,)),
             dma((ny,)), dma((ny,)), dma((ny,)), dma((ny,))],
        ],
        compiler_params=pltpu.CompilerParams(collective_id=1, has_side_effects=True),
    )(plane_parts, depth_parts)


def local(reference_image, deformed, displacement, plane_factors, depth_factors):
    rows, cols = halo_blocks(deformed)
    fields = jnp.einsum("krij,krz->kijz", plane_factors, depth_factors, precision=highest)
    fields = jnp.repeat(fields, KNOT, axis=2)
    residual, prod, mis, sq, energy_parts = strip_sums(
        deformed, rows, cols, displacement, reference_image, fields[0], fields[1])
    prod, mis, sq = node_sums(prod), node_sums(mis), node_sums(sq)
    local_energy = jnp.sum(energy_parts)

    first, second = plane_factors[0], plane_factors[1]
    grad_depth = -jnp.stack([
        jnp.einsum("rij,ijz->rz", first, prod, precision=highest),
        jnp.einsum("rij,ijz->rz", second, mis, precision=highest)])
    first_depth = jnp.einsum("rij,ijz->rz", first * first, sq, precision=highest)
    level_sum = KNOT * KNOT * jnp.sum(second * second, axis=(1, 2))
    grad_plane = -jnp.stack([
        jnp.einsum("rz,ijz->rij", depth_factors[0], prod, precision=highest),
        jnp.einsum("rz,ijz->rij", depth_factors[1], mis, precision=highest)])
    first_diag = jnp.einsum("rz,ijz->rij", depth_factors[0] * depth_factors[0], sq, precision=highest)
    depth_level = KNOT * KNOT * jnp.sum(depth_factors[1] * depth_factors[1], axis=1)

    nz, ny = lax.axis_size("gz"), lax.axis_size("gy")
    plane_terms = jnp.concatenate([grad_plane.reshape(-1), first_diag.reshape(-1)])
    depth_terms = jnp.concatenate([grad_depth.reshape(-1), first_depth.reshape(-1)])
    blank = jnp.zeros((), jnp.float32)
    plane_parts, plane_rows = chunked(plane_terms, jnp.concatenate([depth_level, blank[None]]), nz)
    depth_parts, depth_rows = chunked(depth_terms, jnp.concatenate([level_sum, local_energy[None]]), ny)
    plane_summed, depth_summed = both_sums(plane_parts, depth_parts, plane_rows, depth_rows)
    plane_terms = plane_summed[:, :plane_rows].reshape(-1)
    depth_terms = depth_summed[:, :depth_rows].reshape(-1)
    grad_plane = plane_terms[: grad_plane.size].reshape(grad_plane.shape)
    first_diag = plane_terms[grad_plane.size : grad_plane.size + first_diag.size].reshape(first_diag.shape)
    grad_depth = depth_terms[: grad_depth.size].reshape(grad_depth.shape)
    first_depth = depth_terms[grad_depth.size : grad_depth.size + first_depth.size].reshape(first_depth.shape)
    depth_level = plane_summed[0, plane_rows, :RANK]
    level_sum = depth_summed[0, depth_rows, :RANK]
    energy = jnp.sum(plane_summed[:, plane_rows, RANK])

    nodes_x = plane_factors.shape[2]
    nodes_y = plane_factors.shape[3] * lax.axis_size("gy")
    full_z = depth_factors.shape[2] * lax.axis_size("gz")
    diag_plane = jnp.stack(
        [first_diag, jnp.broadcast_to(depth_level[:, None, None], first_diag.shape)])
    lam_plane = damping * RANK * energy / (nodes_x * nodes_y)
    lam_depth = damping * energy / full_z
    step_plane = -grad_plane / (diag_plane + lam_plane + epsilon)
    diag_depth = jnp.stack([first_depth, jnp.broadcast_to(level_sum[:, None], first_depth.shape)])
    step_depth = -grad_depth / (diag_depth + lam_depth + epsilon)
    return (residual, step_plane, step_depth)


def solution(mesh):
    placed = (
        P(None, "gy", "gz"),
        P(None, "gy", "gz"),
        P(None, None, "gy", "gz"),
        P(None, None, None, "gy"),
        P(None, None, "gz"),
    )
    return jax.shard_map(
        local,
        mesh=mesh,
        in_specs=placed,
        out_specs=(P(None, "gy", "gz"), P(None, None, None, "gy"), P(None, None, "gz")),
        check_vma=False,
    )
```

```python
import functools

import jax
import jax.numpy as jnp
from jax import lax
from jax.experimental import pallas as pl
from jax.experimental.pallas import tpu as pltpu
from jax.sharding import PartitionSpec as P

RANK = 32
KNOT = 8

epsilon = 1e-06
damping = 0.01
highest = lax.Precision.HIGHEST

ROWS = 16
LANES = 256


def neighbours(part, axis, forward):
    count = lax.axis_size(axis)
    if forward:
        pairs = [(i, i + 1) for i in range(count - 1)]
    else:
        pairs = [(i + 1, i) for i in range(count - 1)]
    return lax.ppermute(part, axis, pairs)


def halo_kernel(ny, nz, rows_ref, cols_ref, rows_out, cols_out, rows_got, cols_got,
                send_sems, recv_sems):
    my, mz = lax.axis_index("gy"), lax.axis_index("gz")
    up, down = lax.rem(my + 1, ny), lax.rem(my + ny - 1, ny)
    right, left = lax.rem(mz + 1, nz), lax.rem(mz + nz - 1, nz)
    plan = [
        (rows_ref.at[0], rows_got.at[0], (down, mz)),
        (rows_ref.at[1], rows_got.at[1], (up, mz)),
        (cols_ref.at[0], cols_got.at[0], (my, left)),
        (cols_ref.at[1], cols_got.at[1], (my, right)),
        (cols_ref.at[0], cols_got.at[2], (down, left)),
        (cols_ref.at[0], cols_got.at[3], (up, left)),
        (cols_ref.at[1], cols_got.at[4], (down, right)),
        (cols_ref.at[1], cols_got.at[5], (up, right)),
    ]
    barrier = pltpu.get_barrier_semaphore()
    for _, _, device in plan:
        pl.semaphore_signal(barrier, inc=1, device_id=device,
                            device_id_type=pl.DeviceIdType.MESH)
    pl.semaphore_wait(barrier, len(plan))
    copies = []
    for k, (source, slot, device) in enumerate(plan):
        copy = pltpu.make_async_remote_copy(
            src_ref=source, dst_ref=slot, send_sem=send_sems.at[k], recv_sem=recv_sems.at[k],
            device_id=device, device_id_type=pl.DeviceIdType.MESH)
        copy.start()
        copies.append(copy)
    for copy in copies:
        copy.wait()
    rows_out[...] = rows_got[...]
    cols_out[...] = cols_got[...]


def swap_halos(rows_send, cols_send):
    ny, nz = lax.axis_size("gy"), lax.axis_size("gz")
    dma = pltpu.SemaphoreType.DMA
    rows_shape = rows_send.shape
    cols_shape = (6,) + cols_send.shape[1:]
    return pl.pallas_call(
        functools.partial(halo_kernel, ny, nz),
        out_shape=[jax.ShapeDtypeStruct(rows_shape, rows_send.dtype),
                   jax.ShapeDtypeStruct(cols_shape, cols_send.dtype)],
        in_specs=[pl.BlockSpec(memory_space=pltpu.VMEM)] * 2,
        out_specs=[pl.BlockSpec(memory_space=pltpu.VMEM)] * 2,
        scratch_shapes=[
            pltpu.VMEM(rows_shape, rows_send.dtype),
            pltpu.VMEM(cols_shape, cols_send.dtype),
            dma((8,)),
            dma((8,)),
        ],
        compiler_params=pltpu.CompilerParams(collective_id=2, has_side_effects=True),
    )(rows_send, cols_send)


def halo_blocks(deformed):
    depth_x, width_y, width_z = deformed.shape
    f32 = jnp.float32
    ny, nz = lax.axis_size("gy"), lax.axis_size("gz")
    my, mz = lax.axis_index("gy"), lax.axis_index("gz")
    rows_send = jnp.stack([deformed[:, 0, :], deformed[:, width_y - 1, :]])
    cols_send = jnp.stack([deformed[:, :, 0], deformed[:, :, width_z - 1]])
    rows_got, cols_got = swap_halos(rows_send, cols_send)
    has_up = (my < ny - 1).astype(f32)
    has_down = (my > 0).astype(f32)
    has_right = (mz < nz - 1).astype(f32)
    has_left = (mz > 0).astype(f32)
    rows_got = rows_got.astype(f32)
    cols_got = cols_got.astype(f32)
    high_y = rows_got[0] * has_up
    low_y = rows_got[1] * has_down
    high_z = cols_got[0] * has_right
    low_z = cols_got[1] * has_left
    high_high = cols_got[2][:, 0] * (has_up * has_right)
    low_high = cols_got[3][:, width_y - 1] * (has_down * has_right)
    high_low = cols_got[4][:, 0] * (has_up * has_left)
    low_low = cols_got[5][:, width_y - 1] * (has_down * has_left)
    gap_y = jnp.zeros((depth_x, 6, width_z), f32)
    rows = jnp.concatenate([high_y[:, None], gap_y, low_y[:, None]], axis=1)
    gap = jnp.zeros((depth_x, 6), f32)
    side_high = jnp.concatenate([high_z, high_high[:, None], gap, low_high[:, None]], axis=1)
    side_low = jnp.concatenate([low_z, high_low[:, None], gap, low_low[:, None]], axis=1)
    lanes = lax.broadcasted_iota(jnp.int32, (1, 1, 128), 2)
    cols = jnp.where(lanes == 0, side_high[:, :, None],
                     jnp.where(lanes == 127, side_low[:, :, None], 0.0))
    return rows, cols


def lerp(base, other, weight):
    return base + weight * (other - base)


def strip_kernel(prev_ref, main_ref, next_ref, rows_ref, cols_ref, disp_ref, image_ref,
                 contrast_ref, bright_ref,
                 res_ref, prod_ref, mis_ref, sq_ref, energy_ref, pad_ref, shifts_ref):
    block = pl.program_id(0)
    depth_x = rows_ref.shape[0]
    width_y, width_z = image_ref.shape[1], image_ref.shape[2]
    pad_y, pad_z = pad_ref.shape

    def source_plane(p, plane):
        plane_x = block * KNOT - 1 + p
        valid = jnp.logical_and(plane_x >= 0, plane_x < depth_x)
        safe = jnp.clip(plane_x, 0, depth_x - 1)
        pad_ref[:width_y, :width_z] = plane.astype(jnp.float32)
        pad_ref[width_y:, :width_z] = rows_ref[safe]
        pad_ref[:, width_z:] = cols_ref[safe]
        whole = jnp.where(valid, pad_ref[...], 0.0)
        by_y = (pltpu.roll(whole, 1, 0), whole, pltpu.roll(whole, pad_y - 1, 0))
        for b in range(3):
            part = by_y[b][:width_y]
            by_z = (pltpu.roll(part, 1, 1), part, pltpu.roll(part, pad_z - 1, 1))
            for c in range(3):
                shifts_ref[p, 3 * b + c] = by_z[c][:, :width_z]

    source_plane(0, prev_ref[0])

    def inner_plane(p, carry):
        source_plane(p, main_ref[p - 1])
        return carry

    lax.fori_loop(1, KNOT + 1, inner_plane, 0)
    source_plane(KNOT + 1, next_ref[0])

    chunks_y = width_y // ROWS
    chunks_z = width_z // LANES

    def chunk(k, energy):
        r0 = pl.multiple_of((k // chunks_z) * ROWS, ROWS)
        c0 = pl.multiple_of((k % chunks_z) * LANES, LANES)
        rs = pl.ds(r0, ROWS)
        cs = pl.ds(c0, LANES)
        contrast = contrast_ref[0, rs, cs]
        bright = bright_ref[0, rs, cs]

        def plane(xl, acc):
            prod_acc, mis_acc, sq_acc, e_acc = acc

            def src(a, b, c):
                return shifts_ref[xl + 1 + a, 3 * (b + 1) + (c + 1), rs, cs]

            sx = disp_ref[0, xl, rs, cs].astype(jnp.float32)
            sy = disp_ref[1, xl, rs, cs].astype(jnp.float32)
            sz = disp_ref[2, xl, rs, cs].astype(jnp.float32)
            gx, gy, gz = sx > 0, sy > 0, sz > 0
            ax, ay, az = jnp.abs(sx), jnp.abs(sy), jnp.abs(sz)
            xs = {}
            for b in (-1, 0, 1):
                for c in (-1, 0, 1):
                    xs[b, c] = jnp.where(gx, src(1, b, c), src(-1, b, c))
            y0 = {c: jnp.where(gy, src(0, 1, c), src(0, -1, c)) for c in (-1, 0, 1)}
            y1 = {c: jnp.where(gy, xs[1, c], xs[-1, c]) for c in (-1, 0, 1)}
            centre = src(0, 0, 0)
            z00 = jnp.where(gz, src(0, 0, 1), src(0, 0, -1))
            z01 = jnp.where(gz, y0[1], y0[-1])
            z10 = jnp.where(gz, xs[0, 1], xs[0, -1])
            z11 = jnp.where(gz, y1[1], y1[-1])
            l00 = lerp(centre, z00, az)
            l01 = lerp(y0[0], z01, az)
            l10 = lerp(xs[0, 0], z10, az)
            l11 = lerp(y1[0], z11, az)
            m0 = lerp(l00, l01, ay)
            m1 = lerp(l10, l11, ay)
            warped = lerp(m0, m1, ax)
            values = image_ref[xl, rs, cs].astype(jnp.float32)
            misfit = warped - contrast * values - bright
            res_ref[xl, rs, cs] = misfit.astype(res_ref.dtype)
            return (prod_acc + misfit * values, mis_acc + misfit,
                    sq_acc + values * values, e_acc + misfit * misfit)

        zero = jnp.zeros((ROWS, LANES), jnp.float32)
        prod_acc, mis_acc, sq_acc, e_acc = lax.fori_loop(
            0, KNOT, plane, (zero, zero, zero, energy), unroll=4)
        prod_ref[0, rs, cs] = prod_acc
        mis_ref[0, rs, cs] = mis_acc
        sq_ref[0, rs, cs] = sq_acc
        return e_acc

    energy = lax.fori_loop(0, chunks_y * chunks_z, chunk,
                           jnp.zeros((ROWS, LANES), jnp.float32))
    energy_ref[0] = energy


def strip_sums(deformed, rows, cols, displacement, image, contrast_y, bright_y):
    depth_x, width_y, width_z = image.shape
    nodes = depth_x // KNOT
    f32 = jnp.float32
    block_sum = jax.ShapeDtypeStruct((nodes, width_y, width_z), f32)
    node_spec = pl.BlockSpec((1, width_y, width_z), lambda i: (i, 0, 0))
    plane_spec = pl.BlockSpec((KNOT, width_y, width_z), lambda i: (i, 0, 0))
    return pl.pallas_call(
        strip_kernel,
        grid=(nodes,),
        in_specs=[
            pl.BlockSpec((1, width_y, width_z), lambda i: (jnp.maximum(i * KNOT - 1, 0), 0, 0)),
            plane_spec,
            pl.BlockSpec((1, width_y, width_z),
                         lambda i: (jnp.minimum(i * KNOT + KNOT, depth_x - 1), 0, 0)),
            pl.BlockSpec(memory_space=pltpu.VMEM),
            pl.BlockSpec(memory_space=pltpu.VMEM),
            pl.BlockSpec((3, KNOT, width_y, width_z), lambda i: (0, i, 0, 0)),
            plane_spec,
            node_spec,
            node_spec,
        ],
        out_specs=[
            plane_spec,
            node_spec,
            node_spec,
            node_spec,
            pl.BlockSpec((1, ROWS, LANES), lambda i: (i, 0, 0)),
        ],
        out_shape=[
            jax.ShapeDtypeStruct(image.shape, jnp.bfloat16),
            block_sum,
            block_sum,
            block_sum,
            jax.ShapeDtypeStruct((nodes, ROWS, LANES), f32),
        ],
        scratch_shapes=[
            pltpu.VMEM((width_y + rows.shape[1], width_z + cols.shape[2]), f32),
            pltpu.VMEM((KNOT + 2, 9, width_y, width_z), f32),
        ],
        compiler_params=pltpu.CompilerParams(
            dimension_semantics=("arbitrary",), vmem_limit_bytes=60 * 1024 * 1024),
    )(deformed, deformed, deformed, rows, cols, displacement, image, contrast_y, bright_y)


def node_sums(field):
    nodes, width_y, width_z = field.shape
    return field.reshape(nodes, width_y // KNOT, KNOT, width_z).sum(axis=2)


def exchange(axis, n, me, d, src, buffer, send_sem, recv_sem):
    target = lax.rem(me + d, n)
    return pltpu.make_async_remote_copy(
        src_ref=src(target), dst_ref=buffer.at[me],
        send_sem=send_sem.at[target], recv_sem=recv_sem.at[me],
        device_id={axis: target}, device_id_type=pl.DeviceIdType.MESH)


def arrival(axis, n, me, d, src_ref, buffer, sem):
    source = lax.rem(me + n - d, n)
    return pltpu.make_async_remote_copy(
        src_ref=src_ref, dst_ref=buffer.at[source],
        send_sem=sem.at[source], recv_sem=sem.at[source],
        device_id={axis: source}, device_id_type=pl.DeviceIdType.MESH)


def both_sums_kernel(nz, ny, plane_row, depth_row, plane_ref, depth_ref, plane_out, depth_out,
                     plane_landed, depth_landed, plane_summed, depth_summed,
                     plane_gathered, depth_gathered, sems):
    mz, my = lax.axis_index("gz"), lax.axis_index("gy")
    barrier = pltpu.get_barrier_semaphore()
    for d in range(1, nz):
        pl.semaphore_signal(barrier, inc=1, device_id={"gz": lax.rem(mz + d, nz)},
                            device_id_type=pl.DeviceIdType.MESH)
    for d in range(1, ny):
        pl.semaphore_signal(barrier, inc=1, device_id={"gy": lax.rem(my + d, ny)},
                            device_id_type=pl.DeviceIdType.MESH)
    pl.semaphore_wait(barrier, nz - 1 + ny - 1)
    zs1, zr1, zs2, zr2, ys1, yr1, ys2, yr2 = sems

    z_out = [exchange("gz", nz, mz, d, lambda t: plane_ref.at[t], plane_landed, zs1, zr1)
             for d in range(1, nz)]
    y_out = [exchange("gy", ny, my, d, lambda t: depth_ref.at[t], depth_landed, ys1, yr1)
             for d in range(1, ny)]
    for copy in z_out + y_out:
        copy.start()
    depth_total = depth_ref[my]
    for d in range(1, ny):
        arrival("gy", ny, my, d, depth_ref.at[0], depth_landed, yr1).wait_recv()
        depth_total = depth_total + depth_landed[lax.rem(my + ny - d, ny)]
    depth_summed[...] = depth_total
    plane_total = plane_ref[mz]
    for d in range(1, nz):
        arrival("gz", nz, mz, d, plane_ref.at[0], plane_landed, zr1).wait_recv()
        plane_total = plane_total + plane_landed[lax.rem(mz + nz - d, nz)]
    rows = lax.broadcasted_iota(jnp.int32, plane_total.shape, 0)
    lanes = lax.broadcasted_iota(jnp.int32, plane_total.shape, 1)
    slot = jnp.logical_and(rows == plane_row, lanes == RANK)
    depth_slot = jnp.logical_and(
        lax.broadcasted_iota(jnp.int32, depth_total.shape, 0) == depth_row,
        lax.broadcasted_iota(jnp.int32, depth_total.shape, 1) == RANK)
    column_energy = jnp.sum(jnp.where(depth_slot, depth_total, 0.0))
    plane_total = jnp.where(slot, column_energy, plane_total)
    plane_summed[...] = plane_total
    for copy in z_out + y_out:
        copy.wait_send()

    z_out = [exchange("gz", nz, mz, d, lambda t: plane_summed, plane_gathered, zs2, zr2)
             for d in range(1, nz)]
    y_out = [exchange("gy", ny, my, d, lambda t: depth_summed, depth_gathered, ys2, yr2)
             for d in range(1, ny)]
    for copy in z_out + y_out:
        copy.start()
    plane_out[mz] = plane_total
    depth_out[my] = depth_total
    for d in range(1, nz):
        arrival("gz", nz, mz, d, plane_summed, plane_gathered, zr2).wait_recv()
        source = lax.rem(mz + nz - d, nz)
        plane_out[source] = plane_gathered[source]
    for d in range(1, ny):
        arrival("gy", ny, my, d, depth_summed, depth_gathered, yr2).wait_recv()
        source = lax.rem(my + ny - d, ny)
        depth_out[source] = depth_gathered[source]
    for copy in z_out + y_out:
        copy.wait_send()


def chunked(main, extras, n):
    rows = -(-main.shape[0] // (n * 128))
    main = jnp.pad(main, (0, n * rows * 128 - main.shape[0])).reshape(n, rows, 128)
    tail = jnp.pad(extras, (0, 128 - extras.shape[0]))
    tail = jnp.broadcast_to(tail, (n, 1, 128))
    spare = -(-(rows + 1) // 8) * 8 - rows - 1
    return jnp.concatenate([main, tail, jnp.zeros((n, spare, 128), main.dtype)], axis=1), rows


def both_sums(plane_parts, depth_parts, plane_row, depth_row):
    nz, ny = plane_parts.shape[0], depth_parts.shape[0]
    f32 = jnp.float32
    dma = pltpu.SemaphoreType.DMA
    return pl.pallas_call(
        functools.partial(both_sums_kernel, nz, ny, plane_row, depth_row),
        out_shape=[jax.ShapeDtypeStruct(plane_parts.shape, f32),
                   jax.ShapeDtypeStruct(depth_parts.shape, f32)],
        in_specs=[pl.BlockSpec(memory_space=pltpu.VMEM)] * 2,
        out_specs=[pl.BlockSpec(memory_space=pltpu.VMEM)] * 2,
        scratch_shapes=[
            pltpu.VMEM(plane_parts.shape, f32),
            pltpu.VMEM(depth_parts.shape, f32),
            pltpu.VMEM(plane_parts.shape[1:], f32),
            pltpu.VMEM(depth_parts.shape[1:], f32),
            pltpu.VMEM(plane_parts.shape, f32),
            pltpu.VMEM(depth_parts.shape, f32),
            [dma((nz,)), dma((nz,)), dma((nz,)), dma((nz,)),
             dma((ny,)), dma((ny,)), dma((ny,)), dma((ny,))],
        ],
        compiler_params=pltpu.CompilerParams(collective_id=1, has_side_effects=True),
    )(plane_parts, depth_parts)


def local(reference_image, deformed, displacement, plane_factors, depth_factors):
    rows, cols = halo_blocks(deformed)
    fields = jnp.einsum("krij,krz->kijz", plane_factors, depth_factors, precision=highest)
    fields = jnp.repeat(fields, KNOT, axis=2)
    residual, prod, mis, sq, energy_parts = strip_sums(
        deformed, rows, cols, displacement, reference_image, fields[0], fields[1])
    prod, mis, sq = node_sums(prod), node_sums(mis), node_sums(sq)
    local_energy = jnp.sum(energy_parts)

    first, second = plane_factors[0], plane_factors[1]
    grad_depth = -jnp.stack([
        jnp.einsum("rij,ijz->rz", first, prod, precision=highest),
        jnp.einsum("rij,ijz->rz", second, mis, precision=highest)])
    first_depth = jnp.einsum("rij,ijz->rz", first * first, sq, precision=highest)
    level_sum = KNOT * KNOT * jnp.sum(second * second, axis=(1, 2))
    grad_plane = -jnp.stack([
        jnp.einsum("rz,ijz->rij", depth_factors[0], prod, precision=highest),
        jnp.einsum("rz,ijz->rij", depth_factors[1], mis, precision=highest)])
    first_diag = jnp.einsum("rz,ijz->rij", depth_factors[0] * depth_factors[0], sq, precision=highest)
    depth_level = KNOT * KNOT * jnp.sum(depth_factors[1] * depth_factors[1], axis=1)

    nz, ny = lax.axis_size("gz"), lax.axis_size("gy")
    plane_terms = jnp.concatenate([grad_plane.reshape(-1), first_diag.reshape(-1)])
    depth_terms = jnp.concatenate([grad_depth.reshape(-1), first_depth.reshape(-1)])
    blank = jnp.zeros((), jnp.float32)
    plane_parts, plane_rows = chunked(plane_terms, jnp.concatenate([depth_level, blank[None]]), nz)
    depth_parts, depth_rows = chunked(depth_terms, jnp.concatenate([level_sum, local_energy[None]]), ny)
    plane_summed, depth_summed = both_sums(plane_parts, depth_parts, plane_rows, depth_rows)
    plane_terms = plane_summed[:, :plane_rows].reshape(-1)
    depth_terms = depth_summed[:, :depth_rows].reshape(-1)
    grad_plane = plane_terms[: grad_plane.size].reshape(grad_plane.shape)
    first_diag = plane_terms[grad_plane.size : grad_plane.size + first_diag.size].reshape(first_diag.shape)
    grad_depth = depth_terms[: grad_depth.size].reshape(grad_depth.shape)
    first_depth = depth_terms[grad_depth.size : grad_depth.size + first_depth.size].reshape(first_depth.shape)
    depth_level = plane_summed[0, plane_rows, :RANK]
    level_sum = depth_summed[0, depth_rows, :RANK]
    energy = jnp.sum(plane_summed[:, plane_rows, RANK])

    nodes_x = plane_factors.shape[2]
    nodes_y = plane_factors.shape[3] * lax.axis_size("gy")
    full_z = depth_factors.shape[2] * lax.axis_size("gz")
    diag_plane = jnp.stack(
        [first_diag, jnp.broadcast_to(depth_level[:, None, None], first_diag.shape)])
    lam_plane = damping * RANK * energy / (nodes_x * nodes_y)
    lam_depth = damping * energy / full_z
    step_plane = -grad_plane / (diag_plane + lam_plane + epsilon)
    diag_depth = jnp.stack([first_depth, jnp.broadcast_to(level_sum[:, None], first_depth.shape)])
    step_depth = -grad_depth / (diag_depth + lam_depth + epsilon)
    return (residual, step_plane, step_depth)


def solution(mesh):
    placed = (
        P(None, "gy", "gz"),
        P(None, "gy", "gz"),
        P(None, None, "gy", "gz"),
        P(None, None, None, "gy"),
        P(None, None, "gz"),
    )
    return jax.shard_map(
        local,
        mesh=mesh,
        in_specs=placed,
        out_specs=(P(None, "gy", "gz"), P(None, None, None, "gy"), P(None, None, "gz")),
        check_vma=False,
    )
```

```python
import functools

import jax
import jax.numpy as jnp
from jax import lax
from jax.experimental import pallas as pl
from jax.experimental.pallas import tpu as pltpu
from jax.sharding import PartitionSpec as P

RANK = 32
KNOT = 8

epsilon = 1e-06
damping = 0.01
highest = lax.Precision.HIGHEST

ROWS = 16
LANES = 256


def neighbours(part, axis, forward):
    count = lax.axis_size(axis)
    if forward:
        pairs = [(i, i + 1) for i in range(count - 1)]
    else:
        pairs = [(i + 1, i) for i in range(count - 1)]
    return lax.ppermute(part, axis, pairs)


def halo_kernel(ny, nz, rows_ref, cols_ref, rows_out, cols_out, rows_got, cols_got,
                send_sems, recv_sems):
    my, mz = lax.axis_index("gy"), lax.axis_index("gz")
    up, down = lax.rem(my + 1, ny), lax.rem(my + ny - 1, ny)
    right, left = lax.rem(mz + 1, nz), lax.rem(mz + nz - 1, nz)
    plan = [
        (rows_ref.at[0], rows_got.at[0], (down, mz)),
        (rows_ref.at[1], rows_got.at[1], (up, mz)),
        (cols_ref.at[0], cols_got.at[0], (my, left)),
        (cols_ref.at[1], cols_got.at[1], (my, right)),
        (cols_ref.at[0], cols_got.at[2], (down, left)),
        (cols_ref.at[0], cols_got.at[3], (up, left)),
        (cols_ref.at[1], cols_got.at[4], (down, right)),
        (cols_ref.at[1], cols_got.at[5], (up, right)),
    ]
    barrier = pltpu.get_barrier_semaphore()
    for _, _, device in plan:
        pl.semaphore_signal(barrier, inc=1, device_id=device,
                            device_id_type=pl.DeviceIdType.MESH)
    pl.semaphore_wait(barrier, len(plan))
    copies = []
    for k, (source, slot, device) in enumerate(plan):
        copy = pltpu.make_async_remote_copy(
            src_ref=source, dst_ref=slot, send_sem=send_sems.at[k], recv_sem=recv_sems.at[k],
            device_id=device, device_id_type=pl.DeviceIdType.MESH)
        copy.start()
        copies.append(copy)
    for copy in copies:
        copy.wait()
    rows_out[...] = rows_got[...]
    cols_out[...] = cols_got[...]


def swap_halos(rows_send, cols_send):
    ny, nz = lax.axis_size("gy"), lax.axis_size("gz")
    dma = pltpu.SemaphoreType.DMA
    rows_shape = rows_send.shape
    cols_shape = (6,) + cols_send.shape[1:]
    return pl.pallas_call(
        functools.partial(halo_kernel, ny, nz),
        out_shape=[jax.ShapeDtypeStruct(rows_shape, rows_send.dtype),
                   jax.ShapeDtypeStruct(cols_shape, cols_send.dtype)],
        in_specs=[pl.BlockSpec(memory_space=pltpu.VMEM)] * 2,
        out_specs=[pl.BlockSpec(memory_space=pltpu.VMEM)] * 2,
        scratch_shapes=[
            pltpu.VMEM(rows_shape, rows_send.dtype),
            pltpu.VMEM(cols_shape, cols_send.dtype),
            dma((8,)),
            dma((8,)),
        ],
        compiler_params=pltpu.CompilerParams(collective_id=2, has_side_effects=True),
    )(rows_send, cols_send)


def halo_blocks(deformed):
    depth_x, width_y, width_z = deformed.shape
    f32 = jnp.float32
    ny, nz = lax.axis_size("gy"), lax.axis_size("gz")
    my, mz = lax.axis_index("gy"), lax.axis_index("gz")
    rows_send = jnp.stack([deformed[:, 0, :], deformed[:, width_y - 1, :]])
    cols_send = jnp.stack([deformed[:, :, 0], deformed[:, :, width_z - 1]])
    rows_got, cols_got = swap_halos(rows_send, cols_send)
    has_up = (my < ny - 1).astype(f32)
    has_down = (my > 0).astype(f32)
    has_right = (mz < nz - 1).astype(f32)
    has_left = (mz > 0).astype(f32)
    rows_got = rows_got.astype(f32)
    cols_got = cols_got.astype(f32)
    high_y = rows_got[0] * has_up
    low_y = rows_got[1] * has_down
    high_z = cols_got[0] * has_right
    low_z = cols_got[1] * has_left
    high_high = cols_got[2][:, 0] * (has_up * has_right)
    low_high = cols_got[3][:, width_y - 1] * (has_down * has_right)
    high_low = cols_got[4][:, 0] * (has_up * has_left)
    low_low = cols_got[5][:, width_y - 1] * (has_down * has_left)
    gap_y = jnp.zeros((depth_x, 6, width_z), f32)
    rows = jnp.concatenate([high_y[:, None], gap_y, low_y[:, None]], axis=1)
    gap = jnp.zeros((depth_x, 6), f32)
    side_high = jnp.concatenate([high_z, high_high[:, None], gap, low_high[:, None]], axis=1)
    side_low = jnp.concatenate([low_z, high_low[:, None], gap, low_low[:, None]], axis=1)
    lanes = lax.broadcasted_iota(jnp.int32, (1, 1, 128), 2)
    cols = jnp.where(lanes == 0, side_high[:, :, None],
                     jnp.where(lanes == 127, side_low[:, :, None], 0.0))
    return rows, cols


def lerp(base, other, weight):
    return base + weight * (other - base)


def strip_kernel(prev_ref, main_ref, next_ref, rows_ref, cols_ref, disp_ref, image_ref,
                 contrast_ref, bright_ref,
                 res_ref, prod_ref, mis_ref, sq_ref, energy_ref, pad_ref, shifts_ref):
    block = pl.program_id(0)
    depth_x = rows_ref.shape[0]
    width_y, width_z = image_ref.shape[1], image_ref.shape[2]
    pad_y, pad_z = pad_ref.shape

    def source_plane(p, plane):
        plane_x = block * KNOT - 1 + p
        valid = jnp.logical_and(plane_x >= 0, plane_x < depth_x)
        safe = jnp.clip(plane_x, 0, depth_x - 1)
        pad_ref[:width_y, :width_z] = plane.astype(jnp.float32)
        pad_ref[width_y:, :width_z] = rows_ref[safe]
        pad_ref[:, width_z:] = cols_ref[safe]
        whole = jnp.where(valid, pad_ref[...], 0.0)
        by_y = (pltpu.roll(whole, 1, 0), whole, pltpu.roll(whole, pad_y - 1, 0))
        for b in range(3):
            part = by_y[b][:width_y]
            by_z = (pltpu.roll(part, 1, 1), part, pltpu.roll(part, pad_z - 1, 1))
            for c in range(3):
                shifts_ref[p, 3 * b + c] = by_z[c][:, :width_z]

    source_plane(0, prev_ref[0])

    def inner_plane(p, carry):
        source_plane(p, main_ref[p - 1])
        return carry

    lax.fori_loop(1, KNOT + 1, inner_plane, 0, unroll=2)
    source_plane(KNOT + 1, next_ref[0])

    chunks_y = width_y // ROWS
    chunks_z = width_z // LANES

    def chunk(k, energy):
        r0 = pl.multiple_of((k // chunks_z) * ROWS, ROWS)
        c0 = pl.multiple_of((k % chunks_z) * LANES, LANES)
        rs = pl.ds(r0, ROWS)
        cs = pl.ds(c0, LANES)
        contrast = contrast_ref[0, rs, cs]
        bright = bright_ref[0, rs, cs]

        def plane(xl, acc):
            prod_acc, mis_acc, sq_acc, e_acc = acc

            def src(a, b, c):
                return shifts_ref[xl + 1 + a, 3 * (b + 1) + (c + 1), rs, cs]

            sx = disp_ref[0, xl, rs, cs].astype(jnp.float32)
            sy = disp_ref[1, xl, rs, cs].astype(jnp.float32)
            sz = disp_ref[2, xl, rs, cs].astype(jnp.float32)
            gx, gy, gz = sx > 0, sy > 0, sz > 0
            ax, ay, az = jnp.abs(sx), jnp.abs(sy), jnp.abs(sz)
            xs = {}
            for b in (-1, 0, 1):
                for c in (-1, 0, 1):
                    xs[b, c] = jnp.where(gx, src(1, b, c), src(-1, b, c))
            y0 = {c: jnp.where(gy, src(0, 1, c), src(0, -1, c)) for c in (-1, 0, 1)}
            y1 = {c: jnp.where(gy, xs[1, c], xs[-1, c]) for c in (-1, 0, 1)}
            centre = src(0, 0, 0)
            z00 = jnp.where(gz, src(0, 0, 1), src(0, 0, -1))
            z01 = jnp.where(gz, y0[1], y0[-1])
            z10 = jnp.where(gz, xs[0, 1], xs[0, -1])
            z11 = jnp.where(gz, y1[1], y1[-1])
            l00 = lerp(centre, z00, az)
            l01 = lerp(y0[0], z01, az)
            l10 = lerp(xs[0, 0], z10, az)
            l11 = lerp(y1[0], z11, az)
            m0 = lerp(l00, l01, ay)
            m1 = lerp(l10, l11, ay)
            warped = lerp(m0, m1, ax)
            values = image_ref[xl, rs, cs].astype(jnp.float32)
            misfit = warped - contrast * values - bright
            res_ref[xl, rs, cs] = misfit.astype(res_ref.dtype)
            return (prod_acc + misfit * values, mis_acc + misfit,
                    sq_acc + values * values, e_acc + misfit * misfit)

        zero = jnp.zeros((ROWS, LANES), jnp.float32)
        prod_acc, mis_acc, sq_acc, e_acc = lax.fori_loop(
            0, KNOT, plane, (zero, zero, zero, energy), unroll=4)
        prod_ref[0, rs, cs] = prod_acc
        mis_ref[0, rs, cs] = mis_acc
        sq_ref[0, rs, cs] = sq_acc
        return e_acc

    energy = lax.fori_loop(0, chunks_y * chunks_z, chunk,
                           jnp.zeros((ROWS, LANES), jnp.float32))
    energy_ref[0] = energy


def strip_sums(deformed, rows, cols, displacement, image, contrast_y, bright_y):
    depth_x, width_y, width_z = image.shape
    nodes = depth_x // KNOT
    f32 = jnp.float32
    block_sum = jax.ShapeDtypeStruct((nodes, width_y, width_z), f32)
    node_spec = pl.BlockSpec((1, width_y, width_z), lambda i: (i, 0, 0))
    plane_spec = pl.BlockSpec((KNOT, width_y, width_z), lambda i: (i, 0, 0))
    return pl.pallas_call(
        strip_kernel,
        grid=(nodes,),
        in_specs=[
            pl.BlockSpec((1, width_y, width_z), lambda i: (jnp.maximum(i * KNOT - 1, 0), 0, 0)),
            plane_spec,
            pl.BlockSpec((1, width_y, width_z),
                         lambda i: (jnp.minimum(i * KNOT + KNOT, depth_x - 1), 0, 0)),
            pl.BlockSpec(memory_space=pltpu.VMEM),
            pl.BlockSpec(memory_space=pltpu.VMEM),
            pl.BlockSpec((3, KNOT, width_y, width_z), lambda i: (0, i, 0, 0)),
            plane_spec,
            node_spec,
            node_spec,
        ],
        out_specs=[
            plane_spec,
            node_spec,
            node_spec,
            node_spec,
            pl.BlockSpec((1, ROWS, LANES), lambda i: (i, 0, 0)),
        ],
        out_shape=[
            jax.ShapeDtypeStruct(image.shape, jnp.bfloat16),
            block_sum,
            block_sum,
            block_sum,
            jax.ShapeDtypeStruct((nodes, ROWS, LANES), f32),
        ],
        scratch_shapes=[
            pltpu.VMEM((width_y + rows.shape[1], width_z + cols.shape[2]), f32),
            pltpu.VMEM((KNOT + 2, 9, width_y, width_z), f32),
        ],
        compiler_params=pltpu.CompilerParams(
            dimension_semantics=("arbitrary",), vmem_limit_bytes=60 * 1024 * 1024),
    )(deformed, deformed, deformed, rows, cols, displacement, image, contrast_y, bright_y)


def node_sums(field):
    nodes, width_y, width_z = field.shape
    return field.reshape(nodes, width_y // KNOT, KNOT, width_z).sum(axis=2)


def exchange(axis, n, me, d, src, buffer, send_sem, recv_sem):
    target = lax.rem(me + d, n)
    return pltpu.make_async_remote_copy(
        src_ref=src(target), dst_ref=buffer.at[me],
        send_sem=send_sem.at[target], recv_sem=recv_sem.at[me],
        device_id={axis: target}, device_id_type=pl.DeviceIdType.MESH)


def arrival(axis, n, me, d, src_ref, buffer, sem):
    source = lax.rem(me + n - d, n)
    return pltpu.make_async_remote_copy(
        src_ref=src_ref, dst_ref=buffer.at[source],
        send_sem=sem.at[source], recv_sem=sem.at[source],
        device_id={axis: source}, device_id_type=pl.DeviceIdType.MESH)


def both_sums_kernel(nz, ny, plane_row, depth_row, plane_ref, depth_ref, plane_out, depth_out,
                     plane_landed, depth_landed, plane_summed, depth_summed,
                     plane_gathered, depth_gathered, sems):
    mz, my = lax.axis_index("gz"), lax.axis_index("gy")
    barrier = pltpu.get_barrier_semaphore()
    for d in range(1, nz):
        pl.semaphore_signal(barrier, inc=1, device_id={"gz": lax.rem(mz + d, nz)},
                            device_id_type=pl.DeviceIdType.MESH)
    for d in range(1, ny):
        pl.semaphore_signal(barrier, inc=1, device_id={"gy": lax.rem(my + d, ny)},
                            device_id_type=pl.DeviceIdType.MESH)
    pl.semaphore_wait(barrier, nz - 1 + ny - 1)
    zs1, zr1, zs2, zr2, ys1, yr1, ys2, yr2 = sems

    z_out = [exchange("gz", nz, mz, d, lambda t: plane_ref.at[t], plane_landed, zs1, zr1)
             for d in range(1, nz)]
    y_out = [exchange("gy", ny, my, d, lambda t: depth_ref.at[t], depth_landed, ys1, yr1)
             for d in range(1, ny)]
    for copy in z_out + y_out:
        copy.start()
    depth_total = depth_ref[my]
    for d in range(1, ny):
        arrival("gy", ny, my, d, depth_ref.at[0], depth_landed, yr1).wait_recv()
        depth_total = depth_total + depth_landed[lax.rem(my + ny - d, ny)]
    depth_summed[...] = depth_total
    plane_total = plane_ref[mz]
    for d in range(1, nz):
        arrival("gz", nz, mz, d, plane_ref.at[0], plane_landed, zr1).wait_recv()
        plane_total = plane_total + plane_landed[lax.rem(mz + nz - d, nz)]
    rows = lax.broadcasted_iota(jnp.int32, plane_total.shape, 0)
    lanes = lax.broadcasted_iota(jnp.int32, plane_total.shape, 1)
    slot = jnp.logical_and(rows == plane_row, lanes == RANK)
    depth_slot = jnp.logical_and(
        lax.broadcasted_iota(jnp.int32, depth_total.shape, 0) == depth_row,
        lax.broadcasted_iota(jnp.int32, depth_total.shape, 1) == RANK)
    column_energy = jnp.sum(jnp.where(depth_slot, depth_total, 0.0))
    plane_total = jnp.where(slot, column_energy, plane_total)
    plane_summed[...] = plane_total
    for copy in z_out + y_out:
        copy.wait_send()

    z_out = [exchange("gz", nz, mz, d, lambda t: plane_summed, plane_gathered, zs2, zr2)
             for d in range(1, nz)]
    y_out = [exchange("gy", ny, my, d, lambda t: depth_summed, depth_gathered, ys2, yr2)
             for d in range(1, ny)]
    for copy in z_out + y_out:
        copy.start()
    plane_out[mz] = plane_total
    depth_out[my] = depth_total
    for d in range(1, nz):
        arrival("gz", nz, mz, d, plane_summed, plane_gathered, zr2).wait_recv()
        source = lax.rem(mz + nz - d, nz)
        plane_out[source] = plane_gathered[source]
    for d in range(1, ny):
        arrival("gy", ny, my, d, depth_summed, depth_gathered, yr2).wait_recv()
        source = lax.rem(my + ny - d, ny)
        depth_out[source] = depth_gathered[source]
    for copy in z_out + y_out:
        copy.wait_send()


def chunked(main, extras, n):
    rows = -(-main.shape[0] // (n * 128))
    main = jnp.pad(main, (0, n * rows * 128 - main.shape[0])).reshape(n, rows, 128)
    tail = jnp.pad(extras, (0, 128 - extras.shape[0]))
    tail = jnp.broadcast_to(tail, (n, 1, 128))
    spare = -(-(rows + 1) // 8) * 8 - rows - 1
    return jnp.concatenate([main, tail, jnp.zeros((n, spare, 128), main.dtype)], axis=1), rows


def both_sums(plane_parts, depth_parts, plane_row, depth_row):
    nz, ny = plane_parts.shape[0], depth_parts.shape[0]
    f32 = jnp.float32
    dma = pltpu.SemaphoreType.DMA
    return pl.pallas_call(
        functools.partial(both_sums_kernel, nz, ny, plane_row, depth_row),
        out_shape=[jax.ShapeDtypeStruct(plane_parts.shape, f32),
                   jax.ShapeDtypeStruct(depth_parts.shape, f32)],
        in_specs=[pl.BlockSpec(memory_space=pltpu.VMEM)] * 2,
        out_specs=[pl.BlockSpec(memory_space=pltpu.VMEM)] * 2,
        scratch_shapes=[
            pltpu.VMEM(plane_parts.shape, f32),
            pltpu.VMEM(depth_parts.shape, f32),
            pltpu.VMEM(plane_parts.shape[1:], f32),
            pltpu.VMEM(depth_parts.shape[1:], f32),
            pltpu.VMEM(plane_parts.shape, f32),
            pltpu.VMEM(depth_parts.shape, f32),
            [dma((nz,)), dma((nz,)), dma((nz,)), dma((nz,)),
             dma((ny,)), dma((ny,)), dma((ny,)), dma((ny,))],
        ],
        compiler_params=pltpu.CompilerParams(collective_id=1, has_side_effects=True),
    )(plane_parts, depth_parts)


def local(reference_image, deformed, displacement, plane_factors, depth_factors):
    rows, cols = halo_blocks(deformed)
    fields = jnp.einsum("krij,krz->kijz", plane_factors, depth_factors, precision=highest)
    fields = jnp.repeat(fields, KNOT, axis=2)
    residual, prod, mis, sq, energy_parts = strip_sums(
        deformed, rows, cols, displacement, reference_image, fields[0], fields[1])
    prod, mis, sq = node_sums(prod), node_sums(mis), node_sums(sq)
    local_energy = jnp.sum(energy_parts)

    first, second = plane_factors[0], plane_factors[1]
    grad_depth = -jnp.stack([
        jnp.einsum("rij,ijz->rz", first, prod, precision=highest),
        jnp.einsum("rij,ijz->rz", second, mis, precision=highest)])
    first_depth = jnp.einsum("rij,ijz->rz", first * first, sq, precision=highest)
    level_sum = KNOT * KNOT * jnp.sum(second * second, axis=(1, 2))
    grad_plane = -jnp.stack([
        jnp.einsum("rz,ijz->rij", depth_factors[0], prod, precision=highest),
        jnp.einsum("rz,ijz->rij", depth_factors[1], mis, precision=highest)])
    first_diag = jnp.einsum("rz,ijz->rij", depth_factors[0] * depth_factors[0], sq, precision=highest)
    depth_level = KNOT * KNOT * jnp.sum(depth_factors[1] * depth_factors[1], axis=1)

    nz, ny = lax.axis_size("gz"), lax.axis_size("gy")
    plane_terms = jnp.concatenate([grad_plane.reshape(-1), first_diag.reshape(-1)])
    depth_terms = jnp.concatenate([grad_depth.reshape(-1), first_depth.reshape(-1)])
    blank = jnp.zeros((), jnp.float32)
    plane_parts, plane_rows = chunked(plane_terms, jnp.concatenate([depth_level, blank[None]]), nz)
    depth_parts, depth_rows = chunked(depth_terms, jnp.concatenate([level_sum, local_energy[None]]), ny)
    plane_summed, depth_summed = both_sums(plane_parts, depth_parts, plane_rows, depth_rows)
    plane_terms = plane_summed[:, :plane_rows].reshape(-1)
    depth_terms = depth_summed[:, :depth_rows].reshape(-1)
    grad_plane = plane_terms[: grad_plane.size].reshape(grad_plane.shape)
    first_diag = plane_terms[grad_plane.size : grad_plane.size + first_diag.size].reshape(first_diag.shape)
    grad_depth = depth_terms[: grad_depth.size].reshape(grad_depth.shape)
    first_depth = depth_terms[grad_depth.size : grad_depth.size + first_depth.size].reshape(first_depth.shape)
    depth_level = plane_summed[0, plane_rows, :RANK]
    level_sum = depth_summed[0, depth_rows, :RANK]
    energy = jnp.sum(plane_summed[:, plane_rows, RANK])

    nodes_x = plane_factors.shape[2]
    nodes_y = plane_factors.shape[3] * lax.axis_size("gy")
    full_z = depth_factors.shape[2] * lax.axis_size("gz")
    diag_plane = jnp.stack(
        [first_diag, jnp.broadcast_to(depth_level[:, None, None], first_diag.shape)])
    lam_plane = damping * RANK * energy / (nodes_x * nodes_y)
    lam_depth = damping * energy / full_z
    step_plane = -grad_plane / (diag_plane + lam_plane + epsilon)
    diag_depth = jnp.stack([first_depth, jnp.broadcast_to(level_sum[:, None], first_depth.shape)])
    step_depth = -grad_depth / (diag_depth + lam_depth + epsilon)
    return (residual, step_plane, step_depth)


def solution(mesh):
    placed = (
        P(None, "gy", "gz"),
        P(None, "gy", "gz"),
        P(None, None, "gy", "gz"),
        P(None, None, None, "gy"),
        P(None, None, "gz"),
    )
    return jax.shard_map(
        local,
        mesh=mesh,
        in_specs=placed,
        out_specs=(P(None, "gy", "gz"), P(None, None, None, "gy"), P(None, None, "gz")),
        check_vma=False,
    )
```

```python
import functools

import jax
import jax.numpy as jnp
from jax import lax
from jax.experimental import pallas as pl
from jax.experimental.pallas import tpu as pltpu
from jax.sharding import PartitionSpec as P

RANK = 32
KNOT = 8

epsilon = 1e-06
damping = 0.01
highest = lax.Precision.HIGHEST

ROWS = 16
LANES = 256


def neighbours(part, axis, forward):
    count = lax.axis_size(axis)
    if forward:
        pairs = [(i, i + 1) for i in range(count - 1)]
    else:
        pairs = [(i + 1, i) for i in range(count - 1)]
    return lax.ppermute(part, axis, pairs)


def halo_kernel(ny, nz, rows_ref, cols_ref, rows_out, cols_out, rows_got, cols_got,
                send_sems, recv_sems):
    my, mz = lax.axis_index("gy"), lax.axis_index("gz")
    up, down = lax.rem(my + 1, ny), lax.rem(my + ny - 1, ny)
    right, left = lax.rem(mz + 1, nz), lax.rem(mz + nz - 1, nz)
    plan = [
        (rows_ref.at[0], rows_got.at[0], (down, mz)),
        (rows_ref.at[1], rows_got.at[1], (up, mz)),
        (cols_ref.at[0], cols_got.at[0], (my, left)),
        (cols_ref.at[1], cols_got.at[1], (my, right)),
        (cols_ref.at[0], cols_got.at[2], (down, left)),
        (cols_ref.at[0], cols_got.at[3], (up, left)),
        (cols_ref.at[1], cols_got.at[4], (down, right)),
        (cols_ref.at[1], cols_got.at[5], (up, right)),
    ]
    barrier = pltpu.get_barrier_semaphore()
    for _, _, device in plan:
        pl.semaphore_signal(barrier, inc=1, device_id=device,
                            device_id_type=pl.DeviceIdType.MESH)
    pl.semaphore_wait(barrier, len(plan))
    copies = []
    for k, (source, slot, device) in enumerate(plan):
        copy = pltpu.make_async_remote_copy(
            src_ref=source, dst_ref=slot, send_sem=send_sems.at[k], recv_sem=recv_sems.at[k],
            device_id=device, device_id_type=pl.DeviceIdType.MESH)
        copy.start()
        copies.append(copy)
    for copy in copies:
        copy.wait()
    rows_out[...] = rows_got[...]
    cols_out[...] = cols_got[...]


def swap_halos(rows_send, cols_send):
    ny, nz = lax.axis_size("gy"), lax.axis_size("gz")
    dma = pltpu.SemaphoreType.DMA
    rows_shape = rows_send.shape
    cols_shape = (6,) + cols_send.shape[1:]
    return pl.pallas_call(
        functools.partial(halo_kernel, ny, nz),
        out_shape=[jax.ShapeDtypeStruct(rows_shape, rows_send.dtype),
                   jax.ShapeDtypeStruct(cols_shape, cols_send.dtype)],
        in_specs=[pl.BlockSpec(memory_space=pltpu.VMEM)] * 2,
        out_specs=[pl.BlockSpec(memory_space=pltpu.VMEM)] * 2,
        scratch_shapes=[
            pltpu.VMEM(rows_shape, rows_send.dtype),
            pltpu.VMEM(cols_shape, cols_send.dtype),
            dma((8,)),
            dma((8,)),
        ],
        compiler_params=pltpu.CompilerParams(collective_id=2, has_side_effects=True),
    )(rows_send, cols_send)


def halo_blocks(deformed):
    depth_x, width_y, width_z = deformed.shape
    f32 = jnp.float32
    ny, nz = lax.axis_size("gy"), lax.axis_size("gz")
    my, mz = lax.axis_index("gy"), lax.axis_index("gz")
    rows_send = jnp.stack([deformed[:, 0, :], deformed[:, width_y - 1, :]])
    cols_send = jnp.stack([deformed[:, :, 0], deformed[:, :, width_z - 1]])
    rows_got, cols_got = swap_halos(rows_send, cols_send)
    held = deformed.dtype
    has_up = (my < ny - 1).astype(held)
    has_down = (my > 0).astype(held)
    has_right = (mz < nz - 1).astype(held)
    has_left = (mz > 0).astype(held)
    high_y = rows_got[0] * has_up
    low_y = rows_got[1] * has_down
    high_z = cols_got[0] * has_right
    low_z = cols_got[1] * has_left
    high_high = cols_got[2][:, 0] * (has_up * has_right)
    low_high = cols_got[3][:, width_y - 1] * (has_down * has_right)
    high_low = cols_got[4][:, 0] * (has_up * has_left)
    low_low = cols_got[5][:, width_y - 1] * (has_down * has_left)
    gap_y = jnp.zeros((depth_x, 6, width_z), held)
    rows = jnp.concatenate([high_y[:, None], gap_y, low_y[:, None]], axis=1)
    gap = jnp.zeros((depth_x, 6), held)
    side_high = jnp.concatenate([high_z, high_high[:, None], gap, low_high[:, None]], axis=1)
    side_low = jnp.concatenate([low_z, high_low[:, None], gap, low_low[:, None]], axis=1)
    lanes = lax.broadcasted_iota(jnp.int32, (1, 1, 128), 2)
    cols = jnp.where(lanes == 0, side_high[:, :, None],
                     jnp.where(lanes == 127, side_low[:, :, None], jnp.zeros((), held)))
    return rows, cols


def lerp(base, other, weight):
    return base + weight * (other - base)


def strip_kernel(prev_ref, main_ref, next_ref, rows_ref, cols_ref, disp_ref, image_ref,
                 contrast_ref, bright_ref,
                 res_ref, prod_ref, mis_ref, sq_ref, energy_ref, pad_ref, shifts_ref):
    block = pl.program_id(0)
    depth_x = rows_ref.shape[0]
    width_y, width_z = image_ref.shape[1], image_ref.shape[2]
    pad_y, pad_z = pad_ref.shape

    def source_plane(p, plane):
        plane_x = block * KNOT - 1 + p
        valid = jnp.logical_and(plane_x >= 0, plane_x < depth_x)
        safe = jnp.clip(plane_x, 0, depth_x - 1)
        pad_ref[:width_y, :width_z] = plane.astype(jnp.float32)
        pad_ref[width_y:, :width_z] = rows_ref[safe].astype(jnp.float32)
        pad_ref[:, width_z:] = cols_ref[safe].astype(jnp.float32)
        whole = jnp.where(valid, pad_ref[...], 0.0)
        by_y = (pltpu.roll(whole, 1, 0), whole, pltpu.roll(whole, pad_y - 1, 0))
        for b in range(3):
            part = by_y[b][:width_y]
            by_z = (pltpu.roll(part, 1, 1), part, pltpu.roll(part, pad_z - 1, 1))
            for c in range(3):
                shifts_ref[p, 3 * b + c] = by_z[c][:, :width_z]

    source_plane(0, prev_ref[0])

    def inner_plane(p, carry):
        source_plane(p, main_ref[p - 1])
        return carry

    lax.fori_loop(1, KNOT + 1, inner_plane, 0, unroll=2)
    source_plane(KNOT + 1, next_ref[0])

    chunks_y = width_y // ROWS
    chunks_z = width_z // LANES

    def chunk(k, energy):
        r0 = pl.multiple_of((k // chunks_z) * ROWS, ROWS)
        c0 = pl.multiple_of((k % chunks_z) * LANES, LANES)
        rs = pl.ds(r0, ROWS)
        cs = pl.ds(c0, LANES)
        contrast = contrast_ref[0, rs, cs]
        bright = bright_ref[0, rs, cs]

        def plane(xl, acc):
            prod_acc, mis_acc, sq_acc, e_acc = acc

            def src(a, b, c):
                return shifts_ref[xl + 1 + a, 3 * (b + 1) + (c + 1), rs, cs]

            sx = disp_ref[0, xl, rs, cs].astype(jnp.float32)
            sy = disp_ref[1, xl, rs, cs].astype(jnp.float32)
            sz = disp_ref[2, xl, rs, cs].astype(jnp.float32)
            gx, gy, gz = sx > 0, sy > 0, sz > 0
            ax, ay, az = jnp.abs(sx), jnp.abs(sy), jnp.abs(sz)
            xs = {}
            for b in (-1, 0, 1):
                for c in (-1, 0, 1):
                    xs[b, c] = jnp.where(gx, src(1, b, c), src(-1, b, c))
            y0 = {c: jnp.where(gy, src(0, 1, c), src(0, -1, c)) for c in (-1, 0, 1)}
            y1 = {c: jnp.where(gy, xs[1, c], xs[-1, c]) for c in (-1, 0, 1)}
            centre = src(0, 0, 0)
            z00 = jnp.where(gz, src(0, 0, 1), src(0, 0, -1))
            z01 = jnp.where(gz, y0[1], y0[-1])
            z10 = jnp.where(gz, xs[0, 1], xs[0, -1])
            z11 = jnp.where(gz, y1[1], y1[-1])
            l00 = lerp(centre, z00, az)
            l01 = lerp(y0[0], z01, az)
            l10 = lerp(xs[0, 0], z10, az)
            l11 = lerp(y1[0], z11, az)
            m0 = lerp(l00, l01, ay)
            m1 = lerp(l10, l11, ay)
            warped = lerp(m0, m1, ax)
            values = image_ref[xl, rs, cs].astype(jnp.float32)
            misfit = warped - contrast * values - bright
            res_ref[xl, rs, cs] = misfit.astype(res_ref.dtype)
            return (prod_acc + misfit * values, mis_acc + misfit,
                    sq_acc + values * values, e_acc + misfit * misfit)

        zero = jnp.zeros((ROWS, LANES), jnp.float32)
        prod_acc, mis_acc, sq_acc, e_acc = lax.fori_loop(
            0, KNOT, plane, (zero, zero, zero, energy), unroll=4)
        prod_ref[0, rs, cs] = prod_acc
        mis_ref[0, rs, cs] = mis_acc
        sq_ref[0, rs, cs] = sq_acc
        return e_acc

    energy = lax.fori_loop(0, chunks_y * chunks_z, chunk,
                           jnp.zeros((ROWS, LANES), jnp.float32))
    energy_ref[0] = energy


def strip_sums(deformed, rows, cols, displacement, image, contrast_y, bright_y):
    depth_x, width_y, width_z = image.shape
    nodes = depth_x // KNOT
    f32 = jnp.float32
    block_sum = jax.ShapeDtypeStruct((nodes, width_y, width_z), f32)
    node_spec = pl.BlockSpec((1, width_y, width_z), lambda i: (i, 0, 0))
    plane_spec = pl.BlockSpec((KNOT, width_y, width_z), lambda i: (i, 0, 0))
    return pl.pallas_call(
        strip_kernel,
        grid=(nodes,),
        in_specs=[
            pl.BlockSpec((1, width_y, width_z), lambda i: (jnp.maximum(i * KNOT - 1, 0), 0, 0)),
            plane_spec,
            pl.BlockSpec((1, width_y, width_z),
                         lambda i: (jnp.minimum(i * KNOT + KNOT, depth_x - 1), 0, 0)),
            pl.BlockSpec(memory_space=pltpu.VMEM),
            pl.BlockSpec(memory_space=pltpu.VMEM),
            pl.BlockSpec((3, KNOT, width_y, width_z), lambda i: (0, i, 0, 0)),
            plane_spec,
            node_spec,
            node_spec,
        ],
        out_specs=[
            plane_spec,
            node_spec,
            node_spec,
            node_spec,
            pl.BlockSpec((1, ROWS, LANES), lambda i: (i, 0, 0)),
        ],
        out_shape=[
            jax.ShapeDtypeStruct(image.shape, jnp.bfloat16),
            block_sum,
            block_sum,
            block_sum,
            jax.ShapeDtypeStruct((nodes, ROWS, LANES), f32),
        ],
        scratch_shapes=[
            pltpu.VMEM((width_y + rows.shape[1], width_z + cols.shape[2]), f32),
            pltpu.VMEM((KNOT + 2, 9, width_y, width_z), f32),
        ],
        compiler_params=pltpu.CompilerParams(
            dimension_semantics=("arbitrary",), vmem_limit_bytes=60 * 1024 * 1024),
    )(deformed, deformed, deformed, rows, cols, displacement, image, contrast_y, bright_y)


def node_sums(field):
    nodes, width_y, width_z = field.shape
    return field.reshape(nodes, width_y // KNOT, KNOT, width_z).sum(axis=2)


def exchange(axis, n, me, d, src, buffer, send_sem, recv_sem):
    target = lax.rem(me + d, n)
    return pltpu.make_async_remote_copy(
        src_ref=src(target), dst_ref=buffer.at[me],
        send_sem=send_sem.at[target], recv_sem=recv_sem.at[me],
        device_id={axis: target}, device_id_type=pl.DeviceIdType.MESH)


def arrival(axis, n, me, d, src_ref, buffer, sem):
    source = lax.rem(me + n - d, n)
    return pltpu.make_async_remote_copy(
        src_ref=src_ref, dst_ref=buffer.at[source],
        send_sem=sem.at[source], recv_sem=sem.at[source],
        device_id={axis: source}, device_id_type=pl.DeviceIdType.MESH)


def both_sums_kernel(nz, ny, plane_row, depth_row, plane_ref, depth_ref, plane_out, depth_out,
                     plane_landed, depth_landed, plane_summed, depth_summed,
                     plane_gathered, depth_gathered, sems):
    mz, my = lax.axis_index("gz"), lax.axis_index("gy")
    barrier = pltpu.get_barrier_semaphore()
    for d in range(1, nz):
        pl.semaphore_signal(barrier, inc=1, device_id={"gz": lax.rem(mz + d, nz)},
                            device_id_type=pl.DeviceIdType.MESH)
    for d in range(1, ny):
        pl.semaphore_signal(barrier, inc=1, device_id={"gy": lax.rem(my + d, ny)},
                            device_id_type=pl.DeviceIdType.MESH)
    pl.semaphore_wait(barrier, nz - 1 + ny - 1)
    zs1, zr1, zs2, zr2, ys1, yr1, ys2, yr2 = sems

    z_out = [exchange("gz", nz, mz, d, lambda t: plane_ref.at[t], plane_landed, zs1, zr1)
             for d in range(1, nz)]
    y_out = [exchange("gy", ny, my, d, lambda t: depth_ref.at[t], depth_landed, ys1, yr1)
             for d in range(1, ny)]
    for copy in z_out + y_out:
        copy.start()
    depth_total = depth_ref[my]
    for d in range(1, ny):
        arrival("gy", ny, my, d, depth_ref.at[0], depth_landed, yr1).wait_recv()
        depth_total = depth_total + depth_landed[lax.rem(my + ny - d, ny)]
    depth_summed[...] = depth_total
    plane_total = plane_ref[mz]
    for d in range(1, nz):
        arrival("gz", nz, mz, d, plane_ref.at[0], plane_landed, zr1).wait_recv()
        plane_total = plane_total + plane_landed[lax.rem(mz + nz - d, nz)]
    rows = lax.broadcasted_iota(jnp.int32, plane_total.shape, 0)
    lanes = lax.broadcasted_iota(jnp.int32, plane_total.shape, 1)
    slot = jnp.logical_and(rows == plane_row, lanes == RANK)
    depth_slot = jnp.logical_and(
        lax.broadcasted_iota(jnp.int32, depth_total.shape, 0) == depth_row,
        lax.broadcasted_iota(jnp.int32, depth_total.shape, 1) == RANK)
    column_energy = jnp.sum(jnp.where(depth_slot, depth_total, 0.0))
    plane_total = jnp.where(slot, column_energy, plane_total)
    plane_summed[...] = plane_total
    for copy in z_out + y_out:
        copy.wait_send()

    z_out = [exchange("gz", nz, mz, d, lambda t: plane_summed, plane_gathered, zs2, zr2)
             for d in range(1, nz)]
    y_out = [exchange("gy", ny, my, d, lambda t: depth_summed, depth_gathered, ys2, yr2)
             for d in range(1, ny)]
    for copy in z_out + y_out:
        copy.start()
    plane_out[mz] = plane_total
    depth_out[my] = depth_total
    for d in range(1, nz):
        arrival("gz", nz, mz, d, plane_summed, plane_gathered, zr2).wait_recv()
        source = lax.rem(mz + nz - d, nz)
        plane_out[source] = plane_gathered[source]
    for d in range(1, ny):
        arrival("gy", ny, my, d, depth_summed, depth_gathered, yr2).wait_recv()
        source = lax.rem(my + ny - d, ny)
        depth_out[source] = depth_gathered[source]
    for copy in z_out + y_out:
        copy.wait_send()


def chunked(main, extras, n):
    rows = -(-main.shape[0] // (n * 128))
    main = jnp.pad(main, (0, n * rows * 128 - main.shape[0])).reshape(n, rows, 128)
    tail = jnp.pad(extras, (0, 128 - extras.shape[0]))
    tail = jnp.broadcast_to(tail, (n, 1, 128))
    spare = -(-(rows + 1) // 8) * 8 - rows - 1
    return jnp.concatenate([main, tail, jnp.zeros((n, spare, 128), main.dtype)], axis=1), rows


def both_sums(plane_parts, depth_parts, plane_row, depth_row):
    nz, ny = plane_parts.shape[0], depth_parts.shape[0]
    f32 = jnp.float32
    dma = pltpu.SemaphoreType.DMA
    return pl.pallas_call(
        functools.partial(both_sums_kernel, nz, ny, plane_row, depth_row),
        out_shape=[jax.ShapeDtypeStruct(plane_parts.shape, f32),
                   jax.ShapeDtypeStruct(depth_parts.shape, f32)],
        in_specs=[pl.BlockSpec(memory_space=pltpu.VMEM)] * 2,
        out_specs=[pl.BlockSpec(memory_space=pltpu.VMEM)] * 2,
        scratch_shapes=[
            pltpu.VMEM(plane_parts.shape, f32),
            pltpu.VMEM(depth_parts.shape, f32),
            pltpu.VMEM(plane_parts.shape[1:], f32),
            pltpu.VMEM(depth_parts.shape[1:], f32),
            pltpu.VMEM(plane_parts.shape, f32),
            pltpu.VMEM(depth_parts.shape, f32),
            [dma((nz,)), dma((nz,)), dma((nz,)), dma((nz,)),
             dma((ny,)), dma((ny,)), dma((ny,)), dma((ny,))],
        ],
        compiler_params=pltpu.CompilerParams(collective_id=1, has_side_effects=True),
    )(plane_parts, depth_parts)


def local(reference_image, deformed, displacement, plane_factors, depth_factors):
    rows, cols = halo_blocks(deformed)
    fields = jnp.einsum("krij,krz->kijz", plane_factors, depth_factors, precision=highest)
    fields = jnp.repeat(fields, KNOT, axis=2)
    residual, prod, mis, sq, energy_parts = strip_sums(
        deformed, rows, cols, displacement, reference_image, fields[0], fields[1])
    prod, mis, sq = node_sums(prod), node_sums(mis), node_sums(sq)
    local_energy = jnp.sum(energy_parts)

    first, second = plane_factors[0], plane_factors[1]
    grad_depth = -jnp.stack([
        jnp.einsum("rij,ijz->rz", first, prod, precision=highest),
        jnp.einsum("rij,ijz->rz", second, mis, precision=highest)])
    first_depth = jnp.einsum("rij,ijz->rz", first * first, sq, precision=highest)
    level_sum = KNOT * KNOT * jnp.sum(second * second, axis=(1, 2))
    grad_plane = -jnp.stack([
        jnp.einsum("rz,ijz->rij", depth_factors[0], prod, precision=highest),
        jnp.einsum("rz,ijz->rij", depth_factors[1], mis, precision=highest)])
    first_diag = jnp.einsum("rz,ijz->rij", depth_factors[0] * depth_factors[0], sq, precision=highest)
    depth_level = KNOT * KNOT * jnp.sum(depth_factors[1] * depth_factors[1], axis=1)

    nz, ny = lax.axis_size("gz"), lax.axis_size("gy")
    plane_terms = jnp.concatenate([grad_plane.reshape(-1), first_diag.reshape(-1)])
    depth_terms = jnp.concatenate([grad_depth.reshape(-1), first_depth.reshape(-1)])
    blank = jnp.zeros((), jnp.float32)
    plane_parts, plane_rows = chunked(plane_terms, jnp.concatenate([depth_level, blank[None]]), nz)
    depth_parts, depth_rows = chunked(depth_terms, jnp.concatenate([level_sum, local_energy[None]]), ny)
    plane_summed, depth_summed = both_sums(plane_parts, depth_parts, plane_rows, depth_rows)
    plane_terms = plane_summed[:, :plane_rows].reshape(-1)
    depth_terms = depth_summed[:, :depth_rows].reshape(-1)
    grad_plane = plane_terms[: grad_plane.size].reshape(grad_plane.shape)
    first_diag = plane_terms[grad_plane.size : grad_plane.size + first_diag.size].reshape(first_diag.shape)
    grad_depth = depth_terms[: grad_depth.size].reshape(grad_depth.shape)
    first_depth = depth_terms[grad_depth.size : grad_depth.size + first_depth.size].reshape(first_depth.shape)
    depth_level = plane_summed[0, plane_rows, :RANK]
    level_sum = depth_summed[0, depth_rows, :RANK]
    energy = jnp.sum(plane_summed[:, plane_rows, RANK])

    nodes_x = plane_factors.shape[2]
    nodes_y = plane_factors.shape[3] * lax.axis_size("gy")
    full_z = depth_factors.shape[2] * lax.axis_size("gz")
    diag_plane = jnp.stack(
        [first_diag, jnp.broadcast_to(depth_level[:, None, None], first_diag.shape)])
    lam_plane = damping * RANK * energy / (nodes_x * nodes_y)
    lam_depth = damping * energy / full_z
    step_plane = -grad_plane / (diag_plane + lam_plane + epsilon)
    diag_depth = jnp.stack([first_depth, jnp.broadcast_to(level_sum[:, None], first_depth.shape)])
    step_depth = -grad_depth / (diag_depth + lam_depth + epsilon)
    return (residual, step_plane, step_depth)


def solution(mesh):
    placed = (
        P(None, "gy", "gz"),
        P(None, "gy", "gz"),
        P(None, None, "gy", "gz"),
        P(None, None, None, "gy"),
        P(None, None, "gz"),
    )
    return jax.shard_map(
        local,
        mesh=mesh,
        in_specs=placed,
        out_specs=(P(None, "gy", "gz"), P(None, None, None, "gy"), P(None, None, "gz")),
        check_vma=False,
    )
```

```python
import functools

import jax
import jax.numpy as jnp
from jax import lax
from jax.experimental import pallas as pl
from jax.experimental.pallas import tpu as pltpu
from jax.sharding import PartitionSpec as P

RANK = 32
KNOT = 8

epsilon = 1e-06
damping = 0.01
highest = lax.Precision.HIGHEST

ROWS = 16
LANES = 256


def neighbours(part, axis, forward):
    count = lax.axis_size(axis)
    if forward:
        pairs = [(i, i + 1) for i in range(count - 1)]
    else:
        pairs = [(i + 1, i) for i in range(count - 1)]
    return lax.ppermute(part, axis, pairs)


def halo_kernel(ny, nz, rows_ref, cols_ref, rows_out, cols_out, rows_got, cols_got,
                send_sems, recv_sems):
    my, mz = lax.axis_index("gy"), lax.axis_index("gz")
    up, down = lax.rem(my + 1, ny), lax.rem(my + ny - 1, ny)
    right, left = lax.rem(mz + 1, nz), lax.rem(mz + nz - 1, nz)
    plan = [
        (rows_ref.at[0], rows_got.at[0], (down, mz)),
        (rows_ref.at[1], rows_got.at[1], (up, mz)),
        (cols_ref.at[0], cols_got.at[0], (my, left)),
        (cols_ref.at[1], cols_got.at[1], (my, right)),
        (cols_ref.at[0], cols_got.at[2], (down, left)),
        (cols_ref.at[0], cols_got.at[3], (up, left)),
        (cols_ref.at[1], cols_got.at[4], (down, right)),
        (cols_ref.at[1], cols_got.at[5], (up, right)),
    ]
    barrier = pltpu.get_barrier_semaphore()
    for _, _, device in plan:
        pl.semaphore_signal(barrier, inc=1, device_id=device,
                            device_id_type=pl.DeviceIdType.MESH)
    pl.semaphore_wait(barrier, len(plan))
    copies = []
    for k, (source, slot, device) in enumerate(plan):
        copy = pltpu.make_async_remote_copy(
            src_ref=source, dst_ref=slot, send_sem=send_sems.at[k], recv_sem=recv_sems.at[k],
            device_id=device, device_id_type=pl.DeviceIdType.MESH)
        copy.start()
        copies.append(copy)
    for copy in copies:
        copy.wait()
    rows_out[...] = rows_got[...]
    cols_out[...] = cols_got[...]


def swap_halos(rows_send, cols_send):
    ny, nz = lax.axis_size("gy"), lax.axis_size("gz")
    dma = pltpu.SemaphoreType.DMA
    rows_shape = rows_send.shape
    cols_shape = (6,) + cols_send.shape[1:]
    return pl.pallas_call(
        functools.partial(halo_kernel, ny, nz),
        out_shape=[jax.ShapeDtypeStruct(rows_shape, rows_send.dtype),
                   jax.ShapeDtypeStruct(cols_shape, cols_send.dtype)],
        in_specs=[pl.BlockSpec(memory_space=pltpu.VMEM)] * 2,
        out_specs=[pl.BlockSpec(memory_space=pltpu.VMEM)] * 2,
        scratch_shapes=[
            pltpu.VMEM(rows_shape, rows_send.dtype),
            pltpu.VMEM(cols_shape, cols_send.dtype),
            dma((8,)),
            dma((8,)),
        ],
        compiler_params=pltpu.CompilerParams(collective_id=2, has_side_effects=True),
    )(rows_send, cols_send)


def halo_blocks(deformed):
    depth_x, width_y, width_z = deformed.shape
    f32 = jnp.float32
    ny, nz = lax.axis_size("gy"), lax.axis_size("gz")
    my, mz = lax.axis_index("gy"), lax.axis_index("gz")
    rows_send = jnp.stack([deformed[:, 0, :], deformed[:, width_y - 1, :]])
    cols_send = jnp.stack([deformed[:, :, 0], deformed[:, :, width_z - 1]])
    rows_got, cols_got = swap_halos(rows_send, cols_send)
    held = deformed.dtype
    has_up = (my < ny - 1).astype(held)
    has_down = (my > 0).astype(held)
    has_right = (mz < nz - 1).astype(held)
    has_left = (mz > 0).astype(held)
    high_y = rows_got[0] * has_up
    low_y = rows_got[1] * has_down
    high_z = cols_got[0] * has_right
    low_z = cols_got[1] * has_left
    high_high = cols_got[2][:, 0] * (has_up * has_right)
    low_high = cols_got[3][:, width_y - 1] * (has_down * has_right)
    high_low = cols_got[4][:, 0] * (has_up * has_left)
    low_low = cols_got[5][:, width_y - 1] * (has_down * has_left)
    gap_y = jnp.zeros((depth_x, 6, width_z), held)
    rows = jnp.concatenate([high_y[:, None], gap_y, low_y[:, None]], axis=1)
    gap = jnp.zeros((depth_x, 6), held)
    side_high = jnp.concatenate([high_z, high_high[:, None], gap, low_high[:, None]], axis=1)
    side_low = jnp.concatenate([low_z, high_low[:, None], gap, low_low[:, None]], axis=1)
    lanes = lax.broadcasted_iota(jnp.int32, (1, 1, 128), 2)
    cols = jnp.where(lanes == 0, side_high[:, :, None],
                     jnp.where(lanes == 127, side_low[:, :, None], jnp.zeros((), held)))
    return rows, cols


def lerp(base, other, weight):
    return base + weight * (other - base)


def strip_kernel(prev_ref, main_ref, next_ref, rows_ref, cols_ref, disp_ref, image_ref,
                 contrast_ref, bright_ref,
                 res_ref, prod_ref, mis_ref, sq_ref, energy_ref, pad_ref, shifts_ref):
    block = pl.program_id(0)
    depth_x = rows_ref.shape[0]
    width_y, width_z = image_ref.shape[1], image_ref.shape[2]
    pad_y, pad_z = pad_ref.shape

    def source_plane(p, plane):
        plane_x = block * KNOT - 1 + p
        valid = jnp.logical_and(plane_x >= 0, plane_x < depth_x)
        safe = jnp.clip(plane_x, 0, depth_x - 1)
        pad_ref[:width_y, :width_z] = plane.astype(jnp.float32)
        pad_ref[width_y:, :width_z] = rows_ref[safe].astype(jnp.float32)
        pad_ref[:, width_z:] = cols_ref[safe].astype(jnp.float32)
        whole = jnp.where(valid, pad_ref[...], 0.0)
        by_y = (pltpu.roll(whole, 1, 0), whole, pltpu.roll(whole, pad_y - 1, 0))
        for b in range(3):
            part = by_y[b][:width_y]
            by_z = (pltpu.roll(part, 1, 1), part, pltpu.roll(part, pad_z - 1, 1))
            for c in range(3):
                shifts_ref[p, 3 * b + c] = by_z[c][:, :width_z]

    source_plane(0, prev_ref[0])

    def inner_plane(p, carry):
        source_plane(p, main_ref[p - 1])
        return carry

    lax.fori_loop(1, KNOT + 1, inner_plane, 0, unroll=2)
    source_plane(KNOT + 1, next_ref[0])

    chunks_y = width_y // ROWS
    chunks_z = width_z // LANES

    def chunk(ky, kz, energy):
        r0 = ky * ROWS
        c0 = pl.multiple_of(kz * LANES, LANES)
        rs = pl.ds(r0, ROWS)
        cs = pl.ds(c0, LANES)
        contrast = contrast_ref[0, rs, cs]
        bright = bright_ref[0, rs, cs]

        def plane(xl, acc):
            prod_acc, mis_acc, sq_acc, e_acc = acc

            def src(a, b, c):
                return shifts_ref[xl + 1 + a, 3 * (b + 1) + (c + 1), rs, cs]

            sx = disp_ref[0, xl, rs, cs].astype(jnp.float32)
            sy = disp_ref[1, xl, rs, cs].astype(jnp.float32)
            sz = disp_ref[2, xl, rs, cs].astype(jnp.float32)
            gx, gy, gz = sx > 0, sy > 0, sz > 0
            ax, ay, az = jnp.abs(sx), jnp.abs(sy), jnp.abs(sz)
            xs = {}
            for b in (-1, 0, 1):
                for c in (-1, 0, 1):
                    xs[b, c] = jnp.where(gx, src(1, b, c), src(-1, b, c))
            y0 = {c: jnp.where(gy, src(0, 1, c), src(0, -1, c)) for c in (-1, 0, 1)}
            y1 = {c: jnp.where(gy, xs[1, c], xs[-1, c]) for c in (-1, 0, 1)}
            centre = src(0, 0, 0)
            z00 = jnp.where(gz, src(0, 0, 1), src(0, 0, -1))
            z01 = jnp.where(gz, y0[1], y0[-1])
            z10 = jnp.where(gz, xs[0, 1], xs[0, -1])
            z11 = jnp.where(gz, y1[1], y1[-1])
            l00 = lerp(centre, z00, az)
            l01 = lerp(y0[0], z01, az)
            l10 = lerp(xs[0, 0], z10, az)
            l11 = lerp(y1[0], z11, az)
            m0 = lerp(l00, l01, ay)
            m1 = lerp(l10, l11, ay)
            warped = lerp(m0, m1, ax)
            values = image_ref[xl, rs, cs].astype(jnp.float32)
            misfit = warped - contrast * values - bright
            res_ref[xl, rs, cs] = misfit.astype(res_ref.dtype)
            return (prod_acc + misfit * values, mis_acc + misfit,
                    sq_acc + values * values, e_acc + misfit * misfit)

        zero = jnp.zeros((ROWS, LANES), jnp.float32)
        prod_acc, mis_acc, sq_acc, e_acc = lax.fori_loop(
            0, KNOT, plane, (zero, zero, zero, energy), unroll=4)
        for out_ref, acc in ((prod_ref, prod_acc), (mis_ref, mis_acc), (sq_ref, sq_acc)):
            for n in range(ROWS // KNOT):
                out_ref[0, pl.ds(r0 // KNOT + n, 1), cs] = jnp.sum(
                    acc[n * KNOT : (n + 1) * KNOT], axis=0, keepdims=True)
        return e_acc

    energy = jnp.zeros((ROWS, LANES), jnp.float32)
    for ky in range(chunks_y):
        energy = lax.fori_loop(0, chunks_z, functools.partial(chunk, ky), energy)
    energy_ref[0] = energy


def strip_sums(deformed, rows, cols, displacement, image, contrast_y, bright_y):
    depth_x, width_y, width_z = image.shape
    nodes = depth_x // KNOT
    f32 = jnp.float32
    block_sum = jax.ShapeDtypeStruct((nodes, width_y // KNOT, width_z), f32)
    node_spec = pl.BlockSpec((1, width_y // KNOT, width_z), lambda i: (i, 0, 0))
    field_spec = pl.BlockSpec((1, width_y, width_z), lambda i: (i, 0, 0))
    plane_spec = pl.BlockSpec((KNOT, width_y, width_z), lambda i: (i, 0, 0))
    return pl.pallas_call(
        strip_kernel,
        grid=(nodes,),
        in_specs=[
            pl.BlockSpec((1, width_y, width_z), lambda i: (jnp.maximum(i * KNOT - 1, 0), 0, 0)),
            plane_spec,
            pl.BlockSpec((1, width_y, width_z),
                         lambda i: (jnp.minimum(i * KNOT + KNOT, depth_x - 1), 0, 0)),
            pl.BlockSpec(memory_space=pltpu.VMEM),
            pl.BlockSpec(memory_space=pltpu.VMEM),
            pl.BlockSpec((3, KNOT, width_y, width_z), lambda i: (0, i, 0, 0)),
            plane_spec,
            field_spec,
            field_spec,
        ],
        out_specs=[
            plane_spec,
            node_spec,
            node_spec,
            node_spec,
            pl.BlockSpec((1, ROWS, LANES), lambda i: (i, 0, 0)),
        ],
        out_shape=[
            jax.ShapeDtypeStruct(image.shape, jnp.bfloat16),
            block_sum,
            block_sum,
            block_sum,
            jax.ShapeDtypeStruct((nodes, ROWS, LANES), f32),
        ],
        scratch_shapes=[
            pltpu.VMEM((width_y + rows.shape[1], width_z + cols.shape[2]), f32),
            pltpu.VMEM((KNOT + 2, 9, width_y, width_z), f32),
        ],
        compiler_params=pltpu.CompilerParams(
            dimension_semantics=("arbitrary",), vmem_limit_bytes=60 * 1024 * 1024),
    )(deformed, deformed, deformed, rows, cols, displacement, image, contrast_y, bright_y)


def node_sums(field):
    return field


def exchange(axis, n, me, d, src, buffer, send_sem, recv_sem):
    target = lax.rem(me + d, n)
    return pltpu.make_async_remote_copy(
        src_ref=src(target), dst_ref=buffer.at[me],
        send_sem=send_sem.at[target], recv_sem=recv_sem.at[me],
        device_id={axis: target}, device_id_type=pl.DeviceIdType.MESH)


def arrival(axis, n, me, d, src_ref, buffer, sem):
    source = lax.rem(me + n - d, n)
    return pltpu.make_async_remote_copy(
        src_ref=src_ref, dst_ref=buffer.at[source],
        send_sem=sem.at[source], recv_sem=sem.at[source],
        device_id={axis: source}, device_id_type=pl.DeviceIdType.MESH)


def both_sums_kernel(nz, ny, plane_row, depth_row, plane_ref, depth_ref, plane_out, depth_out,
                     plane_landed, depth_landed, plane_summed, depth_summed,
                     plane_gathered, depth_gathered, sems):
    mz, my = lax.axis_index("gz"), lax.axis_index("gy")
    barrier = pltpu.get_barrier_semaphore()
    for d in range(1, nz):
        pl.semaphore_signal(barrier, inc=1, device_id={"gz": lax.rem(mz + d, nz)},
                            device_id_type=pl.DeviceIdType.MESH)
    for d in range(1, ny):
        pl.semaphore_signal(barrier, inc=1, device_id={"gy": lax.rem(my + d, ny)},
                            device_id_type=pl.DeviceIdType.MESH)
    pl.semaphore_wait(barrier, nz - 1 + ny - 1)
    zs1, zr1, zs2, zr2, ys1, yr1, ys2, yr2 = sems

    z_out = [exchange("gz", nz, mz, d, lambda t: plane_ref.at[t], plane_landed, zs1, zr1)
             for d in range(1, nz)]
    y_out = [exchange("gy", ny, my, d, lambda t: depth_ref.at[t], depth_landed, ys1, yr1)
             for d in range(1, ny)]
    for copy in z_out + y_out:
        copy.start()
    depth_total = depth_ref[my]
    for d in range(1, ny):
        arrival("gy", ny, my, d, depth_ref.at[0], depth_landed, yr1).wait_recv()
        depth_total = depth_total + depth_landed[lax.rem(my + ny - d, ny)]
    depth_summed[...] = depth_total
    plane_total = plane_ref[mz]
    for d in range(1, nz):
        arrival("gz", nz, mz, d, plane_ref.at[0], plane_landed, zr1).wait_recv()
        plane_total = plane_total + plane_landed[lax.rem(mz + nz - d, nz)]
    rows = lax.broadcasted_iota(jnp.int32, plane_total.shape, 0)
    lanes = lax.broadcasted_iota(jnp.int32, plane_total.shape, 1)
    slot = jnp.logical_and(rows == plane_row, lanes == RANK)
    depth_slot = jnp.logical_and(
        lax.broadcasted_iota(jnp.int32, depth_total.shape, 0) == depth_row,
        lax.broadcasted_iota(jnp.int32, depth_total.shape, 1) == RANK)
    column_energy = jnp.sum(jnp.where(depth_slot, depth_total, 0.0))
    plane_total = jnp.where(slot, column_energy, plane_total)
    plane_summed[...] = plane_total
    for copy in z_out + y_out:
        copy.wait_send()

    z_out = [exchange("gz", nz, mz, d, lambda t: plane_summed, plane_gathered, zs2, zr2)
             for d in range(1, nz)]
    y_out = [exchange("gy", ny, my, d, lambda t: depth_summed, depth_gathered, ys2, yr2)
             for d in range(1, ny)]
    for copy in z_out + y_out:
        copy.start()
    plane_out[mz] = plane_total
    depth_out[my] = depth_total
    for d in range(1, nz):
        arrival("gz", nz, mz, d, plane_summed, plane_gathered, zr2).wait_recv()
        source = lax.rem(mz + nz - d, nz)
        plane_out[source] = plane_gathered[source]
    for d in range(1, ny):
        arrival("gy", ny, my, d, depth_summed, depth_gathered, yr2).wait_recv()
        source = lax.rem(my + ny - d, ny)
        depth_out[source] = depth_gathered[source]
    for copy in z_out + y_out:
        copy.wait_send()


def chunked(main, extras, n):
    rows = -(-main.shape[0] // (n * 128))
    main = jnp.pad(main, (0, n * rows * 128 - main.shape[0])).reshape(n, rows, 128)
    tail = jnp.pad(extras, (0, 128 - extras.shape[0]))
    tail = jnp.broadcast_to(tail, (n, 1, 128))
    spare = -(-(rows + 1) // 8) * 8 - rows - 1
    return jnp.concatenate([main, tail, jnp.zeros((n, spare, 128), main.dtype)], axis=1), rows


def both_sums(plane_parts, depth_parts, plane_row, depth_row):
    nz, ny = plane_parts.shape[0], depth_parts.shape[0]
    f32 = jnp.float32
    dma = pltpu.SemaphoreType.DMA
    return pl.pallas_call(
        functools.partial(both_sums_kernel, nz, ny, plane_row, depth_row),
        out_shape=[jax.ShapeDtypeStruct(plane_parts.shape, f32),
                   jax.ShapeDtypeStruct(depth_parts.shape, f32)],
        in_specs=[pl.BlockSpec(memory_space=pltpu.VMEM)] * 2,
        out_specs=[pl.BlockSpec(memory_space=pltpu.VMEM)] * 2,
        scratch_shapes=[
            pltpu.VMEM(plane_parts.shape, f32),
            pltpu.VMEM(depth_parts.shape, f32),
            pltpu.VMEM(plane_parts.shape[1:], f32),
            pltpu.VMEM(depth_parts.shape[1:], f32),
            pltpu.VMEM(plane_parts.shape, f32),
            pltpu.VMEM(depth_parts.shape, f32),
            [dma((nz,)), dma((nz,)), dma((nz,)), dma((nz,)),
             dma((ny,)), dma((ny,)), dma((ny,)), dma((ny,))],
        ],
        compiler_params=pltpu.CompilerParams(collective_id=1, has_side_effects=True),
    )(plane_parts, depth_parts)


def local(reference_image, deformed, displacement, plane_factors, depth_factors):
    rows, cols = halo_blocks(deformed)
    fields = jnp.einsum("krij,krz->kijz", plane_factors, depth_factors, precision=highest)
    fields = jnp.repeat(fields, KNOT, axis=2)
    residual, prod, mis, sq, energy_parts = strip_sums(
        deformed, rows, cols, displacement, reference_image, fields[0], fields[1])
    prod, mis, sq = node_sums(prod), node_sums(mis), node_sums(sq)
    local_energy = jnp.sum(energy_parts)

    first, second = plane_factors[0], plane_factors[1]
    grad_depth = -jnp.stack([
        jnp.einsum("rij,ijz->rz", first, prod, precision=highest),
        jnp.einsum("rij,ijz->rz", second, mis, precision=highest)])
    first_depth = jnp.einsum("rij,ijz->rz", first * first, sq, precision=highest)
    level_sum = KNOT * KNOT * jnp.sum(second * second, axis=(1, 2))
    grad_plane = -jnp.stack([
        jnp.einsum("rz,ijz->rij", depth_factors[0], prod, precision=highest),
        jnp.einsum("rz,ijz->rij", depth_factors[1], mis, precision=highest)])
    first_diag = jnp.einsum("rz,ijz->rij", depth_factors[0] * depth_factors[0], sq, precision=highest)
    depth_level = KNOT * KNOT * jnp.sum(depth_factors[1] * depth_factors[1], axis=1)

    nz, ny = lax.axis_size("gz"), lax.axis_size("gy")
    plane_terms = jnp.concatenate([grad_plane.reshape(-1), first_diag.reshape(-1)])
    depth_terms = jnp.concatenate([grad_depth.reshape(-1), first_depth.reshape(-1)])
    blank = jnp.zeros((), jnp.float32)
    plane_parts, plane_rows = chunked(plane_terms, jnp.concatenate([depth_level, blank[None]]), nz)
    depth_parts, depth_rows = chunked(depth_terms, jnp.concatenate([level_sum, local_energy[None]]), ny)
    plane_summed, depth_summed = both_sums(plane_parts, depth_parts, plane_rows, depth_rows)
    plane_terms = plane_summed[:, :plane_rows].reshape(-1)
    depth_terms = depth_summed[:, :depth_rows].reshape(-1)
    grad_plane = plane_terms[: grad_plane.size].reshape(grad_plane.shape)
    first_diag = plane_terms[grad_plane.size : grad_plane.size + first_diag.size].reshape(first_diag.shape)
    grad_depth = depth_terms[: grad_depth.size].reshape(grad_depth.shape)
    first_depth = depth_terms[grad_depth.size : grad_depth.size + first_depth.size].reshape(first_depth.shape)
    depth_level = plane_summed[0, plane_rows, :RANK]
    level_sum = depth_summed[0, depth_rows, :RANK]
    energy = jnp.sum(plane_summed[:, plane_rows, RANK])

    nodes_x = plane_factors.shape[2]
    nodes_y = plane_factors.shape[3] * lax.axis_size("gy")
    full_z = depth_factors.shape[2] * lax.axis_size("gz")
    diag_plane = jnp.stack(
        [first_diag, jnp.broadcast_to(depth_level[:, None, None], first_diag.shape)])
    lam_plane = damping * RANK * energy / (nodes_x * nodes_y)
    lam_depth = damping * energy / full_z
    step_plane = -grad_plane / (diag_plane + lam_plane + epsilon)
    diag_depth = jnp.stack([first_depth, jnp.broadcast_to(level_sum[:, None], first_depth.shape)])
    step_depth = -grad_depth / (diag_depth + lam_depth + epsilon)
    return (residual, step_plane, step_depth)


def solution(mesh):
    placed = (
        P(None, "gy", "gz"),
        P(None, "gy", "gz"),
        P(None, None, "gy", "gz"),
        P(None, None, None, "gy"),
        P(None, None, "gz"),
    )
    return jax.shard_map(
        local,
        mesh=mesh,
        in_specs=placed,
        out_specs=(P(None, "gy", "gz"), P(None, None, None, "gy"), P(None, None, "gz")),
        check_vma=False,
    )
```

```python
import functools

import jax
import jax.numpy as jnp
from jax import lax
from jax.experimental import pallas as pl
from jax.experimental.pallas import tpu as pltpu
from jax.sharding import PartitionSpec as P

RANK = 32
KNOT = 8

epsilon = 1e-06
damping = 0.01
highest = lax.Precision.HIGHEST

ROWS = 16
LANES = 256
SPAN = 16


def neighbours(part, axis, forward):
    count = lax.axis_size(axis)
    if forward:
        pairs = [(i, i + 1) for i in range(count - 1)]
    else:
        pairs = [(i + 1, i) for i in range(count - 1)]
    return lax.ppermute(part, axis, pairs)


def halo_kernel(ny, nz, rows_ref, cols_ref, rows_out, cols_out, rows_got, cols_got,
                send_sems, recv_sems):
    my, mz = lax.axis_index("gy"), lax.axis_index("gz")
    up, down = lax.rem(my + 1, ny), lax.rem(my + ny - 1, ny)
    right, left = lax.rem(mz + 1, nz), lax.rem(mz + nz - 1, nz)
    plan = [
        (rows_ref.at[0], rows_got.at[0], (down, mz)),
        (rows_ref.at[1], rows_got.at[1], (up, mz)),
        (cols_ref.at[0], cols_got.at[0], (my, left)),
        (cols_ref.at[1], cols_got.at[1], (my, right)),
        (cols_ref.at[0], cols_got.at[2], (down, left)),
        (cols_ref.at[0], cols_got.at[3], (up, left)),
        (cols_ref.at[1], cols_got.at[4], (down, right)),
        (cols_ref.at[1], cols_got.at[5], (up, right)),
    ]
    barrier = pltpu.get_barrier_semaphore()
    for _, _, device in plan:
        pl.semaphore_signal(barrier, inc=1, device_id=device,
                            device_id_type=pl.DeviceIdType.MESH)
    pl.semaphore_wait(barrier, len(plan))
    copies = []
    for k, (source, slot, device) in enumerate(plan):
        copy = pltpu.make_async_remote_copy(
            src_ref=source, dst_ref=slot, send_sem=send_sems.at[k], recv_sem=recv_sems.at[k],
            device_id=device, device_id_type=pl.DeviceIdType.MESH)
        copy.start()
        copies.append(copy)
    for copy in copies:
        copy.wait()
    rows_out[...] = rows_got[...]
    cols_out[...] = cols_got[...]


def swap_halos(rows_send, cols_send):
    ny, nz = lax.axis_size("gy"), lax.axis_size("gz")
    dma = pltpu.SemaphoreType.DMA
    rows_shape = rows_send.shape
    cols_shape = (6,) + cols_send.shape[1:]
    return pl.pallas_call(
        functools.partial(halo_kernel, ny, nz),
        out_shape=[jax.ShapeDtypeStruct(rows_shape, rows_send.dtype),
                   jax.ShapeDtypeStruct(cols_shape, cols_send.dtype)],
        in_specs=[pl.BlockSpec(memory_space=pltpu.VMEM)] * 2,
        out_specs=[pl.BlockSpec(memory_space=pltpu.VMEM)] * 2,
        scratch_shapes=[
            pltpu.VMEM(rows_shape, rows_send.dtype),
            pltpu.VMEM(cols_shape, cols_send.dtype),
            dma((8,)),
            dma((8,)),
        ],
        compiler_params=pltpu.CompilerParams(collective_id=2, has_side_effects=True),
    )(rows_send, cols_send)


def halo_blocks(deformed):
    depth_x, width_y, width_z = deformed.shape
    f32 = jnp.float32
    ny, nz = lax.axis_size("gy"), lax.axis_size("gz")
    my, mz = lax.axis_index("gy"), lax.axis_index("gz")
    rows_send = jnp.stack([deformed[:, 0, :], deformed[:, width_y - 1, :]])
    cols_send = jnp.stack([deformed[:, :, 0], deformed[:, :, width_z - 1]])
    rows_got, cols_got = swap_halos(rows_send, cols_send)
    held = deformed.dtype
    has_up = (my < ny - 1).astype(held)
    has_down = (my > 0).astype(held)
    has_right = (mz < nz - 1).astype(held)
    has_left = (mz > 0).astype(held)
    high_y = rows_got[0] * has_up
    low_y = rows_got[1] * has_down
    high_z = cols_got[0] * has_right
    low_z = cols_got[1] * has_left
    high_high = cols_got[2][:, 0] * (has_up * has_right)
    low_high = cols_got[3][:, width_y - 1] * (has_down * has_right)
    high_low = cols_got[4][:, 0] * (has_up * has_left)
    low_low = cols_got[5][:, width_y - 1] * (has_down * has_left)
    gap_y = jnp.zeros((depth_x, 6, width_z), held)
    rows = jnp.concatenate([high_y[:, None], gap_y, low_y[:, None]], axis=1)
    gap = jnp.zeros((depth_x, 6), held)
    side_high = jnp.concatenate([high_z, high_high[:, None], gap, low_high[:, None]], axis=1)
    side_low = jnp.concatenate([low_z, high_low[:, None], gap, low_low[:, None]], axis=1)
    lanes = lax.broadcasted_iota(jnp.int32, (1, 1, 128), 2)
    cols = jnp.where(lanes == 0, side_high[:, :, None],
                     jnp.where(lanes == 127, side_low[:, :, None], jnp.zeros((), held)))
    return rows, cols


def lerp(base, other, weight):
    return base + weight * (other - base)


def strip_kernel(prev_ref, main_ref, next_ref, rows_ref, cols_ref, disp_ref, image_ref,
                 contrast_ref, bright_ref,
                 res_ref, prod_ref, mis_ref, sq_ref, energy_ref, pad_ref, shifts_ref):
    block = pl.program_id(0)
    depth_x = rows_ref.shape[0]
    width_y, width_z = image_ref.shape[1], image_ref.shape[2]
    pad_y, pad_z = pad_ref.shape

    def source_plane(p, plane):
        plane_x = block * SPAN - 1 + p
        valid = jnp.logical_and(plane_x >= 0, plane_x < depth_x)
        safe = jnp.clip(plane_x, 0, depth_x - 1)
        pad_ref[:width_y, :width_z] = plane.astype(jnp.float32)
        pad_ref[width_y:, :width_z] = rows_ref[safe].astype(jnp.float32)
        pad_ref[:, width_z:] = cols_ref[safe].astype(jnp.float32)
        whole = jnp.where(valid, pad_ref[...], 0.0)
        by_y = (pltpu.roll(whole, 1, 0), whole, pltpu.roll(whole, pad_y - 1, 0))
        for b in range(3):
            part = by_y[b][:width_y]
            by_z = (pltpu.roll(part, 1, 1), part, pltpu.roll(part, pad_z - 1, 1))
            for c in range(3):
                shifts_ref[p, 3 * b + c] = by_z[c][:, :width_z]

    source_plane(0, prev_ref[0])

    def inner_plane(p, carry):
        source_plane(p, main_ref[p - 1])
        return carry

    lax.fori_loop(1, SPAN + 1, inner_plane, 0, unroll=2)
    source_plane(SPAN + 1, next_ref[0])

    chunks_y = width_y // ROWS
    chunks_z = width_z // LANES

    def chunk(n, k, energy):
        r0 = pl.multiple_of((k // chunks_z) * ROWS, ROWS)
        c0 = pl.multiple_of((k % chunks_z) * LANES, LANES)
        rs = pl.ds(r0, ROWS)
        cs = pl.ds(c0, LANES)
        contrast = contrast_ref[n, rs, cs]
        bright = bright_ref[n, rs, cs]

        def plane(step, acc):
            xl = n * KNOT + step
            prod_acc, mis_acc, sq_acc, e_acc = acc

            def src(a, b, c):
                return shifts_ref[xl + 1 + a, 3 * (b + 1) + (c + 1), rs, cs]

            sx = disp_ref[0, xl, rs, cs].astype(jnp.float32)
            sy = disp_ref[1, xl, rs, cs].astype(jnp.float32)
            sz = disp_ref[2, xl, rs, cs].astype(jnp.float32)
            gx, gy, gz = sx > 0, sy > 0, sz > 0
            ax, ay, az = jnp.abs(sx), jnp.abs(sy), jnp.abs(sz)
            xs = {}
            for b in (-1, 0, 1):
                for c in (-1, 0, 1):
                    xs[b, c] = jnp.where(gx, src(1, b, c), src(-1, b, c))
            y0 = {c: jnp.where(gy, src(0, 1, c), src(0, -1, c)) for c in (-1, 0, 1)}
            y1 = {c: jnp.where(gy, xs[1, c], xs[-1, c]) for c in (-1, 0, 1)}
            centre = src(0, 0, 0)
            z00 = jnp.where(gz, src(0, 0, 1), src(0, 0, -1))
            z01 = jnp.where(gz, y0[1], y0[-1])
            z10 = jnp.where(gz, xs[0, 1], xs[0, -1])
            z11 = jnp.where(gz, y1[1], y1[-1])
            l00 = lerp(centre, z00, az)
            l01 = lerp(y0[0], z01, az)
            l10 = lerp(xs[0, 0], z10, az)
            l11 = lerp(y1[0], z11, az)
            m0 = lerp(l00, l01, ay)
            m1 = lerp(l10, l11, ay)
            warped = lerp(m0, m1, ax)
            values = image_ref[xl, rs, cs].astype(jnp.float32)
            misfit = warped - contrast * values - bright
            res_ref[xl, rs, cs] = misfit.astype(res_ref.dtype)
            return (prod_acc + misfit * values, mis_acc + misfit,
                    sq_acc + values * values, e_acc + misfit * misfit)

        zero = jnp.zeros((ROWS, LANES), jnp.float32)
        prod_acc, mis_acc, sq_acc, e_acc = lax.fori_loop(
            0, KNOT, plane, (zero, zero, zero, energy), unroll=4)
        prod_ref[n, rs, cs] = prod_acc
        mis_ref[n, rs, cs] = mis_acc
        sq_ref[n, rs, cs] = sq_acc
        return e_acc

    energy = jnp.zeros((ROWS, LANES), jnp.float32)
    for n in range(SPAN // KNOT):
        energy = lax.fori_loop(0, chunks_y * chunks_z, functools.partial(chunk, n), energy)
    energy_ref[0] = energy


def strip_sums(deformed, rows, cols, displacement, image, contrast_y, bright_y):
    depth_x, width_y, width_z = image.shape
    nodes = depth_x // KNOT
    steps = depth_x // SPAN
    per = SPAN // KNOT
    f32 = jnp.float32
    block_sum = jax.ShapeDtypeStruct((nodes, width_y, width_z), f32)
    node_spec = pl.BlockSpec((per, width_y, width_z), lambda i: (i, 0, 0))
    plane_spec = pl.BlockSpec((SPAN, width_y, width_z), lambda i: (i, 0, 0))
    return pl.pallas_call(
        strip_kernel,
        grid=(steps,),
        in_specs=[
            pl.BlockSpec((1, width_y, width_z), lambda i: (jnp.maximum(i * SPAN - 1, 0), 0, 0)),
            plane_spec,
            pl.BlockSpec((1, width_y, width_z),
                         lambda i: (jnp.minimum(i * SPAN + SPAN, depth_x - 1), 0, 0)),
            pl.BlockSpec(memory_space=pltpu.VMEM),
            pl.BlockSpec(memory_space=pltpu.VMEM),
            pl.BlockSpec((3, SPAN, width_y, width_z), lambda i: (0, i, 0, 0)),
            plane_spec,
            node_spec,
            node_spec,
        ],
        out_specs=[
            plane_spec,
            node_spec,
            node_spec,
            node_spec,
            pl.BlockSpec((1, ROWS, LANES), lambda i: (i, 0, 0)),
        ],
        out_shape=[
            jax.ShapeDtypeStruct(image.shape, jnp.bfloat16),
            block_sum,
            block_sum,
            block_sum,
            jax.ShapeDtypeStruct((steps, ROWS, LANES), f32),
        ],
        scratch_shapes=[
            pltpu.VMEM((width_y + rows.shape[1], width_z + cols.shape[2]), f32),
            pltpu.VMEM((SPAN + 2, 9, width_y, width_z), f32),
        ],
        compiler_params=pltpu.CompilerParams(
            dimension_semantics=("arbitrary",), vmem_limit_bytes=60 * 1024 * 1024),
    )(deformed, deformed, deformed, rows, cols, displacement, image, contrast_y, bright_y)


def node_sums(field):
    nodes, width_y, width_z = field.shape
    return field.reshape(nodes, width_y // KNOT, KNOT, width_z).sum(axis=2)


def exchange(axis, n, me, d, src, buffer, send_sem, recv_sem):
    target = lax.rem(me + d, n)
    return pltpu.make_async_remote_copy(
        src_ref=src(target), dst_ref=buffer.at[me],
        send_sem=send_sem.at[target], recv_sem=recv_sem.at[me],
        device_id={axis: target}, device_id_type=pl.DeviceIdType.MESH)


def arrival(axis, n, me, d, src_ref, buffer, sem):
    source = lax.rem(me + n - d, n)
    return pltpu.make_async_remote_copy(
        src_ref=src_ref, dst_ref=buffer.at[source],
        send_sem=sem.at[source], recv_sem=sem.at[source],
        device_id={axis: source}, device_id_type=pl.DeviceIdType.MESH)


def both_sums_kernel(nz, ny, plane_row, depth_row, plane_ref, depth_ref, plane_out, depth_out,
                     plane_landed, depth_landed, plane_summed, depth_summed,
                     plane_gathered, depth_gathered, sems):
    mz, my = lax.axis_index("gz"), lax.axis_index("gy")
    barrier = pltpu.get_barrier_semaphore()
    for d in range(1, nz):
        pl.semaphore_signal(barrier, inc=1, device_id={"gz": lax.rem(mz + d, nz)},
                            device_id_type=pl.DeviceIdType.MESH)
    for d in range(1, ny):
        pl.semaphore_signal(barrier, inc=1, device_id={"gy": lax.rem(my + d, ny)},
                            device_id_type=pl.DeviceIdType.MESH)
    pl.semaphore_wait(barrier, nz - 1 + ny - 1)
    zs1, zr1, zs2, zr2, ys1, yr1, ys2, yr2 = sems

    z_out = [exchange("gz", nz, mz, d, lambda t: plane_ref.at[t], plane_landed, zs1, zr1)
             for d in range(1, nz)]
    y_out = [exchange("gy", ny, my, d, lambda t: depth_ref.at[t], depth_landed, ys1, yr1)
             for d in range(1, ny)]
    for copy in z_out + y_out:
        copy.start()
    depth_total = depth_ref[my]
    for d in range(1, ny):
        arrival("gy", ny, my, d, depth_ref.at[0], depth_landed, yr1).wait_recv()
        depth_total = depth_total + depth_landed[lax.rem(my + ny - d, ny)]
    depth_summed[...] = depth_total
    plane_total = plane_ref[mz]
    for d in range(1, nz):
        arrival("gz", nz, mz, d, plane_ref.at[0], plane_landed, zr1).wait_recv()
        plane_total = plane_total + plane_landed[lax.rem(mz + nz - d, nz)]
    rows = lax.broadcasted_iota(jnp.int32, plane_total.shape, 0)
    lanes = lax.broadcasted_iota(jnp.int32, plane_total.shape, 1)
    slot = jnp.logical_and(rows == plane_row, lanes == RANK)
    depth_slot = jnp.logical_and(
        lax.broadcasted_iota(jnp.int32, depth_total.shape, 0) == depth_row,
        lax.broadcasted_iota(jnp.int32, depth_total.shape, 1) == RANK)
    column_energy = jnp.sum(jnp.where(depth_slot, depth_total, 0.0))
    plane_total = jnp.where(slot, column_energy, plane_total)
    plane_summed[...] = plane_total
    for copy in z_out + y_out:
        copy.wait_send()

    z_out = [exchange("gz", nz, mz, d, lambda t: plane_summed, plane_gathered, zs2, zr2)
             for d in range(1, nz)]
    y_out = [exchange("gy", ny, my, d, lambda t: depth_summed, depth_gathered, ys2, yr2)
             for d in range(1, ny)]
    for copy in z_out + y_out:
        copy.start()
    plane_out[mz] = plane_total
    depth_out[my] = depth_total
    for d in range(1, nz):
        arrival("gz", nz, mz, d, plane_summed, plane_gathered, zr2).wait_recv()
        source = lax.rem(mz + nz - d, nz)
        plane_out[source] = plane_gathered[source]
    for d in range(1, ny):
        arrival("gy", ny, my, d, depth_summed, depth_gathered, yr2).wait_recv()
        source = lax.rem(my + ny - d, ny)
        depth_out[source] = depth_gathered[source]
    for copy in z_out + y_out:
        copy.wait_send()


def chunked(main, extras, n):
    rows = -(-main.shape[0] // (n * 128))
    main = jnp.pad(main, (0, n * rows * 128 - main.shape[0])).reshape(n, rows, 128)
    tail = jnp.pad(extras, (0, 128 - extras.shape[0]))
    tail = jnp.broadcast_to(tail, (n, 1, 128))
    spare = -(-(rows + 1) // 8) * 8 - rows - 1
    return jnp.concatenate([main, tail, jnp.zeros((n, spare, 128), main.dtype)], axis=1), rows


def both_sums(plane_parts, depth_parts, plane_row, depth_row):
    nz, ny = plane_parts.shape[0], depth_parts.shape[0]
    f32 = jnp.float32
    dma = pltpu.SemaphoreType.DMA
    return pl.pallas_call(
        functools.partial(both_sums_kernel, nz, ny, plane_row, depth_row),
        out_shape=[jax.ShapeDtypeStruct(plane_parts.shape, f32),
                   jax.ShapeDtypeStruct(depth_parts.shape, f32)],
        in_specs=[pl.BlockSpec(memory_space=pltpu.VMEM)] * 2,
        out_specs=[pl.BlockSpec(memory_space=pltpu.VMEM)] * 2,
        scratch_shapes=[
            pltpu.VMEM(plane_parts.shape, f32),
            pltpu.VMEM(depth_parts.shape, f32),
            pltpu.VMEM(plane_parts.shape[1:], f32),
            pltpu.VMEM(depth_parts.shape[1:], f32),
            pltpu.VMEM(plane_parts.shape, f32),
            pltpu.VMEM(depth_parts.shape, f32),
            [dma((nz,)), dma((nz,)), dma((nz,)), dma((nz,)),
             dma((ny,)), dma((ny,)), dma((ny,)), dma((ny,))],
        ],
        compiler_params=pltpu.CompilerParams(collective_id=1, has_side_effects=True),
    )(plane_parts, depth_parts)


def local(reference_image, deformed, displacement, plane_factors, depth_factors):
    rows, cols = halo_blocks(deformed)
    fields = jnp.einsum("krij,krz->kijz", plane_factors, depth_factors, precision=highest)
    fields = jnp.repeat(fields, KNOT, axis=2)
    residual, prod, mis, sq, energy_parts = strip_sums(
        deformed, rows, cols, displacement, reference_image, fields[0], fields[1])
    prod, mis, sq = node_sums(prod), node_sums(mis), node_sums(sq)
    local_energy = jnp.sum(energy_parts)

    first, second = plane_factors[0], plane_factors[1]
    grad_depth = -jnp.stack([
        jnp.einsum("rij,ijz->rz", first, prod, precision=highest),
        jnp.einsum("rij,ijz->rz", second, mis, precision=highest)])
    first_depth = jnp.einsum("rij,ijz->rz", first * first, sq, precision=highest)
    level_sum = KNOT * KNOT * jnp.sum(second * second, axis=(1, 2))
    grad_plane = -jnp.stack([
        jnp.einsum("rz,ijz->rij", depth_factors[0], prod, precision=highest),
        jnp.einsum("rz,ijz->rij", depth_factors[1], mis, precision=highest)])
    first_diag = jnp.einsum("rz,ijz->rij", depth_factors[0] * depth_factors[0], sq, precision=highest)
    depth_level = KNOT * KNOT * jnp.sum(depth_factors[1] * depth_factors[1], axis=1)

    nz, ny = lax.axis_size("gz"), lax.axis_size("gy")
    plane_terms = jnp.concatenate([grad_plane.reshape(-1), first_diag.reshape(-1)])
    depth_terms = jnp.concatenate([grad_depth.reshape(-1), first_depth.reshape(-1)])
    blank = jnp.zeros((), jnp.float32)
    plane_parts, plane_rows = chunked(plane_terms, jnp.concatenate([depth_level, blank[None]]), nz)
    depth_parts, depth_rows = chunked(depth_terms, jnp.concatenate([level_sum, local_energy[None]]), ny)
    plane_summed, depth_summed = both_sums(plane_parts, depth_parts, plane_rows, depth_rows)
    plane_terms = plane_summed[:, :plane_rows].reshape(-1)
    depth_terms = depth_summed[:, :depth_rows].reshape(-1)
    grad_plane = plane_terms[: grad_plane.size].reshape(grad_plane.shape)
    first_diag = plane_terms[grad_plane.size : grad_plane.size + first_diag.size].reshape(first_diag.shape)
    grad_depth = depth_terms[: grad_depth.size].reshape(grad_depth.shape)
    first_depth = depth_terms[grad_depth.size : grad_depth.size + first_depth.size].reshape(first_depth.shape)
    depth_level = plane_summed[0, plane_rows, :RANK]
    level_sum = depth_summed[0, depth_rows, :RANK]
    energy = jnp.sum(plane_summed[:, plane_rows, RANK])

    nodes_x = plane_factors.shape[2]
    nodes_y = plane_factors.shape[3] * lax.axis_size("gy")
    full_z = depth_factors.shape[2] * lax.axis_size("gz")
    diag_plane = jnp.stack(
        [first_diag, jnp.broadcast_to(depth_level[:, None, None], first_diag.shape)])
    lam_plane = damping * RANK * energy / (nodes_x * nodes_y)
    lam_depth = damping * energy / full_z
    step_plane = -grad_plane / (diag_plane + lam_plane + epsilon)
    diag_depth = jnp.stack([first_depth, jnp.broadcast_to(level_sum[:, None], first_depth.shape)])
    step_depth = -grad_depth / (diag_depth + lam_depth + epsilon)
    return (residual, step_plane, step_depth)


def solution(mesh):
    placed = (
        P(None, "gy", "gz"),
        P(None, "gy", "gz"),
        P(None, None, "gy", "gz"),
        P(None, None, None, "gy"),
        P(None, None, "gz"),
    )
    return jax.shard_map(
        local,
        mesh=mesh,
        in_specs=placed,
        out_specs=(P(None, "gy", "gz"), P(None, None, None, "gy"), P(None, None, "gz")),
        check_vma=False,
    )
```

```python
import functools

import jax
import jax.numpy as jnp
from jax import lax
from jax.experimental import pallas as pl
from jax.experimental.pallas import tpu as pltpu
from jax.sharding import PartitionSpec as P

RANK = 32
KNOT = 8

epsilon = 1e-06
damping = 0.01
highest = lax.Precision.HIGHEST

ROWS = 16
LANES = 256
SPAN = 16


def neighbours(part, axis, forward):
    count = lax.axis_size(axis)
    if forward:
        pairs = [(i, i + 1) for i in range(count - 1)]
    else:
        pairs = [(i + 1, i) for i in range(count - 1)]
    return lax.ppermute(part, axis, pairs)


def halo_kernel(ny, nz, rows_ref, cols_ref, rows_out, cols_out, rows_got, cols_got,
                send_sems, recv_sems):
    my, mz = lax.axis_index("gy"), lax.axis_index("gz")
    up, down = lax.rem(my + 1, ny), lax.rem(my + ny - 1, ny)
    right, left = lax.rem(mz + 1, nz), lax.rem(mz + nz - 1, nz)
    plan = [
        (rows_ref.at[0], rows_got.at[0], (down, mz)),
        (rows_ref.at[1], rows_got.at[1], (up, mz)),
        (cols_ref.at[0], cols_got.at[0], (my, left)),
        (cols_ref.at[1], cols_got.at[1], (my, right)),
        (cols_ref.at[0], cols_got.at[2], (down, left)),
        (cols_ref.at[0], cols_got.at[3], (up, left)),
        (cols_ref.at[1], cols_got.at[4], (down, right)),
        (cols_ref.at[1], cols_got.at[5], (up, right)),
    ]
    barrier = pltpu.get_barrier_semaphore()
    for _, _, device in plan:
        pl.semaphore_signal(barrier, inc=1, device_id=device,
                            device_id_type=pl.DeviceIdType.MESH)
    pl.semaphore_wait(barrier, len(plan))
    copies = []
    for k, (source, slot, device) in enumerate(plan):
        copy = pltpu.make_async_remote_copy(
            src_ref=source, dst_ref=slot, send_sem=send_sems.at[k], recv_sem=recv_sems.at[k],
            device_id=device, device_id_type=pl.DeviceIdType.MESH)
        copy.start()
        copies.append(copy)
    for copy in copies:
        copy.wait()
    rows_out[...] = rows_got[...]
    cols_out[...] = cols_got[...]


def swap_halos(rows_send, cols_send):
    ny, nz = lax.axis_size("gy"), lax.axis_size("gz")
    dma = pltpu.SemaphoreType.DMA
    rows_shape = rows_send.shape
    cols_shape = (6,) + cols_send.shape[1:]
    return pl.pallas_call(
        functools.partial(halo_kernel, ny, nz),
        out_shape=[jax.ShapeDtypeStruct(rows_shape, rows_send.dtype),
                   jax.ShapeDtypeStruct(cols_shape, cols_send.dtype)],
        in_specs=[pl.BlockSpec(memory_space=pltpu.VMEM)] * 2,
        out_specs=[pl.BlockSpec(memory_space=pltpu.VMEM)] * 2,
        scratch_shapes=[
            pltpu.VMEM(rows_shape, rows_send.dtype),
            pltpu.VMEM(cols_shape, cols_send.dtype),
            dma((8,)),
            dma((8,)),
        ],
        compiler_params=pltpu.CompilerParams(collective_id=2, has_side_effects=True),
    )(rows_send, cols_send)


def halo_blocks(deformed):
    depth_x, width_y, width_z = deformed.shape
    f32 = jnp.float32
    ny, nz = lax.axis_size("gy"), lax.axis_size("gz")
    my, mz = lax.axis_index("gy"), lax.axis_index("gz")
    rows_send = jnp.stack([deformed[:, 0, :], deformed[:, width_y - 1, :]])
    cols_send = jnp.stack([deformed[:, :, 0], deformed[:, :, width_z - 1]])
    rows_got, cols_got = swap_halos(rows_send, cols_send)
    held = deformed.dtype
    has_up = (my < ny - 1).astype(held)
    has_down = (my > 0).astype(held)
    has_right = (mz < nz - 1).astype(held)
    has_left = (mz > 0).astype(held)
    high_y = rows_got[0] * has_up
    low_y = rows_got[1] * has_down
    high_z = cols_got[0] * has_right
    low_z = cols_got[1] * has_left
    high_high = cols_got[2][:, 0] * (has_up * has_right)
    low_high = cols_got[3][:, width_y - 1] * (has_down * has_right)
    high_low = cols_got[4][:, 0] * (has_up * has_left)
    low_low = cols_got[5][:, width_y - 1] * (has_down * has_left)
    gap_y = jnp.zeros((depth_x, 6, width_z), held)
    rows = jnp.concatenate([high_y[:, None], gap_y, low_y[:, None]], axis=1)
    gap = jnp.zeros((depth_x, 6), held)
    side_high = jnp.concatenate([high_z, high_high[:, None], gap, low_high[:, None]], axis=1)
    side_low = jnp.concatenate([low_z, high_low[:, None], gap, low_low[:, None]], axis=1)
    lanes = lax.broadcasted_iota(jnp.int32, (1, 1, 128), 2)
    cols = jnp.where(lanes == 0, side_high[:, :, None],
                     jnp.where(lanes == 127, side_low[:, :, None], jnp.zeros((), held)))
    return rows, cols


def lerp(base, other, weight):
    return base + weight * (other - base)


def strip_kernel(prev_ref, main_ref, next_ref, rows_ref, cols_ref, disp_ref, image_ref,
                 contrast_ref, bright_ref,
                 res_ref, prod_ref, mis_ref, sq_ref, energy_ref, pad_ref, shifts_ref):
    block = pl.program_id(0)
    depth_x = rows_ref.shape[0]
    width_y, width_z = image_ref.shape[1], image_ref.shape[2]
    pad_y, pad_z = pad_ref.shape

    def source_plane(p, plane):
        plane_x = block * SPAN - 1 + p
        valid = jnp.logical_and(plane_x >= 0, plane_x < depth_x)
        safe = jnp.clip(plane_x, 0, depth_x - 1)
        pad_ref[:width_y, :width_z] = plane.astype(jnp.float32)
        pad_ref[width_y:, :width_z] = rows_ref[safe].astype(jnp.float32)
        pad_ref[:, width_z:] = cols_ref[safe].astype(jnp.float32)
        whole = jnp.where(valid, pad_ref[...], 0.0)
        by_y = (pltpu.roll(whole, 1, 0), whole, pltpu.roll(whole, pad_y - 1, 0))
        for b in range(3):
            part = by_y[b][:width_y]
            by_z = (pltpu.roll(part, 1, 1), part, pltpu.roll(part, pad_z - 1, 1))
            for c in range(3):
                shifts_ref[p, 3 * b + c] = by_z[c][:, :width_z]

    source_plane(0, prev_ref[0])

    def inner_plane(p, carry):
        source_plane(p, main_ref[p - 1])
        return carry

    lax.fori_loop(1, SPAN + 1, inner_plane, 0, unroll=4)
    source_plane(SPAN + 1, next_ref[0])

    chunks_y = width_y // ROWS
    chunks_z = width_z // LANES

    def chunk(n, k, energy):
        r0 = pl.multiple_of((k // chunks_z) * ROWS, ROWS)
        c0 = pl.multiple_of((k % chunks_z) * LANES, LANES)
        rs = pl.ds(r0, ROWS)
        cs = pl.ds(c0, LANES)
        contrast = contrast_ref[n, rs, cs]
        bright = bright_ref[n, rs, cs]

        def plane(step, acc):
            xl = n * KNOT + step
            prod_acc, mis_acc, sq_acc, e_acc = acc

            def src(a, b, c):
                return shifts_ref[xl + 1 + a, 3 * (b + 1) + (c + 1), rs, cs]

            sx = disp_ref[0, xl, rs, cs].astype(jnp.float32)
            sy = disp_ref[1, xl, rs, cs].astype(jnp.float32)
            sz = disp_ref[2, xl, rs, cs].astype(jnp.float32)
            gx, gy, gz = sx > 0, sy > 0, sz > 0
            ax, ay, az = jnp.abs(sx), jnp.abs(sy), jnp.abs(sz)
            xs = {}
            for b in (-1, 0, 1):
                for c in (-1, 0, 1):
                    xs[b, c] = jnp.where(gx, src(1, b, c), src(-1, b, c))
            y0 = {c: jnp.where(gy, src(0, 1, c), src(0, -1, c)) for c in (-1, 0, 1)}
            y1 = {c: jnp.where(gy, xs[1, c], xs[-1, c]) for c in (-1, 0, 1)}
            centre = src(0, 0, 0)
            z00 = jnp.where(gz, src(0, 0, 1), src(0, 0, -1))
            z01 = jnp.where(gz, y0[1], y0[-1])
            z10 = jnp.where(gz, xs[0, 1], xs[0, -1])
            z11 = jnp.where(gz, y1[1], y1[-1])
            l00 = lerp(centre, z00, az)
            l01 = lerp(y0[0], z01, az)
            l10 = lerp(xs[0, 0], z10, az)
            l11 = lerp(y1[0], z11, az)
            m0 = lerp(l00, l01, ay)
            m1 = lerp(l10, l11, ay)
            warped = lerp(m0, m1, ax)
            values = image_ref[xl, rs, cs].astype(jnp.float32)
            misfit = warped - contrast * values - bright
            res_ref[xl, rs, cs] = misfit.astype(res_ref.dtype)
            return (prod_acc + misfit * values, mis_acc + misfit,
                    sq_acc + values * values, e_acc + misfit * misfit)

        zero = jnp.zeros((ROWS, LANES), jnp.float32)
        prod_acc, mis_acc, sq_acc, e_acc = lax.fori_loop(
            0, KNOT, plane, (zero, zero, zero, energy), unroll=4)
        prod_ref[n, rs, cs] = prod_acc
        mis_ref[n, rs, cs] = mis_acc
        sq_ref[n, rs, cs] = sq_acc
        return e_acc

    energy = jnp.zeros((ROWS, LANES), jnp.float32)
    for n in range(SPAN // KNOT):
        energy = lax.fori_loop(0, chunks_y * chunks_z, functools.partial(chunk, n), energy)
    energy_ref[0] = energy


def strip_sums(deformed, rows, cols, displacement, image, contrast_y, bright_y):
    depth_x, width_y, width_z = image.shape
    nodes = depth_x // KNOT
    steps = depth_x // SPAN
    per = SPAN // KNOT
    f32 = jnp.float32
    block_sum = jax.ShapeDtypeStruct((nodes, width_y, width_z), f32)
    node_spec = pl.BlockSpec((per, width_y, width_z), lambda i: (i, 0, 0))
    plane_spec = pl.BlockSpec((SPAN, width_y, width_z), lambda i: (i, 0, 0))
    return pl.pallas_call(
        strip_kernel,
        grid=(steps,),
        in_specs=[
            pl.BlockSpec((1, width_y, width_z), lambda i: (jnp.maximum(i * SPAN - 1, 0), 0, 0)),
            plane_spec,
            pl.BlockSpec((1, width_y, width_z),
                         lambda i: (jnp.minimum(i * SPAN + SPAN, depth_x - 1), 0, 0)),
            pl.BlockSpec(memory_space=pltpu.VMEM),
            pl.BlockSpec(memory_space=pltpu.VMEM),
            pl.BlockSpec((3, SPAN, width_y, width_z), lambda i: (0, i, 0, 0)),
            plane_spec,
            node_spec,
            node_spec,
        ],
        out_specs=[
            plane_spec,
            node_spec,
            node_spec,
            node_spec,
            pl.BlockSpec((1, ROWS, LANES), lambda i: (i, 0, 0)),
        ],
        out_shape=[
            jax.ShapeDtypeStruct(image.shape, jnp.bfloat16),
            block_sum,
            block_sum,
            block_sum,
            jax.ShapeDtypeStruct((steps, ROWS, LANES), f32),
        ],
        scratch_shapes=[
            pltpu.VMEM((width_y + rows.shape[1], width_z + cols.shape[2]), f32),
            pltpu.VMEM((SPAN + 2, 9, width_y, width_z), f32),
        ],
        compiler_params=pltpu.CompilerParams(
            dimension_semantics=("arbitrary",), vmem_limit_bytes=60 * 1024 * 1024),
    )(deformed, deformed, deformed, rows, cols, displacement, image, contrast_y, bright_y)


def node_sums(field):
    nodes, width_y, width_z = field.shape
    return field.reshape(nodes, width_y // KNOT, KNOT, width_z).sum(axis=2)


def exchange(axis, n, me, d, src, buffer, send_sem, recv_sem):
    target = lax.rem(me + d, n)
    return pltpu.make_async_remote_copy(
        src_ref=src(target), dst_ref=buffer.at[me],
        send_sem=send_sem.at[target], recv_sem=recv_sem.at[me],
        device_id={axis: target}, device_id_type=pl.DeviceIdType.MESH)


def arrival(axis, n, me, d, src_ref, buffer, sem):
    source = lax.rem(me + n - d, n)
    return pltpu.make_async_remote_copy(
        src_ref=src_ref, dst_ref=buffer.at[source],
        send_sem=sem.at[source], recv_sem=sem.at[source],
        device_id={axis: source}, device_id_type=pl.DeviceIdType.MESH)


def both_sums_kernel(nz, ny, plane_row, depth_row, plane_ref, depth_ref, plane_out, depth_out,
                     plane_landed, depth_landed, plane_summed, depth_summed,
                     plane_gathered, depth_gathered, sems):
    mz, my = lax.axis_index("gz"), lax.axis_index("gy")
    barrier = pltpu.get_barrier_semaphore()
    for d in range(1, nz):
        pl.semaphore_signal(barrier, inc=1, device_id={"gz": lax.rem(mz + d, nz)},
                            device_id_type=pl.DeviceIdType.MESH)
    for d in range(1, ny):
        pl.semaphore_signal(barrier, inc=1, device_id={"gy": lax.rem(my + d, ny)},
                            device_id_type=pl.DeviceIdType.MESH)
    pl.semaphore_wait(barrier, nz - 1 + ny - 1)
    zs1, zr1, zs2, zr2, ys1, yr1, ys2, yr2 = sems

    z_out = [exchange("gz", nz, mz, d, lambda t: plane_ref.at[t], plane_landed, zs1, zr1)
             for d in range(1, nz)]
    y_out = [exchange("gy", ny, my, d, lambda t: depth_ref.at[t], depth_landed, ys1, yr1)
             for d in range(1, ny)]
    for copy in z_out + y_out:
        copy.start()
    depth_total = depth_ref[my]
    for d in range(1, ny):
        arrival("gy", ny, my, d, depth_ref.at[0], depth_landed, yr1).wait_recv()
        depth_total = depth_total + depth_landed[lax.rem(my + ny - d, ny)]
    depth_summed[...] = depth_total
    plane_total = plane_ref[mz]
    for d in range(1, nz):
        arrival("gz", nz, mz, d, plane_ref.at[0], plane_landed, zr1).wait_recv()
        plane_total = plane_total + plane_landed[lax.rem(mz + nz - d, nz)]
    rows = lax.broadcasted_iota(jnp.int32, plane_total.shape, 0)
    lanes = lax.broadcasted_iota(jnp.int32, plane_total.shape, 1)
    slot = jnp.logical_and(rows == plane_row, lanes == RANK)
    depth_slot = jnp.logical_and(
        lax.broadcasted_iota(jnp.int32, depth_total.shape, 0) == depth_row,
        lax.broadcasted_iota(jnp.int32, depth_total.shape, 1) == RANK)
    column_energy = jnp.sum(jnp.where(depth_slot, depth_total, 0.0))
    plane_total = jnp.where(slot, column_energy, plane_total)
    plane_summed[...] = plane_total
    for copy in z_out + y_out:
        copy.wait_send()

    z_out = [exchange("gz", nz, mz, d, lambda t: plane_summed, plane_gathered, zs2, zr2)
             for d in range(1, nz)]
    y_out = [exchange("gy", ny, my, d, lambda t: depth_summed, depth_gathered, ys2, yr2)
             for d in range(1, ny)]
    for copy in z_out + y_out:
        copy.start()
    plane_out[mz] = plane_total
    depth_out[my] = depth_total
    for d in range(1, nz):
        arrival("gz", nz, mz, d, plane_summed, plane_gathered, zr2).wait_recv()
        source = lax.rem(mz + nz - d, nz)
        plane_out[source] = plane_gathered[source]
    gathered = plane_out[...]
    chunk_row = lax.broadcasted_iota(jnp.int32, gathered.shape, 1)
    chunk_lane = lax.broadcasted_iota(jnp.int32, gathered.shape, 2)
    total_energy = jnp.sum(jnp.where(
        jnp.logical_and(chunk_row == plane_row, chunk_lane == RANK), gathered, 0.0))
    plane_out[0] = jnp.where(jnp.logical_and(rows == plane_row, lanes == RANK + 1),
                             total_energy, gathered[0])
    for d in range(1, ny):
        arrival("gy", ny, my, d, depth_summed, depth_gathered, yr2).wait_recv()
        source = lax.rem(my + ny - d, ny)
        depth_out[source] = depth_gathered[source]
    for copy in z_out + y_out:
        copy.wait_send()


def chunked(main, extras, n):
    rows = -(-main.shape[0] // (n * 128))
    main = jnp.pad(main, (0, n * rows * 128 - main.shape[0])).reshape(n, rows, 128)
    tail = jnp.pad(extras, (0, 128 - extras.shape[0]))
    tail = jnp.broadcast_to(tail, (n, 1, 128))
    spare = -(-(rows + 1) // 8) * 8 - rows - 1
    return jnp.concatenate([main, tail, jnp.zeros((n, spare, 128), main.dtype)], axis=1), rows


def both_sums(plane_parts, depth_parts, plane_row, depth_row):
    nz, ny = plane_parts.shape[0], depth_parts.shape[0]
    f32 = jnp.float32
    dma = pltpu.SemaphoreType.DMA
    return pl.pallas_call(
        functools.partial(both_sums_kernel, nz, ny, plane_row, depth_row),
        out_shape=[jax.ShapeDtypeStruct(plane_parts.shape, f32),
                   jax.ShapeDtypeStruct(depth_parts.shape, f32)],
        in_specs=[pl.BlockSpec(memory_space=pltpu.VMEM)] * 2,
        out_specs=[pl.BlockSpec(memory_space=pltpu.VMEM)] * 2,
        scratch_shapes=[
            pltpu.VMEM(plane_parts.shape, f32),
            pltpu.VMEM(depth_parts.shape, f32),
            pltpu.VMEM(plane_parts.shape[1:], f32),
            pltpu.VMEM(depth_parts.shape[1:], f32),
            pltpu.VMEM(plane_parts.shape, f32),
            pltpu.VMEM(depth_parts.shape, f32),
            [dma((nz,)), dma((nz,)), dma((nz,)), dma((nz,)),
             dma((ny,)), dma((ny,)), dma((ny,)), dma((ny,))],
        ],
        compiler_params=pltpu.CompilerParams(collective_id=1, has_side_effects=True),
    )(plane_parts, depth_parts)


def local(reference_image, deformed, displacement, plane_factors, depth_factors):
    rows, cols = halo_blocks(deformed)
    fields = jnp.einsum("krij,krz->kijz", plane_factors, depth_factors, precision=highest)
    fields = jnp.repeat(fields, KNOT, axis=2)
    residual, prod, mis, sq, energy_parts = strip_sums(
        deformed, rows, cols, displacement, reference_image, fields[0], fields[1])
    prod, mis, sq = node_sums(prod), node_sums(mis), node_sums(sq)
    local_energy = jnp.sum(energy_parts)

    first, second = plane_factors[0], plane_factors[1]
    grad_depth = -jnp.stack([
        jnp.einsum("rij,ijz->rz", first, prod, precision=highest),
        jnp.einsum("rij,ijz->rz", second, mis, precision=highest)])
    first_depth = jnp.einsum("rij,ijz->rz", first * first, sq, precision=highest)
    level_sum = KNOT * KNOT * jnp.sum(second * second, axis=(1, 2))
    grad_plane = -jnp.stack([
        jnp.einsum("rz,ijz->rij", depth_factors[0], prod, precision=highest),
        jnp.einsum("rz,ijz->rij", depth_factors[1], mis, precision=highest)])
    first_diag = jnp.einsum("rz,ijz->rij", depth_factors[0] * depth_factors[0], sq, precision=highest)
    depth_level = KNOT * KNOT * jnp.sum(depth_factors[1] * depth_factors[1], axis=1)

    nz, ny = lax.axis_size("gz"), lax.axis_size("gy")
    plane_terms = jnp.concatenate([grad_plane.reshape(-1), first_diag.reshape(-1)])
    depth_terms = jnp.concatenate([grad_depth.reshape(-1), first_depth.reshape(-1)])
    blank = jnp.zeros((), jnp.float32)
    plane_parts, plane_rows = chunked(plane_terms, jnp.concatenate([depth_level, blank[None]]), nz)
    depth_parts, depth_rows = chunked(depth_terms, jnp.concatenate([level_sum, local_energy[None]]), ny)
    plane_summed, depth_summed = both_sums(plane_parts, depth_parts, plane_rows, depth_rows)
    plane_terms = plane_summed[:, :plane_rows].reshape(-1)
    depth_terms = depth_summed[:, :depth_rows].reshape(-1)
    grad_plane = plane_terms[: grad_plane.size].reshape(grad_plane.shape)
    first_diag = plane_terms[grad_plane.size : grad_plane.size + first_diag.size].reshape(first_diag.shape)
    grad_depth = depth_terms[: grad_depth.size].reshape(grad_depth.shape)
    first_depth = depth_terms[grad_depth.size : grad_depth.size + first_depth.size].reshape(first_depth.shape)
    depth_level = plane_summed[0, plane_rows, :RANK]
    level_sum = depth_summed[0, depth_rows, :RANK]
    energy = plane_summed[0, plane_rows, RANK + 1]

    nodes_x = plane_factors.shape[2]
    nodes_y = plane_factors.shape[3] * lax.axis_size("gy")
    full_z = depth_factors.shape[2] * lax.axis_size("gz")
    diag_plane = jnp.stack(
        [first_diag, jnp.broadcast_to(depth_level[:, None, None], first_diag.shape)])
    lam_plane = damping * RANK * energy / (nodes_x * nodes_y)
    lam_depth = damping * energy / full_z
    step_plane = -grad_plane / (diag_plane + lam_plane + epsilon)
    diag_depth = jnp.stack([first_depth, jnp.broadcast_to(level_sum[:, None], first_depth.shape)])
    step_depth = -grad_depth / (diag_depth + lam_depth + epsilon)
    return (residual, step_plane, step_depth)


def solution(mesh):
    placed = (
        P(None, "gy", "gz"),
        P(None, "gy", "gz"),
        P(None, None, "gy", "gz"),
        P(None, None, None, "gy"),
        P(None, None, "gz"),
    )
    return jax.shard_map(
        local,
        mesh=mesh,
        in_specs=placed,
        out_specs=(P(None, "gy", "gz"), P(None, None, None, "gy"), P(None, None, "gz")),
        check_vma=False,
    )
```

```python
import functools

import jax
import jax.numpy as jnp
from jax import lax
from jax.experimental import pallas as pl
from jax.experimental.pallas import tpu as pltpu
from jax.sharding import PartitionSpec as P

RANK = 32
KNOT = 8

epsilon = 1e-06
damping = 0.01
highest = lax.Precision.HIGHEST

ROWS = 16
LANES = 256
SPAN = 16


def neighbours(part, axis, forward):
    count = lax.axis_size(axis)
    if forward:
        pairs = [(i, i + 1) for i in range(count - 1)]
    else:
        pairs = [(i + 1, i) for i in range(count - 1)]
    return lax.ppermute(part, axis, pairs)


def halo_kernel(ny, nz, rows_ref, cols_ref, rows_out, cols_out, rows_got, cols_got,
                send_sems, recv_sems):
    my, mz = lax.axis_index("gy"), lax.axis_index("gz")
    up, down = lax.rem(my + 1, ny), lax.rem(my + ny - 1, ny)
    right, left = lax.rem(mz + 1, nz), lax.rem(mz + nz - 1, nz)
    plan = [
        (rows_ref.at[0], rows_got.at[0], (down, mz)),
        (rows_ref.at[1], rows_got.at[1], (up, mz)),
        (cols_ref.at[0], cols_got.at[0], (my, left)),
        (cols_ref.at[1], cols_got.at[1], (my, right)),
        (cols_ref.at[0], cols_got.at[2], (down, left)),
        (cols_ref.at[0], cols_got.at[3], (up, left)),
        (cols_ref.at[1], cols_got.at[4], (down, right)),
        (cols_ref.at[1], cols_got.at[5], (up, right)),
    ]
    barrier = pltpu.get_barrier_semaphore()
    for _, _, device in plan:
        pl.semaphore_signal(barrier, inc=1, device_id=device,
                            device_id_type=pl.DeviceIdType.MESH)
    pl.semaphore_wait(barrier, len(plan))
    copies = []
    for k, (source, slot, device) in enumerate(plan):
        copy = pltpu.make_async_remote_copy(
            src_ref=source, dst_ref=slot, send_sem=send_sems.at[k], recv_sem=recv_sems.at[k],
            device_id=device, device_id_type=pl.DeviceIdType.MESH)
        copy.start()
        copies.append(copy)
    for copy in copies:
        copy.wait()
    rows_out[...] = rows_got[...]
    cols_out[...] = cols_got[...]


def swap_halos(rows_send, cols_send):
    ny, nz = lax.axis_size("gy"), lax.axis_size("gz")
    dma = pltpu.SemaphoreType.DMA
    rows_shape = rows_send.shape
    cols_shape = (6,) + cols_send.shape[1:]
    return pl.pallas_call(
        functools.partial(halo_kernel, ny, nz),
        out_shape=[jax.ShapeDtypeStruct(rows_shape, rows_send.dtype),
                   jax.ShapeDtypeStruct(cols_shape, cols_send.dtype)],
        in_specs=[pl.BlockSpec(memory_space=pltpu.VMEM)] * 2,
        out_specs=[pl.BlockSpec(memory_space=pltpu.VMEM)] * 2,
        scratch_shapes=[
            pltpu.VMEM(rows_shape, rows_send.dtype),
            pltpu.VMEM(cols_shape, cols_send.dtype),
            dma((8,)),
            dma((8,)),
        ],
        compiler_params=pltpu.CompilerParams(collective_id=2, has_side_effects=True),
    )(rows_send, cols_send)


def halo_blocks(deformed):
    depth_x, width_y, width_z = deformed.shape
    f32 = jnp.float32
    ny, nz = lax.axis_size("gy"), lax.axis_size("gz")
    my, mz = lax.axis_index("gy"), lax.axis_index("gz")
    rows_send = jnp.stack([deformed[:, 0, :], deformed[:, width_y - 1, :]])
    cols_send = jnp.transpose(deformed[:, :, :: width_z - 1], (2, 0, 1))
    rows_got, cols_got = swap_halos(rows_send, cols_send)
    held = deformed.dtype
    has_up = (my < ny - 1).astype(held)
    has_down = (my > 0).astype(held)
    has_right = (mz < nz - 1).astype(held)
    has_left = (mz > 0).astype(held)
    high_y = rows_got[0] * has_up
    low_y = rows_got[1] * has_down
    high_z = cols_got[0] * has_right
    low_z = cols_got[1] * has_left
    high_high = cols_got[2][:, 0] * (has_up * has_right)
    low_high = cols_got[3][:, width_y - 1] * (has_down * has_right)
    high_low = cols_got[4][:, 0] * (has_up * has_left)
    low_low = cols_got[5][:, width_y - 1] * (has_down * has_left)
    gap_y = jnp.zeros((depth_x, 6, width_z), held)
    rows = jnp.concatenate([high_y[:, None], gap_y, low_y[:, None]], axis=1)
    gap = jnp.zeros((depth_x, 6), held)
    side_high = jnp.concatenate([high_z, high_high[:, None], gap, low_high[:, None]], axis=1)
    side_low = jnp.concatenate([low_z, high_low[:, None], gap, low_low[:, None]], axis=1)
    lanes = lax.broadcasted_iota(jnp.int32, (1, 1, 128), 2)
    cols = jnp.where(lanes == 0, side_high[:, :, None],
                     jnp.where(lanes == 127, side_low[:, :, None], jnp.zeros((), held)))
    return rows, cols


def lerp(base, other, weight):
    return base + weight * (other - base)


def strip_kernel(prev_ref, main_ref, next_ref, rows_ref, cols_ref, disp_ref, image_ref,
                 contrast_ref, bright_ref,
                 res_ref, prod_ref, mis_ref, sq_ref, energy_ref, pad_ref, shifts_ref):
    block = pl.program_id(0)
    depth_x = rows_ref.shape[0]
    width_y, width_z = image_ref.shape[1], image_ref.shape[2]
    pad_y, pad_z = pad_ref.shape

    def source_plane(p, plane):
        plane_x = block * SPAN - 1 + p
        valid = jnp.logical_and(plane_x >= 0, plane_x < depth_x)
        safe = jnp.clip(plane_x, 0, depth_x - 1)
        pad_ref[:width_y, :width_z] = plane.astype(jnp.float32)
        pad_ref[width_y:, :width_z] = rows_ref[safe].astype(jnp.float32)
        pad_ref[:, width_z:] = cols_ref[safe].astype(jnp.float32)
        whole = jnp.where(valid, pad_ref[...], 0.0)
        by_y = (pltpu.roll(whole, 1, 0), whole, pltpu.roll(whole, pad_y - 1, 0))
        for b in range(3):
            part = by_y[b][:width_y]
            by_z = (pltpu.roll(part, 1, 1), part, pltpu.roll(part, pad_z - 1, 1))
            for c in range(3):
                shifts_ref[p, 3 * b + c] = by_z[c][:, :width_z]

    source_plane(0, prev_ref[0])

    def inner_plane(p, carry):
        source_plane(p, main_ref[p - 1])
        return carry

    lax.fori_loop(1, SPAN + 1, inner_plane, 0, unroll=4)
    source_plane(SPAN + 1, next_ref[0])

    chunks_y = width_y // ROWS
    chunks_z = width_z // LANES

    def chunk(n, k, energy):
        r0 = pl.multiple_of((k // chunks_z) * ROWS, ROWS)
        c0 = pl.multiple_of((k % chunks_z) * LANES, LANES)
        rs = pl.ds(r0, ROWS)
        cs = pl.ds(c0, LANES)
        contrast = contrast_ref[n, rs, cs]
        bright = bright_ref[n, rs, cs]

        def plane(step, acc):
            xl = n * KNOT + step
            prod_acc, mis_acc, sq_acc, e_acc = acc

            def src(a, b, c):
                return shifts_ref[xl + 1 + a, 3 * (b + 1) + (c + 1), rs, cs]

            sx = disp_ref[0, xl, rs, cs].astype(jnp.float32)
            sy = disp_ref[1, xl, rs, cs].astype(jnp.float32)
            sz = disp_ref[2, xl, rs, cs].astype(jnp.float32)
            gx, gy, gz = sx > 0, sy > 0, sz > 0
            ax, ay, az = jnp.abs(sx), jnp.abs(sy), jnp.abs(sz)
            xs = {}
            for b in (-1, 0, 1):
                for c in (-1, 0, 1):
                    xs[b, c] = jnp.where(gx, src(1, b, c), src(-1, b, c))
            y0 = {c: jnp.where(gy, src(0, 1, c), src(0, -1, c)) for c in (-1, 0, 1)}
            y1 = {c: jnp.where(gy, xs[1, c], xs[-1, c]) for c in (-1, 0, 1)}
            centre = src(0, 0, 0)
            z00 = jnp.where(gz, src(0, 0, 1), src(0, 0, -1))
            z01 = jnp.where(gz, y0[1], y0[-1])
            z10 = jnp.where(gz, xs[0, 1], xs[0, -1])
            z11 = jnp.where(gz, y1[1], y1[-1])
            l00 = lerp(centre, z00, az)
            l01 = lerp(y0[0], z01, az)
            l10 = lerp(xs[0, 0], z10, az)
            l11 = lerp(y1[0], z11, az)
            m0 = lerp(l00, l01, ay)
            m1 = lerp(l10, l11, ay)
            warped = lerp(m0, m1, ax)
            values = image_ref[xl, rs, cs].astype(jnp.float32)
            misfit = warped - contrast * values - bright
            res_ref[xl, rs, cs] = misfit.astype(res_ref.dtype)
            return (prod_acc + misfit * values, mis_acc + misfit,
                    sq_acc + values * values, e_acc + misfit * misfit)

        zero = jnp.zeros((ROWS, LANES), jnp.float32)
        prod_acc, mis_acc, sq_acc, e_acc = lax.fori_loop(
            0, KNOT, plane, (zero, zero, zero, energy), unroll=4)
        prod_ref[n, rs, cs] = prod_acc
        mis_ref[n, rs, cs] = mis_acc
        sq_ref[n, rs, cs] = sq_acc
        return e_acc

    energy = jnp.zeros((ROWS, LANES), jnp.float32)
    for n in range(SPAN // KNOT):
        energy = lax.fori_loop(0, chunks_y * chunks_z, functools.partial(chunk, n), energy)
    energy_ref[0] = energy


def strip_sums(deformed, rows, cols, displacement, image, contrast_y, bright_y):
    depth_x, width_y, width_z = image.shape
    nodes = depth_x // KNOT
    steps = depth_x // SPAN
    per = SPAN // KNOT
    f32 = jnp.float32
    block_sum = jax.ShapeDtypeStruct((nodes, width_y, width_z), f32)
    node_spec = pl.BlockSpec((per, width_y, width_z), lambda i: (i, 0, 0))
    plane_spec = pl.BlockSpec((SPAN, width_y, width_z), lambda i: (i, 0, 0))
    return pl.pallas_call(
        strip_kernel,
        grid=(steps,),
        in_specs=[
            pl.BlockSpec((1, width_y, width_z), lambda i: (jnp.maximum(i * SPAN - 1, 0), 0, 0)),
            plane_spec,
            pl.BlockSpec((1, width_y, width_z),
                         lambda i: (jnp.minimum(i * SPAN + SPAN, depth_x - 1), 0, 0)),
            pl.BlockSpec(memory_space=pltpu.VMEM),
            pl.BlockSpec(memory_space=pltpu.VMEM),
            pl.BlockSpec((3, SPAN, width_y, width_z), lambda i: (0, i, 0, 0)),
            plane_spec,
            node_spec,
            node_spec,
        ],
        out_specs=[
            plane_spec,
            node_spec,
            node_spec,
            node_spec,
            pl.BlockSpec((1, ROWS, LANES), lambda i: (i, 0, 0)),
        ],
        out_shape=[
            jax.ShapeDtypeStruct(image.shape, jnp.bfloat16),
            block_sum,
            block_sum,
            block_sum,
            jax.ShapeDtypeStruct((steps, ROWS, LANES), f32),
        ],
        scratch_shapes=[
            pltpu.VMEM((width_y + rows.shape[1], width_z + cols.shape[2]), f32),
            pltpu.VMEM((SPAN + 2, 9, width_y, width_z), f32),
        ],
        compiler_params=pltpu.CompilerParams(
            dimension_semantics=("arbitrary",), vmem_limit_bytes=60 * 1024 * 1024),
    )(deformed, deformed, deformed, rows, cols, displacement, image, contrast_y, bright_y)


def node_sums(field):
    nodes, width_y, width_z = field.shape
    return field.reshape(nodes, width_y // KNOT, KNOT, width_z).sum(axis=2)


def exchange(axis, n, me, d, src, buffer, send_sem, recv_sem):
    target = lax.rem(me + d, n)
    return pltpu.make_async_remote_copy(
        src_ref=src(target), dst_ref=buffer.at[me],
        send_sem=send_sem.at[target], recv_sem=recv_sem.at[me],
        device_id={axis: target}, device_id_type=pl.DeviceIdType.MESH)


def arrival(axis, n, me, d, src_ref, buffer, sem):
    source = lax.rem(me + n - d, n)
    return pltpu.make_async_remote_copy(
        src_ref=src_ref, dst_ref=buffer.at[source],
        send_sem=sem.at[source], recv_sem=sem.at[source],
        device_id={axis: source}, device_id_type=pl.DeviceIdType.MESH)


def both_sums_kernel(nz, ny, plane_row, depth_row, plane_ref, depth_ref, plane_out, depth_out,
                     plane_landed, depth_landed, plane_summed, depth_summed,
                     plane_gathered, depth_gathered, sems):
    mz, my = lax.axis_index("gz"), lax.axis_index("gy")
    barrier = pltpu.get_barrier_semaphore()
    for d in range(1, nz):
        pl.semaphore_signal(barrier, inc=1, device_id={"gz": lax.rem(mz + d, nz)},
                            device_id_type=pl.DeviceIdType.MESH)
    for d in range(1, ny):
        pl.semaphore_signal(barrier, inc=1, device_id={"gy": lax.rem(my + d, ny)},
                            device_id_type=pl.DeviceIdType.MESH)
    pl.semaphore_wait(barrier, nz - 1 + ny - 1)
    zs1, zr1, zs2, zr2, ys1, yr1, ys2, yr2 = sems

    z_out = [exchange("gz", nz, mz, d, lambda t: plane_ref.at[t], plane_landed, zs1, zr1)
             for d in range(1, nz)]
    y_out = [exchange("gy", ny, my, d, lambda t: depth_ref.at[t], depth_landed, ys1, yr1)
             for d in range(1, ny)]
    for copy in z_out + y_out:
        copy.start()
    depth_total = depth_ref[my]
    for d in range(1, ny):
        arrival("gy", ny, my, d, depth_ref.at[0], depth_landed, yr1).wait_recv()
        depth_total = depth_total + depth_landed[lax.rem(my + ny - d, ny)]
    depth_summed[...] = depth_total
    plane_total = plane_ref[mz]
    for d in range(1, nz):
        arrival("gz", nz, mz, d, plane_ref.at[0], plane_landed, zr1).wait_recv()
        plane_total = plane_total + plane_landed[lax.rem(mz + nz - d, nz)]
    rows = lax.broadcasted_iota(jnp.int32, plane_total.shape, 0)
    lanes = lax.broadcasted_iota(jnp.int32, plane_total.shape, 1)
    slot = jnp.logical_and(rows == plane_row, lanes == RANK)
    depth_slot = jnp.logical_and(
        lax.broadcasted_iota(jnp.int32, depth_total.shape, 0) == depth_row,
        lax.broadcasted_iota(jnp.int32, depth_total.shape, 1) == RANK)
    column_energy = jnp.sum(jnp.where(depth_slot, depth_total, 0.0))
    plane_total = jnp.where(slot, column_energy, plane_total)
    plane_summed[...] = plane_total
    for copy in z_out + y_out:
        copy.wait_send()

    z_out = [exchange("gz", nz, mz, d, lambda t: plane_summed, plane_gathered, zs2, zr2)
             for d in range(1, nz)]
    y_out = [exchange("gy", ny, my, d, lambda t: depth_summed, depth_gathered, ys2, yr2)
             for d in range(1, ny)]
    for copy in z_out + y_out:
        copy.start()
    plane_out[mz] = plane_total
    depth_out[my] = depth_total
    for d in range(1, nz):
        arrival("gz", nz, mz, d, plane_summed, plane_gathered, zr2).wait_recv()
        source = lax.rem(mz + nz - d, nz)
        plane_out[source] = plane_gathered[source]
    gathered = plane_out[...]
    chunk_row = lax.broadcasted_iota(jnp.int32, gathered.shape, 1)
    chunk_lane = lax.broadcasted_iota(jnp.int32, gathered.shape, 2)
    total_energy = jnp.sum(jnp.where(
        jnp.logical_and(chunk_row == plane_row, chunk_lane == RANK), gathered, 0.0))
    plane_out[0] = jnp.where(jnp.logical_and(rows == plane_row, lanes == RANK + 1),
                             total_energy, gathered[0])
    for d in range(1, ny):
        arrival("gy", ny, my, d, depth_summed, depth_gathered, yr2).wait_recv()
        source = lax.rem(my + ny - d, ny)
        depth_out[source] = depth_gathered[source]
    for copy in z_out + y_out:
        copy.wait_send()


def chunked(main, extras, n):
    rows = -(-main.shape[0] // (n * 128))
    main = jnp.pad(main, (0, n * rows * 128 - main.shape[0])).reshape(n, rows, 128)
    tail = jnp.pad(extras, (0, 128 - extras.shape[0]))
    tail = jnp.broadcast_to(tail, (n, 1, 128))
    spare = -(-(rows + 1) // 8) * 8 - rows - 1
    return jnp.concatenate([main, tail, jnp.zeros((n, spare, 128), main.dtype)], axis=1), rows


def both_sums(plane_parts, depth_parts, plane_row, depth_row):
    nz, ny = plane_parts.shape[0], depth_parts.shape[0]
    f32 = jnp.float32
    dma = pltpu.SemaphoreType.DMA
    return pl.pallas_call(
        functools.partial(both_sums_kernel, nz, ny, plane_row, depth_row),
        out_shape=[jax.ShapeDtypeStruct(plane_parts.shape, f32),
                   jax.ShapeDtypeStruct(depth_parts.shape, f32)],
        in_specs=[pl.BlockSpec(memory_space=pltpu.VMEM)] * 2,
        out_specs=[pl.BlockSpec(memory_space=pltpu.VMEM)] * 2,
        scratch_shapes=[
            pltpu.VMEM(plane_parts.shape, f32),
            pltpu.VMEM(depth_parts.shape, f32),
            pltpu.VMEM(plane_parts.shape[1:], f32),
            pltpu.VMEM(depth_parts.shape[1:], f32),
            pltpu.VMEM(plane_parts.shape, f32),
            pltpu.VMEM(depth_parts.shape, f32),
            [dma((nz,)), dma((nz,)), dma((nz,)), dma((nz,)),
             dma((ny,)), dma((ny,)), dma((ny,)), dma((ny,))],
        ],
        compiler_params=pltpu.CompilerParams(collective_id=1, has_side_effects=True),
    )(plane_parts, depth_parts)


def local(reference_image, deformed, displacement, plane_factors, depth_factors):
    rows, cols = halo_blocks(deformed)
    fields = jnp.einsum("krij,krz->kijz", plane_factors, depth_factors, precision=highest)
    fields = jnp.repeat(fields, KNOT, axis=2)
    residual, prod, mis, sq, energy_parts = strip_sums(
        deformed, rows, cols, displacement, reference_image, fields[0], fields[1])
    prod, mis, sq = node_sums(prod), node_sums(mis), node_sums(sq)
    local_energy = jnp.sum(energy_parts)

    first, second = plane_factors[0], plane_factors[1]
    grad_depth = -jnp.stack([
        jnp.einsum("rij,ijz->rz", first, prod, precision=highest),
        jnp.einsum("rij,ijz->rz", second, mis, precision=highest)])
    first_depth = jnp.einsum("rij,ijz->rz", first * first, sq, precision=highest)
    level_sum = KNOT * KNOT * jnp.sum(second * second, axis=(1, 2))
    grad_plane = -jnp.stack([
        jnp.einsum("rz,ijz->rij", depth_factors[0], prod, precision=highest),
        jnp.einsum("rz,ijz->rij", depth_factors[1], mis, precision=highest)])
    first_diag = jnp.einsum("rz,ijz->rij", depth_factors[0] * depth_factors[0], sq, precision=highest)
    depth_level = KNOT * KNOT * jnp.sum(depth_factors[1] * depth_factors[1], axis=1)

    nz, ny = lax.axis_size("gz"), lax.axis_size("gy")
    plane_terms = jnp.concatenate([grad_plane.reshape(-1), first_diag.reshape(-1)])
    depth_terms = jnp.concatenate([grad_depth.reshape(-1), first_depth.reshape(-1)])
    blank = jnp.zeros((), jnp.float32)
    plane_parts, plane_rows = chunked(plane_terms, jnp.concatenate([depth_level, blank[None]]), nz)
    depth_parts, depth_rows = chunked(depth_terms, jnp.concatenate([level_sum, local_energy[None]]), ny)
    plane_summed, depth_summed = both_sums(plane_parts, depth_parts, plane_rows, depth_rows)
    plane_terms = plane_summed[:, :plane_rows].reshape(-1)
    depth_terms = depth_summed[:, :depth_rows].reshape(-1)
    grad_plane = plane_terms[: grad_plane.size].reshape(grad_plane.shape)
    first_diag = plane_terms[grad_plane.size : grad_plane.size + first_diag.size].reshape(first_diag.shape)
    grad_depth = depth_terms[: grad_depth.size].reshape(grad_depth.shape)
    first_depth = depth_terms[grad_depth.size : grad_depth.size + first_depth.size].reshape(first_depth.shape)
    depth_level = plane_summed[0, plane_rows, :RANK]
    level_sum = depth_summed[0, depth_rows, :RANK]
    energy = plane_summed[0, plane_rows, RANK + 1]

    nodes_x = plane_factors.shape[2]
    nodes_y = plane_factors.shape[3] * lax.axis_size("gy")
    full_z = depth_factors.shape[2] * lax.axis_size("gz")
    diag_plane = jnp.stack(
        [first_diag, jnp.broadcast_to(depth_level[:, None, None], first_diag.shape)])
    lam_plane = damping * RANK * energy / (nodes_x * nodes_y)
    lam_depth = damping * energy / full_z
    step_plane = -grad_plane / (diag_plane + lam_plane + epsilon)
    diag_depth = jnp.stack([first_depth, jnp.broadcast_to(level_sum[:, None], first_depth.shape)])
    step_depth = -grad_depth / (diag_depth + lam_depth + epsilon)
    return (residual, step_plane, step_depth)


def solution(mesh):
    placed = (
        P(None, "gy", "gz"),
        P(None, "gy", "gz"),
        P(None, None, "gy", "gz"),
        P(None, None, None, "gy"),
        P(None, None, "gz"),
    )
    return jax.shard_map(
        local,
        mesh=mesh,
        in_specs=placed,
        out_specs=(P(None, "gy", "gz"), P(None, None, None, "gy"), P(None, None, "gz")),
        check_vma=False,
    )
```

```python
import functools

import jax
import jax.numpy as jnp
from jax import lax
from jax.experimental import pallas as pl
from jax.experimental.pallas import tpu as pltpu
from jax.sharding import PartitionSpec as P

RANK = 32
KNOT = 8

epsilon = 1e-06
damping = 0.01
highest = lax.Precision.HIGHEST

ROWS = 16
LANES = 256
SPAN = 16


def neighbours(part, axis, forward):
    count = lax.axis_size(axis)
    if forward:
        pairs = [(i, i + 1) for i in range(count - 1)]
    else:
        pairs = [(i + 1, i) for i in range(count - 1)]
    return lax.ppermute(part, axis, pairs)


def halo_kernel(ny, nz, rows_ref, cols_ref, rows_out, cols_out, rows_got, cols_got,
                send_sems, recv_sems):
    my, mz = lax.axis_index("gy"), lax.axis_index("gz")
    up, down = lax.rem(my + 1, ny), lax.rem(my + ny - 1, ny)
    right, left = lax.rem(mz + 1, nz), lax.rem(mz + nz - 1, nz)
    plan = [
        (rows_ref.at[0], rows_got.at[0], (down, mz)),
        (rows_ref.at[1], rows_got.at[1], (up, mz)),
        (cols_ref.at[0], cols_got.at[0], (my, left)),
        (cols_ref.at[1], cols_got.at[1], (my, right)),
        (cols_ref.at[0], cols_got.at[2], (down, left)),
        (cols_ref.at[0], cols_got.at[3], (up, left)),
        (cols_ref.at[1], cols_got.at[4], (down, right)),
        (cols_ref.at[1], cols_got.at[5], (up, right)),
    ]
    barrier = pltpu.get_barrier_semaphore()
    for _, _, device in plan:
        pl.semaphore_signal(barrier, inc=1, device_id=device,
                            device_id_type=pl.DeviceIdType.MESH)
    pl.semaphore_wait(barrier, len(plan))
    copies = []
    for k, (source, slot, device) in enumerate(plan):
        copy = pltpu.make_async_remote_copy(
            src_ref=source, dst_ref=slot, send_sem=send_sems.at[k], recv_sem=recv_sems.at[k],
            device_id=device, device_id_type=pl.DeviceIdType.MESH)
        copy.start()
        copies.append(copy)
    for copy in copies:
        copy.wait()
    rows_out[...] = rows_got[...]
    cols_out[...] = cols_got[...]


def swap_halos(rows_send, cols_send):
    ny, nz = lax.axis_size("gy"), lax.axis_size("gz")
    dma = pltpu.SemaphoreType.DMA
    rows_shape = rows_send.shape
    cols_shape = (6,) + cols_send.shape[1:]
    return pl.pallas_call(
        functools.partial(halo_kernel, ny, nz),
        out_shape=[jax.ShapeDtypeStruct(rows_shape, rows_send.dtype),
                   jax.ShapeDtypeStruct(cols_shape, cols_send.dtype)],
        in_specs=[pl.BlockSpec(memory_space=pltpu.VMEM)] * 2,
        out_specs=[pl.BlockSpec(memory_space=pltpu.VMEM)] * 2,
        scratch_shapes=[
            pltpu.VMEM(rows_shape, rows_send.dtype),
            pltpu.VMEM(cols_shape, cols_send.dtype),
            dma((8,)),
            dma((8,)),
        ],
        compiler_params=pltpu.CompilerParams(collective_id=2, has_side_effects=True),
    )(rows_send, cols_send)


def halo_blocks(deformed):
    depth_x, width_y, width_z = deformed.shape
    f32 = jnp.float32
    ny, nz = lax.axis_size("gy"), lax.axis_size("gz")
    my, mz = lax.axis_index("gy"), lax.axis_index("gz")
    rows_send = jnp.stack([deformed[:, 0, :], deformed[:, width_y - 1, :]])
    cols_send = jnp.stack([deformed[:, :, 0], deformed[:, :, width_z - 1]])
    rows_got, cols_got = swap_halos(rows_send, cols_send)
    held = deformed.dtype
    has_up = (my < ny - 1).astype(held)
    has_down = (my > 0).astype(held)
    has_right = (mz < nz - 1).astype(held)
    has_left = (mz > 0).astype(held)
    high_y = rows_got[0] * has_up
    low_y = rows_got[1] * has_down
    high_z = cols_got[0] * has_right
    low_z = cols_got[1] * has_left
    high_high = cols_got[2][:, 0] * (has_up * has_right)
    low_high = cols_got[3][:, width_y - 1] * (has_down * has_right)
    high_low = cols_got[4][:, 0] * (has_up * has_left)
    low_low = cols_got[5][:, width_y - 1] * (has_down * has_left)
    gap_y = jnp.zeros((depth_x, 6, width_z), held)
    rows = jnp.concatenate([high_y[:, None], gap_y, low_y[:, None]], axis=1)
    gap = jnp.zeros((depth_x, 6), held)
    side_high = jnp.concatenate([high_z, high_high[:, None], gap, low_high[:, None]], axis=1)
    side_low = jnp.concatenate([low_z, high_low[:, None], gap, low_low[:, None]], axis=1)
    lanes = lax.broadcasted_iota(jnp.int32, (1, 1, 128), 2)
    cols = jnp.where(lanes == 0, side_high[:, :, None],
                     jnp.where(lanes == 127, side_low[:, :, None], jnp.zeros((), held)))
    return rows, cols


def lerp(base, other, weight):
    return base + weight * (other - base)


def strip_kernel(prev_ref, main_ref, next_ref, rows_ref, cols_ref, disp_ref, image_ref,
                 fields_ref,
                 res_ref, prod_ref, mis_ref, sq_ref, energy_ref, pad_ref, shifts_ref):
    block = pl.program_id(0)
    depth_x = rows_ref.shape[0]
    width_y, width_z = image_ref.shape[1], image_ref.shape[2]
    pad_y, pad_z = pad_ref.shape

    def source_plane(p, plane):
        plane_x = block * SPAN - 1 + p
        valid = jnp.logical_and(plane_x >= 0, plane_x < depth_x)
        safe = jnp.clip(plane_x, 0, depth_x - 1)
        pad_ref[:width_y, :width_z] = plane.astype(jnp.float32)
        pad_ref[width_y:, :width_z] = rows_ref[safe].astype(jnp.float32)
        pad_ref[:, width_z:] = cols_ref[safe].astype(jnp.float32)
        whole = jnp.where(valid, pad_ref[...], 0.0)
        by_y = (pltpu.roll(whole, 1, 0), whole, pltpu.roll(whole, pad_y - 1, 0))
        for b in range(3):
            part = by_y[b][:width_y]
            by_z = (pltpu.roll(part, 1, 1), part, pltpu.roll(part, pad_z - 1, 1))
            for c in range(3):
                shifts_ref[p, 3 * b + c] = by_z[c][:, :width_z]

    source_plane(0, prev_ref[0])

    def inner_plane(p, carry):
        source_plane(p, main_ref[p - 1])
        return carry

    lax.fori_loop(1, SPAN + 1, inner_plane, 0, unroll=4)
    source_plane(SPAN + 1, next_ref[0])

    chunks_y = width_y // ROWS
    chunks_z = width_z // LANES

    def chunk(n, k, energy):
        r0 = pl.multiple_of((k // chunks_z) * ROWS, ROWS)
        c0 = pl.multiple_of((k % chunks_z) * LANES, LANES)
        rs = pl.ds(r0, ROWS)
        cs = pl.ds(c0, LANES)
        j0 = r0 // KNOT
        upper = lax.broadcasted_iota(jnp.int32, (ROWS, LANES), 0) < KNOT
        node = lax.broadcasted_iota(jnp.int32, (KNOT, LANES), 0)

        def node_row(kind, j):
            return jnp.sum(jnp.where(node == j, fields_ref[kind, n, :, cs], 0.0),
                           axis=0, keepdims=True)

        contrast = jnp.where(upper, node_row(0, j0), node_row(0, j0 + 1))
        bright = jnp.where(upper, node_row(1, j0), node_row(1, j0 + 1))

        def plane(step, acc):
            xl = n * KNOT + step
            prod_acc, mis_acc, sq_acc, e_acc = acc

            def src(a, b, c):
                return shifts_ref[xl + 1 + a, 3 * (b + 1) + (c + 1), rs, cs]

            sx = disp_ref[0, xl, rs, cs].astype(jnp.float32)
            sy = disp_ref[1, xl, rs, cs].astype(jnp.float32)
            sz = disp_ref[2, xl, rs, cs].astype(jnp.float32)
            gx, gy, gz = sx > 0, sy > 0, sz > 0
            ax, ay, az = jnp.abs(sx), jnp.abs(sy), jnp.abs(sz)
            xs = {}
            for b in (-1, 0, 1):
                for c in (-1, 0, 1):
                    xs[b, c] = jnp.where(gx, src(1, b, c), src(-1, b, c))
            y0 = {c: jnp.where(gy, src(0, 1, c), src(0, -1, c)) for c in (-1, 0, 1)}
            y1 = {c: jnp.where(gy, xs[1, c], xs[-1, c]) for c in (-1, 0, 1)}
            centre = src(0, 0, 0)
            z00 = jnp.where(gz, src(0, 0, 1), src(0, 0, -1))
            z01 = jnp.where(gz, y0[1], y0[-1])
            z10 = jnp.where(gz, xs[0, 1], xs[0, -1])
            z11 = jnp.where(gz, y1[1], y1[-1])
            l00 = lerp(centre, z00, az)
            l01 = lerp(y0[0], z01, az)
            l10 = lerp(xs[0, 0], z10, az)
            l11 = lerp(y1[0], z11, az)
            m0 = lerp(l00, l01, ay)
            m1 = lerp(l10, l11, ay)
            warped = lerp(m0, m1, ax)
            values = image_ref[xl, rs, cs].astype(jnp.float32)
            misfit = warped - contrast * values - bright
            res_ref[xl, rs, cs] = misfit.astype(res_ref.dtype)
            return (prod_acc + misfit * values, mis_acc + misfit,
                    sq_acc + values * values, e_acc + misfit * misfit)

        zero = jnp.zeros((ROWS, LANES), jnp.float32)
        prod_acc, mis_acc, sq_acc, e_acc = lax.fori_loop(
            0, KNOT, plane, (zero, zero, zero, energy), unroll=4)
        prod_ref[n, rs, cs] = prod_acc
        mis_ref[n, rs, cs] = mis_acc
        sq_ref[n, rs, cs] = sq_acc
        return e_acc

    energy = jnp.zeros((ROWS, LANES), jnp.float32)
    for n in range(SPAN // KNOT):
        energy = lax.fori_loop(0, chunks_y * chunks_z, functools.partial(chunk, n), energy)
    energy_ref[0] = energy


def strip_sums(deformed, rows, cols, displacement, image, fields):
    depth_x, width_y, width_z = image.shape
    nodes = depth_x // KNOT
    steps = depth_x // SPAN
    per = SPAN // KNOT
    f32 = jnp.float32
    block_sum = jax.ShapeDtypeStruct((nodes, width_y, width_z), f32)
    node_spec = pl.BlockSpec((per, width_y, width_z), lambda i: (i, 0, 0))
    plane_spec = pl.BlockSpec((SPAN, width_y, width_z), lambda i: (i, 0, 0))
    return pl.pallas_call(
        strip_kernel,
        grid=(steps,),
        in_specs=[
            pl.BlockSpec((1, width_y, width_z), lambda i: (jnp.maximum(i * SPAN - 1, 0), 0, 0)),
            plane_spec,
            pl.BlockSpec((1, width_y, width_z),
                         lambda i: (jnp.minimum(i * SPAN + SPAN, depth_x - 1), 0, 0)),
            pl.BlockSpec(memory_space=pltpu.VMEM),
            pl.BlockSpec(memory_space=pltpu.VMEM),
            pl.BlockSpec((3, SPAN, width_y, width_z), lambda i: (0, i, 0, 0)),
            plane_spec,
            pl.BlockSpec((2, per) + fields.shape[2:], lambda i: (0, i, 0, 0)),
        ],
        out_specs=[
            plane_spec,
            node_spec,
            node_spec,
            node_spec,
            pl.BlockSpec((1, ROWS, LANES), lambda i: (i, 0, 0)),
        ],
        out_shape=[
            jax.ShapeDtypeStruct(image.shape, jnp.bfloat16),
            block_sum,
            block_sum,
            block_sum,
            jax.ShapeDtypeStruct((steps, ROWS, LANES), f32),
        ],
        scratch_shapes=[
            pltpu.VMEM((width_y + rows.shape[1], width_z + cols.shape[2]), f32),
            pltpu.VMEM((SPAN + 2, 9, width_y, width_z), f32),
        ],
        compiler_params=pltpu.CompilerParams(
            dimension_semantics=("arbitrary",), vmem_limit_bytes=60 * 1024 * 1024),
    )(deformed, deformed, deformed, rows, cols, displacement, image, fields)


def node_sums(field):
    nodes, width_y, width_z = field.shape
    return field.reshape(nodes, width_y // KNOT, KNOT, width_z).sum(axis=2)


def exchange(axis, n, me, d, src, buffer, send_sem, recv_sem):
    target = lax.rem(me + d, n)
    return pltpu.make_async_remote_copy(
        src_ref=src(target), dst_ref=buffer.at[me],
        send_sem=send_sem.at[target], recv_sem=recv_sem.at[me],
        device_id={axis: target}, device_id_type=pl.DeviceIdType.MESH)


def arrival(axis, n, me, d, src_ref, buffer, sem):
    source = lax.rem(me + n - d, n)
    return pltpu.make_async_remote_copy(
        src_ref=src_ref, dst_ref=buffer.at[source],
        send_sem=sem.at[source], recv_sem=sem.at[source],
        device_id={axis: source}, device_id_type=pl.DeviceIdType.MESH)


def both_sums_kernel(nz, ny, plane_row, depth_row, plane_ref, depth_ref, plane_out, depth_out,
                     plane_landed, depth_landed, plane_summed, depth_summed,
                     plane_gathered, depth_gathered, sems):
    mz, my = lax.axis_index("gz"), lax.axis_index("gy")
    barrier = pltpu.get_barrier_semaphore()
    for d in range(1, nz):
        pl.semaphore_signal(barrier, inc=1, device_id={"gz": lax.rem(mz + d, nz)},
                            device_id_type=pl.DeviceIdType.MESH)
    for d in range(1, ny):
        pl.semaphore_signal(barrier, inc=1, device_id={"gy": lax.rem(my + d, ny)},
                            device_id_type=pl.DeviceIdType.MESH)
    pl.semaphore_wait(barrier, nz - 1 + ny - 1)
    zs1, zr1, zs2, zr2, ys1, yr1, ys2, yr2 = sems

    z_out = [exchange("gz", nz, mz, d, lambda t: plane_ref.at[t], plane_landed, zs1, zr1)
             for d in range(1, nz)]
    y_out = [exchange("gy", ny, my, d, lambda t: depth_ref.at[t], depth_landed, ys1, yr1)
             for d in range(1, ny)]
    for copy in z_out + y_out:
        copy.start()
    depth_total = depth_ref[my]
    for d in range(1, ny):
        arrival("gy", ny, my, d, depth_ref.at[0], depth_landed, yr1).wait_recv()
        depth_total = depth_total + depth_landed[lax.rem(my + ny - d, ny)]
    depth_summed[...] = depth_total
    plane_total = plane_ref[mz]
    for d in range(1, nz):
        arrival("gz", nz, mz, d, plane_ref.at[0], plane_landed, zr1).wait_recv()
        plane_total = plane_total + plane_landed[lax.rem(mz + nz - d, nz)]
    rows = lax.broadcasted_iota(jnp.int32, plane_total.shape, 0)
    lanes = lax.broadcasted_iota(jnp.int32, plane_total.shape, 1)
    slot = jnp.logical_and(rows == plane_row, lanes == RANK)
    depth_slot = jnp.logical_and(
        lax.broadcasted_iota(jnp.int32, depth_total.shape, 0) == depth_row,
        lax.broadcasted_iota(jnp.int32, depth_total.shape, 1) == RANK)
    column_energy = jnp.sum(jnp.where(depth_slot, depth_total, 0.0))
    plane_total = jnp.where(slot, column_energy, plane_total)
    plane_summed[...] = plane_total
    for copy in z_out + y_out:
        copy.wait_send()

    z_out = [exchange("gz", nz, mz, d, lambda t: plane_summed, plane_gathered, zs2, zr2)
             for d in range(1, nz)]
    y_out = [exchange("gy", ny, my, d, lambda t: depth_summed, depth_gathered, ys2, yr2)
             for d in range(1, ny)]
    for copy in z_out + y_out:
        copy.start()
    plane_out[mz] = plane_total
    depth_out[my] = depth_total
    for d in range(1, nz):
        arrival("gz", nz, mz, d, plane_summed, plane_gathered, zr2).wait_recv()
        source = lax.rem(mz + nz - d, nz)
        plane_out[source] = plane_gathered[source]
    gathered = plane_out[...]
    chunk_row = lax.broadcasted_iota(jnp.int32, gathered.shape, 1)
    chunk_lane = lax.broadcasted_iota(jnp.int32, gathered.shape, 2)
    total_energy = jnp.sum(jnp.where(
        jnp.logical_and(chunk_row == plane_row, chunk_lane == RANK), gathered, 0.0))
    plane_out[0] = jnp.where(jnp.logical_and(rows == plane_row, lanes == RANK + 1),
                             total_energy, gathered[0])
    for d in range(1, ny):
        arrival("gy", ny, my, d, depth_summed, depth_gathered, yr2).wait_recv()
        source = lax.rem(my + ny - d, ny)
        depth_out[source] = depth_gathered[source]
    for copy in z_out + y_out:
        copy.wait_send()


def chunked(main, extras, n):
    rows = -(-main.shape[0] // (n * 128))
    main = jnp.pad(main, (0, n * rows * 128 - main.shape[0])).reshape(n, rows, 128)
    tail = jnp.pad(extras, (0, 128 - extras.shape[0]))
    tail = jnp.broadcast_to(tail, (n, 1, 128))
    spare = -(-(rows + 1) // 8) * 8 - rows - 1
    return jnp.concatenate([main, tail, jnp.zeros((n, spare, 128), main.dtype)], axis=1), rows


def both_sums(plane_parts, depth_parts, plane_row, depth_row):
    nz, ny = plane_parts.shape[0], depth_parts.shape[0]
    f32 = jnp.float32
    dma = pltpu.SemaphoreType.DMA
    return pl.pallas_call(
        functools.partial(both_sums_kernel, nz, ny, plane_row, depth_row),
        out_shape=[jax.ShapeDtypeStruct(plane_parts.shape, f32),
                   jax.ShapeDtypeStruct(depth_parts.shape, f32)],
        in_specs=[pl.BlockSpec(memory_space=pltpu.VMEM)] * 2,
        out_specs=[pl.BlockSpec(memory_space=pltpu.VMEM)] * 2,
        scratch_shapes=[
            pltpu.VMEM(plane_parts.shape, f32),
            pltpu.VMEM(depth_parts.shape, f32),
            pltpu.VMEM(plane_parts.shape[1:], f32),
            pltpu.VMEM(depth_parts.shape[1:], f32),
            pltpu.VMEM(plane_parts.shape, f32),
            pltpu.VMEM(depth_parts.shape, f32),
            [dma((nz,)), dma((nz,)), dma((nz,)), dma((nz,)),
             dma((ny,)), dma((ny,)), dma((ny,)), dma((ny,))],
        ],
        compiler_params=pltpu.CompilerParams(collective_id=1, has_side_effects=True),
    )(plane_parts, depth_parts)


def local(reference_image, deformed, displacement, plane_factors, depth_factors):
    rows, cols = halo_blocks(deformed)
    fields = jnp.einsum("krij,krz->kijz", plane_factors, depth_factors, precision=highest)
    residual, prod, mis, sq, energy_parts = strip_sums(
        deformed, rows, cols, displacement, reference_image, fields)
    prod, mis, sq = node_sums(prod), node_sums(mis), node_sums(sq)
    local_energy = jnp.sum(energy_parts)

    first, second = plane_factors[0], plane_factors[1]
    grad_depth = -jnp.stack([
        jnp.einsum("rij,ijz->rz", first, prod, precision=highest),
        jnp.einsum("rij,ijz->rz", second, mis, precision=highest)])
    first_depth = jnp.einsum("rij,ijz->rz", first * first, sq, precision=highest)
    level_sum = KNOT * KNOT * jnp.sum(second * second, axis=(1, 2))
    grad_plane = -jnp.stack([
        jnp.einsum("rz,ijz->rij", depth_factors[0], prod, precision=highest),
        jnp.einsum("rz,ijz->rij", depth_factors[1], mis, precision=highest)])
    first_diag = jnp.einsum("rz,ijz->rij", depth_factors[0] * depth_factors[0], sq, precision=highest)
    depth_level = KNOT * KNOT * jnp.sum(depth_factors[1] * depth_factors[1], axis=1)

    nz, ny = lax.axis_size("gz"), lax.axis_size("gy")
    plane_terms = jnp.concatenate([grad_plane.reshape(-1), first_diag.reshape(-1)])
    depth_terms = jnp.concatenate([grad_depth.reshape(-1), first_depth.reshape(-1)])
    blank = jnp.zeros((), jnp.float32)
    plane_parts, plane_rows = chunked(plane_terms, jnp.concatenate([depth_level, blank[None]]), nz)
    depth_parts, depth_rows = chunked(depth_terms, jnp.concatenate([level_sum, local_energy[None]]), ny)
    plane_summed, depth_summed = both_sums(plane_parts, depth_parts, plane_rows, depth_rows)
    plane_terms = plane_summed[:, :plane_rows].reshape(-1)
    depth_terms = depth_summed[:, :depth_rows].reshape(-1)
    grad_plane = plane_terms[: grad_plane.size].reshape(grad_plane.shape)
    first_diag = plane_terms[grad_plane.size : grad_plane.size + first_diag.size].reshape(first_diag.shape)
    grad_depth = depth_terms[: grad_depth.size].reshape(grad_depth.shape)
    first_depth = depth_terms[grad_depth.size : grad_depth.size + first_depth.size].reshape(first_depth.shape)
    depth_level = plane_summed[0, plane_rows, :RANK]
    level_sum = depth_summed[0, depth_rows, :RANK]
    energy = plane_summed[0, plane_rows, RANK + 1]

    nodes_x = plane_factors.shape[2]
    nodes_y = plane_factors.shape[3] * lax.axis_size("gy")
    full_z = depth_factors.shape[2] * lax.axis_size("gz")
    diag_plane = jnp.stack(
        [first_diag, jnp.broadcast_to(depth_level[:, None, None], first_diag.shape)])
    lam_plane = damping * RANK * energy / (nodes_x * nodes_y)
    lam_depth = damping * energy / full_z
    step_plane = -grad_plane / (diag_plane + lam_plane + epsilon)
    diag_depth = jnp.stack([first_depth, jnp.broadcast_to(level_sum[:, None], first_depth.shape)])
    step_depth = -grad_depth / (diag_depth + lam_depth + epsilon)
    return (residual, step_plane, step_depth)


def solution(mesh):
    placed = (
        P(None, "gy", "gz"),
        P(None, "gy", "gz"),
        P(None, None, "gy", "gz"),
        P(None, None, None, "gy"),
        P(None, None, "gz"),
    )
    return jax.shard_map(
        local,
        mesh=mesh,
        in_specs=placed,
        out_specs=(P(None, "gy", "gz"), P(None, None, None, "gy"), P(None, None, "gz")),
        check_vma=False,
    )
```

```python
import functools

import jax
import jax.numpy as jnp
from jax import lax
from jax.experimental import pallas as pl
from jax.experimental.pallas import tpu as pltpu
from jax.sharding import PartitionSpec as P

RANK = 32
KNOT = 8

epsilon = 1e-06
damping = 0.01
highest = lax.Precision.HIGHEST

ROWS = 16
LANES = 256
SPAN = 16


def neighbours(part, axis, forward):
    count = lax.axis_size(axis)
    if forward:
        pairs = [(i, i + 1) for i in range(count - 1)]
    else:
        pairs = [(i + 1, i) for i in range(count - 1)]
    return lax.ppermute(part, axis, pairs)


def halo_kernel(ny, nz, rows_ref, cols_ref, rows_out, cols_out, rows_got, cols_got,
                send_sems, recv_sems):
    my, mz = lax.axis_index("gy"), lax.axis_index("gz")
    up, down = lax.rem(my + 1, ny), lax.rem(my + ny - 1, ny)
    right, left = lax.rem(mz + 1, nz), lax.rem(mz + nz - 1, nz)
    plan = [
        (rows_ref.at[0], rows_got.at[0], (down, mz)),
        (rows_ref.at[1], rows_got.at[1], (up, mz)),
        (cols_ref.at[0], cols_got.at[0], (my, left)),
        (cols_ref.at[1], cols_got.at[1], (my, right)),
        (cols_ref.at[0], cols_got.at[2], (down, left)),
        (cols_ref.at[0], cols_got.at[3], (up, left)),
        (cols_ref.at[1], cols_got.at[4], (down, right)),
        (cols_ref.at[1], cols_got.at[5], (up, right)),
    ]
    barrier = pltpu.get_barrier_semaphore()
    for _, _, device in plan:
        pl.semaphore_signal(barrier, inc=1, device_id=device,
                            device_id_type=pl.DeviceIdType.MESH)
    pl.semaphore_wait(barrier, len(plan))
    copies = []
    for k, (source, slot, device) in enumerate(plan):
        copy = pltpu.make_async_remote_copy(
            src_ref=source, dst_ref=slot, send_sem=send_sems.at[k], recv_sem=recv_sems.at[k],
            device_id=device, device_id_type=pl.DeviceIdType.MESH)
        copy.start()
        copies.append(copy)
    for copy in copies:
        copy.wait()
    rows_out[...] = rows_got[...]
    cols_out[...] = cols_got[...]


def swap_halos(rows_send, cols_send):
    ny, nz = lax.axis_size("gy"), lax.axis_size("gz")
    dma = pltpu.SemaphoreType.DMA
    rows_shape = rows_send.shape
    cols_shape = (6,) + cols_send.shape[1:]
    return pl.pallas_call(
        functools.partial(halo_kernel, ny, nz),
        out_shape=[jax.ShapeDtypeStruct(rows_shape, rows_send.dtype),
                   jax.ShapeDtypeStruct(cols_shape, cols_send.dtype)],
        in_specs=[pl.BlockSpec(memory_space=pltpu.VMEM)] * 2,
        out_specs=[pl.BlockSpec(memory_space=pltpu.VMEM)] * 2,
        scratch_shapes=[
            pltpu.VMEM(rows_shape, rows_send.dtype),
            pltpu.VMEM(cols_shape, cols_send.dtype),
            dma((8,)),
            dma((8,)),
        ],
        compiler_params=pltpu.CompilerParams(collective_id=2, has_side_effects=True),
    )(rows_send, cols_send)


def halo_blocks(deformed):
    depth_x, width_y, width_z = deformed.shape
    f32 = jnp.float32
    ny, nz = lax.axis_size("gy"), lax.axis_size("gz")
    my, mz = lax.axis_index("gy"), lax.axis_index("gz")
    rows_send = jnp.stack([deformed[:, 0, :], deformed[:, width_y - 1, :]])
    cols_send = jnp.stack([deformed[:, :, 0], deformed[:, :, width_z - 1]])
    rows_got, cols_got = swap_halos(rows_send, cols_send)
    held = deformed.dtype
    has_up = (my < ny - 1).astype(held)
    has_down = (my > 0).astype(held)
    has_right = (mz < nz - 1).astype(held)
    has_left = (mz > 0).astype(held)
    high_y = rows_got[0] * has_up
    low_y = rows_got[1] * has_down
    high_z = cols_got[0] * has_right
    low_z = cols_got[1] * has_left
    high_high = cols_got[2][:, 0] * (has_up * has_right)
    low_high = cols_got[3][:, width_y - 1] * (has_down * has_right)
    high_low = cols_got[4][:, 0] * (has_up * has_left)
    low_low = cols_got[5][:, width_y - 1] * (has_down * has_left)
    gap_y = jnp.zeros((depth_x, 6, width_z), held)
    rows = jnp.concatenate([high_y[:, None], gap_y, low_y[:, None]], axis=1)
    gap = jnp.zeros((depth_x, 6), held)
    side_high = jnp.concatenate([high_z, high_high[:, None], gap, low_high[:, None]], axis=1)
    side_low = jnp.concatenate([low_z, high_low[:, None], gap, low_low[:, None]], axis=1)
    lanes = lax.broadcasted_iota(jnp.int32, (1, 1, 128), 2)
    cols = jnp.where(lanes == 0, side_high[:, :, None],
                     jnp.where(lanes == 127, side_low[:, :, None], jnp.zeros((), held)))
    return rows, cols


def lerp(base, other, weight):
    return base + weight * (other - base)


def strip_kernel(prev_ref, main_ref, next_ref, rows_ref, cols_ref, disp_ref, image_ref,
                 contrast_ref, bright_ref,
                 res_ref, prod_ref, mis_ref, sq_ref, energy_ref, pad_ref, shifts_ref):
    block = pl.program_id(0)
    depth_x = rows_ref.shape[0]
    width_y, width_z = image_ref.shape[1], image_ref.shape[2]
    pad_y, pad_z = pad_ref.shape

    def source_plane(p, plane):
        plane_x = block * SPAN - 1 + p
        valid = jnp.logical_and(plane_x >= 0, plane_x < depth_x)
        safe = jnp.clip(plane_x, 0, depth_x - 1)
        pad_ref[:width_y, :width_z] = plane.astype(jnp.float32)
        pad_ref[width_y:, :width_z] = rows_ref[safe].astype(jnp.float32)
        pad_ref[:, width_z:] = cols_ref[safe].astype(jnp.float32)
        whole = jnp.where(valid, pad_ref[...], 0.0)
        by_y = (pltpu.roll(whole, 1, 0), whole, pltpu.roll(whole, pad_y - 1, 0))
        for b in range(3):
            part = by_y[b][:width_y]
            by_z = (pltpu.roll(part, 1, 1), part, pltpu.roll(part, pad_z - 1, 1))
            for c in range(3):
                shifts_ref[p, 3 * b + c] = by_z[c][:, :width_z]

    source_plane(0, prev_ref[0])

    def inner_plane(p, carry):
        source_plane(p, main_ref[p - 1])
        return carry

    lax.fori_loop(1, SPAN + 1, inner_plane, 0, unroll=8)
    source_plane(SPAN + 1, next_ref[0])

    chunks_y = width_y // ROWS
    chunks_z = width_z // LANES

    def chunk(n, k, energy):
        r0 = pl.multiple_of((k // chunks_z) * ROWS, ROWS)
        c0 = pl.multiple_of((k % chunks_z) * LANES, LANES)
        rs = pl.ds(r0, ROWS)
        cs = pl.ds(c0, LANES)
        contrast = contrast_ref[n, rs, cs]
        bright = bright_ref[n, rs, cs]

        def plane(step, acc):
            xl = n * KNOT + step
            prod_acc, mis_acc, sq_acc, e_acc = acc

            def src(a, b, c):
                return shifts_ref[xl + 1 + a, 3 * (b + 1) + (c + 1), rs, cs]

            sx = disp_ref[0, xl, rs, cs].astype(jnp.float32)
            sy = disp_ref[1, xl, rs, cs].astype(jnp.float32)
            sz = disp_ref[2, xl, rs, cs].astype(jnp.float32)
            gx, gy, gz = sx > 0, sy > 0, sz > 0
            ax, ay, az = jnp.abs(sx), jnp.abs(sy), jnp.abs(sz)
            xs = {}
            for b in (-1, 0, 1):
                for c in (-1, 0, 1):
                    xs[b, c] = jnp.where(gx, src(1, b, c), src(-1, b, c))
            y0 = {c: jnp.where(gy, src(0, 1, c), src(0, -1, c)) for c in (-1, 0, 1)}
            y1 = {c: jnp.where(gy, xs[1, c], xs[-1, c]) for c in (-1, 0, 1)}
            centre = src(0, 0, 0)
            z00 = jnp.where(gz, src(0, 0, 1), src(0, 0, -1))
            z01 = jnp.where(gz, y0[1], y0[-1])
            z10 = jnp.where(gz, xs[0, 1], xs[0, -1])
            z11 = jnp.where(gz, y1[1], y1[-1])
            l00 = lerp(centre, z00, az)
            l01 = lerp(y0[0], z01, az)
            l10 = lerp(xs[0, 0], z10, az)
            l11 = lerp(y1[0], z11, az)
            m0 = lerp(l00, l01, ay)
            m1 = lerp(l10, l11, ay)
            warped = lerp(m0, m1, ax)
            values = image_ref[xl, rs, cs].astype(jnp.float32)
            misfit = warped - contrast * values - bright
            res_ref[xl, rs, cs] = misfit.astype(res_ref.dtype)
            return (prod_acc + misfit * values, mis_acc + misfit,
                    sq_acc + values * values, e_acc + misfit * misfit)

        zero = jnp.zeros((ROWS, LANES), jnp.float32)
        prod_acc, mis_acc, sq_acc, e_acc = lax.fori_loop(
            0, KNOT, plane, (zero, zero, zero, energy), unroll=4)
        prod_ref[n, rs, cs] = prod_acc
        mis_ref[n, rs, cs] = mis_acc
        sq_ref[n, rs, cs] = sq_acc
        return e_acc

    energy = jnp.zeros((ROWS, LANES), jnp.float32)
    for n in range(SPAN // KNOT):
        energy = lax.fori_loop(0, chunks_y * chunks_z, functools.partial(chunk, n), energy)
    energy_ref[0] = energy


def strip_sums(deformed, rows, cols, displacement, image, contrast_y, bright_y):
    depth_x, width_y, width_z = image.shape
    nodes = depth_x // KNOT
    steps = depth_x // SPAN
    per = SPAN // KNOT
    f32 = jnp.float32
    block_sum = jax.ShapeDtypeStruct((nodes, width_y, width_z), f32)
    node_spec = pl.BlockSpec((per, width_y, width_z), lambda i: (i, 0, 0))
    plane_spec = pl.BlockSpec((SPAN, width_y, width_z), lambda i: (i, 0, 0))
    return pl.pallas_call(
        strip_kernel,
        grid=(steps,),
        in_specs=[
            pl.BlockSpec((1, width_y, width_z), lambda i: (jnp.maximum(i * SPAN - 1, 0), 0, 0)),
            plane_spec,
            pl.BlockSpec((1, width_y, width_z),
                         lambda i: (jnp.minimum(i * SPAN + SPAN, depth_x - 1), 0, 0)),
            pl.BlockSpec(memory_space=pltpu.VMEM),
            pl.BlockSpec(memory_space=pltpu.VMEM),
            pl.BlockSpec((3, SPAN, width_y, width_z), lambda i: (0, i, 0, 0)),
            plane_spec,
            node_spec,
            node_spec,
        ],
        out_specs=[
            plane_spec,
            node_spec,
            node_spec,
            node_spec,
            pl.BlockSpec((1, ROWS, LANES), lambda i: (i, 0, 0)),
        ],
        out_shape=[
            jax.ShapeDtypeStruct(image.shape, jnp.bfloat16),
            block_sum,
            block_sum,
            block_sum,
            jax.ShapeDtypeStruct((steps, ROWS, LANES), f32),
        ],
        scratch_shapes=[
            pltpu.VMEM((width_y + rows.shape[1], width_z + cols.shape[2]), f32),
            pltpu.VMEM((SPAN + 2, 9, width_y, width_z), f32),
        ],
        compiler_params=pltpu.CompilerParams(
            dimension_semantics=("arbitrary",), vmem_limit_bytes=60 * 1024 * 1024),
    )(deformed, deformed, deformed, rows, cols, displacement, image, contrast_y, bright_y)


def node_sums(field):
    nodes, width_y, width_z = field.shape
    return field.reshape(nodes, width_y // KNOT, KNOT, width_z).sum(axis=2)


def exchange(axis, n, me, d, src, buffer, send_sem, recv_sem):
    target = lax.rem(me + d, n)
    return pltpu.make_async_remote_copy(
        src_ref=src(target), dst_ref=buffer.at[me],
        send_sem=send_sem.at[target], recv_sem=recv_sem.at[me],
        device_id={axis: target}, device_id_type=pl.DeviceIdType.MESH)


def arrival(axis, n, me, d, src_ref, buffer, sem):
    source = lax.rem(me + n - d, n)
    return pltpu.make_async_remote_copy(
        src_ref=src_ref, dst_ref=buffer.at[source],
        send_sem=sem.at[source], recv_sem=sem.at[source],
        device_id={axis: source}, device_id_type=pl.DeviceIdType.MESH)


def both_sums_kernel(nz, ny, plane_row, depth_row, plane_ref, depth_ref, plane_out, depth_out,
                     plane_landed, depth_landed, plane_summed, depth_summed,
                     plane_gathered, depth_gathered, sems):
    mz, my = lax.axis_index("gz"), lax.axis_index("gy")
    barrier = pltpu.get_barrier_semaphore()
    for d in range(1, nz):
        pl.semaphore_signal(barrier, inc=1, device_id={"gz": lax.rem(mz + d, nz)},
                            device_id_type=pl.DeviceIdType.MESH)
    for d in range(1, ny):
        pl.semaphore_signal(barrier, inc=1, device_id={"gy": lax.rem(my + d, ny)},
                            device_id_type=pl.DeviceIdType.MESH)
    pl.semaphore_wait(barrier, nz - 1 + ny - 1)
    zs1, zr1, zs2, zr2, ys1, yr1, ys2, yr2 = sems

    z_out = [exchange("gz", nz, mz, d, lambda t: plane_ref.at[t], plane_landed, zs1, zr1)
             for d in range(1, nz)]
    y_out = [exchange("gy", ny, my, d, lambda t: depth_ref.at[t], depth_landed, ys1, yr1)
             for d in range(1, ny)]
    for copy in z_out + y_out:
        copy.start()
    depth_total = depth_ref[my]
    for d in range(1, ny):
        arrival("gy", ny, my, d, depth_ref.at[0], depth_landed, yr1).wait_recv()
        depth_total = depth_total + depth_landed[lax.rem(my + ny - d, ny)]
    depth_summed[...] = depth_total
    plane_total = plane_ref[mz]
    for d in range(1, nz):
        arrival("gz", nz, mz, d, plane_ref.at[0], plane_landed, zr1).wait_recv()
        plane_total = plane_total + plane_landed[lax.rem(mz + nz - d, nz)]
    rows = lax.broadcasted_iota(jnp.int32, plane_total.shape, 0)
    lanes = lax.broadcasted_iota(jnp.int32, plane_total.shape, 1)
    slot = jnp.logical_and(rows == plane_row, lanes == RANK)
    depth_slot = jnp.logical_and(
        lax.broadcasted_iota(jnp.int32, depth_total.shape, 0) == depth_row,
        lax.broadcasted_iota(jnp.int32, depth_total.shape, 1) == RANK)
    column_energy = jnp.sum(jnp.where(depth_slot, depth_total, 0.0))
    plane_total = jnp.where(slot, column_energy, plane_total)
    plane_summed[...] = plane_total
    for copy in z_out + y_out:
        copy.wait_send()

    z_out = [exchange("gz", nz, mz, d, lambda t: plane_summed, plane_gathered, zs2, zr2)
             for d in range(1, nz)]
    y_out = [exchange("gy", ny, my, d, lambda t: depth_summed, depth_gathered, ys2, yr2)
             for d in range(1, ny)]
    for copy in z_out + y_out:
        copy.start()
    plane_out[mz] = plane_total
    depth_out[my] = depth_total
    for d in range(1, nz):
        arrival("gz", nz, mz, d, plane_summed, plane_gathered, zr2).wait_recv()
        source = lax.rem(mz + nz - d, nz)
        plane_out[source] = plane_gathered[source]
    gathered = plane_out[...]
    chunk_row = lax.broadcasted_iota(jnp.int32, gathered.shape, 1)
    chunk_lane = lax.broadcasted_iota(jnp.int32, gathered.shape, 2)
    total_energy = jnp.sum(jnp.where(
        jnp.logical_and(chunk_row == plane_row, chunk_lane == RANK), gathered, 0.0))
    plane_out[0] = jnp.where(jnp.logical_and(rows == plane_row, lanes == RANK + 1),
                             total_energy, gathered[0])
    for d in range(1, ny):
        arrival("gy", ny, my, d, depth_summed, depth_gathered, yr2).wait_recv()
        source = lax.rem(my + ny - d, ny)
        depth_out[source] = depth_gathered[source]
    for copy in z_out + y_out:
        copy.wait_send()


def chunked(main, extras, n):
    rows = -(-main.shape[0] // (n * 128))
    main = jnp.pad(main, (0, n * rows * 128 - main.shape[0])).reshape(n, rows, 128)
    tail = jnp.pad(extras, (0, 128 - extras.shape[0]))
    tail = jnp.broadcast_to(tail, (n, 1, 128))
    spare = -(-(rows + 1) // 8) * 8 - rows - 1
    return jnp.concatenate([main, tail, jnp.zeros((n, spare, 128), main.dtype)], axis=1), rows


def both_sums(plane_parts, depth_parts, plane_row, depth_row):
    nz, ny = plane_parts.shape[0], depth_parts.shape[0]
    f32 = jnp.float32
    dma = pltpu.SemaphoreType.DMA
    return pl.pallas_call(
        functools.partial(both_sums_kernel, nz, ny, plane_row, depth_row),
        out_shape=[jax.ShapeDtypeStruct(plane_parts.shape, f32),
                   jax.ShapeDtypeStruct(depth_parts.shape, f32)],
        in_specs=[pl.BlockSpec(memory_space=pltpu.VMEM)] * 2,
        out_specs=[pl.BlockSpec(memory_space=pltpu.VMEM)] * 2,
        scratch_shapes=[
            pltpu.VMEM(plane_parts.shape, f32),
            pltpu.VMEM(depth_parts.shape, f32),
            pltpu.VMEM(plane_parts.shape[1:], f32),
            pltpu.VMEM(depth_parts.shape[1:], f32),
            pltpu.VMEM(plane_parts.shape, f32),
            pltpu.VMEM(depth_parts.shape, f32),
            [dma((nz,)), dma((nz,)), dma((nz,)), dma((nz,)),
             dma((ny,)), dma((ny,)), dma((ny,)), dma((ny,))],
        ],
        compiler_params=pltpu.CompilerParams(collective_id=1, has_side_effects=True),
    )(plane_parts, depth_parts)


def local(reference_image, deformed, displacement, plane_factors, depth_factors):
    rows, cols = halo_blocks(deformed)
    fields = jnp.einsum("krij,krz->kijz", plane_factors, depth_factors, precision=highest)
    fields = jnp.repeat(fields, KNOT, axis=2)
    residual, prod, mis, sq, energy_parts = strip_sums(
        deformed, rows, cols, displacement, reference_image, fields[0], fields[1])
    prod, mis, sq = node_sums(prod), node_sums(mis), node_sums(sq)
    local_energy = jnp.sum(energy_parts)

    first, second = plane_factors[0], plane_factors[1]
    grad_depth = -jnp.stack([
        jnp.einsum("rij,ijz->rz", first, prod, precision=highest),
        jnp.einsum("rij,ijz->rz", second, mis, precision=highest)])
    first_depth = jnp.einsum("rij,ijz->rz", first * first, sq, precision=highest)
    level_sum = KNOT * KNOT * jnp.sum(second * second, axis=(1, 2))
    grad_plane = -jnp.stack([
        jnp.einsum("rz,ijz->rij", depth_factors[0], prod, precision=highest),
        jnp.einsum("rz,ijz->rij", depth_factors[1], mis, precision=highest)])
    first_diag = jnp.einsum("rz,ijz->rij", depth_factors[0] * depth_factors[0], sq, precision=highest)
    depth_level = KNOT * KNOT * jnp.sum(depth_factors[1] * depth_factors[1], axis=1)

    nz, ny = lax.axis_size("gz"), lax.axis_size("gy")
    plane_terms = jnp.concatenate([grad_plane.reshape(-1), first_diag.reshape(-1)])
    depth_terms = jnp.concatenate([grad_depth.reshape(-1), first_depth.reshape(-1)])
    blank = jnp.zeros((), jnp.float32)
    plane_parts, plane_rows = chunked(plane_terms, jnp.concatenate([depth_level, blank[None]]), nz)
    depth_parts, depth_rows = chunked(depth_terms, jnp.concatenate([level_sum, local_energy[None]]), ny)
    plane_summed, depth_summed = both_sums(plane_parts, depth_parts, plane_rows, depth_rows)
    plane_terms = plane_summed[:, :plane_rows].reshape(-1)
    depth_terms = depth_summed[:, :depth_rows].reshape(-1)
    grad_plane = plane_terms[: grad_plane.size].reshape(grad_plane.shape)
    first_diag = plane_terms[grad_plane.size : grad_plane.size + first_diag.size].reshape(first_diag.shape)
    grad_depth = depth_terms[: grad_depth.size].reshape(grad_depth.shape)
    first_depth = depth_terms[grad_depth.size : grad_depth.size + first_depth.size].reshape(first_depth.shape)
    depth_level = plane_summed[0, plane_rows, :RANK]
    level_sum = depth_summed[0, depth_rows, :RANK]
    energy = plane_summed[0, plane_rows, RANK + 1]

    nodes_x = plane_factors.shape[2]
    nodes_y = plane_factors.shape[3] * lax.axis_size("gy")
    full_z = depth_factors.shape[2] * lax.axis_size("gz")
    diag_plane = jnp.stack(
        [first_diag, jnp.broadcast_to(depth_level[:, None, None], first_diag.shape)])
    lam_plane = damping * RANK * energy / (nodes_x * nodes_y)
    lam_depth = damping * energy / full_z
    step_plane = -grad_plane / (diag_plane + lam_plane + epsilon)
    diag_depth = jnp.stack([first_depth, jnp.broadcast_to(level_sum[:, None], first_depth.shape)])
    step_depth = -grad_depth / (diag_depth + lam_depth + epsilon)
    return (residual, step_plane, step_depth)


def solution(mesh):
    placed = (
        P(None, "gy", "gz"),
        P(None, "gy", "gz"),
        P(None, None, "gy", "gz"),
        P(None, None, None, "gy"),
        P(None, None, "gz"),
    )
    return jax.shard_map(
        local,
        mesh=mesh,
        in_specs=placed,
        out_specs=(P(None, "gy", "gz"), P(None, None, None, "gy"), P(None, None, "gz")),
        check_vma=False,
    )
```
